32 devices in a mesh: seq: 8 (over z, y), exp: 4 (over x, core).
Axes of the slice: x: 2, y: 2, z: 4, core: 2. Of those that a mesh axis runs over, the one named last changes fastest.
Arguments:
- tokens: bfloat16 [32, 1024, 768], P('exp', 'seq'), may hold values from -6 to 6
- segment_ids: int32 [32, 1024], P('exp', 'seq'), may hold values from 0 to 3, never falling along the last dimension, each value on 1 to 512 neighbouring positions
- routes: int32 [32, 1024], P('exp', 'seq'), may hold values from 0 to 3, as said below
- slot_index: int32 [32, 1024], P('exp', 'seq'), may hold values from 0 to 320, as said below
- norm_gain: bfloat16 [768], P('exp'), may hold values from 0.5 to 1.5
- in_proj: bfloat16 [768, 3072], P(None, 'exp'), may hold values from -0.21875 to 0.21875
- conv_weight: bfloat16 [4, 1536], P(None, 'exp'), may hold values from -3 to 3
- conv_bias: bfloat16 [1536], P('exp'), may hold values from -3 to 3
- x_proj: bfloat16 [1536, 80], P('exp'), may hold values from -0.15625 to 0.15625
- dt_proj: bfloat16 [48, 1536], P(None, 'exp'), may hold values from -0.875 to 0.875
- dt_bias: bfloat16 [1536], P('exp'), may hold values from -4.5 to -2.5
- a_log: bfloat16 [1536, 16], P('exp'), may hold values from -9 to 1.5
- d_skip: bfloat16 [1536], P('exp'), may hold values from 0.5 to 1.5
- out_proj: bfloat16 [1536, 768], P('exp'), may hold values from -0.3125 to 0.3125
- moe_gain: bfloat16 [768], P('exp'), may hold values from 0.5 to 1.5
- router: bfloat16 [768, 4], P('exp'), may hold values from -0.15625 to 0.15625
- expert_up: bfloat16 [4, 768, 3072], P('exp'), may hold values from -0.21875 to 0.21875
- expert_down: bfloat16 [4, 3072, 768], P('exp'), may hold values from -0.625 to 0.625
- cotangent: bfloat16 [32, 1024, 768], P('exp', 'seq'), may hold values from -6 to 6
Outputs:
- block_out: bfloat16 [32, 1024, 768], P('exp', 'seq')
- tokens_grad: float32 [32, 1024, 768], P('exp', 'seq')
- norm_gain_grad: float32 [768], P('exp')
- in_proj_grad: float32 [768, 3072], P(None, 'exp')
- conv_weight_grad: float32 [4, 1536], P(None, 'exp')
- conv_bias_grad: float32 [1536], P('exp')
- x_proj_grad: float32 [1536, 80], P('exp')
- dt_proj_grad: float32 [48, 1536], P(None, 'exp')
- dt_bias_grad: float32 [1536], P('exp')
- a_log_grad: float32 [1536, 16], P('exp')
- d_skip_grad: float32 [1536], P('exp')
- out_proj_grad: float32 [1536, 768], P('exp')
- moe_gain_grad: float32 [768], P('exp')
- router_grad: float32 [768, 4], P('exp')
- expert_up_grad: float32 [4, 768, 3072], P('exp')
- expert_down_grad: float32 [4, 3072, 768], P('exp')
The draws below stay inside these ranges and needn't reach their ends.
Inputs may be any that keep to these rules, and one draw needn't show every extreme that they name: `routes`: the expert that each token goes to. `slot_index`: the rank of the token, counted in order of sequence and then position, among the tokens of its device's block of 8 sequences by 128 positions that go to the same expert; 320 where that rank is 320 or more, and the token is dropped.
All inputs are finite; a program needn't handle non-finite values.
Results may differ from the reference program's by a relative error of at most 0.02.
Values may be sent and summed in bfloat16 or wider, within the bound.
A program may use at most 384 MiB of HBM per device.

```python
import math
import jax
import jax.numpy as jnp
import numpy as np
from jax import lax

D = 768
DI = 1536
NSTATE = 16
RANK = 48
KCONV = 4
FF = 3072
EXPERTS = 4
SEQ_DEV = 8
SEQ_PART = 128
LEN = 1024
SEQS = 32
CAP = 320
DOCS = 4


def route_table(key):
    blocks_exp = SEQS // SEQ_DEV
    blocks_seq = LEN // SEQ_PART
    block_rows = SEQ_DEV * SEQ_PART
    own_key = jax.random.fold_in(key, 7)
    drawn = jax.random.randint(jax.random.fold_in(own_key, 1), (blocks_exp, blocks_seq, block_rows), 0, EXPERTS + 2)
    favored = jax.random.randint(jax.random.fold_in(own_key, 2), (blocks_exp, blocks_seq, 1), 0, EXPERTS)
    route_vals = jnp.where(drawn >= EXPERTS, favored, drawn).astype(jnp.int32)
    onehot = (route_vals[..., None] == jnp.arange(EXPERTS)[None, None, None, :]).astype(jnp.int32)
    ranks = jnp.sum((jnp.cumsum(onehot, axis=2) - 1) * onehot, -1)
    capacity = 5 * SEQ_DEV * SEQ_PART // (4 * EXPERTS)
    slot_vals = jnp.minimum(ranks, capacity).astype(jnp.int32)

    def unblock(values):
        values = values.reshape(blocks_exp, blocks_seq, SEQ_DEV, SEQ_PART)
        return jnp.transpose(values, (0, 2, 1, 3)).reshape(SEQS, LEN)
    return (unblock(route_vals), unblock(slot_vals))


def draw_routes(key, part):
    return route_table(key)[0]


def draw_slot_index(key, part):
    return route_table(key)[1]


def steps_of(key, extent, split, smallest, largest):
    factor_of = 1.0
    for axis_at, shards_of in split:
        steps = jax.random.uniform(jax.random.fold_in(jax.random.fold_in(key, 6), axis_at), (shards_of,), jnp.float32, smallest / len(split), largest / len(split))
        factor_of = factor_of * jnp.repeat(jnp.exp(steps), extent[axis_at] // shards_of).reshape((-1,) + (1,) * (len(extent) - 1 - axis_at))
    return factor_of


def length_profile(amount, total, reach, skew):
    loads = [(1 << 20) // math.isqrt(grade ** skew) + 1 for grade in range(2, amount + 1)]
    spare, counts = total - reach - (amount - 1), [1] * (amount - 1)
    while spare > 0:
        movable = [i for i in range(amount - 1) if counts[i] < reach]
        whole, left = sum([loads[i] for i in movable]), spare
        for i in movable:
            extra = min(reach - counts[i], max(1, left * loads[i] // whole), spare)
            counts[i] = counts[i] + extra
            spare = spare - extra
    return np.array([reach] + counts)


def uneven(rng, count, total, limit, slope):
    if count == 2:
        one = jax.random.randint(rng, (), max(1, total - limit), min(limit, total - 1) + 1)
        return jnp.stack([one, total - one])
    sizes = jnp.asarray(length_profile(count, total, limit, slope), jnp.int32)
    pairs = (count - 1) // 2
    giver, sink = sizes[1:1 + 2 * pairs:2], sizes[2:2 + 2 * pairs:2]
    slack = jnp.minimum(giver - 1, limit - sink)
    shifted = jax.random.randint(jax.random.fold_in(rng, 1), (pairs,), 0, 1 << 20) % (slack + 1)
    sizes = sizes.at[1:1 + 2 * pairs:2].set(giver - shifted).at[2:2 + 2 * pairs:2].set(sink + shifted)
    return sizes[jax.random.permutation(jax.random.fold_in(rng, 2), count)]


def normal_values(key, shape, scale, bound, pieces=(), kind=jnp.bfloat16):
    level = steps_of(key, shape, pieces, -0.22, 0.18) if pieces else 1.0
    values = jax.random.normal(key, shape, jnp.float32) * scale * level
    return jnp.minimum(jnp.maximum(values, -bound), bound).astype(kind)


def setup_inputs(seed: int = 0) -> dict:
    seeds = jax.random.split(jax.random.key(seed), 20)
    tokens = normal_values(seeds[0], (SEQS, LEN, D), 1.0, 6.0, ((0, 4), (1, 8)))
    segment_ids = jax.vmap(lambda own: jnp.searchsorted(jnp.cumsum(uneven(own, DOCS, LEN, LEN // 2, 0)), jnp.arange(LEN), side="right"))(jax.random.split(seeds[1], SEQS)).reshape((SEQS, LEN)).astype(jnp.int32)
    routes = draw_routes(jax.random.fold_in(seeds[19], 71), 0)
    slot_index = draw_slot_index(jax.random.fold_in(seeds[19], 71), 0)
    norm_gain = jnp.clip(1.0 + 0.1 * jax.random.normal(seeds[4], (D,), jnp.float32), 0.5, 1.5).astype(jnp.bfloat16)
    in_proj = normal_values(seeds[5], (D, 2 * DI), D ** -0.5, 0.21875, ((1, 4),))
    conv_weight = normal_values(seeds[6], (KCONV, DI), KCONV ** -0.5, 3.0, ((1, 4),))
    conv_bias = normal_values(seeds[7], (DI,), 0.5, 3.0, ((0, 4),))
    x_proj = normal_values(seeds[8], (DI, RANK + 2 * NSTATE), DI ** -0.5, 0.15625, ((0, 4),))
    dt_proj = normal_values(seeds[9], (RANK, DI), RANK ** -0.5, 0.875, ((1, 4),))
    dt_bias = jnp.clip(-4.5 + 2.0 * jax.random.uniform(seeds[10], (DI,), jnp.float32) ** steps_of(seeds[10], (DI,), ((0, 4),), -0.2, 0.2), -4.5, -2.5).astype(jnp.bfloat16)
    a_log = jnp.clip(-9.0 + 10.5 * jax.random.uniform(seeds[11], (DI, NSTATE), jnp.float32) ** steps_of(seeds[11], (DI, NSTATE), ((0, 4),), -0.2, 0.2), -9.0, 1.5).astype(jnp.bfloat16)
    d_skip = jnp.clip(0.5 + 1.0 * jax.random.uniform(seeds[12], (DI,), jnp.float32) ** steps_of(seeds[12], (DI,), ((0, 4),), -0.2, 0.2), 0.5, 1.5).astype(jnp.bfloat16)
    out_proj = normal_values(seeds[13], (DI, D), (DI // 4) ** -0.5, 0.3125, ((0, 4),))
    moe_gain = jnp.clip(1.0 + 0.1 * jax.random.normal(seeds[14], (D,), jnp.float32), 0.5, 1.5).astype(jnp.bfloat16)
    router = normal_values(seeds[15], (D, EXPERTS), (2 * D) ** -0.5, 0.15625, ((0, 4),))
    expert_up = normal_values(seeds[16], (EXPERTS, D, FF), D ** -0.5, 0.21875, ((0, 4),))
    expert_down = normal_values(seeds[17], (EXPERTS, FF, D), (FF // 32) ** -0.5, 0.625, ((0, 4),))
    cotangent = normal_values(seeds[18], (SEQS, LEN, D), 1.0, 6.0, ((0, 4), (1, 8)))
    return dict(tokens=tokens, segment_ids=segment_ids, routes=routes, slot_index=slot_index, norm_gain=norm_gain, in_proj=in_proj, conv_weight=conv_weight, conv_bias=conv_bias, x_proj=x_proj, dt_proj=dt_proj, dt_bias=dt_bias, a_log=a_log, d_skip=d_skip, out_proj=out_proj, moe_gain=moe_gain, router=router, expert_up=expert_up, expert_down=expert_down, cotangent=cotangent)


@jax.custom_vjp
def low(v):
    return lax.optimization_barrier(v.astype(jnp.bfloat16)).astype(jnp.float32)

@jax.custom_vjp
def low_back(v):
    return v

def low_keep(v):
    return (low(v), None)

def low_pass(kept, grad):
    return (grad,)

def back_keep(v):
    return (v, None)

def back_low(kept, grad):
    return (low(grad),)
low.defvjp(low_keep, low_pass)
low_back.defvjp(back_keep, back_low)
epsilon = 1e-05
highest = lax.Precision.HIGHEST

def matmul(left, right):
    return jnp.matmul(left, right, precision=highest)

def rms_norm(values, gain):
    return values * lax.rsqrt(lax.optimization_barrier(jnp.mean(values * values, -1, keepdims=True)) + epsilon) * gain

def scan_step(state, item, a_mat):
    step_t, b_t, c_t, x_t, keep_t = item
    decay = jnp.exp(step_t[:, :, None] * a_mat) * keep_t[:, None, None]
    state = decay * state + (step_t * x_t)[:, :, None] * b_t[:, None, :]
    return (state, lax.optimization_barrier(jnp.sum(state * c_t[:, None, :], -1)))

def selective_scan(step_size, b_rows, c_rows, conv_value, keep_mask, a_mat):
    seq_count, length = (step_size.shape[0], step_size.shape[1])

    def to_blocks(values):
        values = jnp.moveaxis(values, 1, 0)
        return values.reshape((length // 8, 8) + values.shape[1:])
    items = tuple((to_blocks(v) for v in (step_size, b_rows, c_rows, conv_value, keep_mask)))

    def run_block(carry, item):
        return lax.scan(lambda state, entry: scan_step(state, entry, a_mat), carry, item)
    start = jnp.zeros((seq_count, a_mat.shape[0], a_mat.shape[1]), jnp.float32)
    unused, outputs = lax.scan(jax.checkpoint(run_block), start, items)
    return jnp.moveaxis(outputs.reshape((length,) + outputs.shape[2:]), 0, 1)

def expert_apply(item):
    rows_in, up_w, down_w = item
    pre_act = low_back(matmul(rows_in, up_w))
    active = low(jax.nn.gelu(pre_act, approximate=False))
    return low(low_back(matmul(active, down_w)))

def forward(tokens, norm_gain, in_proj, conv_weight, conv_bias, x_proj, dt_proj, dt_bias, a_log, d_skip, out_proj, moe_gain, router, expert_up, expert_down, segment_ids, routes, slot_index):
    seq_count, length, width = tokens.shape
    inner = out_proj.shape[0]
    normed = low(rms_norm(tokens, norm_gain))
    projected = low_back(matmul(normed, in_proj))
    conv_input = low(projected[..., :inner])
    gate_pre = projected[..., inner:]
    doc_ids = (segment_ids + 1).astype(jnp.float32)
    ext_ids = jnp.pad(doc_ids, ((0, 0), (KCONV - 1, 0)))
    ext_rows = jnp.pad(conv_input, ((0, 0), (KCONV - 1, 0), (0, 0)))
    total = conv_bias + jnp.zeros_like(conv_input)
    for offset in range(KCONV):
        match = (ext_ids[:, offset:offset + length] == doc_ids).astype(jnp.float32)
        total = total + conv_weight[offset] * ext_rows[:, offset:offset + length] * match[:, :, None]
    keep_mask = (ext_ids[:, KCONV - 2:KCONV - 2 + length] == doc_ids).astype(jnp.float32)
    conv_value = low(jax.nn.silu(total))
    mixed_proj = low_back(matmul(conv_value, x_proj))
    rate_low = low(mixed_proj[..., :RANK])
    b_rows = mixed_proj[..., RANK:RANK + NSTATE]
    c_rows = mixed_proj[..., RANK + NSTATE:]
    step_size = jax.nn.softplus(low_back(matmul(rate_low, dt_proj)) + dt_bias)
    a_mat = -jnp.exp(a_log)
    scan_out = selective_scan(step_size, b_rows, c_rows, conv_value, keep_mask, a_mat)
    mixed_rows = low((scan_out + d_skip * conv_value) * jax.nn.silu(gate_pre))
    hidden_one = tokens + low_back(matmul(mixed_rows, out_proj))
    moe_low = low(rms_norm(hidden_one, moe_gain))
    logits = matmul(moe_low, router)
    router_prob = jax.nn.softmax(logits, -1)
    onehot = (routes[:, :, None] == jnp.arange(EXPERTS)[None, None, :]).astype(jnp.float32)
    gate_prob = lax.optimization_barrier(jnp.sum(router_prob * onehot, -1))
    block_count = seq_count // SEQ_DEV * (length // SEQ_PART)
    block_id = jnp.arange(seq_count)[:, None] // SEQ_DEV * (length // SEQ_PART) + jnp.arange(length)[None, :] // SEQ_PART
    target = jnp.where(slot_index < CAP, (routes * block_count + block_id) * CAP + slot_index, EXPERTS * block_count * CAP).astype(jnp.int32)
    target = target.reshape(-1)
    send_rows = low_back(moe_low).reshape(-1, width)
    buffer = jnp.zeros((EXPERTS * block_count * CAP, width), jnp.float32).at[target].set(send_rows, mode='drop')
    buffer = buffer.reshape(EXPERTS, block_count * CAP, width)
    outputs = lax.map(jax.checkpoint(expert_apply), (buffer, expert_up, expert_down))
    expert_tok = jnp.take(outputs.reshape(-1, width), target, axis=0, mode='fill', fill_value=0.0).reshape(tokens.shape)
    return hidden_one + gate_prob[:, :, None] * expert_tok

def reference(tokens, segment_ids, routes, slot_index, norm_gain, in_proj, conv_weight, conv_bias, x_proj, dt_proj, dt_bias, a_log, d_skip, out_proj, moe_gain, router, expert_up, expert_down, cotangent):
    floats = tuple((v.astype(jnp.float32) for v in (tokens, norm_gain, in_proj, conv_weight, conv_bias, x_proj, dt_proj, dt_bias, a_log, d_skip, out_proj, moe_gain, router, expert_up, expert_down)))

    def run(*values):
        return forward(*values, segment_ids, routes, slot_index)
    result, pull = jax.vjp(run, *floats)
    grads = pull(cotangent.astype(jnp.float32))
    return (result.astype(jnp.bfloat16), grads[0], grads[1], grads[2], grads[3], grads[4], grads[5], grads[6], grads[7], grads[8], grads[9], grads[10], grads[11], grads[12], grads[13], grads[14])
```

```python
import functools

import jax
import jax.numpy as jnp
from jax import lax
from jax.experimental import pallas as pl
from jax.experimental.pallas import tpu as pltpu
from jax.sharding import PartitionSpec as P

f32, bf16 = jnp.float32, jnp.bfloat16
highest = lax.Precision.HIGHEST
LANES = 128
MESH = pl.DeviceIdType.MESH
epsilon = 1e-05
log2e = 1.4426950408889634
cut = 1e8
ln2 = 0.6931471805599453
vmem_cap = 58 << 20


def tree_sum(parts):
    parts = list(parts)
    while len(parts) > 1:
        paired = [parts[i] + parts[i + 1] for i in range(0, len(parts) - 1, 2)]
        parts = paired + parts[len(parts) - len(parts) % 2 :]
    return parts[0]


UN = dict(state=8, scan=8, adj=8, fwd=4, bwd=4)


def spread(rows_ref, pick_ref, outs, states, group):
    steps = rows_ref.shape[0] // group
    chunk = 16
    wide = 2 * LANES

    @pl.loop(0, steps // chunk)
    def _(i):
        rows = rows_ref[pl.ds(pl.multiple_of(i * chunk * group, chunk * group), chunk * group), :]
        for which, out_ref in outs:
            for n in range(0, states, 2):
                at = (which * states + n) * LANES
                part = jnp.dot(rows, pick_ref[:, at : at + wide], preferred_element_type=f32)
                for k in range(2):
                    out_ref[pl.ds(i * chunk, chunk), n + k] = part[:, k * LANES : (k + 1) * LANES].reshape(
                        chunk, group, LANES
                    )


def softplus(v):
    return jnp.maximum(v, 0.0) + jnp.log1p(jnp.exp(-jnp.abs(v)))


class Carry:
    def __init__(self, step, ends, total, a_all, held, got, sent, send_sem, recv_sem):
        self.step, self.ends, self.total, self.a_all = step, ends, total, a_all
        self.held, self.got, self.sent, self.send_sem, self.recv_sem = held, got, sent, send_sem, recv_sem
        self.place, self.peers = lax.axis_index("seq"), lax.axis_size("seq")
        self.rank = self.place if step > 0 else self.peers - 1 - self.place
        self.count, self.states = ends.shape[0], ends.shape[1]
        self.has_before, self.has_after = self.rank > 0, self.rank < self.peers - 1
        self.lag = jnp.minimum(self.rank, self.count)

    def enter(self, devices=1, hosted=None):
        spot = lax.axis_index("exp")
        barrier = pltpu.get_barrier_semaphore()

        @pl.when(self.has_before)
        def _():
            pl.semaphore_signal(barrier, inc=1, device_id={"seq": self.place - self.step}, device_id_type=MESH)

        @pl.when(self.has_after)
        def _():
            pl.semaphore_signal(barrier, inc=1, device_id={"seq": self.place + self.step}, device_id_type=MESH)

        for hop in range(1, devices):
            pl.semaphore_signal(barrier, inc=1, device_id={"exp": lax.rem(spot + hop, devices)}, device_id_type=MESH)
        neighbours = self.has_before.astype(jnp.int32) + self.has_after.astype(jnp.int32)
        extra = devices - 1
        if hosted is not None:
            hosted.enter(barrier)
            extra += 2
        pl.semaphore_wait(barrier, neighbours + extra)

    def hop(self, u):
        return pltpu.make_async_remote_copy(
            src_ref=self.sent.at[u], dst_ref=self.got.at[u], send_sem=self.send_sem.at[u], recv_sem=self.recv_sem.at[u],
            device_id={"seq": self.place + self.step}, device_id_type=MESH,
        )

    def handle(self, at):
        u = at - self.lag

        @pl.when(jnp.logical_and(u >= 0, u < self.count))
        def _():
            @pl.when(self.has_before)
            def _():
                self.hop(u).wait_recv()
                self.held[u] = self.got[u].astype(f32)

            @pl.when(jnp.logical_not(self.has_before))
            def _():
                self.held[u] = jnp.zeros(self.held.shape[1:], f32)

            @pl.when(self.has_after)
            def _():
                for n in range(self.states):
                    decay = jnp.exp2(self.a_all[u, n : n + 1, :] * self.total[u])
                    self.sent[u, n] = (self.ends[u, n] + decay * self.held[u, n]).astype(bf16)
                self.hop(u).start()

    def leave(self):
        @pl.loop(0, self.count)
        def _(u):
            @pl.when(self.has_after)
            def _():
                self.hop(u).wait_send()


def forward_kernel(
    rate_ref, wdt_ref, bias_ref, conv_ref, bc_ref, pick_ref, match_ref, a_all, gate_ref, skip_ref, cot_ref, target_ref,
    step_ref, z_ref, mixed_ref, start_ref, total_ref, cot_out,
    cot_got, kb_ref, b_all, c_all, step_all, ends, staged, cot_send, cot_recv, got, sent, send_sem, recv_sem, *, states, group, devices,
):
    at = pl.program_id(0)
    count = a_all.shape[0]
    j = lax.rem(at, count)
    carry_of = Carry(1, ends, total_ref, a_all, start_ref, got, sent, send_sem, recv_sem)
    rows = conv_ref.shape[0]
    moved = Dispatch(cot_ref, target_ref, cot_got, staged, cot_send, cot_recv, devices)

    @pl.when(at == 0)
    def _():
        carry_of.enter(devices)
        moved.start()
        kb_ref[...] = broad_cut(match_ref)
        spread(bc_ref, pick_ref, ((0, b_all), (1, c_all)), states, group)

    @pl.when(at < count)
    def _():
        pre = jnp.dot(rate_ref[...], wdt_ref[...], preferred_element_type=f32) + bias_ref[...]
        step = softplus(pre)
        step_ref[...] = step
        step_all[j] = step
        a_rows = [jnp.broadcast_to(a_all[j, n : n + 1, :], (group, LANES)) for n in range(states)]
        un = UN["state"]

        def body(i, carry):
            total, state = carry
            base = pl.multiple_of(i * un * group, un * group)
            x_two = conv_ref[pl.ds(base, un * group), :].astype(f32)
            for k in range(un):
                here = pl.ds(pl.multiple_of(base + k * group, group), group)
                dt = step_ref[here, :]
                masked = dt + kb_ref[here, :]
                u = dt * x_two[k * group : (k + 1) * group]
                total = total + masked
                state = [
                    jnp.exp2(masked * a_rows[n]) * state[n] + u * b_all[un * i + k, n] for n in range(states)
                ]
            return total, state

        zero = jnp.zeros((group, LANES), f32)
        total, state = lax.fori_loop(0, rows // (un * group), body, (zero, [zero] * states))
        total_ref[j] = total
        for n in range(states):
            ends[j, n] = state[n]

    carry_of.handle(at)

    @pl.when(at >= count)
    def _():
        a_rows = [jnp.broadcast_to(a_all[j, n : n + 1, :], (group, LANES)) for n in range(states)]
        un = UN["scan"]

        def body(i, state):
            base = pl.multiple_of(i * un * group, un * group)
            x_two = conv_ref[pl.ds(base, un * group), :].astype(f32)
            outs = []
            for k in range(un):
                here = pl.ds(pl.multiple_of(base + k * group, group), group)
                dt = step_all[j, here, :]
                masked = dt + kb_ref[here, :]
                u = dt * x_two[k * group : (k + 1) * group]
                state = [
                    jnp.exp2(masked * a_rows[n]) * state[n] + u * b_all[un * i + k, n] for n in range(states)
                ]
                outs.append(tree_sum(state[n] * c_all[un * i + k, n] for n in range(states)))
            whole = pl.ds(base, un * group)
            gate = gate_ref[whole, :]
            z = jnp.concatenate(outs, 0) + skip_ref[...] * x_two
            z_ref[whole, :] = z
            mixed_ref[whole, :] = (z * (gate * jax.nn.sigmoid(gate))).astype(bf16)
            return state

        lax.fori_loop(0, rows // (un * group), body, [start_ref[j, n] for n in range(states)])

    @pl.when(at == 2 * count - 1)
    def _():
        carry_of.leave()
        moved.wait()
        cot_out[...] = cot_got[...]


def broad_cut(match_ref):
    keep = match_ref[:, match_ref.shape[1] - 1 :]
    return jnp.broadcast_to((1.0 - keep) * cut, (match_ref.shape[0], LANES))


def backward_kernel(
    mg_ref, gate_ref, z_ref, step_ref, conv_ref, bc_ref, pick_ref, match_ref, a_all, total_ref, start_ref, rate_ref, wdt_ref,
    bias_ref, skip_ref, back_ref, *refs, states, group, devices, peers,
):
    sources, refs = refs[:2], refs[2:]
    first_step, spread_steps, _ = hosting_plan(peers, a_all.shape[0])
    opening = None
    if first_step:
        opening, refs = refs[:2], refs[2:]
    gg_ref, low_ref, cg_ref, small_ref, mpg_ref, tok_ref = refs[:6]
    landed, result, buffers, host_sems, spread_pair = refs[6:8], refs[8:10], refs[10:14], refs[14:18], refs[18:20]
    (
        back_send, back_recv, back_own, kb_ref, b_all, c_all, b_acc, c_acc, kept, dt_grad, g_all, rate_acc, ends, last, got, sent, send_sem,
        recv_sem,
    ) = refs[20:]
    at = pl.program_id(0)
    count = a_all.shape[0]
    j = lax.rem(at, count)
    carry_of = Carry(-1, ends, total_ref, a_all, last, got, sent, send_sem, recv_sem)
    steps = conv_ref.shape[0] // group
    rank = rate_ref.shape[1]
    zero = jnp.zeros((group, LANES), f32)
    spot = lax.axis_index("exp")
    shared = HostedSpread(peers, spread_pair, result, 0, spread_steps)
    hosted = HostedSum(
        peers, host_sems, sources, landed, buffers, first_step, peers - 1, opening=opening, spread=shared
    )
    planned = first_step > 0

    def back_copy(hop):
        peer = lax.rem(spot + hop, devices)
        return pltpu.make_async_remote_copy(
            src_ref=back_ref.at[peer], dst_ref=tok_ref.at[spot], send_sem=back_send.at[hop - 1],
            recv_sem=back_recv.at[hop - 1], device_id={"exp": peer}, device_id_type=MESH,
        )

    def own_copy():
        return pltpu.make_async_copy(back_ref.at[spot], tok_ref.at[spot], back_own.at[0])

    @pl.when(at == 0)
    def _():
        carry_of.enter(devices, hosted)
        hosted.open()
        own_copy().start()
        for hop in range(1, devices):
            back_copy(hop).start()
        kb_ref[...] = broad_cut(match_ref)
        spread(bc_ref, pick_ref, ((0, b_all), (1, c_all)), states, group)
        rate_acc[...] = jnp.zeros_like(rate_acc)

        @pl.loop(0, steps)
        def _(t):
            none = jnp.zeros((states, group, LANES), f32)
            b_acc[t] = none
            c_acc[t] = none

    if planned:

        @pl.when(at == 7)
        def _():
            hosted.fetch(jnp.int32(3))

        @pl.when(at == 8)
        def _():
            hosted.add(jnp.int32(3))

        @pl.when(jnp.logical_and(lax.rem(at, 2) == 1, jnp.logical_and(at >= 13, at <= 17)))
        def _():
            hosted.add(lax.div(at - 5, 2))

        @pl.when(at == 19)
        def _():
            shared.hand(jnp.int32(0))

    @pl.when(at < count)
    def _():
        a_rows = [jnp.broadcast_to(a_all[j, n : n + 1, :], (group, LANES)) for n in range(states)]
        un = UN["adj"]

        def body(i, q):
            base = pl.multiple_of((steps // un - 1 - i) * un * group, un * group)
            whole = pl.ds(base, un * group)
            mixed_grad, gate = mg_ref[whole, :], gate_ref[whole, :]
            sig = jax.nn.sigmoid(gate)
            g_rows = mixed_grad * (gate * sig)
            g_all[j, whole, :] = g_rows.astype(bf16)
            gg_ref[whole, :] = (mixed_grad * z_ref[whole, :] * (sig * (1.0 + gate * (1.0 - sig)))).astype(bf16)
            for k in reversed(range(un)):
                t = un * (steps // un - 1 - i) + k
                here = pl.ds(pl.multiple_of(base + k * group, group), group)
                masked = step_ref[here, :] + kb_ref[here, :]
                g = g_rows[k * group : (k + 1) * group]
                q = [jnp.exp2(masked * a_rows[n]) * (c_all[t, n] * g + q[n]) for n in range(states)]
            return q

        q = lax.fori_loop(0, steps // un, body, [zero] * states)
        for n in range(states):
            ends[j, n] = q[n]

    carry_of.handle(at)

    @pl.when(at >= count)
    def _():
        a_rows = [jnp.broadcast_to(a_all[j, n : n + 1, :], (group, LANES)) for n in range(states)]
        fu, bu = UN["fwd"], UN["bwd"]

        def forward(i, state):
            base = pl.multiple_of(i * fu * group, fu * group)
            x_two = conv_ref[pl.ds(base, fu * group), :].astype(f32)
            g_two = g_all[j, pl.ds(base, fu * group), :].astype(f32)
            for k in range(fu):
                t = fu * i + k
                here = pl.ds(pl.multiple_of(base + k * group, group), group)
                dt = step_ref[here, :]
                masked = dt + kb_ref[here, :]
                g = g_two[k * group : (k + 1) * group]
                u = dt * x_two[k * group : (k + 1) * group]
                for n in range(states):
                    kept[t, n] = state[n]
                state = [jnp.exp2(masked * a_rows[n]) * state[n] + u * b_all[t, n] for n in range(states)]
                for n in range(states):
                    c_acc[t, n] += state[n] * g
            return state

        lax.fori_loop(0, steps // fu, forward, [start_ref[0, n] for n in range(states)])
        if planned:
            even = lax.rem(at, 2) == 0

            @pl.when(jnp.logical_and(even, at <= 16))
            def _():
                hosted.fetch(lax.div(at - 4, 2))

            @pl.when(jnp.logical_and(even, at >= 20))
            def _():
                shared.hand(lax.div(at - 18, 2))

        skip = skip_ref[...]

        def backward(i, carry):
            q, a_sum, skip_sum = carry
            base = pl.multiple_of((steps // bu - 1 - i) * bu * group, bu * group)
            x_two = conv_ref[pl.ds(base, bu * group), :].astype(f32)
            g_two = g_all[j, pl.ds(base, bu * group), :].astype(f32)
            for k in reversed(range(bu)):
                t = bu * (steps // bu - 1 - i) + k
                here = pl.ds(pl.multiple_of(base + k * group, group), group)
                dt = step_ref[here, :]
                masked = dt + kb_ref[here, :]
                g = g_two[k * group : (k + 1) * group]
                x = x_two[k * group : (k + 1) * group]
                u = dt * x
                skip_sum = skip_sum + g * x
                lam = [c_all[t, n] * g + q[n] for n in range(states)]
                for n in range(states):
                    b_acc[t, n] += lam[n] * u
                s_one = tree_sum(lam[n] * b_all[t, n] for n in range(states))
                q = [jnp.exp2(masked * a_rows[n]) * lam[n] for n in range(states)]
                w = [q[n] * kept[t, n] for n in range(states)]
                s_two = tree_sum(w[n] * a_rows[n] for n in range(states))
                a_sum = [a_sum[n] + dt * w[n] for n in range(states)]
                cg_ref[here, :] = skip * g + dt * s_one
                dt_grad[here, :] = x * s_one + ln2 * s_two
            return q, a_sum, skip_sum

        q, a_sum, skip_sum = lax.fori_loop(
            0, steps // bu, backward, ([last[j, n] for n in range(states)], [zero] * states, zero)
        )
        pre = jnp.dot(rate_ref[...], wdt_ref[...], preferred_element_type=f32) + bias_ref[...]
        pre_grad = dt_grad[...] * jax.nn.sigmoid(pre)
        low = pre_grad.astype(bf16)
        low_ref[...] = low
        rate_acc[...] += lax.dot_general(low, wdt_ref[...], (((1,), (1,)), ((), ())), preferred_element_type=f32)
        rows_of = [lax.dot_general(rate_ref[...], low, (((0,), (0,)), ((), ())), preferred_element_type=f32)]
        rows_of += [jnp.sum(a_sum[n], 0, keepdims=True) * a_all[j, n : n + 1, :] * ln2 for n in range(states)]
        rows_of += [jnp.sum(pre_grad, 0, keepdims=True), jnp.sum(skip_sum, 0, keepdims=True)]
        spare = small_ref.shape[0] - rank - states - 2
        small_ref[...] = jnp.concatenate(rows_of + [jnp.zeros((spare, LANES), f32)], 0).astype(bf16)

    @pl.when(at == 2 * count - 1)
    def _():
        carry_of.leave()
        if planned:
            shared.hand(jnp.int32(3))
        else:

            @pl.loop(0, peers - 1)
            def _(s):
                hosted.fetch(s)
                hosted.add(s)

            @pl.loop(0, peers - 1)
            def _(s):
                shared.hand(s)

        hosted.finish()
        shared.finish(False)
        own_copy().wait()
        for hop in range(1, devices):
            back_copy(hop).wait()
        mpg_ref[:, :rank] = rate_acc[...].astype(bf16)
        lane = lax.broadcasted_iota(jnp.int32, (LANES, 2 * states), 1)
        total = jnp.zeros((steps * group, 2 * states), f32)
        for n in range(states):
            for column, acc in ((n, b_acc), (states + n, c_acc)):
                rows = acc[:, n].reshape(steps * group, LANES)
                pick = (lane == column).astype(f32)
                total = total + jnp.dot(rows, pick, precision=highest, preferred_element_type=f32)
        mpg_ref[:, rank:] = total.astype(bf16)


def rows_block(rows):
    return pl.BlockSpec((rows, LANES), lambda j: (0, j))


def whole_block(shape):
    return pl.BlockSpec(shape, lambda j: (0,) * len(shape))


def state_block(states, group):
    return pl.BlockSpec((1, states, group, LANES), lambda j: (j, 0, 0, 0))


def shape_of(shape, dtype):
    return jax.ShapeDtypeStruct(shape, dtype)


def params():
    return pltpu.CompilerParams(vmem_limit_bytes=vmem_cap)


def carry_scratch(shape):
    return [
        pltpu.VMEM(shape, bf16), pltpu.VMEM(shape, bf16), pltpu.SemaphoreType.DMA((shape[0],)),
        pltpu.SemaphoreType.DMA((shape[0],)),
    ]


def forward_scan(rate_low, w_dt, bias, conv_low, bc, pick, match, a_blocks, gate, skip, cot, target, capacity, group, devices):
    rows, inner = conv_low.shape
    count, states, _ = a_blocks.shape
    rank = rate_low.shape[1]
    first = lambda at: (0, jnp.minimum(at, count - 1))
    both = lambda at: (0, lax.rem(at, count))
    second = lambda at: (0, jnp.maximum(at - count, 0))
    shape = (count, states, group, LANES)
    big = pltpu.VMEM((rows // group, states, group, LANES), f32)
    return pl.pallas_call(
        functools.partial(forward_kernel, states=states, group=group, devices=devices),
        grid=(2 * count,),
        in_specs=[
            whole_block((rows, rank)), pl.BlockSpec((rank, LANES), first), pl.BlockSpec((1, LANES), first),
            pl.BlockSpec((rows, LANES), both), whole_block(bc.shape), whole_block(pick.shape),
            whole_block(match.shape), whole_block(a_blocks.shape), pl.BlockSpec((rows, LANES), second),
            pl.BlockSpec((1, LANES), second), whole_block(cot.shape), whole_block((1, rows)),
        ],
        out_specs=[
            pl.BlockSpec((rows, LANES), first), pl.BlockSpec((rows, LANES), second), pl.BlockSpec((rows, LANES), second),
            whole_block(shape), whole_block((count, group, LANES)), whole_block((devices, capacity, cot.shape[1])),
        ],
        out_shape=[
            shape_of((rows, inner), f32), shape_of((rows, inner), f32), shape_of((rows, inner), bf16),
            shape_of(shape, f32), shape_of((count, group, LANES), f32), shape_of((devices, capacity, cot.shape[1]), bf16),
        ],
        scratch_shapes=[pltpu.VMEM((devices, capacity, cot.shape[1]), bf16), pltpu.VMEM((rows, LANES), f32), big, big]
        + [pltpu.VMEM((count, rows, LANES), f32), pltpu.VMEM(shape, f32)]
        + [pltpu.VMEM((devices - 1, capacity, cot.shape[1]), bf16)]
        + [pltpu.SemaphoreType.DMA((devices - 1,)), pltpu.SemaphoreType.DMA((devices - 1,))] + carry_scratch(shape),
        compiler_params=pltpu.CompilerParams(collective_id=0, has_side_effects=True, vmem_limit_bytes=vmem_cap),
        name="forward_scan",
    )(rate_low, w_dt, bias, conv_low, bc, pick, match, a_blocks, gate, skip, cot, target[None, :])


def backward_scan(mixed_grad, gate, z, step, conv_low, bc, pick, match, a_blocks, total, start, rate_low, w_dt, bias, skip, back, sources, partial, group, devices):
    rows, inner = conv_low.shape
    count, states, _ = a_blocks.shape
    rank = rate_low.shape[1]
    small_rows = -(-(rank + states + 2) // 16) * 16
    peers, pieces = sources[0].shape[1], [v.shape[2:] for v in sources]
    first_step, spread_steps, _ = hosting_plan(peers, count)
    dma = pltpu.SemaphoreType.DMA
    extra = list(sources) + (list(partial) if first_step else [])
    first = lambda at: (0, jnp.minimum(at, count - 1))
    both = lambda at: (0, lax.rem(at, count))
    second = lambda at: (0, jnp.maximum(at - count, 0))
    shape = (count, states, group, LANES)
    big = pltpu.VMEM((rows // group, states, group, LANES), f32)
    return pl.pallas_call(
        functools.partial(backward_kernel, states=states, group=group, devices=devices, peers=peers),
        grid=(2 * count,),
        in_specs=[
            pl.BlockSpec((rows, LANES), first), pl.BlockSpec((rows, LANES), first), pl.BlockSpec((rows, LANES), first),
            pl.BlockSpec((rows, LANES), both), pl.BlockSpec((rows, LANES), second), whole_block(bc.shape),
            whole_block(pick.shape), whole_block(match.shape), whole_block(a_blocks.shape), whole_block(total.shape),
            pl.BlockSpec((1, states, group, LANES), lambda at: (jnp.maximum(at - count, 0), 0, 0, 0)),
            whole_block((rows, rank)), pl.BlockSpec((rank, LANES), second), pl.BlockSpec((1, LANES), second),
            pl.BlockSpec((1, LANES), second), pl.BlockSpec(memory_space=pl.ANY),
        ]
        + any_specs(len(extra)),
        out_specs=[
            pl.BlockSpec((rows, LANES), lambda at: (0, jnp.minimum(at, count - 1) + count)),
            pl.BlockSpec((rows, LANES), second), pl.BlockSpec((rows, LANES), second),
            pl.BlockSpec((small_rows, LANES), second), whole_block((rows, rank + 2 * states)),
        ]
        + any_specs(5),
        out_shape=[
            shape_of((rows, 2 * inner), bf16), shape_of((rows, inner), bf16), shape_of((rows, inner), f32),
            shape_of((small_rows, inner), bf16), shape_of((rows, rank + 2 * states), bf16), shape_of(back.shape, bf16),
        ]
        + [shape_of((2, peers - 1 - first_step) + p, bf16) for p in pieces]
        + [shape_of(v.shape, bf16) for v in sources],
        scratch_shapes=sum_buffers(pieces) + sum_sems(peers - 1 - first_step) + spread_sems(spread_steps)
        + [dma((devices - 1,)), dma((devices - 1,)), dma((1,))]
        + [pltpu.VMEM((rows, LANES), f32), big, big, big, big, big]
        + [pltpu.VMEM((rows, LANES), f32), pltpu.VMEM((count, rows, LANES), bf16)]
        + [pltpu.VMEM((rows, rank), f32), pltpu.VMEM(shape, f32), pltpu.VMEM(shape, f32)] + carry_scratch(shape),
        compiler_params=pltpu.CompilerParams(collective_id=1, has_side_effects=True, vmem_limit_bytes=64 << 20),
        name="backward_scan",
    )(mixed_grad, gate, z, step, conv_low, bc, pick, match, a_blocks, total, start, rate_low, w_dt, bias, skip, back, *extra)


def split_three(v):
    high = v.astype(bf16)
    rest = v - high.astype(f32)
    mid = rest.astype(bf16)
    low = (rest - mid.astype(f32)).astype(bf16)
    return jnp.concatenate([high, mid, low], -1)


def pick_matrix(columns):
    eye = (jnp.arange(columns)[:, None] == jnp.arange(columns * LANES)[None, :] // LANES).astype(bf16)
    return jnp.concatenate([eye] * 3, 0)

def broad_match(match_ref, wide):
    @pl.when(pl.program_id(0) == 0)
    def _():
        for k in range(match_ref.shape[1]):
            wide[k] = jnp.broadcast_to(match_ref[:, k : k + 1], wide.shape[1:])


def front_kernel(
    token_ref, before_ref, gain_ref, wc_ref, wg_ref, cw_ref, cb_ref, compact_ref, wx_ref, ci_ref, low_ref, gate_ref, mixed_ref,
    normed_ref, rows_f, match_ref, *, halo, group,
):
    rows = low_ref.shape[0]
    broad_match(compact_ref, match_ref)

    @pl.when(pl.program_id(0) == 0)
    def _():
        def put(at, source):
            values = source.astype(f32)
            scale = lax.rsqrt(jnp.mean(values * values, -1, keepdims=True) + epsilon)
            normed_ref[at, :] = (values * scale * gain_ref[...]).astype(bf16)

        put(slice(0, halo), before_ref[...])
        tile = 256

        @pl.loop(0, rows // tile)
        def _(i):
            put(pl.ds(pl.multiple_of(halo + i * tile, halo), tile), token_ref[pl.ds(pl.multiple_of(i * tile, tile), tile), :])

    taps = cw_ref.shape[0]
    ci = jnp.dot(normed_ref[...], wc_ref[...], preferred_element_type=f32).astype(bf16)
    ci_ref[...] = ci
    rows_f[...] = ci.astype(f32)
    total = conv_total(rows_f, cw_ref, cb_ref, match_ref, halo, group, rows, taps)
    low = (total * jax.nn.sigmoid(total)).astype(bf16)
    low_ref[...] = low
    gate_ref[...] = jnp.dot(normed_ref[halo:, :], wg_ref[...], preferred_element_type=f32)
    part = jnp.dot(low, wx_ref[...], preferred_element_type=f32)

    @pl.when(pl.program_id(0) == 0)
    def _():
        mixed_ref[...] = part

    @pl.when(pl.program_id(0) > 0)
    def _():
        mixed_ref[...] += part


def conv_total(rows_f, cw_ref, cb_ref, match_ref, halo, group, rows, taps):
    total = cb_ref[...] + cw_ref[taps - 1 : taps, :] * rows_f[halo : halo + rows, :]
    for k in range(taps - 1):
        at = halo - (taps - 1 - k) * group
        total = total + cw_ref[k : k + 1, :] * rows_f[at : at + rows, :] * match_ref[k]
    return total


def front(token_low, before_rows, gain, w_in, conv_w, conv_b, match, w_x, halo, group, lanes):
    width, inner = w_in.shape[0], w_in.shape[1] // 2
    total_rows = token_low.shape[0] + halo
    rows, taps, mixed_width = total_rows - halo, conv_w.shape[0], w_x.shape[1]
    count = inner // lanes
    cols = lambda r: pl.BlockSpec((r, lanes), lambda j: (0, j))
    return pl.pallas_call(
        functools.partial(front_kernel, halo=halo, group=group),
        grid=(count,),
        in_specs=[
            whole_block(token_low.shape), whole_block(before_rows.shape), whole_block(gain.shape), cols(width),
            pl.BlockSpec((width, lanes), lambda j: (0, j + count)),
            cols(taps), cols(1), whole_block(match.shape), pl.BlockSpec((lanes, mixed_width), lambda j: (j, 0)),
        ],
        out_specs=[cols(total_rows), cols(rows), cols(rows), whole_block((rows, mixed_width)), whole_block((total_rows, width))],
        out_shape=[
            shape_of((total_rows, inner), bf16), shape_of((rows, inner), bf16), shape_of((rows, inner), f32),
            shape_of((rows, mixed_width), f32), shape_of((total_rows, width), bf16),
        ],
        scratch_shapes=[pltpu.VMEM((total_rows, lanes), f32), pltpu.VMEM((match.shape[1], rows, lanes), f32)],
        compiler_params=params(),
        name="front",
    )(token_low, before_rows, gain, w_in, w_in, conv_w, conv_b, match, w_x)


def conv_back_kernel(
    cg_ref, low_ref, mpg_ref, wx_ref, ci_ref, cw_ref, cb_ref, compact_ref, proj_ref, outg_ref, up_in, down_in, pg_ref, ext_ref,
    small_ref, outo_ref, up_ref, down_ref, rows_f, ext, match_ref, near_got, passed, far_got, send_sem, recv_sem, *spread_pair,
    halo, group, first_step, last_step,
):
    spread = None
    if last_step > first_step:
        spread = HostedSpread(up_ref.shape[1], spread_pair, (up_ref, down_ref), first_step, last_step)
    broad_match(compact_ref, match_ref)
    spot = lax.axis_index("exp")
    near = spot + 1 - 2 * lax.rem(spot, 2)
    far = lax.rem(spot + 2, 4)
    across = lax.rem(near + 2, 4)
    rows_out = outo_ref.shape[0]

    def share_of(k):
        return pl.ds(pl.multiple_of(k * rows_out, rows_out), rows_out)

    def move(source, target, slot, device):
        return pltpu.make_async_remote_copy(
            src_ref=source, dst_ref=target, send_sem=send_sem.at[slot], recv_sem=recv_sem.at[slot],
            device_id={"exp": device}, device_id_type=MESH,
        )

    def near_move(slot):
        return move(outg_ref.at[share_of(across if slot else near)], near_got.at[slot], slot, near)

    def far_move():
        return move(passed, far_got, 2, far)

    @pl.when(pl.program_id(0) == 0)
    def _():
        barrier = pltpu.get_barrier_semaphore()
        for device in (near, far):
            pl.semaphore_signal(barrier, inc=1, device_id={"exp": device}, device_id_type=MESH)
        if spread:
            spread.enter(barrier)
        pl.semaphore_wait(barrier, 4 if spread else 2)
        if spread:
            spread.open()
        near_move(1).start()
        near_move(0).start()

    rows = pg_ref.shape[0]
    taps = cw_ref.shape[0]
    grad = cg_ref[...] + lax.dot_general(
        mpg_ref[...], wx_ref[...], (((1,), (1,)), ((), ())), preferred_element_type=f32
    )
    rows_f[...] = ci_ref[...].astype(f32)
    total = conv_total(rows_f, cw_ref, cb_ref, match_ref, halo, group, rows, taps)
    sig = jax.nn.sigmoid(total)
    grad = grad * (sig * (1.0 + total * (1.0 - sig)))
    x_part = lax.dot_general(mpg_ref[...], low_ref[...], (((0,), (0,)), ((), ())), preferred_element_type=f32)
    taps_grad = [None] * taps
    ext[:halo, :] = jnp.zeros((halo, ext.shape[1]), f32)
    ext[halo:, :] = grad * cw_ref[taps - 1 : taps, :]
    taps_grad[taps - 1] = jnp.sum(grad * rows_f[halo:, :], 0, keepdims=True)
    for k in range(taps - 1):
        at = halo - (taps - 1 - k) * group
        own = grad * match_ref[k]
        taps_grad[k] = jnp.sum(own * rows_f[at : at + rows, :], 0, keepdims=True)
        ext[at : at + rows, :] += own * cw_ref[k : k + 1, :]
    pg_ref[...] = ext[halo:, :].astype(bf16)
    ext_ref[:halo, :] = ext[:halo, :]
    ext_ref[halo:, :] = ext[rows:, :]
    spare = small_ref.shape[0] - x_part.shape[0] - taps - 1
    parts = [x_part] + taps_grad + [jnp.sum(grad, 0, keepdims=True), jnp.zeros((spare, ext.shape[1]), f32)]
    small_ref[...] = jnp.concatenate(parts, 0).astype(bf16)

    @pl.when(pl.program_id(0) == 0)
    def _():
        near_move(1).wait_recv()
        passed[...] = (outg_ref[share_of(far), :].astype(f32) + near_got[1].astype(f32)).astype(bf16)
        far_move().start()
        near_move(0).wait_recv()
        outo_ref[...] = outg_ref[share_of(spot), :].astype(f32) + near_got[0].astype(f32)

    @pl.when(pl.program_id(0) == pl.num_programs(0) - 1)
    def _():
        far_move().wait_recv()
        outo_ref[...] += far_got[...].astype(f32)
        for slot in range(2):
            near_move(slot).wait_send()
        far_move().wait_send()
        if spread:
            spread.hand(jnp.int32(first_step))
            spread.finish(True)


def conv_back(cg, conv_low, mpg, w_x, ci, conv_w, conv_b, match, proj, out_grad, results, steps, halo, group, lanes, devices):
    out_shape = (out_grad.shape[0] // devices, out_grad.shape[1])
    dma = pltpu.SemaphoreType.DMA
    rows, inner = cg.shape
    taps, mixed_width = conv_w.shape[0], w_x.shape[1]
    small_rows = -(-(mixed_width + taps + 1) // 16) * 16
    cols = lambda r: pl.BlockSpec((r, lanes), lambda j: (0, j))
    return pl.pallas_call(
        functools.partial(conv_back_kernel, halo=halo, group=group, first_step=steps[0], last_step=steps[1]),
        grid=(inner // lanes,),
        in_specs=[
            cols(rows), cols(rows), whole_block((rows, mixed_width)), pl.BlockSpec((lanes, mixed_width), lambda j: (j, 0)),
            cols(rows + halo), cols(taps), cols(1), whole_block(match.shape),
            pl.BlockSpec(memory_space=pl.ANY), pl.BlockSpec(memory_space=pltpu.VMEM),
        ]
        + any_specs(2),
        out_specs=[cols(rows), cols(2 * halo), cols(small_rows), whole_block(out_shape)] + any_specs(2),
        out_shape=[shape_of(proj.shape, bf16), shape_of((2 * halo, inner), f32), shape_of((small_rows, inner), bf16)]
        + [shape_of(out_shape, f32)]
        + [shape_of(v.shape, bf16) for v in results],
        scratch_shapes=[pltpu.VMEM((rows + halo, lanes), f32), pltpu.VMEM((rows + halo, lanes), f32)]
        + [pltpu.VMEM((match.shape[1], rows, lanes), f32), pltpu.VMEM((2,) + out_shape, bf16)]
        + [pltpu.VMEM(out_shape, bf16), pltpu.VMEM(out_shape, bf16), dma((3,)), dma((3,))]
        + (spread_sems(steps[1] - steps[0]) if steps[1] > steps[0] else []),
        input_output_aliases={8: 0, 10: 4, 11: 5},
        compiler_params=pltpu.CompilerParams(collective_id=6, has_side_effects=True, vmem_limit_bytes=vmem_cap),
        name="conv_back",
    )(cg, conv_low, mpg, w_x, ci, conv_w, conv_b, match, proj, out_grad, *results)

def expert_kernel(
    rows_ref, cot_ref, up_ref, down_ref, out_ref, back_ref, upg_ref, downg_ref, grad, out_acc, back_acc, active, pre_grad, *, tile
):
    first = pl.program_id(0) == 0
    final = pl.program_id(0) == pl.num_programs(0) - 1
    slots, width = cot_ref.shape
    tiles = [slice(i * tile, (i + 1) * tile) for i in range(slots // tile)]

    @pl.when(first)
    def _():
        for at in tiles:
            parts = rows_ref[at, width : width + LANES].astype(f32)
            gate = parts[:, 0:1] + parts[:, 1:2] + parts[:, 2:3]
            grad[at, :] = (gate * cot_ref[at, :].astype(f32)).astype(bf16)
            out_acc[at, :] = jnp.zeros((tile, width), f32)
            back_acc[at, :] = jnp.zeros((tile, width), f32)

    for at in tiles:
        pre = jnp.dot(rows_ref[at, :width], up_ref[...], preferred_element_type=f32)
        act_grad = lax.dot_general(grad[at, :], down_ref[...], (((1,), (1,)), ((), ())), preferred_element_type=f32)
        half = 0.5 * lax.erf(pre * 0.7071067811865476) + 0.5
        active[at, :] = (pre * half).astype(bf16)
        slope = half + pre * (jnp.exp(pre * pre * -0.5) * 0.3989422804014327)
        pre_grad[at, :] = (act_grad * slope).astype(bf16)
    for at in tiles:
        out_acc[at, :] += jnp.dot(active[at, :], down_ref[...], preferred_element_type=f32)
        back_acc[at, :] += lax.dot_general(
            pre_grad[at, :], up_ref[...], (((1,), (1,)), ((), ())), preferred_element_type=f32
        )
    downg_ref[...] = lax.dot_general(
        active[...], grad[...], (((0,), (0,)), ((), ())), preferred_element_type=f32
    ).astype(bf16)
    upg_ref[...] = lax.dot_general(
        rows_ref[:, :width], pre_grad[...], (((0,), (0,)), ((), ())), preferred_element_type=f32
    ).astype(bf16)

    @pl.when(final)
    def _():
        for at in tiles:
            out = out_acc[at, :].astype(bf16)
            out_ref[at, :] = out
            back_ref[at, :width] = back_acc[at, :].astype(bf16)
            dot = jnp.sum(out.astype(f32) * cot_ref[at, :].astype(f32), -1, keepdims=True)
            back_ref[at, width:] = in_parts(dot)


def in_parts(column):
    high = column.astype(bf16).astype(f32)
    mid = (column - high).astype(bf16).astype(f32)
    lane = lax.broadcasted_iota(jnp.int32, (column.shape[0], LANES), 1)
    low = column - high - mid
    return jnp.where(lane == 0, high, jnp.where(lane == 1, mid, jnp.where(lane == 2, low, 0.0))).astype(bf16)


def one_expert(rows, cot, up, down):
    slots, width = cot.shape
    hidden = up.shape[1]
    hidden_tile, tile = hidden // 6, slots // 2
    full = whole_block((slots, width))
    broad = whole_block((slots, width + LANES))
    cols = pl.BlockSpec((width, hidden_tile), lambda j: (0, j))
    deep = pl.BlockSpec((hidden_tile, width), lambda j: (j, 0))
    return pl.pallas_call(
        functools.partial(expert_kernel, tile=tile),
        grid=(hidden // hidden_tile,),
        in_specs=[broad, full, cols, deep],
        out_specs=[full, broad, cols, deep],
        out_shape=[
            shape_of((slots, width), bf16), shape_of((slots, width + LANES), bf16), shape_of((width, hidden), bf16),
            shape_of((hidden, width), bf16),
        ],
        scratch_shapes=[
            pltpu.VMEM((slots, width), bf16), pltpu.VMEM((slots, width), f32), pltpu.VMEM((slots, width), f32),
            pltpu.VMEM((slots, hidden_tile), bf16), pltpu.VMEM((slots, hidden_tile), bf16),
        ],
        compiler_params=params(),
        name="one_expert",
    )(rows, cot, up, down)


def exp_barrier(spot, devices, hosted=None):
    barrier = pltpu.get_barrier_semaphore()
    if hosted:
        hosted.enter(barrier)
    for hop in range(1, devices):
        pl.semaphore_signal(barrier, inc=1, device_id={"exp": lax.rem(spot + hop, devices)}, device_id_type=MESH)
    pl.semaphore_wait(barrier, devices + 1 if hosted else devices - 1)


class Dispatch:
    def __init__(self, rows_ref, target_ref, got_ref, staged, send_sem, recv_sem, devices):
        self.rows_ref, self.target_ref, self.got_ref, self.staged = rows_ref, target_ref, got_ref, staged
        self.send_sem, self.recv_sem, self.devices = send_sem, recv_sem, devices
        self.spot = lax.axis_index("exp")
        self.hops = [h for h in range(devices // 2, devices)] + [h for h in range(1, devices // 2)]

    def packed(self, k):
        capacity = self.got_ref.shape[1]
        slot = lax.broadcasted_iota(jnp.int32, (capacity, self.rows_ref.shape[0]), 0) + k * capacity
        pick = jnp.where(slot == self.target_ref[...], 1.0, 0.0).astype(bf16)
        return jnp.dot(pick, self.rows_ref[...], preferred_element_type=f32).astype(bf16)

    def copy(self, hop):
        return pltpu.make_async_remote_copy(
            src_ref=self.staged.at[hop - 1], dst_ref=self.got_ref.at[self.spot], send_sem=self.send_sem.at[hop - 1],
            recv_sem=self.recv_sem.at[hop - 1], device_id={"exp": lax.rem(self.spot + hop, self.devices)},
            device_id_type=MESH,
        )

    def start(self):
        for hop in self.hops:
            self.staged[hop - 1] = self.packed(lax.rem(self.spot + hop, self.devices))
            self.copy(hop).start()
        self.got_ref[self.spot] = self.packed(self.spot)

    def wait(self):
        for hop in self.hops:
            self.copy(hop).wait()


def route_kernel(
    mixed_ref, wout_ref, token_ref, gain_ref, router_ref, route_ref, target_ref, hidden_ref, rows_ref, prob_ref, got_ref,
    staged, send_sem, recv_sem, *, devices, experts, tile,
):
    exp_barrier(lax.axis_index("exp"), devices)
    width = wout_ref.shape[1]

    @pl.loop(0, mixed_ref.shape[0] // tile)
    def _(i):
        at = pl.ds(pl.multiple_of(i * tile, tile), tile)
        hidden = token_ref[at, :].astype(f32) + jnp.dot(mixed_ref[at, :], wout_ref[...], preferred_element_type=f32)
        hidden_ref[at, :] = hidden
        scale = lax.rsqrt(jnp.mean(hidden * hidden, -1, keepdims=True) + epsilon)
        low = (hidden * scale * gain_ref[...]).astype(bf16)
        rows_ref[at, :width] = low
        logits = jnp.dot(low, router_ref[...], preferred_element_type=f32)
        lane = lax.broadcasted_iota(jnp.int32, logits.shape, 1)
        logits = jnp.where(lane < experts, logits, -1e30)
        raised = jnp.exp(logits - jnp.max(logits, -1, keepdims=True))
        prob = raised / jnp.sum(raised, -1, keepdims=True)
        prob_ref[at, :] = prob
        gate = jnp.sum(jnp.where(lane == route_ref[at, :], prob, 0.0), -1, keepdims=True)
        rows_ref[at, width:] = in_parts(gate)

    moved = Dispatch(rows_ref, target_ref, got_ref, staged, send_sem, recv_sem, devices)
    moved.start()
    moved.wait()


def routed(mixed_low, w_out, token_low, gain, router_wide, route_col, target, capacity, devices, experts):
    vm = pl.BlockSpec(memory_space=pltpu.VMEM)
    dma = pltpu.SemaphoreType.DMA
    rows, width = token_low.shape
    return pl.pallas_call(
        functools.partial(route_kernel, devices=devices, experts=experts, tile=256),
        in_specs=[vm] * 7,
        out_specs=[vm] * 4,
        out_shape=[
            shape_of((rows, width), f32), shape_of((rows, width + LANES), bf16), shape_of((rows, LANES), f32),
            shape_of((devices, capacity, width + LANES), bf16),
        ],
        scratch_shapes=[pltpu.VMEM((devices - 1, capacity, width + LANES), bf16), dma((devices - 1,)), dma((devices - 1,))],
        compiler_params=pltpu.CompilerParams(collective_id=3, has_side_effects=True, vmem_limit_bytes=vmem_cap),
        name="routed",
    )(mixed_low, w_out, token_low, gain, router_wide, route_col, target[None, :])


def collect_kernel(
    sent_ref, target_ref, route_ref, rows_ref, prob_ref, hidden_ref, cot_ref, gain_ref, router_ref, *refs, devices, hops,
    tile, peers, first_step,
):
    hosted = None
    if first_step:
        sources, refs = refs[:2], refs[2:]
    hidden_grad_ref, branch_ref, gain_grad_ref, router_grad_ref = refs[:4]
    got, total, send_sem, recv_sem = refs[-4:]
    if first_step:
        hosted = HostedSum(
            peers, refs[12:16], sources, refs[4:6], refs[8:12], 0, first_step, partial=refs[6:8]
        )
    spot = lax.axis_index("exp")
    capacity = got.shape[1]
    count, width = hidden_ref.shape
    exp_barrier(spot, devices, hosted)
    if hosted:
        hosted.open()
    copies = []
    for hop in hops:
        peer = lax.rem(spot + hop, devices)
        c = pltpu.make_async_remote_copy(
            src_ref=sent_ref.at[peer], dst_ref=got.at[devices - hop - 1], send_sem=send_sem.at[hop - 1],
            recv_sem=recv_sem.at[hop - 1], device_id={"exp": peer}, device_id_type=MESH,
        )
        c.start()
        copies.append(c)

    def spread_back(k, rows):
        slot = lax.broadcasted_iota(jnp.int32, (count, capacity), 1) + k * capacity
        pick = jnp.where(slot == target_ref[...], 1.0, 0.0).astype(bf16)
        return jnp.dot(pick, rows, preferred_element_type=f32)

    total[...] = spread_back(spot, sent_ref[spot])
    for at, (hop, c) in enumerate(zip(hops, copies)):
        c.wait_recv()
        if hosted and at < first_step - 1:
            hosted.fetch(jnp.int32(at))
            hosted.add(jnp.int32(at))
        total[...] += spread_back(lax.rem(spot + devices - hop, devices), got[devices - hop - 1])
    gain_grad_ref[...] = jnp.zeros_like(gain_grad_ref)
    router_grad_ref[...] = jnp.zeros_like(router_grad_ref)

    @pl.loop(0, count // tile)
    def _(i):
        at = pl.ds(pl.multiple_of(i * tile, tile), tile)
        parts = total[at, width:]
        gate_grad = parts[:, 0:1] + parts[:, 1:2] + parts[:, 2:3]
        prob = prob_ref[at, :]
        chosen = jnp.where(lax.broadcasted_iota(jnp.int32, prob.shape, 1) == route_ref[at, :], 1.0, 0.0)
        gate = jnp.sum(prob * chosen, -1, keepdims=True)
        logit_grad = prob * (chosen - gate) * gate_grad
        router_grad_ref[...] += lax.dot_general(
            logit_grad, rows_ref[at, :width].astype(f32), (((0,), (0,)), ((), ())), precision=highest,
            preferred_element_type=f32,
        )
        grad = total[at, :width] + jnp.dot(
            logit_grad, router_ref[...], precision=highest, preferred_element_type=f32
        )
        hidden = hidden_ref[at, :]
        scale = lax.rsqrt(jnp.mean(hidden * hidden, -1, keepdims=True) + epsilon)
        unit = hidden * scale
        gain_grad_ref[...] += jnp.sum(grad * unit, 0, keepdims=True)
        scaled = grad * gain_ref[...]
        hidden_grad = cot_ref[at, :].astype(f32) + scale * (
            scaled - unit * jnp.mean(scaled * unit, -1, keepdims=True)
        )
        hidden_grad_ref[at, :] = hidden_grad
        branch_ref[at, :] = hidden_grad.astype(bf16)

    for c in copies:
        c.wait_send()
    if hosted:
        hosted.fetch(jnp.int32(first_step - 1))
        hosted.add(jnp.int32(first_step - 1))
        hosted.finish()


def collect(blocks, target, route_col, rows, prob, hidden, cot, gain, router_t, sources, first_step, devices):
    vm = pl.BlockSpec(memory_space=pltpu.VMEM)
    dma = pltpu.SemaphoreType.DMA
    capacity, wide = blocks.shape[1:]
    count, width = hidden.shape
    peers, pieces = sources[0].shape[1], [v.shape[2:] for v in sources]
    extra = list(sources) if first_step else []
    more, scratch = [], []
    if first_step:
        more = [shape_of((2, first_step) + p, bf16) for p in pieces] + [shape_of((2,) + p, bf16) for p in pieces]
        scratch = sum_buffers(pieces) + sum_sems(first_step)
    return pl.pallas_call(
        functools.partial(collect_kernel, devices=devices, hops=(2, 3, 1), tile=256, peers=peers, first_step=first_step),
        in_specs=[vm] * 9 + any_specs(len(extra)),
        out_specs=[vm] * 4 + any_specs(len(more)),
        out_shape=[
            shape_of((count, width), f32), shape_of((count, width), bf16), shape_of((1, width), f32),
            shape_of((LANES, width), f32),
        ]
        + more,
        scratch_shapes=scratch
        + [
            pltpu.VMEM((devices - 1, capacity, wide), bf16), pltpu.VMEM((count, wide), f32), dma((devices - 1,)),
            dma((devices - 1,)),
        ],
        compiler_params=pltpu.CompilerParams(collective_id=4, has_side_effects=True, vmem_limit_bytes=vmem_cap),
        name="collect",
    )(blocks, target[:, None], route_col, rows, prob, hidden, cot, gain, router_t, *extra)

SEGMENTS = 4
STARTS = (-4, 1, 3, 6)


def ring_order(place, peers):
    odd = lax.rem(place, 2)
    half = lax.div(place, 2)
    return half + odd * (peers - 1 - 2 * half)


def ring_member(position, peers):
    back = lax.div(2 * position, peers)
    return 2 * position + back * (2 * (peers - 1) + 1 - 4 * position)


class Rings:
    def __init__(self, own, total, sent, landed, send, recv, bases, sizes, peers):
        place = lax.axis_index("seq")
        self.own, self.total, self.sent, self.landed, self.send, self.recv = own, total, sent, landed, send, recv
        self.bases, self.sizes, self.peers = bases, sizes, peers
        self.position = ring_order(place, peers)
        self.after = ring_member(lax.rem(self.position + 1, peers), peers)
        self.before = ring_member(lax.rem(self.position + peers - 1, peers), peers)

    def rows(self, ring, steps):
        sign = 1 if ring % 2 == 0 else -1
        chunk = self.sizes[ring] // self.peers
        c = lax.rem(self.position + sign * steps + 2 * self.peers, self.peers)
        return pl.ds(pl.multiple_of(self.bases[ring] + c * chunk, 16), chunk)

    def target(self, ring):
        return {"seq": self.after if ring % 2 == 0 else self.before}

    def first(self, ring, s):
        chunk = self.sizes[ring] // self.peers
        return pltpu.make_async_remote_copy(
            src_ref=self.sent.at[ring, s, pl.ds(0, chunk)], dst_ref=self.landed.at[ring, s, pl.ds(0, chunk)],
            send_sem=self.send.at[ring, s], recv_sem=self.recv.at[ring, s], device_id=self.target(ring),
            device_id_type=MESH,
        )

    def second(self, ring, s):
        part = self.total.at[self.rows(ring, 1 - s)]
        at = self.peers - 1 + s
        return pltpu.make_async_remote_copy(
            src_ref=part, dst_ref=part, send_sem=self.send.at[ring, at], recv_sem=self.recv.at[ring, at],
            device_id=self.target(ring), device_id_type=MESH,
        )

    def begin(self, ring):
        chunk = self.sizes[ring] // self.peers
        self.sent[ring, 0, pl.ds(0, chunk)] = self.own[self.rows(ring, 0), :].astype(bf16)
        self.first(ring, 0).start()

    def advance(self, ring, s):
        peers, chunk = self.peers, self.sizes[ring] // self.peers

        @pl.when(jnp.logical_and(s >= 1, s <= peers - 2))
        def _():
            self.first(ring, s - 1).wait_recv()
            summed = self.landed[ring, s - 1, pl.ds(0, chunk)].astype(f32) + self.own[self.rows(ring, -s), :]
            self.sent[ring, s, pl.ds(0, chunk)] = summed.astype(bf16)
            self.first(ring, s).start()

        @pl.when(s == peers - 1)
        def _():
            self.first(ring, peers - 2).wait_recv()
            summed = self.landed[ring, peers - 2, pl.ds(0, chunk)].astype(f32) + self.own[self.rows(ring, 1), :]
            self.total[self.rows(ring, 1), :] = summed.astype(bf16)
            self.second(ring, 0).start()

        @pl.when(jnp.logical_and(s >= peers, s <= 2 * peers - 3))
        def _():
            self.second(ring, s - peers).wait_recv()
            self.second(ring, s - peers + 1).start()

        @pl.when(s == 2 * peers - 2)
        def _():
            self.second(ring, peers - 2).wait_recv()

    def drain(self):
        @pl.loop(0, self.peers - 1)
        def _(s):
            for ring in range(len(self.sizes)):
                self.first(ring, s).wait_send()
                self.second(ring, s).wait_send()


def finish_kernel(
    proj_ref, normed_ref, win_ref, outo_ref, small_ref, gain_ref, token_ref, hiddeng_ref, hidden_ref, rows_ref, target_ref,
    tok_ref, up_in, down_in,
    in_sum_ref, out_sum_ref, small_sum_ref, tokens_grad_ref, block_ref, up_ref, down_ref,
    own, total, near_stage, small_all, gain_part, near_in, near_small, far_in, far_small, pass_in, pass_small, sent, landed, near_send, near_recv, far_send, far_recv, ring_send, ring_recv,
    *spread_pair, peers, bases, sizes, halo, tile, gain_row, first_step, last_step,
):
    spot = lax.axis_index("exp")
    width, wide = near_in.shape[1:]
    rows_out = outo_ref.shape[0]
    rows_small, share = near_small.shape[1:]
    folds = wide // share
    count = proj_ref.shape[0]
    third = width // 3
    near = spot + 1 - 2 * lax.rem(spot, 2)
    far = lax.rem(spot + 2, 4)
    across = lax.rem(near + 2, 4)
    rings = Rings(own, total, sent, landed, ring_send, ring_recv, bases, sizes, peers)
    barrier = pltpu.get_barrier_semaphore()
    for device in ({"exp": near}, {"exp": far}, {"seq": rings.after}, {"seq": rings.before}):
        pl.semaphore_signal(barrier, inc=1, device_id=device, device_id_type=MESH)
    pl.semaphore_wait(barrier, 4)
    spread = None
    if last_step > first_step:
        spread = HostedSpread(peers, spread_pair, (up_ref, down_ref), first_step, last_step)
        spread.open()

    def columns(k, size):
        return pl.ds(pl.multiple_of(k * size, size), size)

    def copy(source, target, send, recv, device):
        return pltpu.make_async_remote_copy(
            src_ref=source, dst_ref=target, send_sem=send, recv_sem=recv, device_id=device, device_id_type=MESH
        )

    def in_rows(i):
        return slice(i * third, (i + 1) * third)

    def near_copy(slot, piece):
        k = across if slot else near
        if piece == 4:
            source, target = small_all.at[:, columns(k, share)], near_small.at[slot]
        else:
            at = pl.ds((piece - 1) * third, third)
            source, target = near_stage.at[slot, at], near_in.at[slot, at]
        return copy(source, target, near_send.at[slot, piece], near_recv.at[slot, piece], {"exp": near})

    def far_copy(piece):
        if piece == 4:
            source, target = pass_small, far_small
        else:
            at = pl.ds((piece - 1) * third, third)
            source, target = pass_in.at[at], far_in.at[at]
        return copy(source, target, far_send.at[piece], far_recv.at[piece], {"exp": far})

    def in_tile(i, k):
        part = lax.dot_general(
            normed_ref[pl.ds(halo, count), in_rows(i)], proj_ref[:, columns(k, wide)], (((0,), (0,)), ((), ())),
            preferred_element_type=f32,
        )
        scaled = part * win_ref[in_rows(i), columns(k, wide)].astype(f32)
        gain_part[in_rows(i), :] += tree_sum(scaled[:, h * LANES : (h + 1) * LANES] for h in range(wide // LANES))
        return part

    def into_own(base, values, add):
        size = values.shape[0]
        for h in range(values.shape[1] // share):
            at = slice(base + h * size, base + (h + 1) * size)
            part = values[:, h * share : (h + 1) * share]
            if add:
                own[at, :] += part
            else:
                own[at, :] = part

    def pad_own(n, used):
        if used < sizes[n]:
            own[bases[n] + used : bases[n] + sizes[n], :] = jnp.zeros((sizes[n] - used, share), f32)

    small_base = bases[3] + folds * third
    into_own(bases[0], outo_ref[...], False)
    pad_own(0, folds * rows_out)
    rings.begin(0)
    gain_part[...] = jnp.zeros_like(gain_part)
    small_all[...] = small_ref[...]
    for i in range(3):
        for slot, k in ((1, across), (0, near)):
            near_stage[slot, in_rows(i), :] = in_tile(i, k).astype(bf16)
            near_copy(slot, 1 + i).start()
        distant = in_tile(i, far)
        near_copy(1, 1 + i).wait_recv()
        pass_in[in_rows(i), :] = (distant + near_in[1, in_rows(i), :].astype(f32)).astype(bf16)
        far_copy(1 + i).start()
        mine = in_tile(i, spot)
        near_copy(0, 1 + i).wait_recv()
        into_own(bases[1 + i], mine + near_in[0, in_rows(i), :].astype(f32), False)
        pad_own(1 + i, folds * third)
        rings.advance(0, jnp.int32(1 + i))
    quarter = width // 4
    for k in range(4):
        part = jnp.sum(gain_part[k * quarter : (k + 1) * quarter, :], -1, keepdims=True)
        eye = lax.broadcasted_iota(jnp.int32, (quarter, quarter), 0) == lax.broadcasted_iota(
            jnp.int32, (quarter, quarter), 1
        )
        row = jnp.sum(jnp.where(eye, part, 0.0), 0, keepdims=True) / gain_ref[:, k * quarter : (k + 1) * quarter]
        group = slice(gain_row, gain_row + 16)
        old = small_all[group, k * share : k * share + quarter].astype(f32)
        top = lax.broadcasted_iota(jnp.int32, old.shape, 0) == 0
        small_all[group, k * share : k * share + quarter] = jnp.where(top, row, old).astype(bf16)
    for slot in (1, 0):
        near_copy(slot, 4).start()
    near_copy(1, 4).wait_recv()
    pass_small[...] = (small_all[:, columns(far, share)].astype(f32) + near_small[1].astype(f32)).astype(bf16)
    far_copy(4).start()
    near_copy(0, 4).wait_recv()
    own[small_base : small_base + rows_small, :] = (
        small_all[:, columns(spot, share)].astype(f32) + near_small[0].astype(f32)
    )
    def arrived(ring):
        far_copy(ring).wait_recv()
        into_own(bases[ring], far_in[in_rows(ring - 1), :].astype(f32), True)
        if ring == SEGMENTS - 1:
            far_copy(4).wait_recv()
            own[small_base : small_base + rows_small, :] += far_small[...].astype(f32)
        rings.begin(ring)

    def place_rows(out_ref, values, i):
        group = out_ref.shape[0]
        steps = tile // group
        values = jnp.swapaxes(values.reshape(steps, group, width), 0, 1)
        out_ref[:, pl.ds(pl.multiple_of(i * steps, steps), steps), :] = values.astype(out_ref.dtype)

    def token_tile(i):
        at = pl.ds(pl.multiple_of(i * tile, tile), tile)
        grad = lax.dot_general(proj_ref[at, :], win_ref[...], (((1,), (1,)), ((), ())), preferred_element_type=f32)
        values = token_ref[at, :].astype(f32)
        scale = lax.rsqrt(jnp.mean(values * values, -1, keepdims=True) + epsilon)
        unit = values * scale
        scaled = grad * gain_ref[...]
        total_grad = hiddeng_ref[at, :] + scale * (scaled - unit * jnp.mean(scaled * unit, -1, keepdims=True))
        place_rows(tokens_grad_ref, total_grad, i)

    def block_tile(i):
        at = pl.ds(pl.multiple_of(i * tile, tile), tile)
        capacity = tok_ref.shape[1]
        parts = rows_ref[at, width:].astype(f32)
        gate = parts[:, 0:1] + parts[:, 1:2] + parts[:, 2:3]
        tok = jnp.zeros((tile, width), f32)
        for k in range(tok_ref.shape[0]):
            slot = lax.broadcasted_iota(jnp.int32, (tile, capacity), 1) + k * capacity
            pick = jnp.where(slot == target_ref[at, :], 1.0, 0.0).astype(bf16)
            tok = tok + jnp.dot(pick, tok_ref[k], preferred_element_type=f32)
        place_rows(block_ref, hidden_ref[at, :] + gate * tok, i)

    tiles = count // tile

    @pl.loop(0, 2 * peers - 1 + STARTS[-1])
    def _(turn):
        for ring in range(SEGMENTS):
            step = turn - STARTS[ring]
            if ring:

                @pl.when(step == 0)
                def _():
                    arrived(ring)

            rings.advance(ring, step)

        if spread:
            for n in range(last_step - first_step):

                @pl.when(turn == 4 + 6 * n)
                def _():
                    spread.hand(jnp.int32(first_step + n))

        @pl.when(turn < tiles)
        def _():
            token_tile(turn)

        @pl.when(jnp.logical_and(turn >= tiles, turn < 2 * tiles))
        def _():
            block_tile(turn - tiles)

    for i in range(3):
        for h in range(folds):
            at = slice(bases[1 + i] + h * third, bases[1 + i] + (h + 1) * third)
            in_sum_ref[in_rows(i), h * share : (h + 1) * share] = total[at, :].astype(f32)
    for h in range(folds):
        at = slice(bases[0] + h * rows_out, bases[0] + (h + 1) * rows_out)
        out_sum_ref[:, h * share : (h + 1) * share] = total[at, :].astype(f32)
    small_sum_ref[...] = total[small_base : small_base + rows_small, :].astype(f32)
    for piece in range(1, 5):
        for slot in (1, 0):
            near_copy(slot, piece).wait_send()
        far_copy(piece).wait_send()
    rings.drain()
    if spread:
        spread.finish(True)


def finish(proj, normed_ext, w_in, out_own, small, gain, token_low, hidden_grad, hidden_one, moe_rows, target, tok, results, steps, gain_row, group):
    peers, devices = lax.axis_size("seq"), lax.axis_size("exp")
    count, width = token_low.shape
    wide, rows_out = proj.shape[1] // devices, out_own.shape[0]
    rows_small, share = small.shape[0], small.shape[1] // devices
    folds, third, unit = wide // share, width // 3, 16 * peers
    used = (folds * rows_out, folds * third, folds * third, folds * third + rows_small)
    sizes = tuple(-(-u // unit) * unit for u in used)
    bases = tuple(sum(sizes[:i]) for i in range(SEGMENTS))
    length, chunk = sum(sizes), max(sizes) // peers
    vm = pl.BlockSpec(memory_space=pltpu.VMEM)
    dma = pltpu.SemaphoreType.DMA
    shapes = ((width, wide), (rows_small, share))
    return pl.pallas_call(
        functools.partial(
            finish_kernel, peers=peers, bases=bases, sizes=sizes, halo=normed_ext.shape[0] - count, tile=256,
            gain_row=gain_row, first_step=steps[0], last_step=steps[1],
        ),
        in_specs=[vm] * 12 + any_specs(2),
        out_specs=[vm] * 5 + any_specs(2),
        out_shape=[
            shape_of((width, wide), f32), shape_of((rows_out, wide), f32), shape_of((rows_small, share), f32),
            shape_of((group, count // group, width), f32), shape_of((group, count // group, width), bf16),
        ]
        + [shape_of(v.shape, bf16) for v in results],
        scratch_shapes=[
            pltpu.VMEM((length, share), f32), pltpu.VMEM((length, share), bf16), pltpu.VMEM((2, width, wide), bf16),
            pltpu.VMEM(small.shape, bf16), pltpu.VMEM((width, LANES), f32),
        ]
        + [pltpu.VMEM((2,) + s, bf16) for s in shapes]
        + [pltpu.VMEM(s, bf16) for s in shapes]
        + [pltpu.VMEM(s, bf16) for s in shapes]
        + [pltpu.VMEM((SEGMENTS, peers - 1, chunk, share), bf16)] * 2
        + [dma((2, 5)), dma((2, 5)), dma((5,)), dma((5,)), dma((SEGMENTS, 2 * peers - 2)), dma((SEGMENTS, 2 * peers - 2))]
        + (spread_sems(steps[1] - steps[0]) if steps[1] > steps[0] else []),
        input_output_aliases={12: 5, 13: 6},
        compiler_params=pltpu.CompilerParams(collective_id=2, has_side_effects=True, vmem_limit_bytes=64 << 20),
        name="finish",
    )(
        proj, normed_ext, w_in, out_own, small, gain, token_low, hidden_grad, hidden_one, moe_rows, target[:, None], tok, *results,
    )

PIECES = 2


def gather_kernel(in_ref, small_ref, edge_ref, ids_ref, win_ref, wsmall_ref, before_ref, before_ids, near_sems, far_sems, pair_sems, edge_sems, own_sem):
    place, peers = lax.axis_index("seq"), lax.axis_size("seq")
    spot = lax.axis_index("exp")
    near = spot + 1 - 2 * lax.rem(spot, 2)
    far = lax.rem(spot + 2, 4)
    bit = lax.rem(place, 2)
    pair = place + 1 - 2 * bit
    width, wide = in_ref.shape
    share = small_ref.shape[1]
    chunk = width // 2 // PIECES
    has_before, has_after = place > 0, place < peers - 1
    barrier = pltpu.get_barrier_semaphore()
    for target in ({"exp": near}, {"exp": far}, {"seq": pair}):
        pl.semaphore_signal(barrier, inc=1, device_id=target, device_id_type=MESH)

    @pl.when(has_before)
    def _():
        pl.semaphore_signal(barrier, inc=1, device_id={"seq": place - 1}, device_id_type=MESH)

    @pl.when(has_after)
    def _():
        pl.semaphore_signal(barrier, inc=1, device_id={"seq": place + 1}, device_id_type=MESH)

    pl.semaphore_wait(barrier, 3 + has_before.astype(jnp.int32) + has_after.astype(jnp.int32))

    def columns(ref, k, size):
        return ref.at[:, pl.ds(pl.multiple_of(k * size, size), size)]

    def rows(k, half, piece):
        at = pl.multiple_of((half * PIECES + piece) * chunk, chunk)
        return win_ref.at[pl.ds(at, chunk), pl.ds(pl.multiple_of(k * wide, wide), wide)]

    def copy(source, target, sems, slot, device):
        return pltpu.make_async_remote_copy(
            src_ref=source, dst_ref=target, send_sem=sems.at[0, slot], recv_sem=sems.at[1, slot], device_id=device,
            device_id_type=MESH,
        )

    def edge_copies():
        return (
            copy(edge_ref, before_ref, edge_sems, 0, {"seq": place + 1}),
            copy(ids_ref, before_ids, edge_sems, 1, {"seq": place + 1}),
        )

    outward = []
    for piece in range(PIECES):
        at = pl.multiple_of((bit * PIECES + piece) * chunk, chunk)
        outward.append(copy(in_ref.at[pl.ds(at, chunk), :], rows(spot, bit, piece), far_sems, piece, {"exp": far}))
    outward.insert(0, copy(small_ref, columns(wsmall_ref, spot, share), far_sems, PIECES, {"exp": far}))
    for c in outward:
        c.start()
    beside = [
        copy(small_ref, columns(wsmall_ref, spot, share), near_sems, 0, {"exp": near}),
        copy(in_ref, columns(win_ref, spot, wide), near_sems, 1, {"exp": near}),
    ]
    for c in beside:
        c.start()

    @pl.when(has_after)
    def _():
        for c in edge_copies():
            c.start()

    @pl.when(jnp.logical_not(has_before))
    def _():
        before_ref[...] = jnp.zeros_like(before_ref)
        before_ids[...] = jnp.zeros_like(before_ids)

    own = [
        pltpu.make_async_copy(in_ref, columns(win_ref, spot, wide), own_sem.at[0]),
        pltpu.make_async_copy(small_ref, columns(wsmall_ref, spot, share), own_sem.at[1]),
    ]
    for c in own:
        c.start()
    outward[0].wait_recv()
    beside.append(copy(columns(wsmall_ref, far, share), columns(wsmall_ref, far, share), near_sems, 2, {"exp": near}))
    beside[-1].start()
    crossing = []
    for piece in range(PIECES):
        outward[1 + piece].wait_recv()
        part = rows(far, bit, piece)
        crossing.append(copy(part, part, pair_sems, piece, {"seq": pair}))
        crossing[-1].start()
        beside.append(copy(part, part, near_sems, 3 + piece, {"exp": near}))
        beside[-1].start()
    for piece in range(PIECES):
        crossing[piece].wait_recv()
        part = rows(far, 1 - bit, piece)
        beside.append(copy(part, part, near_sems, 3 + PIECES + piece, {"exp": near}))
        beside[-1].start()
    for c in beside:
        c.wait_recv()
    for c in outward + beside + crossing:
        c.wait_send()
    for c in own:
        c.wait()

    @pl.when(has_before)
    def _():
        for c in edge_copies():
            c.wait_recv()

    @pl.when(has_after)
    def _():
        for c in edge_copies():
            c.wait_send()


def gather_weights(in_shard, small, edge, ids, devices):
    vm = pl.BlockSpec(memory_space=pltpu.VMEM)
    dma = pltpu.SemaphoreType.DMA
    return pl.pallas_call(
        gather_kernel,
        in_specs=[pl.BlockSpec(memory_space=pl.ANY), vm, vm, vm],
        out_specs=[pl.BlockSpec(memory_space=pl.ANY), vm, vm, vm],
        out_shape=[
            shape_of((in_shard.shape[0], in_shard.shape[1] * devices), bf16),
            shape_of((small.shape[0], small.shape[1] * devices), bf16), shape_of(edge.shape, edge.dtype),
            shape_of(ids.shape, ids.dtype),
        ],
        scratch_shapes=[dma((2, 3 + 2 * PIECES)), dma((2, PIECES + 1)), dma((2, PIECES)), dma((2, 2)), dma((2,))],
        compiler_params=pltpu.CompilerParams(collective_id=5, has_side_effects=True, vmem_limit_bytes=32 << 20),
        name="gather_weights",
    )(in_shard, small, edge, ids)

def hosting_plan(peers, count):
    if peers == 8 and count == 12:
        return 3, 4, 5
    return 0, peers - 1, peers - 1


class Hosted:
    def __init__(self, peers, send, recv):
        place = lax.axis_index("seq")
        self.peers, self.send, self.recv = peers, send, recv
        self.position = ring_order(place, peers)
        self.after = ring_member(lax.rem(self.position + 1, peers), peers)
        self.before = ring_member(lax.rem(self.position + peers - 1, peers), peers)

    def enter(self, barrier):
        for device in (self.after, self.before):
            pl.semaphore_signal(barrier, inc=1, device_id={"seq": device}, device_id_type=MESH)

    def chunk(self, ring, steps):
        sign = 1 if ring == 0 else -1
        return lax.rem(self.position + sign * steps + 2 * self.peers, self.peers)

    def remote(self, lane, source, target, slot):
        return pltpu.make_async_remote_copy(
            src_ref=source, dst_ref=target, send_sem=self.send.at[lane, slot], recv_sem=self.recv.at[lane, slot],
            device_id={"seq": self.after if lane % 2 == 0 else self.before}, device_id_type=MESH,
        )


class HostedSum(Hosted):
    def __init__(self, peers, sems, sources, landed, buffers, first, last, opening=None, partial=None, spread=None):
        self.load, self.keep = sems[2], sems[3]
        super().__init__(peers, sems[0], sems[1])
        self.sources, self.landed, self.first, self.last = sources, landed, first, last
        self.own, self.got = buffers[:2], buffers[2:]
        self.opening, self.partial, self.spread = opening, partial, spread
        self.lanes = [(2 * a + ring, a, ring) for a in range(2) for ring in range(2)]

    def opened(self, lane, a, ring):
        source = self.opening[a].at[ring] if self.opening else self.sources[a].at[ring, self.chunk(ring, -self.first)]
        return self.remote(lane, source, self.landed[a].at[ring, 0], 0)

    def passing(self, lane, a, ring, s):
        slot = s - self.first
        return self.remote(lane, self.own[a].at[ring, lax.rem(s, 2)], self.landed[a].at[ring, slot], slot)

    def loads(self, lane, a, ring, s):
        return (
            pltpu.make_async_copy(self.landed[a].at[ring, s - self.first], self.got[a].at[ring], self.load.at[lane, 0]),
            pltpu.make_async_copy(
                self.sources[a].at[ring, self.chunk(ring, -s - 1)], self.own[a].at[ring, lax.rem(s + 1, 2)],
                self.load.at[lane, 1],
            ),
        )

    def kept(self, lane, a, ring):
        source = self.own[a].at[ring, self.last % 2]
        if self.partial:
            return pltpu.make_async_copy(source, self.partial[a].at[ring], self.keep.at[lane])
        return pltpu.make_async_copy(source, self.spread.result[a].at[ring, self.chunk(ring, 1)], self.keep.at[lane])

    def closing(self, lane, a, ring):
        target = self.spread.result[a].at[ring, self.chunk(ring, 1)]
        return self.spread.remote(lane, self.own[a].at[ring, self.last % 2], target, 0)

    def open(self):
        for q in self.lanes:
            self.opened(*q).start()

    def fetch(self, s):
        for q in self.lanes:
            self.passing(*q, s).wait_recv()

            @pl.when(s >= self.first + 2)
            def _():
                self.passing(*q, s - 1).wait_send()

            for c in self.loads(*q, s):
                c.start()

    def add(self, s):
        for q in self.lanes:
            lane, a, ring = q
            for c in self.loads(*q, s):
                c.wait()
            slot = lax.rem(s + 1, 2)
            self.own[a][ring, slot] = (self.own[a][ring, slot].astype(f32) + self.got[a][ring].astype(f32)).astype(bf16)

            @pl.when(s < self.last - 1)
            def _():
                self.passing(*q, s + 1).start()

            @pl.when(s == self.last - 1)
            def _():
                self.kept(*q).start()
                if self.spread:
                    self.closing(*q).start()

    def finish(self):
        for q in self.lanes:
            self.opened(*q).wait_send()
            if self.last - 1 > self.first:
                self.passing(*q, self.last - 1).wait_send()
            self.kept(*q).wait()
            if self.spread:
                self.closing(*q).wait_send()


class HostedSpread(Hosted):
    def __init__(self, peers, sems, result, first, last):
        super().__init__(peers, sems[0], sems[1])
        self.result, self.first, self.last = result, first, last
        self.lanes = [(2 * a + ring, a, ring) for a in range(2) for ring in range(2)]

    def handing(self, lane, a, ring, s):
        part = self.result[a].at[ring, self.chunk(ring, 1 - s)]
        return self.remote(lane, part, part, s - self.first)

    def open(self):
        for q in self.lanes:
            self.handing(*q, self.first).start()

    def hand(self, s):
        for q in self.lanes:
            self.handing(*q, s).wait_recv()

            @pl.when(s < self.last - 1)
            def _():
                self.handing(*q, s + 1).start()

    def finish(self, opened):
        for q in self.lanes:

            @pl.loop(self.first + (0 if opened else 1), self.last)
            def _(s):
                self.handing(*q, s).wait_send()


def any_specs(count):
    return [pl.BlockSpec(memory_space=pl.ANY)] * count


def sum_buffers(pieces):
    return [pltpu.VMEM((2, 2) + p, bf16) for p in pieces] + [pltpu.VMEM((2,) + p, bf16) for p in pieces]


def sum_sems(steps):
    dma = pltpu.SemaphoreType.DMA
    return [dma((4, steps)), dma((4, steps)), dma((4, 2)), dma((4,))]


def spread_sems(steps):
    return [pltpu.SemaphoreType.DMA((4, steps)), pltpu.SemaphoreType.DMA((4, steps))]

def rms_norm(values, gain):
    return values * lax.rsqrt(jnp.mean(values * values, -1, keepdims=True) + epsilon) * gain


def passed_along(value, axis, steps):
    count = lax.axis_size(axis)
    initial, last = (max(0, -steps), min(count, count - steps))
    return lax.ppermute(value, axis, [(source, source + steps) for source in range(initial, last)])


def by_time(values):
    values = jnp.swapaxes(values, 0, 1)
    return values.reshape((values.shape[0] * values.shape[1],) + values.shape[2:])


def packed_small(norm_gain, conv_weight, conv_bias, x_proj, dt_proj, dt_bias, a_log, d_skip, moe_gain, router):
    share = conv_bias.shape[0]
    packed = [conv_weight, conv_bias[None], x_proj.T, dt_proj, dt_bias[None], a_log.T, d_skip[None]]
    narrow = jnp.concatenate([norm_gain[None], moe_gain[None], router.T], 0)
    total = jnp.concatenate(packed + [narrow.reshape(-1, share)], 0)
    return jnp.pad(total, ((0, -total.shape[0] % 16), (0, 0))), [p.shape[0] for p in packed], narrow.shape


def unpacked_small(whole, counts, narrow_shape, devices):
    out, at = [], 0
    for c in counts:
        out.append(whole[at : at + c])
        at += c
    share = whole.shape[1] // devices
    fold = narrow_shape[0] * narrow_shape[1] // share
    rest = whole[at : at + fold].reshape(fold, devices, share).transpose(1, 0, 2).reshape((devices,) + narrow_shape)
    rest = rest.transpose(1, 0, 2).reshape(narrow_shape[0], -1)
    return out, rest[0], rest[1], rest[2:].T


def local(
    tokens, segment_ids, routes, slot_index, norm_gain, in_proj, conv_weight, conv_bias, x_proj, dt_proj, dt_bias,
    a_log, d_skip, out_proj, moe_gain, router, expert_up, expert_down, cotangent,
):
    seq_count, part_len, width = tokens.shape
    row_count = seq_count * part_len
    group = seq_count
    kernel_len = conv_weight.shape[0]
    state_width = a_log.shape[1]
    rank_width = dt_proj.shape[0]
    halo = kernel_len * group
    devices = lax.axis_size("exp")
    doc_ids = segment_ids + 1
    edge_start = part_len - kernel_len
    token_low = by_time(tokens)
    edge_ids = jnp.pad(doc_ids[:, edge_start:], ((0, 0), (0, LANES - kernel_len)))
    small_shard, counts, narrow_shape = packed_small(
        norm_gain, conv_weight, conv_bias, x_proj, dt_proj, dt_bias, a_log, d_skip, moe_gain, router
    )
    w_in, small_whole, before_rows, before_ids = gather_weights(
        in_proj, small_shard, token_low[row_count - halo :], edge_ids, devices
    )
    out_proj, small_whole = lax.optimization_barrier((out_proj, small_whole))
    w_out = lax.all_gather(out_proj, "exp", axis=0, tiled=True)
    (w_conv, b_conv, w_x_t, w_dt, b_dt, log_decay, skip_gain), gain_one, gain_two, w_router = unpacked_small(
        small_whole, counts, narrow_shape, devices
    )
    inner_width = w_out.shape[0]
    expert_total = w_router.shape[1]
    capacity = 5 * row_count // (4 * expert_total)
    blocks = inner_width // LANES

    ext_ids = jnp.concatenate([before_ids[:, :kernel_len], doc_ids], 1)
    match = jnp.stack([ext_ids[:, 1 + k : 1 + k + part_len] == doc_ids for k in range(kernel_len - 1)])
    match = jnp.transpose(match, (2, 1, 0)).reshape(row_count, kernel_len - 1).astype(f32)
    lanes = 2 * LANES
    gain_one = gain_one.astype(f32)[None]
    gain_two = gain_two.astype(f32)[None]
    route_rows = by_time(routes)
    slot_rows = by_time(slot_index)
    target = jnp.where(
        slot_rows < capacity, route_rows * capacity + slot_rows, expert_total * capacity
    )
    cot_rows = by_time(cotangent)
    w_conv, b_conv = w_conv.astype(f32), b_conv.astype(f32)
    w_x = w_x_t.T
    ci, conv_low, gate, mixed, normed_ext = front(
        token_low, before_rows, gain_one, w_in, w_conv, b_conv, match, w_x, halo, group, lanes
    )
    rate_low = mixed[:, :rank_width].astype(bf16)
    bc = split_three(mixed[:, rank_width:])
    pick = pick_matrix(2 * state_width)
    bias = b_dt.astype(f32)
    skip = skip_gain.astype(f32)
    a_mat = -jnp.exp(log_decay.astype(f32))
    a2 = a_mat * log2e
    a_blocks = a2.reshape(state_width, blocks, LANES).transpose(1, 0, 2)
    step, z, mixed_low, start, total, cot_recv = forward_scan(
        rate_low, w_dt, bias, conv_low, bc, pick, match, a_blocks, gate, skip, cot_rows, target, capacity, group, devices
    )
    route_col = route_rows[:, None]
    router_wide = jnp.pad(w_router, ((0, 0), (0, LANES - expert_total)))
    hidden_one, moe_rows, prob, received = routed(
        mixed_low, w_out, token_low, gain_two, router_wide, route_col, target, capacity, devices, expert_total
    )
    expert_out, rows_back, up_grad, down_grad = one_expert(
        received.reshape(devices * capacity, width + LANES), cot_recv.reshape(devices * capacity, width),
        expert_up[0], expert_down[0],
    )
    peers = lax.axis_size("seq")
    first_step, spread_first, spread_second = hosting_plan(peers, blocks)
    sources = [up_grad.reshape(2, peers, -1, up_grad.shape[1]), down_grad.reshape(2, peers, -1, width)]
    hidden_grad, branch_grad, gain_two_grad, router_grad_t, *hosted = collect(
        rows_back.reshape(devices, capacity, width + LANES), target, route_col, moe_rows, prob, hidden_one, cot_rows,
        gain_two, router_wide.astype(f32).T, sources, first_step, devices,
    )
    out_proj_grad = jnp.dot(mixed_low.T, branch_grad, preferred_element_type=f32)
    mixed_grad = jnp.dot(branch_grad, w_out.T, preferred_element_type=f32)
    proj, rate_pre_low, cg, small_one, mixed_proj_grad, tok, *hosted = backward_scan(
        mixed_grad, gate, z, step, conv_low, bc, pick, match, a_blocks, total, start, rate_low, w_dt, bias, skip,
        expert_out.reshape(devices, capacity, width), sources, hosted[2:], group, devices,
    )
    proj, ends, small_two, out_own, *results = conv_back(
        cg, conv_low, mixed_proj_grad, w_x, ci, w_conv, b_conv, match, proj, out_proj_grad.astype(bf16), hosted[2:],
        (spread_first, spread_second), halo, group, lanes, devices,
    )
    edge_back = passed_along(ends[:halo].astype(bf16), "seq", -1).astype(f32)
    proj = lax.dynamic_update_slice(proj, (ends[halo:] + edge_back).astype(bf16), (row_count - halo, 0))

    narrow = jnp.concatenate([jnp.zeros_like(gain_two_grad), gain_two_grad, router_grad_t[:expert_total]], 0)
    share, own_width = inner_width // devices, width // devices
    narrow = narrow.reshape(narrow.shape[0], devices, own_width)
    narrow = jnp.pad(narrow, ((0, -narrow.shape[0] % 16), (0, 0), (0, share - own_width))).astype(bf16)
    packed = jnp.concatenate([small_one, small_two, narrow.reshape(-1, inner_width)], 0)
    gain_row = small_one.shape[0] + small_two.shape[0]
    in_sum, out_sum, sums, tokens_grad, block_out, up_sum, down_sum = finish(
        proj, normed_ext, w_in, out_own, packed, gain_one, token_low, hidden_grad, hidden_one, moe_rows,
        target, tok, results, (spread_second, peers - 1), gain_row, group,
    )
    at, own = 0, []
    for first, rows in (
        (0, rank_width), (rank_width, state_width), (rank_width + state_width, 1), (rank_width + state_width + 1, 1)
    ):
        own.append(sums[first : first + rows])
    at = small_one.shape[0]
    mixed_width = mixed_proj_grad.shape[1]
    for first, rows in ((0, mixed_width), (mixed_width, kernel_len), (mixed_width + kernel_len, 1)):
        own.append(sums[at + first : at + first + rows])
    at += small_two.shape[0]
    own_narrow = sums[at : at + 2 + expert_total, :own_width]
    return (
        block_out,
        tokens_grad,
        own_narrow[0],
        in_sum,
        own[5],
        own[6][0],
        own[4].T,
        own[0],
        own[2][0],
        own[1].T,
        own[3][0],
        out_sum,
        own_narrow[1],
        own_narrow[2:].T,
        up_sum.reshape(expert_up.shape).astype(f32),
        down_sum.reshape(expert_down.shape).astype(f32),
    )


def solution(mesh):
    in_specs = (
        P("exp", "seq", None),
        P("exp", "seq"),
        P("exp", "seq"),
        P("exp", "seq"),
        P("exp"),
        P(None, "exp"),
        P(None, "exp"),
        P("exp"),
        P("exp", None),
        P(None, "exp"),
        P("exp"),
        P("exp", None),
        P("exp"),
        P("exp", None),
        P("exp"),
        P("exp", None),
        P("exp", None, None),
        P("exp", None, None),
        P("exp", "seq", None),
    )
    out_specs = (
        P("exp", "seq", None),
        P("exp", "seq", None),
        P("exp"),
        P(None, "exp"),
        P(None, "exp"),
        P("exp"),
        P("exp", None),
        P(None, "exp"),
        P("exp"),
        P("exp", None),
        P("exp"),
        P("exp", None),
        P("exp"),
        P("exp", None),
        P("exp", None, None),
        P("exp", None, None),
    )
    return jax.shard_map(local, mesh=mesh, in_specs=in_specs, out_specs=out_specs, check_vma=False)
```

```python
import functools

import jax
import jax.numpy as jnp
from jax import lax
from jax.experimental import pallas as pl
from jax.experimental.pallas import tpu as pltpu
from jax.sharding import PartitionSpec as P

f32, bf16 = jnp.float32, jnp.bfloat16
highest = lax.Precision.HIGHEST
LANES = 128
MESH = pl.DeviceIdType.MESH
epsilon = 1e-05
log2e = 1.4426950408889634
cut = 1e8
ln2 = 0.6931471805599453
vmem_cap = 58 << 20


def tree_sum(parts):
    parts = list(parts)
    while len(parts) > 1:
        paired = [parts[i] + parts[i + 1] for i in range(0, len(parts) - 1, 2)]
        parts = paired + parts[len(parts) - len(parts) % 2 :]
    return parts[0]


UN = dict(state=8, scan=8, adj=8, fwd=4, bwd=4)


def spread(rows_ref, pick_ref, outs, states, group):
    steps = rows_ref.shape[0] // group
    chunk = 16
    wide = 2 * LANES

    @pl.loop(0, steps // chunk)
    def _(i):
        rows = rows_ref[pl.ds(pl.multiple_of(i * chunk * group, chunk * group), chunk * group), :]
        for which, out_ref in outs:
            for n in range(0, states, 2):
                at = (which * states + n) * LANES
                part = jnp.dot(rows, pick_ref[:, at : at + wide], preferred_element_type=f32)
                for k in range(2):
                    out_ref[pl.ds(i * chunk, chunk), n + k] = part[:, k * LANES : (k + 1) * LANES].reshape(
                        chunk, group, LANES
                    )


def softplus(v):
    return jnp.maximum(v, 0.0) + jnp.log1p(jnp.exp(-jnp.abs(v)))


class Carry:
    def __init__(self, step, ends, total, a_all, held, got, sent, send_sem, recv_sem):
        self.step, self.ends, self.total, self.a_all = step, ends, total, a_all
        self.held, self.got, self.sent, self.send_sem, self.recv_sem = held, got, sent, send_sem, recv_sem
        self.place, self.peers = lax.axis_index("seq"), lax.axis_size("seq")
        self.rank = self.place if step > 0 else self.peers - 1 - self.place
        self.count, self.states = ends.shape[0], ends.shape[1]
        self.has_before, self.has_after = self.rank > 0, self.rank < self.peers - 1
        self.lag = jnp.minimum(self.rank, self.count)

    def enter(self, devices=1):
        spot = lax.axis_index("exp")
        barrier = pltpu.get_barrier_semaphore()

        @pl.when(self.has_before)
        def _():
            pl.semaphore_signal(barrier, inc=1, device_id={"seq": self.place - self.step}, device_id_type=MESH)

        @pl.when(self.has_after)
        def _():
            pl.semaphore_signal(barrier, inc=1, device_id={"seq": self.place + self.step}, device_id_type=MESH)

        for hop in range(1, devices):
            pl.semaphore_signal(barrier, inc=1, device_id={"exp": lax.rem(spot + hop, devices)}, device_id_type=MESH)
        neighbours = self.has_before.astype(jnp.int32) + self.has_after.astype(jnp.int32)
        pl.semaphore_wait(barrier, neighbours + (devices - 1))

    def hop(self, u):
        return pltpu.make_async_remote_copy(
            src_ref=self.sent.at[u], dst_ref=self.got.at[u], send_sem=self.send_sem.at[u], recv_sem=self.recv_sem.at[u],
            device_id={"seq": self.place + self.step}, device_id_type=MESH,
        )

    def handle(self, at):
        u = at - self.lag

        @pl.when(jnp.logical_and(u >= 0, u < self.count))
        def _():
            @pl.when(self.has_before)
            def _():
                self.hop(u).wait_recv()
                self.held[u] = self.got[u].astype(f32)

            @pl.when(jnp.logical_not(self.has_before))
            def _():
                self.held[u] = jnp.zeros(self.held.shape[1:], f32)

            @pl.when(self.has_after)
            def _():
                for n in range(self.states):
                    decay = jnp.exp2(self.a_all[u, n : n + 1, :] * self.total[u])
                    self.sent[u, n] = (self.ends[u, n] + decay * self.held[u, n]).astype(bf16)
                self.hop(u).start()

    def leave(self):
        @pl.loop(0, self.count)
        def _(u):
            @pl.when(self.has_after)
            def _():
                self.hop(u).wait_send()


def forward_kernel(
    rate_ref, wdt_ref, bias_ref, conv_ref, bc_ref, pick_ref, match_ref, a_all, gate_ref, skip_ref, cot_ref, target_ref,
    step_ref, z_ref, mixed_ref, start_ref, total_ref, cot_out,
    cot_got, kb_ref, b_all, c_all, step_all, ends, staged, cot_send, cot_recv, got, sent, send_sem, recv_sem, *, states, group, devices,
):
    at = pl.program_id(0)
    count = a_all.shape[0]
    j = lax.rem(at, count)
    carry_of = Carry(1, ends, total_ref, a_all, start_ref, got, sent, send_sem, recv_sem)
    rows = conv_ref.shape[0]
    moved = Dispatch(cot_ref, target_ref, cot_got, staged, cot_send, cot_recv, devices)

    @pl.when(at == 0)
    def _():
        carry_of.enter(devices)
        moved.start()
        kb_ref[...] = broad_cut(match_ref)
        spread(bc_ref, pick_ref, ((0, b_all), (1, c_all)), states, group)

    @pl.when(at < count)
    def _():
        pre = jnp.dot(rate_ref[...], wdt_ref[...], preferred_element_type=f32) + bias_ref[...]
        step = softplus(pre)
        step_ref[...] = step
        step_all[j] = step
        a_rows = [jnp.broadcast_to(a_all[j, n : n + 1, :], (group, LANES)) for n in range(states)]
        un = UN["state"]

        def body(i, carry):
            total, state = carry
            base = pl.multiple_of(i * un * group, un * group)
            x_two = conv_ref[pl.ds(base, un * group), :].astype(f32)
            for k in range(un):
                here = pl.ds(pl.multiple_of(base + k * group, group), group)
                dt = step_ref[here, :]
                masked = dt + kb_ref[here, :]
                u = dt * x_two[k * group : (k + 1) * group]
                total = total + masked
                state = [
                    jnp.exp2(masked * a_rows[n]) * state[n] + u * b_all[un * i + k, n] for n in range(states)
                ]
            return total, state

        zero = jnp.zeros((group, LANES), f32)
        total, state = lax.fori_loop(0, rows // (un * group), body, (zero, [zero] * states))
        total_ref[j] = total
        for n in range(states):
            ends[j, n] = state[n]

    carry_of.handle(at)

    @pl.when(at >= count)
    def _():
        a_rows = [jnp.broadcast_to(a_all[j, n : n + 1, :], (group, LANES)) for n in range(states)]
        un = UN["scan"]

        def body(i, state):
            base = pl.multiple_of(i * un * group, un * group)
            x_two = conv_ref[pl.ds(base, un * group), :].astype(f32)
            outs = []
            for k in range(un):
                here = pl.ds(pl.multiple_of(base + k * group, group), group)
                dt = step_all[j, here, :]
                masked = dt + kb_ref[here, :]
                u = dt * x_two[k * group : (k + 1) * group]
                state = [
                    jnp.exp2(masked * a_rows[n]) * state[n] + u * b_all[un * i + k, n] for n in range(states)
                ]
                outs.append(tree_sum(state[n] * c_all[un * i + k, n] for n in range(states)))
            whole = pl.ds(base, un * group)
            gate = gate_ref[whole, :]
            z = jnp.concatenate(outs, 0) + skip_ref[...] * x_two
            z_ref[whole, :] = z
            mixed_ref[whole, :] = (z * (gate * jax.nn.sigmoid(gate))).astype(bf16)
            return state

        lax.fori_loop(0, rows // (un * group), body, [start_ref[j, n] for n in range(states)])

    @pl.when(at == 2 * count - 1)
    def _():
        carry_of.leave()
        moved.wait()
        cot_out[...] = cot_got[...]


def broad_cut(match_ref):
    keep = match_ref[:, match_ref.shape[1] - 1 :]
    return jnp.broadcast_to((1.0 - keep) * cut, (match_ref.shape[0], LANES))


def backward_kernel(
    mg_ref, gate_ref, z_ref, step_ref, conv_ref, bc_ref, pick_ref, match_ref, a_all, total_ref, start_ref, rate_ref, wdt_ref,
    bias_ref, skip_ref, back_ref, outg_ref,
    gg_ref, low_ref, cg_ref, small_ref, mpg_ref, tok_ref, outo_ref,
    near_got, passed, far_got, mine, out_send, out_recv, out_load, back_send, back_recv, back_own, kb_ref, b_all, c_all, b_acc, c_acc, kept, dt_grad, g_all, rate_acc, ends, last, got, sent, send_sem, recv_sem, *, states, group, devices,
):
    at = pl.program_id(0)
    count = a_all.shape[0]
    j = lax.rem(at, count)
    carry_of = Carry(-1, ends, total_ref, a_all, last, got, sent, send_sem, recv_sem)
    steps = conv_ref.shape[0] // group
    rank = rate_ref.shape[1]
    zero = jnp.zeros((group, LANES), f32)
    spot = lax.axis_index("exp")

    def back_copy(hop):
        peer = lax.rem(spot + hop, devices)
        return pltpu.make_async_remote_copy(
            src_ref=back_ref.at[peer], dst_ref=tok_ref.at[spot], send_sem=back_send.at[hop - 1],
            recv_sem=back_recv.at[hop - 1], device_id={"exp": peer}, device_id_type=MESH,
        )

    near = spot + 1 - 2 * lax.rem(spot, 2)
    far = lax.rem(spot + 2, 4)
    across = lax.rem(near + 2, 4)
    rows_out = mine.shape[0]

    def out_rows(k):
        return outg_ref.at[pl.ds(pl.multiple_of(k * rows_out, rows_out), rows_out), :]

    def out_move(slot):
        if slot == 2:
            source, target, device = passed, far_got, far
        else:
            source, target, device = out_rows(across if slot else near), near_got.at[slot], near
        return pltpu.make_async_remote_copy(
            src_ref=source, dst_ref=target, send_sem=out_send.at[slot], recv_sem=out_recv.at[slot],
            device_id={"exp": device}, device_id_type=MESH,
        )

    def out_loads():
        return (
            pltpu.make_async_copy(out_rows(far), passed, out_load.at[0]),
            pltpu.make_async_copy(out_rows(spot), mine, out_load.at[1]),
        )

    def out_store():
        return pltpu.make_async_copy(mine, outo_ref, out_load.at[2])

    def own_copy():
        return pltpu.make_async_copy(back_ref.at[spot], tok_ref.at[spot], back_own.at[0])

    @pl.when(at == 0)
    def _():
        carry_of.enter(devices)
        out_move(1).start()
        out_move(0).start()
        for c in out_loads():
            c.start()
        own_copy().start()
        for hop in range(1, devices):
            back_copy(hop).start()
        kb_ref[...] = broad_cut(match_ref)
        spread(bc_ref, pick_ref, ((0, b_all), (1, c_all)), states, group)
        rate_acc[...] = jnp.zeros_like(rate_acc)

        @pl.loop(0, steps)
        def _(t):
            none = jnp.zeros((states, group, LANES), f32)
            b_acc[t] = none
            c_acc[t] = none

    @pl.when(at == 1)
    def _():
        for c in out_loads():
            c.wait()
        out_move(1).wait_recv()
        passed[...] = (passed[...].astype(f32) + near_got[1].astype(f32)).astype(bf16)
        out_move(2).start()

    @pl.when(at == 2 * count - 1)
    def _():
        out_move(0).wait_recv()
        out_move(2).wait_recv()
        mine[...] = (mine[...].astype(f32) + near_got[0].astype(f32) + far_got[...].astype(f32)).astype(bf16)
        out_store().start()

    @pl.when(at < count)
    def _():
        a_rows = [jnp.broadcast_to(a_all[j, n : n + 1, :], (group, LANES)) for n in range(states)]
        un = UN["adj"]

        def body(i, q):
            base = pl.multiple_of((steps // un - 1 - i) * un * group, un * group)
            whole = pl.ds(base, un * group)
            mixed_grad, gate = mg_ref[whole, :], gate_ref[whole, :]
            sig = jax.nn.sigmoid(gate)
            g_rows = mixed_grad * (gate * sig)
            g_all[j, whole, :] = g_rows.astype(bf16)
            gg_ref[whole, :] = (mixed_grad * z_ref[whole, :] * (sig * (1.0 + gate * (1.0 - sig)))).astype(bf16)
            for k in reversed(range(un)):
                t = un * (steps // un - 1 - i) + k
                here = pl.ds(pl.multiple_of(base + k * group, group), group)
                masked = step_ref[here, :] + kb_ref[here, :]
                g = g_rows[k * group : (k + 1) * group]
                q = [jnp.exp2(masked * a_rows[n]) * (c_all[t, n] * g + q[n]) for n in range(states)]
            return q

        q = lax.fori_loop(0, steps // un, body, [zero] * states)
        for n in range(states):
            ends[j, n] = q[n]

    carry_of.handle(at)

    @pl.when(at >= count)
    def _():
        a_rows = [jnp.broadcast_to(a_all[j, n : n + 1, :], (group, LANES)) for n in range(states)]
        fu, bu = UN["fwd"], UN["bwd"]

        def forward(i, state):
            base = pl.multiple_of(i * fu * group, fu * group)
            x_two = conv_ref[pl.ds(base, fu * group), :].astype(f32)
            g_two = g_all[j, pl.ds(base, fu * group), :].astype(f32)
            for k in range(fu):
                t = fu * i + k
                here = pl.ds(pl.multiple_of(base + k * group, group), group)
                dt = step_ref[here, :]
                masked = dt + kb_ref[here, :]
                g = g_two[k * group : (k + 1) * group]
                u = dt * x_two[k * group : (k + 1) * group]
                for n in range(states):
                    kept[t, n] = state[n]
                state = [jnp.exp2(masked * a_rows[n]) * state[n] + u * b_all[t, n] for n in range(states)]
                for n in range(states):
                    c_acc[t, n] += state[n] * g
            return state

        lax.fori_loop(0, steps // fu, forward, [start_ref[0, n] for n in range(states)])
        skip = skip_ref[...]

        def backward(i, carry):
            q, a_sum, skip_sum = carry
            base = pl.multiple_of((steps // bu - 1 - i) * bu * group, bu * group)
            x_two = conv_ref[pl.ds(base, bu * group), :].astype(f32)
            g_two = g_all[j, pl.ds(base, bu * group), :].astype(f32)
            for k in reversed(range(bu)):
                t = bu * (steps // bu - 1 - i) + k
                here = pl.ds(pl.multiple_of(base + k * group, group), group)
                dt = step_ref[here, :]
                masked = dt + kb_ref[here, :]
                g = g_two[k * group : (k + 1) * group]
                x = x_two[k * group : (k + 1) * group]
                u = dt * x
                skip_sum = skip_sum + g * x
                lam = [c_all[t, n] * g + q[n] for n in range(states)]
                for n in range(states):
                    b_acc[t, n] += lam[n] * u
                s_one = tree_sum(lam[n] * b_all[t, n] for n in range(states))
                q = [jnp.exp2(masked * a_rows[n]) * lam[n] for n in range(states)]
                w = [q[n] * kept[t, n] for n in range(states)]
                s_two = tree_sum(w[n] * a_rows[n] for n in range(states))
                a_sum = [a_sum[n] + dt * w[n] for n in range(states)]
                cg_ref[here, :] = skip * g + dt * s_one
                dt_grad[here, :] = x * s_one + ln2 * s_two
            return q, a_sum, skip_sum

        q, a_sum, skip_sum = lax.fori_loop(
            0, steps // bu, backward, ([last[j, n] for n in range(states)], [zero] * states, zero)
        )
        pre = jnp.dot(rate_ref[...], wdt_ref[...], preferred_element_type=f32) + bias_ref[...]
        pre_grad = dt_grad[...] * jax.nn.sigmoid(pre)
        low = pre_grad.astype(bf16)
        low_ref[...] = low
        rate_acc[...] += lax.dot_general(low, wdt_ref[...], (((1,), (1,)), ((), ())), preferred_element_type=f32)
        rows_of = [lax.dot_general(rate_ref[...], low, (((0,), (0,)), ((), ())), preferred_element_type=f32)]
        rows_of += [jnp.sum(a_sum[n], 0, keepdims=True) * a_all[j, n : n + 1, :] * ln2 for n in range(states)]
        rows_of += [jnp.sum(pre_grad, 0, keepdims=True), jnp.sum(skip_sum, 0, keepdims=True)]
        spare = small_ref.shape[0] - rank - states - 2
        small_ref[...] = jnp.concatenate(rows_of + [jnp.zeros((spare, LANES), f32)], 0).astype(bf16)

    @pl.when(at == 2 * count - 1)
    def _():
        carry_of.leave()
        out_store().wait()
        for slot in range(3):
            out_move(slot).wait_send()
        own_copy().wait()
        for hop in range(1, devices):
            back_copy(hop).wait()
        mpg_ref[:, :rank] = rate_acc[...].astype(bf16)
        lane = lax.broadcasted_iota(jnp.int32, (2 * LANES, 2 * states), 1)
        own = lax.broadcasted_iota(jnp.int32, (2 * LANES, 2 * states), 0) // LANES * states
        total = jnp.zeros((steps * group, 2 * states), f32)
        for n in range(states):
            both = [acc[:, n].reshape(steps * group, LANES) for acc in (b_acc, c_acc)]
            rows = jnp.concatenate(both, 1)
            pick = jnp.where(lane == own + n, 1.0, 0.0).astype(bf16)
            high = rows.astype(bf16)
            rest = (rows - high.astype(f32)).astype(bf16)
            total = total + jnp.dot(high, pick, preferred_element_type=f32)
            total = total + jnp.dot(rest, pick, preferred_element_type=f32)
        mpg_ref[:, rank:] = total.astype(bf16)


def rows_block(rows):
    return pl.BlockSpec((rows, LANES), lambda j: (0, j))


def whole_block(shape):
    return pl.BlockSpec(shape, lambda j: (0,) * len(shape))


def state_block(states, group):
    return pl.BlockSpec((1, states, group, LANES), lambda j: (j, 0, 0, 0))


def shape_of(shape, dtype):
    return jax.ShapeDtypeStruct(shape, dtype)


def params():
    return pltpu.CompilerParams(vmem_limit_bytes=vmem_cap)


def carry_scratch(shape):
    return [
        pltpu.VMEM(shape, bf16), pltpu.VMEM(shape, bf16), pltpu.SemaphoreType.DMA((shape[0],)),
        pltpu.SemaphoreType.DMA((shape[0],)),
    ]


def forward_scan(rate_low, w_dt, bias, conv_low, bc, pick, match, a_blocks, gate, skip, cot, target, capacity, group, devices):
    rows, inner = conv_low.shape
    count, states, _ = a_blocks.shape
    rank = rate_low.shape[1]
    first = lambda at: (0, jnp.minimum(at, count - 1))
    both = lambda at: (0, lax.rem(at, count))
    second = lambda at: (0, jnp.maximum(at - count, 0))
    shape = (count, states, group, LANES)
    big = pltpu.VMEM((rows // group, states, group, LANES), f32)
    return pl.pallas_call(
        functools.partial(forward_kernel, states=states, group=group, devices=devices),
        grid=(2 * count,),
        in_specs=[
            whole_block((rows, rank)), pl.BlockSpec((rank, LANES), first), pl.BlockSpec((1, LANES), first),
            pl.BlockSpec((rows, LANES), both), whole_block(bc.shape), whole_block(pick.shape),
            whole_block(match.shape), whole_block(a_blocks.shape), pl.BlockSpec((rows, LANES), second),
            pl.BlockSpec((1, LANES), second), whole_block(cot.shape), whole_block((1, rows)),
        ],
        out_specs=[
            pl.BlockSpec((rows, LANES), first), pl.BlockSpec((rows, LANES), second), pl.BlockSpec((rows, LANES), second),
            whole_block(shape), whole_block((count, group, LANES)), whole_block((devices, capacity, cot.shape[1])),
        ],
        out_shape=[
            shape_of((rows, inner), f32), shape_of((rows, inner), f32), shape_of((rows, inner), bf16),
            shape_of(shape, f32), shape_of((count, group, LANES), f32), shape_of((devices, capacity, cot.shape[1]), bf16),
        ],
        scratch_shapes=[pltpu.VMEM((devices, capacity, cot.shape[1]), bf16), pltpu.VMEM((rows, LANES), f32), big, big]
        + [pltpu.VMEM((count, rows, LANES), f32), pltpu.VMEM(shape, f32)]
        + [pltpu.VMEM((devices - 1, capacity, cot.shape[1]), bf16)]
        + [pltpu.SemaphoreType.DMA((devices - 1,)), pltpu.SemaphoreType.DMA((devices - 1,))] + carry_scratch(shape),
        compiler_params=pltpu.CompilerParams(collective_id=0, has_side_effects=True, vmem_limit_bytes=vmem_cap),
        name="forward_scan",
    )(rate_low, w_dt, bias, conv_low, bc, pick, match, a_blocks, gate, skip, cot, target[None, :])


def backward_scan(mixed_grad, gate, z, step, conv_low, bc, pick, match, a_blocks, total, start, rate_low, w_dt, bias, skip, back, out_grad, group, devices):
    rows, inner = conv_low.shape
    count, states, _ = a_blocks.shape
    rank = rate_low.shape[1]
    small_rows = -(-(rank + states + 2) // 16) * 16
    out_piece = (out_grad.shape[0] // devices, out_grad.shape[1])
    dma = pltpu.SemaphoreType.DMA
    first = lambda at: (0, jnp.minimum(at, count - 1))
    both = lambda at: (0, lax.rem(at, count))
    second = lambda at: (0, jnp.maximum(at - count, 0))
    shape = (count, states, group, LANES)
    big = pltpu.VMEM((rows // group, states, group, LANES), f32)
    return pl.pallas_call(
        functools.partial(backward_kernel, states=states, group=group, devices=devices),
        grid=(2 * count,),
        in_specs=[
            pl.BlockSpec((rows, LANES), first), pl.BlockSpec((rows, LANES), first), pl.BlockSpec((rows, LANES), first),
            pl.BlockSpec((rows, LANES), both), pl.BlockSpec((rows, LANES), second), whole_block(bc.shape),
            whole_block(pick.shape), whole_block(match.shape), whole_block(a_blocks.shape), whole_block(total.shape),
            pl.BlockSpec((1, states, group, LANES), lambda at: (jnp.maximum(at - count, 0), 0, 0, 0)),
            whole_block((rows, rank)), pl.BlockSpec((rank, LANES), second), pl.BlockSpec((1, LANES), second),
            pl.BlockSpec((1, LANES), second), pl.BlockSpec(memory_space=pl.ANY), pl.BlockSpec(memory_space=pl.ANY),
        ],
        out_specs=[
            pl.BlockSpec((rows, LANES), lambda at: (0, jnp.minimum(at, count - 1) + count)),
            pl.BlockSpec((rows, LANES), second), pl.BlockSpec((rows, LANES), second),
            pl.BlockSpec((small_rows, LANES), second), whole_block((rows, rank + 2 * states)),
            pl.BlockSpec(memory_space=pl.ANY), pl.BlockSpec(memory_space=pl.ANY),
        ],
        out_shape=[
            shape_of((rows, 2 * inner), bf16), shape_of((rows, inner), bf16), shape_of((rows, inner), f32),
            shape_of((small_rows, inner), bf16), shape_of((rows, rank + 2 * states), bf16), shape_of(back.shape, bf16),
            shape_of(out_piece, bf16),
        ],
        scratch_shapes=[pltpu.VMEM((2,) + out_piece, bf16), pltpu.VMEM(out_piece, bf16), pltpu.VMEM(out_piece, bf16)]
        + [pltpu.VMEM(out_piece, bf16), dma((3,)), dma((3,)), dma((3,)), dma((devices - 1,)), dma((devices - 1,))]
        + [dma((1,)), pltpu.VMEM((rows, LANES), f32), big, big, big, big, big]
        + [pltpu.VMEM((rows, LANES), f32), pltpu.VMEM((count, rows, LANES), bf16)]
        + [pltpu.VMEM((rows, rank), f32), pltpu.VMEM(shape, f32), pltpu.VMEM(shape, f32)] + carry_scratch(shape),
        compiler_params=pltpu.CompilerParams(collective_id=1, has_side_effects=True, vmem_limit_bytes=64 << 20),
        name="backward_scan",
    )(mixed_grad, gate, z, step, conv_low, bc, pick, match, a_blocks, total, start, rate_low, w_dt, bias, skip, back, out_grad)


def split_three(v):
    high = v.astype(bf16)
    rest = v - high.astype(f32)
    mid = rest.astype(bf16)
    low = (rest - mid.astype(f32)).astype(bf16)
    return jnp.concatenate([high, mid, low], -1)


def pick_matrix(columns):
    eye = (jnp.arange(columns)[:, None] == jnp.arange(columns * LANES)[None, :] // LANES).astype(bf16)
    return jnp.concatenate([eye] * 3, 0)

def broad_match(match_ref, wide):
    @pl.when(pl.program_id(0) == 0)
    def _():
        for k in range(match_ref.shape[1]):
            wide[k] = jnp.broadcast_to(match_ref[:, k : k + 1], wide.shape[1:])


def front_kernel(
    token_ref, before_ref, gain_ref, wc_ref, wg_ref, cw_ref, cb_ref, compact_ref, wx_ref, ci_ref, low_ref, gate_ref, mixed_ref,
    normed_ref, rows_f, match_ref, *, halo, group,
):
    rows = low_ref.shape[0]
    broad_match(compact_ref, match_ref)

    @pl.when(pl.program_id(0) == 0)
    def _():
        def put(at, source):
            values = source.astype(f32)
            scale = lax.rsqrt(jnp.mean(values * values, -1, keepdims=True) + epsilon)
            normed_ref[at, :] = (values * scale * gain_ref[...]).astype(bf16)

        put(slice(0, halo), before_ref[...])
        tile = 256

        @pl.loop(0, rows // tile)
        def _(i):
            put(pl.ds(pl.multiple_of(halo + i * tile, halo), tile), token_ref[pl.ds(pl.multiple_of(i * tile, tile), tile), :])

    taps = cw_ref.shape[0]
    ci = jnp.dot(normed_ref[...], wc_ref[...], preferred_element_type=f32).astype(bf16)
    ci_ref[...] = ci
    rows_f[...] = ci.astype(f32)
    total = conv_total(rows_f, cw_ref, cb_ref, match_ref, halo, group, rows, taps)
    low = (total * jax.nn.sigmoid(total)).astype(bf16)
    low_ref[...] = low
    gate_ref[...] = jnp.dot(normed_ref[halo:, :], wg_ref[...], preferred_element_type=f32)
    part = jnp.dot(low, wx_ref[...], preferred_element_type=f32)

    @pl.when(pl.program_id(0) == 0)
    def _():
        mixed_ref[...] = part

    @pl.when(pl.program_id(0) > 0)
    def _():
        mixed_ref[...] += part


def conv_total(rows_f, cw_ref, cb_ref, match_ref, halo, group, rows, taps):
    total = cb_ref[...] + cw_ref[taps - 1 : taps, :] * rows_f[halo : halo + rows, :]
    for k in range(taps - 1):
        at = halo - (taps - 1 - k) * group
        total = total + cw_ref[k : k + 1, :] * rows_f[at : at + rows, :] * match_ref[k]
    return total


def front(token_low, before_rows, gain, w_in, conv_w, conv_b, match, w_x, halo, group, lanes):
    width, inner = w_in.shape[0], w_in.shape[1] // 2
    total_rows = token_low.shape[0] + halo
    rows, taps, mixed_width = total_rows - halo, conv_w.shape[0], w_x.shape[1]
    count = inner // lanes
    cols = lambda r: pl.BlockSpec((r, lanes), lambda j: (0, j))
    return pl.pallas_call(
        functools.partial(front_kernel, halo=halo, group=group),
        grid=(count,),
        in_specs=[
            whole_block(token_low.shape), whole_block(before_rows.shape), whole_block(gain.shape), cols(width),
            pl.BlockSpec((width, lanes), lambda j: (0, j + count)),
            cols(taps), cols(1), whole_block(match.shape), pl.BlockSpec((lanes, mixed_width), lambda j: (j, 0)),
        ],
        out_specs=[cols(total_rows), cols(rows), cols(rows), whole_block((rows, mixed_width)), whole_block((total_rows, width))],
        out_shape=[
            shape_of((total_rows, inner), bf16), shape_of((rows, inner), bf16), shape_of((rows, inner), f32),
            shape_of((rows, mixed_width), f32), shape_of((total_rows, width), bf16),
        ],
        scratch_shapes=[pltpu.VMEM((total_rows, lanes), f32), pltpu.VMEM((match.shape[1], rows, lanes), f32)],
        compiler_params=params(),
        name="front",
    )(token_low, before_rows, gain, w_in, w_in, conv_w, conv_b, match, w_x)


def conv_back_kernel(
    cg_ref, low_ref, mpg_ref, wx_ref, ci_ref, cw_ref, cb_ref, compact_ref, proj_ref, pg_ref, ext_ref, small_ref, rows_f, ext, match_ref,
    *, halo, group,
):
    broad_match(compact_ref, match_ref)
    rows = pg_ref.shape[0]
    taps = cw_ref.shape[0]
    grad = cg_ref[...] + lax.dot_general(
        mpg_ref[...], wx_ref[...], (((1,), (1,)), ((), ())), preferred_element_type=f32
    )
    rows_f[...] = ci_ref[...].astype(f32)
    total = conv_total(rows_f, cw_ref, cb_ref, match_ref, halo, group, rows, taps)
    sig = jax.nn.sigmoid(total)
    grad = grad * (sig * (1.0 + total * (1.0 - sig)))
    x_part = lax.dot_general(mpg_ref[...], low_ref[...], (((0,), (0,)), ((), ())), preferred_element_type=f32)
    taps_grad = [None] * taps
    ext[:halo, :] = jnp.zeros((halo, ext.shape[1]), f32)
    ext[halo:, :] = grad * cw_ref[taps - 1 : taps, :]
    taps_grad[taps - 1] = jnp.sum(grad * rows_f[halo:, :], 0, keepdims=True)
    for k in range(taps - 1):
        at = halo - (taps - 1 - k) * group
        own = grad * match_ref[k]
        taps_grad[k] = jnp.sum(own * rows_f[at : at + rows, :], 0, keepdims=True)
        ext[at : at + rows, :] += own * cw_ref[k : k + 1, :]
    pg_ref[...] = ext[halo:, :].astype(bf16)
    ext_ref[:halo, :] = ext[:halo, :]
    ext_ref[halo:, :] = ext[rows:, :]
    spare = small_ref.shape[0] - x_part.shape[0] - taps - 1
    parts = [x_part] + taps_grad + [jnp.sum(grad, 0, keepdims=True), jnp.zeros((spare, ext.shape[1]), f32)]
    small_ref[...] = jnp.concatenate(parts, 0).astype(bf16)


def conv_back(cg, conv_low, mpg, w_x, ci, conv_w, conv_b, match, proj, halo, group, lanes):
    rows, inner = cg.shape
    taps, mixed_width = conv_w.shape[0], w_x.shape[1]
    small_rows = -(-(mixed_width + taps + 1) // 16) * 16
    cols = lambda r: pl.BlockSpec((r, lanes), lambda j: (0, j))
    return pl.pallas_call(
        functools.partial(conv_back_kernel, halo=halo, group=group),
        grid=(inner // lanes,),
        in_specs=[
            cols(rows), cols(rows), whole_block((rows, mixed_width)), pl.BlockSpec((lanes, mixed_width), lambda j: (j, 0)),
            cols(rows + halo), cols(taps), cols(1), whole_block(match.shape),
            pl.BlockSpec(memory_space=pl.ANY),
        ],
        out_specs=[cols(rows), cols(2 * halo), cols(small_rows)],
        out_shape=[shape_of(proj.shape, bf16), shape_of((2 * halo, inner), f32), shape_of((small_rows, inner), bf16)],
        scratch_shapes=[pltpu.VMEM((rows + halo, lanes), f32), pltpu.VMEM((rows + halo, lanes), f32)]
        + [pltpu.VMEM((match.shape[1], rows, lanes), f32)],
        input_output_aliases={8: 0},
        compiler_params=params(),
        name="conv_back",
    )(cg, conv_low, mpg, w_x, ci, conv_w, conv_b, match, proj)

def expert_kernel(
    rows_ref, cot_ref, up_ref, down_ref, out_ref, back_ref, upg_ref, downg_ref, grad, out_acc, back_acc, active, pre_grad, *, tile
):
    first = pl.program_id(0) == 0
    final = pl.program_id(0) == pl.num_programs(0) - 1
    slots, width = cot_ref.shape
    tiles = [slice(i * tile, (i + 1) * tile) for i in range(slots // tile)]

    @pl.when(first)
    def _():
        for at in tiles:
            parts = rows_ref[at, width : width + LANES].astype(f32)
            gate = parts[:, 0:1] + parts[:, 1:2] + parts[:, 2:3]
            grad[at, :] = (gate * cot_ref[at, :].astype(f32)).astype(bf16)
            out_acc[at, :] = jnp.zeros((tile, width), f32)
            back_acc[at, :] = jnp.zeros((tile, width), f32)

    for at in tiles:
        pre = jnp.dot(rows_ref[at, :width], up_ref[...], preferred_element_type=f32)
        act_grad = lax.dot_general(grad[at, :], down_ref[...], (((1,), (1,)), ((), ())), preferred_element_type=f32)
        half = 0.5 * lax.erf(pre * 0.7071067811865476) + 0.5
        active[at, :] = (pre * half).astype(bf16)
        slope = half + pre * (jnp.exp(pre * pre * -0.5) * 0.3989422804014327)
        pre_grad[at, :] = (act_grad * slope).astype(bf16)
    for at in tiles:
        out_acc[at, :] += jnp.dot(active[at, :], down_ref[...], preferred_element_type=f32)
        back_acc[at, :] += lax.dot_general(
            pre_grad[at, :], up_ref[...], (((1,), (1,)), ((), ())), preferred_element_type=f32
        )
    downg_ref[...] = lax.dot_general(
        active[...], grad[...], (((0,), (0,)), ((), ())), preferred_element_type=f32
    ).astype(bf16)
    upg_ref[...] = lax.dot_general(
        rows_ref[:, :width], pre_grad[...], (((0,), (0,)), ((), ())), preferred_element_type=f32
    ).astype(bf16)

    @pl.when(final)
    def _():
        for at in tiles:
            out = out_acc[at, :].astype(bf16)
            out_ref[at, :] = out
            back_ref[at, :width] = back_acc[at, :].astype(bf16)
            dot = jnp.sum(out.astype(f32) * cot_ref[at, :].astype(f32), -1, keepdims=True)
            back_ref[at, width:] = in_parts(dot)


def in_parts(column):
    high = column.astype(bf16).astype(f32)
    mid = (column - high).astype(bf16).astype(f32)
    lane = lax.broadcasted_iota(jnp.int32, (column.shape[0], LANES), 1)
    low = column - high - mid
    return jnp.where(lane == 0, high, jnp.where(lane == 1, mid, jnp.where(lane == 2, low, 0.0))).astype(bf16)


def one_expert(rows, cot, up, down):
    slots, width = cot.shape
    hidden = up.shape[1]
    hidden_tile, tile = hidden // 6, slots // 2
    full = whole_block((slots, width))
    broad = whole_block((slots, width + LANES))
    cols = pl.BlockSpec((width, hidden_tile), lambda j: (0, j))
    deep = pl.BlockSpec((hidden_tile, width), lambda j: (j, 0))
    return pl.pallas_call(
        functools.partial(expert_kernel, tile=tile),
        grid=(hidden // hidden_tile,),
        in_specs=[broad, full, cols, deep],
        out_specs=[full, broad, cols, deep],
        out_shape=[
            shape_of((slots, width), bf16), shape_of((slots, width + LANES), bf16), shape_of((width, hidden), bf16),
            shape_of((hidden, width), bf16),
        ],
        scratch_shapes=[
            pltpu.VMEM((slots, width), bf16), pltpu.VMEM((slots, width), f32), pltpu.VMEM((slots, width), f32),
            pltpu.VMEM((slots, hidden_tile), bf16), pltpu.VMEM((slots, hidden_tile), bf16),
        ],
        compiler_params=params(),
        name="one_expert",
    )(rows, cot, up, down)


def exp_barrier(spot, devices):
    barrier = pltpu.get_barrier_semaphore()
    for hop in range(1, devices):
        pl.semaphore_signal(barrier, inc=1, device_id={"exp": lax.rem(spot + hop, devices)}, device_id_type=MESH)
    pl.semaphore_wait(barrier, devices - 1)


class Dispatch:
    def __init__(self, rows_ref, target_ref, got_ref, staged, send_sem, recv_sem, devices):
        self.rows_ref, self.target_ref, self.got_ref, self.staged = rows_ref, target_ref, got_ref, staged
        self.send_sem, self.recv_sem, self.devices = send_sem, recv_sem, devices
        self.spot = lax.axis_index("exp")
        self.hops = [h for h in range(devices // 2, devices)] + [h for h in range(1, devices // 2)]

    def packed(self, k):
        capacity = self.got_ref.shape[1]
        slot = lax.broadcasted_iota(jnp.int32, (capacity, self.rows_ref.shape[0]), 0) + k * capacity
        pick = jnp.where(slot == self.target_ref[...], 1.0, 0.0).astype(bf16)
        return jnp.dot(pick, self.rows_ref[...], preferred_element_type=f32).astype(bf16)

    def copy(self, hop):
        return pltpu.make_async_remote_copy(
            src_ref=self.staged.at[hop - 1], dst_ref=self.got_ref.at[self.spot], send_sem=self.send_sem.at[hop - 1],
            recv_sem=self.recv_sem.at[hop - 1], device_id={"exp": lax.rem(self.spot + hop, self.devices)},
            device_id_type=MESH,
        )

    def start(self):
        for hop in self.hops:
            self.staged[hop - 1] = self.packed(lax.rem(self.spot + hop, self.devices))
            self.copy(hop).start()
        self.got_ref[self.spot] = self.packed(self.spot)

    def wait(self):
        for hop in self.hops:
            self.copy(hop).wait()


def route_kernel(
    mixed_ref, wout_ref, token_ref, gain_ref, router_ref, route_ref, target_ref, hidden_ref, rows_ref, prob_ref, got_ref,
    staged, send_sem, recv_sem, *, devices, experts, tile,
):
    exp_barrier(lax.axis_index("exp"), devices)
    width = wout_ref.shape[1]

    @pl.loop(0, mixed_ref.shape[0] // tile)
    def _(i):
        at = pl.ds(pl.multiple_of(i * tile, tile), tile)
        hidden = token_ref[at, :].astype(f32) + jnp.dot(mixed_ref[at, :], wout_ref[...], preferred_element_type=f32)
        hidden_ref[at, :] = hidden
        scale = lax.rsqrt(jnp.mean(hidden * hidden, -1, keepdims=True) + epsilon)
        low = (hidden * scale * gain_ref[...]).astype(bf16)
        rows_ref[at, :width] = low
        logits = jnp.dot(low, router_ref[...], preferred_element_type=f32)
        lane = lax.broadcasted_iota(jnp.int32, logits.shape, 1)
        logits = jnp.where(lane < experts, logits, -1e30)
        raised = jnp.exp(logits - jnp.max(logits, -1, keepdims=True))
        prob = raised / jnp.sum(raised, -1, keepdims=True)
        prob_ref[at, :] = prob
        gate = jnp.sum(jnp.where(lane == route_ref[at, :], prob, 0.0), -1, keepdims=True)
        rows_ref[at, width:] = in_parts(gate)

    moved = Dispatch(rows_ref, target_ref, got_ref, staged, send_sem, recv_sem, devices)
    moved.start()
    moved.wait()


def routed(mixed_low, w_out, token_low, gain, router_wide, route_col, target, capacity, devices, experts):
    vm = pl.BlockSpec(memory_space=pltpu.VMEM)
    dma = pltpu.SemaphoreType.DMA
    rows, width = token_low.shape
    return pl.pallas_call(
        functools.partial(route_kernel, devices=devices, experts=experts, tile=256),
        in_specs=[vm] * 7,
        out_specs=[vm] * 4,
        out_shape=[
            shape_of((rows, width), f32), shape_of((rows, width + LANES), bf16), shape_of((rows, LANES), f32),
            shape_of((devices, capacity, width + LANES), bf16),
        ],
        scratch_shapes=[pltpu.VMEM((devices - 1, capacity, width + LANES), bf16), dma((devices - 1,)), dma((devices - 1,))],
        compiler_params=pltpu.CompilerParams(collective_id=3, has_side_effects=True, vmem_limit_bytes=vmem_cap),
        name="routed",
    )(mixed_low, w_out, token_low, gain, router_wide, route_col, target[None, :])


def collect_kernel(
    sent_ref, target_ref, route_ref, rows_ref, prob_ref, hidden_ref, cot_ref, gain_ref, router_ref,
    hidden_grad_ref, branch_ref, gain_grad_ref, router_grad_ref, got, total, send_sem, recv_sem, *, devices, hops, tile,
):
    spot = lax.axis_index("exp")
    capacity = got.shape[1]
    count, width = hidden_ref.shape
    exp_barrier(spot, devices)
    copies = []
    for hop in hops:
        peer = lax.rem(spot + hop, devices)
        c = pltpu.make_async_remote_copy(
            src_ref=sent_ref.at[peer], dst_ref=got.at[devices - hop - 1], send_sem=send_sem.at[hop - 1],
            recv_sem=recv_sem.at[hop - 1], device_id={"exp": peer}, device_id_type=MESH,
        )
        c.start()
        copies.append(c)

    def spread_back(k, rows):
        slot = lax.broadcasted_iota(jnp.int32, (count, capacity), 1) + k * capacity
        pick = jnp.where(slot == target_ref[...], 1.0, 0.0).astype(bf16)
        return jnp.dot(pick, rows, preferred_element_type=f32)

    total[...] = spread_back(spot, sent_ref[spot])
    for hop, c in zip(hops, copies):
        c.wait_recv()
        total[...] += spread_back(lax.rem(spot + devices - hop, devices), got[devices - hop - 1])
    gain_grad_ref[...] = jnp.zeros_like(gain_grad_ref)
    router_grad_ref[...] = jnp.zeros_like(router_grad_ref)

    @pl.loop(0, count // tile)
    def _(i):
        at = pl.ds(pl.multiple_of(i * tile, tile), tile)
        parts = total[at, width:]
        gate_grad = parts[:, 0:1] + parts[:, 1:2] + parts[:, 2:3]
        prob = prob_ref[at, :]
        chosen = jnp.where(lax.broadcasted_iota(jnp.int32, prob.shape, 1) == route_ref[at, :], 1.0, 0.0)
        gate = jnp.sum(prob * chosen, -1, keepdims=True)
        logit_grad = prob * (chosen - gate) * gate_grad
        router_grad_ref[...] += lax.dot_general(
            logit_grad, rows_ref[at, :width].astype(f32), (((0,), (0,)), ((), ())), precision=highest,
            preferred_element_type=f32,
        )
        grad = total[at, :width] + jnp.dot(
            logit_grad, router_ref[...], precision=highest, preferred_element_type=f32
        )
        hidden = hidden_ref[at, :]
        scale = lax.rsqrt(jnp.mean(hidden * hidden, -1, keepdims=True) + epsilon)
        unit = hidden * scale
        gain_grad_ref[...] += jnp.sum(grad * unit, 0, keepdims=True)
        scaled = grad * gain_ref[...]
        hidden_grad = cot_ref[at, :].astype(f32) + scale * (
            scaled - unit * jnp.mean(scaled * unit, -1, keepdims=True)
        )
        hidden_grad_ref[at, :] = hidden_grad
        branch_ref[at, :] = hidden_grad.astype(bf16)

    for c in copies:
        c.wait_send()


def collect(blocks, target, route_col, rows, prob, hidden, cot, gain, router_t, devices):
    vm = pl.BlockSpec(memory_space=pltpu.VMEM)
    dma = pltpu.SemaphoreType.DMA
    capacity, wide = blocks.shape[1:]
    count, width = hidden.shape
    return pl.pallas_call(
        functools.partial(collect_kernel, devices=devices, hops=(2, 3, 1), tile=256),
        in_specs=[vm] * 9,
        out_specs=[vm] * 4,
        out_shape=[
            shape_of((count, width), f32), shape_of((count, width), bf16), shape_of((1, width), f32),
            shape_of((LANES, width), f32),
        ],
        scratch_shapes=[
            pltpu.VMEM((devices - 1, capacity, wide), bf16), pltpu.VMEM((count, wide), f32), dma((devices - 1,)),
            dma((devices - 1,)),
        ],
        compiler_params=pltpu.CompilerParams(collective_id=4, has_side_effects=True, vmem_limit_bytes=vmem_cap),
        name="collect",
    )(blocks, target[:, None], route_col, rows, prob, hidden, cot, gain, router_t)

SEGMENTS = 4
STARTS = (-4, 1, 3, 6)


def ring_order(place, peers):
    odd = lax.rem(place, 2)
    half = lax.div(place, 2)
    return half + odd * (peers - 1 - 2 * half)


def ring_member(position, peers):
    back = lax.div(2 * position, peers)
    return 2 * position + back * (2 * (peers - 1) + 1 - 4 * position)


class Rings:
    def __init__(self, own, total, sent, landed, send, recv, bases, sizes, peers):
        place = lax.axis_index("seq")
        self.own, self.total, self.sent, self.landed, self.send, self.recv = own, total, sent, landed, send, recv
        self.bases, self.sizes, self.peers = bases, sizes, peers
        self.position = ring_order(place, peers)
        self.after = ring_member(lax.rem(self.position + 1, peers), peers)
        self.before = ring_member(lax.rem(self.position + peers - 1, peers), peers)

    def rows(self, ring, steps):
        sign = 1 if ring % 2 == 0 else -1
        chunk = self.sizes[ring] // self.peers
        c = lax.rem(self.position + sign * steps + 2 * self.peers, self.peers)
        return pl.ds(pl.multiple_of(self.bases[ring] + c * chunk, 16), chunk)

    def target(self, ring):
        return {"seq": self.after if ring % 2 == 0 else self.before}

    def first(self, ring, s):
        chunk = self.sizes[ring] // self.peers
        return pltpu.make_async_remote_copy(
            src_ref=self.sent.at[ring, s, pl.ds(0, chunk)], dst_ref=self.landed.at[ring, s, pl.ds(0, chunk)],
            send_sem=self.send.at[ring, s], recv_sem=self.recv.at[ring, s], device_id=self.target(ring),
            device_id_type=MESH,
        )

    def second(self, ring, s):
        part = self.total.at[self.rows(ring, 1 - s)]
        at = self.peers - 1 + s
        return pltpu.make_async_remote_copy(
            src_ref=part, dst_ref=part, send_sem=self.send.at[ring, at], recv_sem=self.recv.at[ring, at],
            device_id=self.target(ring), device_id_type=MESH,
        )

    def begin(self, ring):
        chunk = self.sizes[ring] // self.peers
        self.sent[ring, 0, pl.ds(0, chunk)] = self.own[self.rows(ring, 0), :].astype(bf16)
        self.first(ring, 0).start()

    def advance(self, ring, s):
        peers, chunk = self.peers, self.sizes[ring] // self.peers

        @pl.when(jnp.logical_and(s >= 1, s <= peers - 2))
        def _():
            self.first(ring, s - 1).wait_recv()
            summed = self.landed[ring, s - 1, pl.ds(0, chunk)].astype(f32) + self.own[self.rows(ring, -s), :]
            self.sent[ring, s, pl.ds(0, chunk)] = summed.astype(bf16)
            self.first(ring, s).start()

        @pl.when(s == peers - 1)
        def _():
            self.first(ring, peers - 2).wait_recv()
            summed = self.landed[ring, peers - 2, pl.ds(0, chunk)].astype(f32) + self.own[self.rows(ring, 1), :]
            self.total[self.rows(ring, 1), :] = summed.astype(bf16)
            self.second(ring, 0).start()

        @pl.when(jnp.logical_and(s >= peers, s <= 2 * peers - 3))
        def _():
            self.second(ring, s - peers).wait_recv()
            self.second(ring, s - peers + 1).start()

        @pl.when(s == 2 * peers - 2)
        def _():
            self.second(ring, peers - 2).wait_recv()

    def drain(self):
        @pl.loop(0, self.peers - 1)
        def _(s):
            for ring in range(len(self.sizes)):
                self.first(ring, s).wait_send()
                self.second(ring, s).wait_send()


def finish_kernel(
    proj_ref, normed_ref, win_ref, outo_ref, small_ref, gain_ref, token_ref, hiddeng_ref, hidden_ref, rows_ref, target_ref,
    tok_ref,
    in_sum_ref, out_sum_ref, small_sum_ref, tokens_grad_ref, block_ref,
    own, total, near_stage, small_all, gain_part, near_in, near_small, far_in, far_small, pass_in, pass_small, sent, landed, near_send, near_recv, far_send, far_recv, ring_send, ring_recv,
    *, peers, bases, sizes, halo, tile, gain_row,
):
    spot = lax.axis_index("exp")
    width, wide = near_in.shape[1:]
    rows_out = outo_ref.shape[0]
    rows_small, share = near_small.shape[1:]
    folds = wide // share
    count = proj_ref.shape[0]
    third = width // 3
    near = spot + 1 - 2 * lax.rem(spot, 2)
    far = lax.rem(spot + 2, 4)
    across = lax.rem(near + 2, 4)
    rings = Rings(own, total, sent, landed, ring_send, ring_recv, bases, sizes, peers)
    barrier = pltpu.get_barrier_semaphore()
    for device in ({"exp": near}, {"exp": far}, {"seq": rings.after}, {"seq": rings.before}):
        pl.semaphore_signal(barrier, inc=1, device_id=device, device_id_type=MESH)
    pl.semaphore_wait(barrier, 4)

    def columns(k, size):
        return pl.ds(pl.multiple_of(k * size, size), size)

    def copy(source, target, send, recv, device):
        return pltpu.make_async_remote_copy(
            src_ref=source, dst_ref=target, send_sem=send, recv_sem=recv, device_id=device, device_id_type=MESH
        )

    def in_rows(i):
        return slice(i * third, (i + 1) * third)

    def near_copy(slot, piece):
        k = across if slot else near
        if piece == 4:
            source, target = small_all.at[:, columns(k, share)], near_small.at[slot]
        else:
            at = pl.ds((piece - 1) * third, third)
            source, target = near_stage.at[slot, at], near_in.at[slot, at]
        return copy(source, target, near_send.at[slot, piece], near_recv.at[slot, piece], {"exp": near})

    def far_copy(piece):
        if piece == 4:
            source, target = pass_small, far_small
        else:
            at = pl.ds((piece - 1) * third, third)
            source, target = pass_in.at[at], far_in.at[at]
        return copy(source, target, far_send.at[piece], far_recv.at[piece], {"exp": far})

    def in_tile(i, k):
        part = lax.dot_general(
            normed_ref[pl.ds(halo, count), in_rows(i)], proj_ref[:, columns(k, wide)], (((0,), (0,)), ((), ())),
            preferred_element_type=f32,
        )
        scaled = part * win_ref[in_rows(i), columns(k, wide)].astype(f32)
        gain_part[in_rows(i), :] += tree_sum(scaled[:, h * LANES : (h + 1) * LANES] for h in range(wide // LANES))
        return part

    def into_own(base, values, add):
        size = values.shape[0]
        for h in range(values.shape[1] // share):
            at = slice(base + h * size, base + (h + 1) * size)
            part = values[:, h * share : (h + 1) * share]
            if add:
                own[at, :] += part
            else:
                own[at, :] = part

    def pad_own(n, used):
        if used < sizes[n]:
            own[bases[n] + used : bases[n] + sizes[n], :] = jnp.zeros((sizes[n] - used, share), f32)

    small_base = bases[3] + folds * third
    into_own(bases[0], outo_ref[...].astype(f32), False)
    pad_own(0, folds * rows_out)
    rings.begin(0)
    gain_part[...] = jnp.zeros_like(gain_part)
    small_all[...] = small_ref[...]
    for i in range(3):
        for slot, k in ((1, across), (0, near)):
            near_stage[slot, in_rows(i), :] = in_tile(i, k).astype(bf16)
            near_copy(slot, 1 + i).start()
        distant = in_tile(i, far)
        near_copy(1, 1 + i).wait_recv()
        pass_in[in_rows(i), :] = (distant + near_in[1, in_rows(i), :].astype(f32)).astype(bf16)
        far_copy(1 + i).start()
        mine = in_tile(i, spot)
        near_copy(0, 1 + i).wait_recv()
        into_own(bases[1 + i], mine + near_in[0, in_rows(i), :].astype(f32), False)
        pad_own(1 + i, folds * third)
        rings.advance(0, jnp.int32(1 + i))
    quarter = width // 4
    for k in range(4):
        part = jnp.sum(gain_part[k * quarter : (k + 1) * quarter, :], -1, keepdims=True)
        eye = lax.broadcasted_iota(jnp.int32, (quarter, quarter), 0) == lax.broadcasted_iota(
            jnp.int32, (quarter, quarter), 1
        )
        row = jnp.sum(jnp.where(eye, part, 0.0), 0, keepdims=True) / gain_ref[:, k * quarter : (k + 1) * quarter]
        group = slice(gain_row, gain_row + 16)
        old = small_all[group, k * share : k * share + quarter].astype(f32)
        top = lax.broadcasted_iota(jnp.int32, old.shape, 0) == 0
        small_all[group, k * share : k * share + quarter] = jnp.where(top, row, old).astype(bf16)
    for slot in (1, 0):
        near_copy(slot, 4).start()
    near_copy(1, 4).wait_recv()
    pass_small[...] = (small_all[:, columns(far, share)].astype(f32) + near_small[1].astype(f32)).astype(bf16)
    far_copy(4).start()
    near_copy(0, 4).wait_recv()
    own[small_base : small_base + rows_small, :] = (
        small_all[:, columns(spot, share)].astype(f32) + near_small[0].astype(f32)
    )
    def arrived(ring):
        far_copy(ring).wait_recv()
        into_own(bases[ring], far_in[in_rows(ring - 1), :].astype(f32), True)
        if ring == SEGMENTS - 1:
            far_copy(4).wait_recv()
            own[small_base : small_base + rows_small, :] += far_small[...].astype(f32)
        rings.begin(ring)

    def place_rows(out_ref, values, i):
        group = out_ref.shape[0]
        steps = tile // group
        values = jnp.swapaxes(values.reshape(steps, group, width), 0, 1)
        out_ref[:, pl.ds(pl.multiple_of(i * steps, steps), steps), :] = values.astype(out_ref.dtype)

    def token_tile(i):
        at = pl.ds(pl.multiple_of(i * tile, tile), tile)
        grad = lax.dot_general(proj_ref[at, :], win_ref[...], (((1,), (1,)), ((), ())), preferred_element_type=f32)
        values = token_ref[at, :].astype(f32)
        scale = lax.rsqrt(jnp.mean(values * values, -1, keepdims=True) + epsilon)
        unit = values * scale
        scaled = grad * gain_ref[...]
        total_grad = hiddeng_ref[at, :] + scale * (scaled - unit * jnp.mean(scaled * unit, -1, keepdims=True))
        place_rows(tokens_grad_ref, total_grad, i)

    def block_tile(i):
        at = pl.ds(pl.multiple_of(i * tile, tile), tile)
        capacity = tok_ref.shape[1]
        parts = rows_ref[at, width:].astype(f32)
        gate = parts[:, 0:1] + parts[:, 1:2] + parts[:, 2:3]
        tok = jnp.zeros((tile, width), f32)
        for k in range(tok_ref.shape[0]):
            slot = lax.broadcasted_iota(jnp.int32, (tile, capacity), 1) + k * capacity
            pick = jnp.where(slot == target_ref[at, :], 1.0, 0.0).astype(bf16)
            tok = tok + jnp.dot(pick, tok_ref[k], preferred_element_type=f32)
        place_rows(block_ref, hidden_ref[at, :] + gate * tok, i)

    tiles = count // tile

    @pl.loop(0, 2 * peers - 1 + STARTS[-1])
    def _(turn):
        for ring in range(SEGMENTS):
            step = turn - STARTS[ring]
            if ring:

                @pl.when(step == 0)
                def _():
                    arrived(ring)

            rings.advance(ring, step)

        @pl.when(turn < tiles)
        def _():
            token_tile(turn)

        @pl.when(jnp.logical_and(turn >= tiles, turn < 2 * tiles))
        def _():
            block_tile(turn - tiles)

    for i in range(3):
        for h in range(folds):
            at = slice(bases[1 + i] + h * third, bases[1 + i] + (h + 1) * third)
            in_sum_ref[in_rows(i), h * share : (h + 1) * share] = total[at, :].astype(f32)
    for h in range(folds):
        at = slice(bases[0] + h * rows_out, bases[0] + (h + 1) * rows_out)
        out_sum_ref[:, h * share : (h + 1) * share] = total[at, :].astype(f32)
    small_sum_ref[...] = total[small_base : small_base + rows_small, :].astype(f32)
    for piece in range(1, 5):
        for slot in (1, 0):
            near_copy(slot, piece).wait_send()
        far_copy(piece).wait_send()
    rings.drain()


def finish(proj, normed_ext, w_in, out_own, small, gain, token_low, hidden_grad, hidden_one, moe_rows, target, tok, gain_row, group):
    peers, devices = lax.axis_size("seq"), lax.axis_size("exp")
    count, width = token_low.shape
    wide, rows_out = proj.shape[1] // devices, out_own.shape[0]
    rows_small, share = small.shape[0], small.shape[1] // devices
    folds, third, unit = wide // share, width // 3, 16 * peers
    used = (folds * rows_out, folds * third, folds * third, folds * third + rows_small)
    sizes = tuple(-(-u // unit) * unit for u in used)
    bases = tuple(sum(sizes[:i]) for i in range(SEGMENTS))
    length, chunk = sum(sizes), max(sizes) // peers
    vm = pl.BlockSpec(memory_space=pltpu.VMEM)
    dma = pltpu.SemaphoreType.DMA
    shapes = ((width, wide), (rows_small, share))
    return pl.pallas_call(
        functools.partial(
            finish_kernel, peers=peers, bases=bases, sizes=sizes, halo=normed_ext.shape[0] - count, tile=256,
            gain_row=gain_row,
        ),
        in_specs=[vm] * 12,
        out_specs=[vm] * 5,
        out_shape=[
            shape_of((width, wide), f32), shape_of((rows_out, wide), f32), shape_of((rows_small, share), f32),
            shape_of((group, count // group, width), f32), shape_of((group, count // group, width), bf16),
        ],
        scratch_shapes=[
            pltpu.VMEM((length, share), f32), pltpu.VMEM((length, share), bf16), pltpu.VMEM((2, width, wide), bf16),
            pltpu.VMEM(small.shape, bf16), pltpu.VMEM((width, LANES), f32),
        ]
        + [pltpu.VMEM((2,) + s, bf16) for s in shapes]
        + [pltpu.VMEM(s, bf16) for s in shapes]
        + [pltpu.VMEM(s, bf16) for s in shapes]
        + [pltpu.VMEM((SEGMENTS, peers - 1, chunk, share), bf16)] * 2
        + [dma((2, 5)), dma((2, 5)), dma((5,)), dma((5,)), dma((SEGMENTS, 2 * peers - 2)), dma((SEGMENTS, 2 * peers - 2))],
        compiler_params=pltpu.CompilerParams(collective_id=2, has_side_effects=True, vmem_limit_bytes=64 << 20),
        name="finish",
    )(
        proj, normed_ext, w_in, out_own, small, gain, token_low, hidden_grad, hidden_one, moe_rows, target[:, None], tok
    )

PIECES = 2


def gather_kernel(in_ref, small_ref, edge_ref, ids_ref, win_ref, wsmall_ref, before_ref, before_ids, near_sems, far_sems, pair_sems, edge_sems, own_sem):
    place, peers = lax.axis_index("seq"), lax.axis_size("seq")
    spot = lax.axis_index("exp")
    near = spot + 1 - 2 * lax.rem(spot, 2)
    far = lax.rem(spot + 2, 4)
    bit = lax.rem(place, 2)
    pair = place + 1 - 2 * bit
    width, wide = in_ref.shape
    share = small_ref.shape[1]
    chunk = width // 2 // PIECES
    has_before, has_after = place > 0, place < peers - 1
    barrier = pltpu.get_barrier_semaphore()
    for target in ({"exp": near}, {"exp": far}, {"seq": pair}):
        pl.semaphore_signal(barrier, inc=1, device_id=target, device_id_type=MESH)

    @pl.when(has_before)
    def _():
        pl.semaphore_signal(barrier, inc=1, device_id={"seq": place - 1}, device_id_type=MESH)

    @pl.when(has_after)
    def _():
        pl.semaphore_signal(barrier, inc=1, device_id={"seq": place + 1}, device_id_type=MESH)

    pl.semaphore_wait(barrier, 3 + has_before.astype(jnp.int32) + has_after.astype(jnp.int32))

    def columns(ref, k, size):
        return ref.at[:, pl.ds(pl.multiple_of(k * size, size), size)]

    def rows(k, half, piece):
        at = pl.multiple_of((half * PIECES + piece) * chunk, chunk)
        return win_ref.at[pl.ds(at, chunk), pl.ds(pl.multiple_of(k * wide, wide), wide)]

    def copy(source, target, sems, slot, device):
        return pltpu.make_async_remote_copy(
            src_ref=source, dst_ref=target, send_sem=sems.at[0, slot], recv_sem=sems.at[1, slot], device_id=device,
            device_id_type=MESH,
        )

    def edge_copies():
        return (
            copy(edge_ref, before_ref, edge_sems, 0, {"seq": place + 1}),
            copy(ids_ref, before_ids, edge_sems, 1, {"seq": place + 1}),
        )

    outward = []
    for piece in range(PIECES):
        at = pl.multiple_of((bit * PIECES + piece) * chunk, chunk)
        outward.append(copy(in_ref.at[pl.ds(at, chunk), :], rows(spot, bit, piece), far_sems, piece, {"exp": far}))
    outward.insert(0, copy(small_ref, columns(wsmall_ref, spot, share), far_sems, PIECES, {"exp": far}))
    for c in outward:
        c.start()
    beside = [
        copy(small_ref, columns(wsmall_ref, spot, share), near_sems, 0, {"exp": near}),
        copy(in_ref, columns(win_ref, spot, wide), near_sems, 1, {"exp": near}),
    ]
    for c in beside:
        c.start()

    @pl.when(has_after)
    def _():
        for c in edge_copies():
            c.start()

    @pl.when(jnp.logical_not(has_before))
    def _():
        before_ref[...] = jnp.zeros_like(before_ref)
        before_ids[...] = jnp.zeros_like(before_ids)

    own = [
        pltpu.make_async_copy(in_ref, columns(win_ref, spot, wide), own_sem.at[0]),
        pltpu.make_async_copy(small_ref, columns(wsmall_ref, spot, share), own_sem.at[1]),
    ]
    for c in own:
        c.start()
    outward[0].wait_recv()
    beside.append(copy(columns(wsmall_ref, far, share), columns(wsmall_ref, far, share), near_sems, 2, {"exp": near}))
    beside[-1].start()
    crossing = []
    for piece in range(PIECES):
        outward[1 + piece].wait_recv()
        part = rows(far, bit, piece)
        crossing.append(copy(part, part, pair_sems, piece, {"seq": pair}))
        crossing[-1].start()
        beside.append(copy(part, part, near_sems, 3 + piece, {"exp": near}))
        beside[-1].start()
    for piece in range(PIECES):
        crossing[piece].wait_recv()
        part = rows(far, 1 - bit, piece)
        beside.append(copy(part, part, near_sems, 3 + PIECES + piece, {"exp": near}))
        beside[-1].start()
    for c in beside:
        c.wait_recv()
    for c in outward + beside + crossing:
        c.wait_send()
    for c in own:
        c.wait()

    @pl.when(has_before)
    def _():
        for c in edge_copies():
            c.wait_recv()

    @pl.when(has_after)
    def _():
        for c in edge_copies():
            c.wait_send()


def gather_weights(in_shard, small, edge, ids, devices):
    vm = pl.BlockSpec(memory_space=pltpu.VMEM)
    dma = pltpu.SemaphoreType.DMA
    return pl.pallas_call(
        gather_kernel,
        in_specs=[pl.BlockSpec(memory_space=pl.ANY), vm, vm, vm],
        out_specs=[pl.BlockSpec(memory_space=pl.ANY), vm, vm, vm],
        out_shape=[
            shape_of((in_shard.shape[0], in_shard.shape[1] * devices), bf16),
            shape_of((small.shape[0], small.shape[1] * devices), bf16), shape_of(edge.shape, edge.dtype),
            shape_of(ids.shape, ids.dtype),
        ],
        scratch_shapes=[dma((2, 3 + 2 * PIECES)), dma((2, PIECES + 1)), dma((2, PIECES)), dma((2, 2)), dma((2,))],
        compiler_params=pltpu.CompilerParams(collective_id=5, has_side_effects=True, vmem_limit_bytes=32 << 20),
        name="gather_weights",
    )(in_shard, small, edge, ids)

def rms_norm(values, gain):
    return values * lax.rsqrt(jnp.mean(values * values, -1, keepdims=True) + epsilon) * gain


def passed_along(value, axis, steps):
    count = lax.axis_size(axis)
    initial, last = (max(0, -steps), min(count, count - steps))
    return lax.ppermute(value, axis, [(source, source + steps) for source in range(initial, last)])


def by_time(values):
    values = jnp.swapaxes(values, 0, 1)
    return values.reshape((values.shape[0] * values.shape[1],) + values.shape[2:])


def packed_small(norm_gain, conv_weight, conv_bias, x_proj, dt_proj, dt_bias, a_log, d_skip, moe_gain, router):
    share = conv_bias.shape[0]
    packed = [conv_weight, conv_bias[None], x_proj.T, dt_proj, dt_bias[None], a_log.T, d_skip[None]]
    narrow = jnp.concatenate([norm_gain[None], moe_gain[None], router.T], 0)
    total = jnp.concatenate(packed + [narrow.reshape(-1, share)], 0)
    return jnp.pad(total, ((0, -total.shape[0] % 16), (0, 0))), [p.shape[0] for p in packed], narrow.shape


def unpacked_small(whole, counts, narrow_shape, devices):
    out, at = [], 0
    for c in counts:
        out.append(whole[at : at + c])
        at += c
    share = whole.shape[1] // devices
    fold = narrow_shape[0] * narrow_shape[1] // share
    rest = whole[at : at + fold].reshape(fold, devices, share).transpose(1, 0, 2).reshape((devices,) + narrow_shape)
    rest = rest.transpose(1, 0, 2).reshape(narrow_shape[0], -1)
    return out, rest[0], rest[1], rest[2:].T


def local(
    tokens, segment_ids, routes, slot_index, norm_gain, in_proj, conv_weight, conv_bias, x_proj, dt_proj, dt_bias,
    a_log, d_skip, out_proj, moe_gain, router, expert_up, expert_down, cotangent,
):
    seq_count, part_len, width = tokens.shape
    row_count = seq_count * part_len
    group = seq_count
    kernel_len = conv_weight.shape[0]
    state_width = a_log.shape[1]
    rank_width = dt_proj.shape[0]
    halo = kernel_len * group
    devices = lax.axis_size("exp")
    doc_ids = segment_ids + 1
    edge_start = part_len - kernel_len
    token_low = by_time(tokens)
    edge_ids = jnp.pad(doc_ids[:, edge_start:], ((0, 0), (0, LANES - kernel_len)))
    small_shard, counts, narrow_shape = packed_small(
        norm_gain, conv_weight, conv_bias, x_proj, dt_proj, dt_bias, a_log, d_skip, moe_gain, router
    )
    w_in, small_whole, before_rows, before_ids = gather_weights(
        in_proj, small_shard, token_low[row_count - halo :], edge_ids, devices
    )
    out_proj, small_whole = lax.optimization_barrier((out_proj, small_whole))
    w_out = lax.all_gather(out_proj, "exp", axis=0, tiled=True)
    (w_conv, b_conv, w_x_t, w_dt, b_dt, log_decay, skip_gain), gain_one, gain_two, w_router = unpacked_small(
        small_whole, counts, narrow_shape, devices
    )
    inner_width = w_out.shape[0]
    expert_total = w_router.shape[1]
    capacity = 5 * row_count // (4 * expert_total)
    blocks = inner_width // LANES

    ext_ids = jnp.concatenate([before_ids[:, :kernel_len], doc_ids], 1)
    match = jnp.stack([ext_ids[:, 1 + k : 1 + k + part_len] == doc_ids for k in range(kernel_len - 1)])
    match = jnp.transpose(match, (2, 1, 0)).reshape(row_count, kernel_len - 1).astype(f32)
    lanes = 2 * LANES
    gain_one = gain_one.astype(f32)[None]
    gain_two = gain_two.astype(f32)[None]
    route_rows = by_time(routes)
    slot_rows = by_time(slot_index)
    target = jnp.where(
        slot_rows < capacity, route_rows * capacity + slot_rows, expert_total * capacity
    )
    cot_rows = by_time(cotangent)
    w_conv, b_conv = w_conv.astype(f32), b_conv.astype(f32)
    w_x = w_x_t.T
    ci, conv_low, gate, mixed, normed_ext = front(
        token_low, before_rows, gain_one, w_in, w_conv, b_conv, match, w_x, halo, group, lanes
    )
    rate_low = mixed[:, :rank_width].astype(bf16)
    bc = split_three(mixed[:, rank_width:])
    pick = pick_matrix(2 * state_width)
    bias = b_dt.astype(f32)
    skip = skip_gain.astype(f32)
    a_mat = -jnp.exp(log_decay.astype(f32))
    a2 = a_mat * log2e
    a_blocks = a2.reshape(state_width, blocks, LANES).transpose(1, 0, 2)
    step, z, mixed_low, start, total, cot_recv = forward_scan(
        rate_low, w_dt, bias, conv_low, bc, pick, match, a_blocks, gate, skip, cot_rows, target, capacity, group, devices
    )
    route_col = route_rows[:, None]
    router_wide = jnp.pad(w_router, ((0, 0), (0, LANES - expert_total)))
    hidden_one, moe_rows, prob, received = routed(
        mixed_low, w_out, token_low, gain_two, router_wide, route_col, target, capacity, devices, expert_total
    )
    expert_out, rows_back, up_grad, down_grad = one_expert(
        received.reshape(devices * capacity, width + LANES), cot_recv.reshape(devices * capacity, width),
        expert_up[0], expert_down[0],
    )
    hidden_grad, branch_grad, gain_two_grad, router_grad_t = collect(
        rows_back.reshape(devices, capacity, width + LANES), target, route_col, moe_rows, prob, hidden_one, cot_rows,
        gain_two, router_wide.astype(f32).T, devices,
    )
    peers = lax.axis_size("seq")
    order = [list(range(0, peers, 2)) + list(range(peers - 1, 0, -2))]

    def scattered(values):
        return lax.psum_scatter(values, "seq", scatter_dimension=0, axis_index_groups=order, tiled=True)

    def regathered(part):
        return lax.all_gather(part, "seq", axis=0, axis_index_groups=order, tiled=True)

    down_part = scattered(down_grad)
    up_part = scattered(up_grad)
    out_proj_grad = jnp.dot(mixed_low.T, branch_grad, preferred_element_type=f32)
    mixed_grad = jnp.dot(branch_grad, w_out.T, preferred_element_type=f32)
    down_part, mixed_grad = lax.optimization_barrier((down_part, mixed_grad))
    down_sum = regathered(down_part)
    proj, rate_pre_low, cg, small_one, mixed_proj_grad, tok, out_own = backward_scan(
        mixed_grad, gate, z, step, conv_low, bc, pick, match, a_blocks, total, start, rate_low, w_dt, bias, skip,
        expert_out.reshape(devices, capacity, width), out_proj_grad.astype(bf16), group, devices,
    )
    up_part, cg = lax.optimization_barrier((up_part, cg))
    up_sum = regathered(up_part)
    proj, ends, small_two = conv_back(
        cg, conv_low, mixed_proj_grad, w_x, ci, w_conv, b_conv, match, proj, halo, group, lanes
    )
    edge_back = passed_along(ends[:halo].astype(bf16), "seq", -1).astype(f32)
    proj = lax.dynamic_update_slice(proj, (ends[halo:] + edge_back).astype(bf16), (row_count - halo, 0))

    narrow = jnp.concatenate([jnp.zeros_like(gain_two_grad), gain_two_grad, router_grad_t[:expert_total]], 0)
    share, own_width = inner_width // devices, width // devices
    narrow = narrow.reshape(narrow.shape[0], devices, own_width)
    narrow = jnp.pad(narrow, ((0, -narrow.shape[0] % 16), (0, 0), (0, share - own_width))).astype(bf16)
    packed = jnp.concatenate([small_one, small_two, narrow.reshape(-1, inner_width)], 0)
    gain_row = small_one.shape[0] + small_two.shape[0]
    in_sum, out_sum, sums, tokens_grad, block_out = finish(
        proj, normed_ext, w_in, out_own, packed, gain_one, token_low, hidden_grad, hidden_one, moe_rows,
        target, tok, gain_row, group,
    )
    at, own = 0, []
    for first, rows in (
        (0, rank_width), (rank_width, state_width), (rank_width + state_width, 1), (rank_width + state_width + 1, 1)
    ):
        own.append(sums[first : first + rows])
    at = small_one.shape[0]
    mixed_width = mixed_proj_grad.shape[1]
    for first, rows in ((0, mixed_width), (mixed_width, kernel_len), (mixed_width + kernel_len, 1)):
        own.append(sums[at + first : at + first + rows])
    at += small_two.shape[0]
    own_narrow = sums[at : at + 2 + expert_total, :own_width]
    return (
        block_out,
        tokens_grad,
        own_narrow[0],
        in_sum,
        own[5],
        own[6][0],
        own[4].T,
        own[0],
        own[2][0],
        own[1].T,
        own[3][0],
        out_sum,
        own_narrow[1],
        own_narrow[2:].T,
        up_sum.astype(f32)[None],
        down_sum.astype(f32)[None],
    )


def solution(mesh):
    in_specs = (
        P("exp", "seq", None),
        P("exp", "seq"),
        P("exp", "seq"),
        P("exp", "seq"),
        P("exp"),
        P(None, "exp"),
        P(None, "exp"),
        P("exp"),
        P("exp", None),
        P(None, "exp"),
        P("exp"),
        P("exp", None),
        P("exp"),
        P("exp", None),
        P("exp"),
        P("exp", None),
        P("exp", None, None),
        P("exp", None, None),
        P("exp", "seq", None),
    )
    out_specs = (
        P("exp", "seq", None),
        P("exp", "seq", None),
        P("exp"),
        P(None, "exp"),
        P(None, "exp"),
        P("exp"),
        P("exp", None),
        P(None, "exp"),
        P("exp"),
        P("exp", None),
        P("exp"),
        P("exp", None),
        P("exp"),
        P("exp", None),
        P("exp", None, None),
        P("exp", None, None),
    )
    return jax.shard_map(local, mesh=mesh, in_specs=in_specs, out_specs=out_specs, check_vma=False)
```

```python
import functools

import jax
import jax.numpy as jnp
from jax import lax
from jax.experimental import pallas as pl
from jax.experimental.pallas import tpu as pltpu
from jax.sharding import PartitionSpec as P

f32, bf16 = jnp.float32, jnp.bfloat16
highest = lax.Precision.HIGHEST
LANES = 128
MESH = pl.DeviceIdType.MESH
epsilon = 1e-05
log2e = 1.4426950408889634
cut = 1e8
ln2 = 0.6931471805599453
vmem_cap = 58 << 20


def tree_sum(parts):
    parts = list(parts)
    while len(parts) > 1:
        paired = [parts[i] + parts[i + 1] for i in range(0, len(parts) - 1, 2)]
        parts = paired + parts[len(parts) - len(parts) % 2 :]
    return parts[0]


UN = dict(state=8, scan=8, adj=8, fwd=4, bwd=4)


def spread(rows_ref, pick_ref, outs, states, group):
    shape = pick_ref.shape
    row = lax.broadcasted_iota(jnp.int32, shape, 0)
    lane = lax.broadcasted_iota(jnp.int32, shape, 1)
    pick_ref[...] = jnp.where(lax.rem(row, 2 * states) == lax.div(lane, LANES), 1.0, 0.0).astype(bf16)
    steps = rows_ref.shape[0] // group
    chunk = 16
    wide = 2 * LANES

    @pl.loop(0, steps // chunk)
    def _(i):
        rows = rows_ref[pl.ds(pl.multiple_of(i * chunk * group, chunk * group), chunk * group), :]
        for which, out_ref in outs:
            for n in range(0, states, 2):
                at = (which * states + n) * LANES
                part = jnp.dot(rows, pick_ref[:, at : at + wide], preferred_element_type=f32)
                for k in range(2):
                    out_ref[pl.ds(i * chunk, chunk), n + k] = part[:, k * LANES : (k + 1) * LANES].reshape(
                        chunk, group, LANES
                    )


def softplus(v):
    return jnp.maximum(v, 0.0) + jnp.log1p(jnp.exp(-jnp.abs(v)))


class Carry:
    def __init__(self, step, ends, total, a_all, held, got, sent, send_sem, recv_sem):
        self.step, self.ends, self.total, self.a_all = step, ends, total, a_all
        self.held, self.got, self.sent, self.send_sem, self.recv_sem = held, got, sent, send_sem, recv_sem
        self.place, self.peers = lax.axis_index("seq"), lax.axis_size("seq")
        self.rank = self.place if step > 0 else self.peers - 1 - self.place
        self.count, self.states = ends.shape[0], ends.shape[1]
        self.has_before, self.has_after = self.rank > 0, self.rank < self.peers - 1
        self.lag = jnp.minimum(self.rank, self.count)

    def enter(self, devices=1):
        spot = lax.axis_index("exp")
        barrier = pltpu.get_barrier_semaphore()

        @pl.when(self.has_before)
        def _():
            pl.semaphore_signal(barrier, inc=1, device_id={"seq": self.place - self.step}, device_id_type=MESH)

        @pl.when(self.has_after)
        def _():
            pl.semaphore_signal(barrier, inc=1, device_id={"seq": self.place + self.step}, device_id_type=MESH)

        for hop in range(1, devices):
            pl.semaphore_signal(barrier, inc=1, device_id={"exp": lax.rem(spot + hop, devices)}, device_id_type=MESH)
        neighbours = self.has_before.astype(jnp.int32) + self.has_after.astype(jnp.int32)
        pl.semaphore_wait(barrier, neighbours + (devices - 1))

    def hop(self, u):
        return pltpu.make_async_remote_copy(
            src_ref=self.sent.at[u], dst_ref=self.got.at[u], send_sem=self.send_sem.at[u], recv_sem=self.recv_sem.at[u],
            device_id={"seq": self.place + self.step}, device_id_type=MESH,
        )

    def handle(self, at):
        u = at - self.lag

        @pl.when(jnp.logical_and(u >= 0, u < self.count))
        def _():
            @pl.when(self.has_before)
            def _():
                self.hop(u).wait_recv()
                self.held[u] = self.got[u].astype(f32)

            @pl.when(jnp.logical_not(self.has_before))
            def _():
                self.held[u] = jnp.zeros(self.held.shape[1:], f32)

            @pl.when(self.has_after)
            def _():
                for n in range(self.states):
                    decay = jnp.exp2(self.a_all[u, n : n + 1, :] * self.total[u])
                    self.sent[u, n] = (self.ends[u, n] + decay * self.held[u, n]).astype(bf16)
                self.hop(u).start()

    def leave(self):
        @pl.loop(0, self.count)
        def _(u):
            @pl.when(self.has_after)
            def _():
                self.hop(u).wait_send()


def forward_kernel(
    rate_ref, wdt_ref, bias_ref, conv_ref, bc_ref, match_ref, a_all, gate_ref, skip_ref, cot_ref, target_ref,
    step_ref, z_ref, mixed_ref, start_ref, total_ref, cot_out,
    cot_got, pick_ref, kb_ref, b_all, c_all, step_all, ends, staged, cot_send, cot_recv, got, sent, send_sem, recv_sem, *, states, group, devices,
):
    at = pl.program_id(0)
    count = a_all.shape[0]
    j = lax.rem(at, count)
    carry_of = Carry(1, ends, total_ref, a_all, start_ref, got, sent, send_sem, recv_sem)
    rows = conv_ref.shape[0]
    moved = Dispatch(cot_ref, target_ref, cot_got, staged, cot_send, cot_recv, devices)

    @pl.when(at == 0)
    def _():
        carry_of.enter(devices)
        moved.start()
        kb_ref[...] = broad_cut(match_ref)
        spread(bc_ref, pick_ref, ((0, b_all), (1, c_all)), states, group)

    @pl.when(at < count)
    def _():
        pre = jnp.dot(rate_ref[...], wdt_ref[...], preferred_element_type=f32) + bias_ref[...]
        step = softplus(pre)
        step_ref[...] = step
        step_all[j] = step
        a_rows = [jnp.broadcast_to(a_all[j, n : n + 1, :], (group, LANES)) for n in range(states)]
        un = UN["state"]

        def body(i, carry):
            total, state = carry
            base = pl.multiple_of(i * un * group, un * group)
            x_two = conv_ref[pl.ds(base, un * group), :].astype(f32)
            for k in range(un):
                here = pl.ds(pl.multiple_of(base + k * group, group), group)
                dt = step_ref[here, :]
                masked = dt + kb_ref[here, :]
                u = dt * x_two[k * group : (k + 1) * group]
                total = total + masked
                state = [
                    jnp.exp2(masked * a_rows[n]) * state[n] + u * b_all[un * i + k, n] for n in range(states)
                ]
            return total, state

        zero = jnp.zeros((group, LANES), f32)
        total, state = lax.fori_loop(0, rows // (un * group), body, (zero, [zero] * states))
        total_ref[j] = total
        for n in range(states):
            ends[j, n] = state[n]

    carry_of.handle(at)

    @pl.when(at >= count)
    def _():
        a_rows = [jnp.broadcast_to(a_all[j, n : n + 1, :], (group, LANES)) for n in range(states)]
        un = UN["scan"]

        def body(i, state):
            base = pl.multiple_of(i * un * group, un * group)
            x_two = conv_ref[pl.ds(base, un * group), :].astype(f32)
            outs = []
            for k in range(un):
                here = pl.ds(pl.multiple_of(base + k * group, group), group)
                dt = step_all[j, here, :]
                masked = dt + kb_ref[here, :]
                u = dt * x_two[k * group : (k + 1) * group]
                state = [
                    jnp.exp2(masked * a_rows[n]) * state[n] + u * b_all[un * i + k, n] for n in range(states)
                ]
                outs.append(tree_sum(state[n] * c_all[un * i + k, n] for n in range(states)))
            whole = pl.ds(base, un * group)
            gate = gate_ref[whole, :]
            z = jnp.concatenate(outs, 0) + skip_ref[...] * x_two
            z_ref[whole, :] = z
            mixed_ref[whole, :] = (z * (gate * jax.nn.sigmoid(gate))).astype(bf16)
            return state

        lax.fori_loop(0, rows // (un * group), body, [start_ref[j, n] for n in range(states)])

    @pl.when(at == 2 * count - 1)
    def _():
        carry_of.leave()
        moved.wait()
        cot_out[...] = cot_got[...]


def broad_cut(match_ref):
    keep = match_ref[:, match_ref.shape[1] - 1 :]
    return jnp.broadcast_to((1.0 - keep) * cut, (match_ref.shape[0], LANES))


def backward_kernel(
    mg_ref, gate_ref, z_ref, step_ref, conv_ref, bc_ref, match_ref, a_all, total_ref, start_ref, rate_ref, wdt_ref,
    bias_ref, skip_ref, back_ref, outg_ref,
    gg_ref, low_ref, cg_ref, small_ref, mpg_ref, tok_ref, outo_ref,
    near_got, passed, far_got, mine, out_send, out_recv, out_load, back_send, back_recv, back_own, pick_ref, kb_ref, b_all, c_all, b_acc, c_acc, kept, dt_grad, g_all, rate_acc, ends, last, got, sent, send_sem, recv_sem, *, states, group, devices,
):
    at = pl.program_id(0)
    count = a_all.shape[0]
    j = lax.rem(at, count)
    carry_of = Carry(-1, ends, total_ref, a_all, last, got, sent, send_sem, recv_sem)
    steps = conv_ref.shape[0] // group
    rank = rate_ref.shape[1]
    zero = jnp.zeros((group, LANES), f32)
    spot = lax.axis_index("exp")

    def back_copy(hop):
        peer = lax.rem(spot + hop, devices)
        return pltpu.make_async_remote_copy(
            src_ref=back_ref.at[peer], dst_ref=tok_ref.at[spot], send_sem=back_send.at[hop - 1],
            recv_sem=back_recv.at[hop - 1], device_id={"exp": peer}, device_id_type=MESH,
        )

    near = spot + 1 - 2 * lax.rem(spot, 2)
    far = lax.rem(spot + 2, 4)
    across = lax.rem(near + 2, 4)
    rows_out = mine.shape[0]

    def out_rows(k):
        return outg_ref.at[pl.ds(pl.multiple_of(k * rows_out, rows_out), rows_out), :]

    def out_move(slot):
        if slot == 2:
            source, target, device = passed, far_got, far
        else:
            source, target, device = out_rows(across if slot else near), near_got.at[slot], near
        return pltpu.make_async_remote_copy(
            src_ref=source, dst_ref=target, send_sem=out_send.at[slot], recv_sem=out_recv.at[slot],
            device_id={"exp": device}, device_id_type=MESH,
        )

    def out_loads():
        return (
            pltpu.make_async_copy(out_rows(far), passed, out_load.at[0]),
            pltpu.make_async_copy(out_rows(spot), mine, out_load.at[1]),
        )

    def out_store():
        return pltpu.make_async_copy(mine, outo_ref, out_load.at[2])

    def own_copy():
        return pltpu.make_async_copy(back_ref.at[spot], tok_ref.at[spot], back_own.at[0])

    @pl.when(at == 0)
    def _():
        carry_of.enter(devices)
        out_move(1).start()
        out_move(0).start()
        for c in out_loads():
            c.start()
        own_copy().start()
        for hop in range(1, devices):
            back_copy(hop).start()
        kb_ref[...] = broad_cut(match_ref)
        spread(bc_ref, pick_ref, ((0, b_all), (1, c_all)), states, group)
        rate_acc[...] = jnp.zeros_like(rate_acc)

        @pl.loop(0, steps)
        def _(t):
            none = jnp.zeros((states, group, LANES), f32)
            b_acc[t] = none
            c_acc[t] = none

    @pl.when(at == 1)
    def _():
        for c in out_loads():
            c.wait()
        out_move(1).wait_recv()
        passed[...] = (passed[...].astype(f32) + near_got[1].astype(f32)).astype(bf16)
        out_move(2).start()

    @pl.when(at == 2 * count - 1)
    def _():
        out_move(0).wait_recv()
        out_move(2).wait_recv()
        mine[...] = (mine[...].astype(f32) + near_got[0].astype(f32) + far_got[...].astype(f32)).astype(bf16)
        out_store().start()

    @pl.when(at < count)
    def _():
        a_rows = [jnp.broadcast_to(a_all[j, n : n + 1, :], (group, LANES)) for n in range(states)]
        un = UN["adj"]

        def body(i, q):
            base = pl.multiple_of((steps // un - 1 - i) * un * group, un * group)
            whole = pl.ds(base, un * group)
            mixed_grad, gate = mg_ref[whole, :], gate_ref[whole, :]
            sig = jax.nn.sigmoid(gate)
            g_rows = mixed_grad * (gate * sig)
            g_all[j, whole, :] = g_rows.astype(bf16)
            gg_ref[whole, :] = (mixed_grad * z_ref[whole, :] * (sig * (1.0 + gate * (1.0 - sig)))).astype(bf16)
            for k in reversed(range(un)):
                t = un * (steps // un - 1 - i) + k
                here = pl.ds(pl.multiple_of(base + k * group, group), group)
                masked = step_ref[here, :] + kb_ref[here, :]
                g = g_rows[k * group : (k + 1) * group]
                q = [jnp.exp2(masked * a_rows[n]) * (c_all[t, n] * g + q[n]) for n in range(states)]
            return q

        q = lax.fori_loop(0, steps // un, body, [zero] * states)
        for n in range(states):
            ends[j, n] = q[n]

    carry_of.handle(at)

    @pl.when(at >= count)
    def _():
        a_rows = [jnp.broadcast_to(a_all[j, n : n + 1, :], (group, LANES)) for n in range(states)]
        fu, bu = UN["fwd"], UN["bwd"]

        def forward(i, state):
            base = pl.multiple_of(i * fu * group, fu * group)
            x_two = conv_ref[pl.ds(base, fu * group), :].astype(f32)
            g_two = g_all[j, pl.ds(base, fu * group), :].astype(f32)
            for k in range(fu):
                t = fu * i + k
                here = pl.ds(pl.multiple_of(base + k * group, group), group)
                dt = step_ref[here, :]
                masked = dt + kb_ref[here, :]
                g = g_two[k * group : (k + 1) * group]
                u = dt * x_two[k * group : (k + 1) * group]
                for n in range(states):
                    kept[t, n] = state[n]
                state = [jnp.exp2(masked * a_rows[n]) * state[n] + u * b_all[t, n] for n in range(states)]
                for n in range(states):
                    c_acc[t, n] += state[n] * g
            return state

        lax.fori_loop(0, steps // fu, forward, [start_ref[0, n] for n in range(states)])
        skip = skip_ref[...]

        def backward(i, carry):
            q, a_sum, skip_sum = carry
            base = pl.multiple_of((steps // bu - 1 - i) * bu * group, bu * group)
            x_two = conv_ref[pl.ds(base, bu * group), :].astype(f32)
            g_two = g_all[j, pl.ds(base, bu * group), :].astype(f32)
            for k in reversed(range(bu)):
                t = bu * (steps // bu - 1 - i) + k
                here = pl.ds(pl.multiple_of(base + k * group, group), group)
                dt = step_ref[here, :]
                masked = dt + kb_ref[here, :]
                g = g_two[k * group : (k + 1) * group]
                x = x_two[k * group : (k + 1) * group]
                u = dt * x
                skip_sum = skip_sum + g * x
                lam = [c_all[t, n] * g + q[n] for n in range(states)]
                for n in range(states):
                    b_acc[t, n] += lam[n] * u
                s_one = tree_sum(lam[n] * b_all[t, n] for n in range(states))
                q = [jnp.exp2(masked * a_rows[n]) * lam[n] for n in range(states)]
                w = [q[n] * kept[t, n] for n in range(states)]
                s_two = tree_sum(w[n] * a_rows[n] for n in range(states))
                a_sum = [a_sum[n] + dt * w[n] for n in range(states)]
                cg_ref[here, :] = skip * g + dt * s_one
                dt_grad[here, :] = x * s_one + ln2 * s_two
            return q, a_sum, skip_sum

        q, a_sum, skip_sum = lax.fori_loop(
            0, steps // bu, backward, ([last[j, n] for n in range(states)], [zero] * states, zero)
        )
        pre = jnp.dot(rate_ref[...], wdt_ref[...], preferred_element_type=f32) + bias_ref[...]
        pre_grad = dt_grad[...] * jax.nn.sigmoid(pre)
        low = pre_grad.astype(bf16)
        low_ref[...] = low
        rate_acc[...] += lax.dot_general(low, wdt_ref[...], (((1,), (1,)), ((), ())), preferred_element_type=f32)
        rows_of = [lax.dot_general(rate_ref[...], low, (((0,), (0,)), ((), ())), preferred_element_type=f32)]
        rows_of += [jnp.sum(a_sum[n], 0, keepdims=True) * a_all[j, n : n + 1, :] * ln2 for n in range(states)]
        rows_of += [jnp.sum(pre_grad, 0, keepdims=True), jnp.sum(skip_sum, 0, keepdims=True)]
        spare = small_ref.shape[0] - rank - states - 2
        small_ref[...] = jnp.concatenate(rows_of + [jnp.zeros((spare, LANES), f32)], 0).astype(bf16)

    @pl.when(at == 2 * count - 1)
    def _():
        carry_of.leave()
        out_store().wait()
        for slot in range(3):
            out_move(slot).wait_send()
        own_copy().wait()
        for hop in range(1, devices):
            back_copy(hop).wait()
        mpg_ref[:, :rank] = rate_acc[...].astype(bf16)
        lane = lax.broadcasted_iota(jnp.int32, (2 * LANES, 2 * states), 1)
        own = lax.broadcasted_iota(jnp.int32, (2 * LANES, 2 * states), 0) // LANES * states
        total = jnp.zeros((steps * group, 2 * states), f32)
        for n in range(states):
            both = [acc[:, n].reshape(steps * group, LANES) for acc in (b_acc, c_acc)]
            rows = jnp.concatenate(both, 1)
            pick = jnp.where(lane == own + n, 1.0, 0.0).astype(bf16)
            high = rows.astype(bf16)
            rest = (rows - high.astype(f32)).astype(bf16)
            total = total + jnp.dot(high, pick, preferred_element_type=f32)
            total = total + jnp.dot(rest, pick, preferred_element_type=f32)
        mpg_ref[:, rank:] = total.astype(bf16)


def rows_block(rows):
    return pl.BlockSpec((rows, LANES), lambda j: (0, j))


def whole_block(shape):
    return pl.BlockSpec(shape, lambda j: (0,) * len(shape))


def state_block(states, group):
    return pl.BlockSpec((1, states, group, LANES), lambda j: (j, 0, 0, 0))


def shape_of(shape, dtype):
    return jax.ShapeDtypeStruct(shape, dtype)


def params():
    return pltpu.CompilerParams(vmem_limit_bytes=vmem_cap)


def carry_scratch(shape):
    return [
        pltpu.VMEM(shape, bf16), pltpu.VMEM(shape, bf16), pltpu.SemaphoreType.DMA((shape[0],)),
        pltpu.SemaphoreType.DMA((shape[0],)),
    ]


def forward_scan(rate_low, w_dt, bias, conv_low, bc, match, a_blocks, gate, skip, cot, target, capacity, group, devices):
    rows, inner = conv_low.shape
    count, states, _ = a_blocks.shape
    rank = rate_low.shape[1]
    first = lambda at: (0, jnp.minimum(at, count - 1))
    both = lambda at: (0, lax.rem(at, count))
    second = lambda at: (0, jnp.maximum(at - count, 0))
    shape = (count, states, group, LANES)
    big = pltpu.VMEM((rows // group, states, group, LANES), f32)
    return pl.pallas_call(
        functools.partial(forward_kernel, states=states, group=group, devices=devices),
        grid=(2 * count,),
        in_specs=[
            whole_block((rows, rank)), pl.BlockSpec((rank, LANES), first), pl.BlockSpec((1, LANES), first),
            pl.BlockSpec((rows, LANES), both), whole_block(bc.shape),
            whole_block(match.shape), whole_block(a_blocks.shape), pl.BlockSpec((rows, LANES), second),
            pl.BlockSpec((1, LANES), second), whole_block(cot.shape), whole_block((1, rows)),
        ],
        out_specs=[
            pl.BlockSpec((rows, LANES), first), pl.BlockSpec((rows, LANES), second), pl.BlockSpec((rows, LANES), second),
            whole_block(shape), whole_block((count, group, LANES)), whole_block((devices, capacity, cot.shape[1])),
        ],
        out_shape=[
            shape_of((rows, inner), f32), shape_of((rows, inner), f32), shape_of((rows, inner), bf16),
            shape_of(shape, f32), shape_of((count, group, LANES), f32), shape_of((devices, capacity, cot.shape[1]), bf16),
        ],
        scratch_shapes=[pltpu.VMEM((devices, capacity, cot.shape[1]), bf16), pltpu.VMEM((bc.shape[1], 2 * states * LANES), bf16)]
        + [pltpu.VMEM((rows, LANES), f32), big, big]
        + [pltpu.VMEM((count, rows, LANES), f32), pltpu.VMEM(shape, f32)]
        + [pltpu.VMEM((devices - 1, capacity, cot.shape[1]), bf16)]
        + [pltpu.SemaphoreType.DMA((devices - 1,)), pltpu.SemaphoreType.DMA((devices - 1,))] + carry_scratch(shape),
        compiler_params=pltpu.CompilerParams(collective_id=0, has_side_effects=True, vmem_limit_bytes=vmem_cap),
        name="forward_scan",
    )(rate_low, w_dt, bias, conv_low, bc, match, a_blocks, gate, skip, cot, target[None, :])


def backward_scan(mixed_grad, gate, z, step, conv_low, bc, match, a_blocks, total, start, rate_low, w_dt, bias, skip, back, out_grad, group, devices):
    rows, inner = conv_low.shape
    count, states, _ = a_blocks.shape
    rank = rate_low.shape[1]
    small_rows = -(-(rank + states + 2) // 16) * 16
    out_piece = (out_grad.shape[0] // devices, out_grad.shape[1])
    dma = pltpu.SemaphoreType.DMA
    first = lambda at: (0, jnp.minimum(at, count - 1))
    both = lambda at: (0, lax.rem(at, count))
    second = lambda at: (0, jnp.maximum(at - count, 0))
    shape = (count, states, group, LANES)
    big = pltpu.VMEM((rows // group, states, group, LANES), f32)
    return pl.pallas_call(
        functools.partial(backward_kernel, states=states, group=group, devices=devices),
        grid=(2 * count,),
        in_specs=[
            pl.BlockSpec((rows, LANES), first), pl.BlockSpec((rows, LANES), first), pl.BlockSpec((rows, LANES), first),
            pl.BlockSpec((rows, LANES), both), pl.BlockSpec((rows, LANES), second), whole_block(bc.shape),
            whole_block(match.shape), whole_block(a_blocks.shape), whole_block(total.shape),
            pl.BlockSpec((1, states, group, LANES), lambda at: (jnp.maximum(at - count, 0), 0, 0, 0)),
            whole_block((rows, rank)), pl.BlockSpec((rank, LANES), second), pl.BlockSpec((1, LANES), second),
            pl.BlockSpec((1, LANES), second), pl.BlockSpec(memory_space=pl.ANY), pl.BlockSpec(memory_space=pl.ANY),
        ],
        out_specs=[
            pl.BlockSpec((rows, LANES), lambda at: (0, jnp.minimum(at, count - 1) + count)),
            pl.BlockSpec((rows, LANES), second), pl.BlockSpec((rows, LANES), second),
            pl.BlockSpec((small_rows, LANES), second), whole_block((rows, rank + 2 * states)),
            pl.BlockSpec(memory_space=pl.ANY), pl.BlockSpec(memory_space=pl.ANY),
        ],
        out_shape=[
            shape_of((rows, 2 * inner), bf16), shape_of((rows, inner), bf16), shape_of((rows, inner), f32),
            shape_of((small_rows, inner), bf16), shape_of((rows, rank + 2 * states), bf16), shape_of(back.shape, bf16),
            shape_of(out_piece, bf16),
        ],
        scratch_shapes=[pltpu.VMEM((2,) + out_piece, bf16), pltpu.VMEM(out_piece, bf16), pltpu.VMEM(out_piece, bf16)]
        + [pltpu.VMEM(out_piece, bf16), dma((3,)), dma((3,)), dma((3,)), dma((devices - 1,)), dma((devices - 1,))]
        + [dma((1,)), pltpu.VMEM((bc.shape[1], 2 * states * LANES), bf16), pltpu.VMEM((rows, LANES), f32), big, big, big, big, big]
        + [pltpu.VMEM((rows, LANES), f32), pltpu.VMEM((count, rows, LANES), bf16)]
        + [pltpu.VMEM((rows, rank), f32), pltpu.VMEM(shape, f32), pltpu.VMEM(shape, f32)] + carry_scratch(shape),
        compiler_params=pltpu.CompilerParams(collective_id=1, has_side_effects=True, vmem_limit_bytes=64 << 20),
        name="backward_scan",
    )(mixed_grad, gate, z, step, conv_low, bc, match, a_blocks, total, start, rate_low, w_dt, bias, skip, back, out_grad)

def broad_match(match_ref, wide):
    @pl.when(pl.program_id(0) == 0)
    def _():
        for k in range(match_ref.shape[1]):
            wide[k] = jnp.broadcast_to(match_ref[:, k : k + 1], wide.shape[1:])


def front_kernel(
    token_ref, before_ref, gain_ref, wc_ref, wg_ref, cw_ref, cb_ref, compact_ref, wx_ref, ci_ref, low_ref, gate_ref, rate_ref, bc_ref,
    normed_ref, mixed_ref, rows_f, match_ref, *, halo, group,
):
    rows = low_ref.shape[0]
    broad_match(compact_ref, match_ref)

    @pl.when(pl.program_id(0) == 0)
    def _():
        def put(at, source):
            values = source.astype(f32)
            scale = lax.rsqrt(jnp.mean(values * values, -1, keepdims=True) + epsilon)
            normed_ref[at, :] = (values * scale * gain_ref[...]).astype(bf16)

        put(slice(0, halo), before_ref[...])
        tile = 256

        @pl.loop(0, rows // tile)
        def _(i):
            put(pl.ds(pl.multiple_of(halo + i * tile, halo), tile), token_ref[pl.ds(pl.multiple_of(i * tile, tile), tile), :])

    taps = cw_ref.shape[0]
    ci = jnp.dot(normed_ref[...], wc_ref[...], preferred_element_type=f32).astype(bf16)
    ci_ref[...] = ci
    rows_f[...] = ci.astype(f32)
    total = conv_total(rows_f, cw_ref, cb_ref, match_ref, halo, group, rows, taps)
    low = (total * jax.nn.sigmoid(total)).astype(bf16)
    low_ref[...] = low
    gate_ref[...] = jnp.dot(normed_ref[halo:, :], wg_ref[...], preferred_element_type=f32)
    part = jnp.dot(low, wx_ref[...], preferred_element_type=f32)

    @pl.when(pl.program_id(0) == 0)
    def _():
        mixed_ref[...] = part

    @pl.when(pl.program_id(0) > 0)
    def _():
        mixed_ref[...] += part

    @pl.when(pl.program_id(0) == pl.num_programs(0) - 1)
    def _():
        rank, wide = rate_ref.shape[1], bc_ref.shape[1] // 3
        rate_ref[...] = mixed_ref[:, :rank].astype(bf16)
        rest = mixed_ref[:, rank:]
        for k in range(3):
            part_low = rest.astype(bf16)
            bc_ref[:, k * wide : (k + 1) * wide] = part_low
            rest = rest - part_low.astype(f32)


def conv_total(rows_f, cw_ref, cb_ref, match_ref, halo, group, rows, taps):
    total = cb_ref[...] + cw_ref[taps - 1 : taps, :] * rows_f[halo : halo + rows, :]
    for k in range(taps - 1):
        at = halo - (taps - 1 - k) * group
        total = total + cw_ref[k : k + 1, :] * rows_f[at : at + rows, :] * match_ref[k]
    return total


def front(token_low, before_rows, gain, w_in, conv_w, conv_b, match, w_x, rank, halo, group, lanes):
    width, inner = w_in.shape[0], w_in.shape[1] // 2
    total_rows = token_low.shape[0] + halo
    rows, taps, mixed_width = total_rows - halo, conv_w.shape[0], w_x.shape[1]
    count = inner // lanes
    cols = lambda r: pl.BlockSpec((r, lanes), lambda j: (0, j))
    return pl.pallas_call(
        functools.partial(front_kernel, halo=halo, group=group),
        grid=(count,),
        in_specs=[
            whole_block(token_low.shape), whole_block(before_rows.shape), whole_block(gain.shape), cols(width),
            pl.BlockSpec((width, lanes), lambda j: (0, j + count)),
            cols(taps), cols(1), whole_block(match.shape), pl.BlockSpec((lanes, mixed_width), lambda j: (j, 0)),
        ],
        out_specs=[
            cols(total_rows), cols(rows), cols(rows), whole_block((rows, rank)), whole_block((rows, 3 * (mixed_width - rank))),
            whole_block((total_rows, width)),
        ],
        out_shape=[
            shape_of((total_rows, inner), bf16), shape_of((rows, inner), bf16), shape_of((rows, inner), f32),
            shape_of((rows, rank), bf16), shape_of((rows, 3 * (mixed_width - rank)), bf16), shape_of((total_rows, width), bf16),
        ],
        scratch_shapes=[pltpu.VMEM((rows, mixed_width), f32), pltpu.VMEM((total_rows, lanes), f32), pltpu.VMEM((match.shape[1], rows, lanes), f32)],
        compiler_params=params(),
        name="front",
    )(token_low, before_rows, gain, w_in, w_in, conv_w, conv_b, match, w_x)


def conv_back_kernel(
    cg_ref, low_ref, mpg_ref, wx_ref, ci_ref, cw_ref, cb_ref, compact_ref, proj_ref, pg_ref, ext_ref, small_ref, rows_f, ext, match_ref,
    *, halo, group,
):
    broad_match(compact_ref, match_ref)
    rows = pg_ref.shape[0]
    taps = cw_ref.shape[0]
    grad = cg_ref[...] + lax.dot_general(
        mpg_ref[...], wx_ref[...], (((1,), (1,)), ((), ())), preferred_element_type=f32
    )
    rows_f[...] = ci_ref[...].astype(f32)
    total = conv_total(rows_f, cw_ref, cb_ref, match_ref, halo, group, rows, taps)
    sig = jax.nn.sigmoid(total)
    grad = grad * (sig * (1.0 + total * (1.0 - sig)))
    x_part = lax.dot_general(mpg_ref[...], low_ref[...], (((0,), (0,)), ((), ())), preferred_element_type=f32)
    taps_grad = [None] * taps
    ext[:halo, :] = jnp.zeros((halo, ext.shape[1]), f32)
    ext[halo:, :] = grad * cw_ref[taps - 1 : taps, :]
    taps_grad[taps - 1] = jnp.sum(grad * rows_f[halo:, :], 0, keepdims=True)
    for k in range(taps - 1):
        at = halo - (taps - 1 - k) * group
        own = grad * match_ref[k]
        taps_grad[k] = jnp.sum(own * rows_f[at : at + rows, :], 0, keepdims=True)
        ext[at : at + rows, :] += own * cw_ref[k : k + 1, :]
    pg_ref[...] = ext[halo:, :].astype(bf16)
    ext_ref[:halo, :] = ext[:halo, :]
    ext_ref[halo:, :] = ext[rows:, :]
    spare = small_ref.shape[0] - x_part.shape[0] - taps - 1
    parts = [x_part] + taps_grad + [jnp.sum(grad, 0, keepdims=True), jnp.zeros((spare, ext.shape[1]), f32)]
    small_ref[...] = jnp.concatenate(parts, 0).astype(bf16)


def conv_back(cg, conv_low, mpg, w_x, ci, conv_w, conv_b, match, proj, halo, group, lanes):
    rows, inner = cg.shape
    taps, mixed_width = conv_w.shape[0], w_x.shape[1]
    small_rows = -(-(mixed_width + taps + 1) // 16) * 16
    cols = lambda r: pl.BlockSpec((r, lanes), lambda j: (0, j))
    return pl.pallas_call(
        functools.partial(conv_back_kernel, halo=halo, group=group),
        grid=(inner // lanes,),
        in_specs=[
            cols(rows), cols(rows), whole_block((rows, mixed_width)), pl.BlockSpec((lanes, mixed_width), lambda j: (j, 0)),
            cols(rows + halo), cols(taps), cols(1), whole_block(match.shape),
            pl.BlockSpec(memory_space=pl.ANY),
        ],
        out_specs=[cols(rows), cols(2 * halo), cols(small_rows)],
        out_shape=[shape_of(proj.shape, bf16), shape_of((2 * halo, inner), f32), shape_of((small_rows, inner), bf16)],
        scratch_shapes=[pltpu.VMEM((rows + halo, lanes), f32), pltpu.VMEM((rows + halo, lanes), f32)]
        + [pltpu.VMEM((match.shape[1], rows, lanes), f32)],
        input_output_aliases={8: 0},
        compiler_params=params(),
        name="conv_back",
    )(cg, conv_low, mpg, w_x, ci, conv_w, conv_b, match, proj)

def expert_kernel(
    rows_ref, cot_ref, up_ref, down_ref, out_ref, back_ref, upg_ref, downg_ref, grad, out_acc, back_acc, active, pre_grad, *, tile
):
    first = pl.program_id(0) == 0
    final = pl.program_id(0) == pl.num_programs(0) - 1
    slots, width = cot_ref.shape
    tiles = [slice(i * tile, (i + 1) * tile) for i in range(slots // tile)]

    @pl.when(first)
    def _():
        for at in tiles:
            parts = rows_ref[at, width : width + LANES].astype(f32)
            gate = parts[:, 0:1] + parts[:, 1:2] + parts[:, 2:3]
            grad[at, :] = (gate * cot_ref[at, :].astype(f32)).astype(bf16)
            out_acc[at, :] = jnp.zeros((tile, width), f32)
            back_acc[at, :] = jnp.zeros((tile, width), f32)

    for at in tiles:
        pre = jnp.dot(rows_ref[at, :width], up_ref[...], preferred_element_type=f32)
        act_grad = lax.dot_general(grad[at, :], down_ref[...], (((1,), (1,)), ((), ())), preferred_element_type=f32)
        half = 0.5 * lax.erf(pre * 0.7071067811865476) + 0.5
        active[at, :] = (pre * half).astype(bf16)
        slope = half + pre * (jnp.exp(pre * pre * -0.5) * 0.3989422804014327)
        pre_grad[at, :] = (act_grad * slope).astype(bf16)
    for at in tiles:
        out_acc[at, :] += jnp.dot(active[at, :], down_ref[...], preferred_element_type=f32)
        back_acc[at, :] += lax.dot_general(
            pre_grad[at, :], up_ref[...], (((1,), (1,)), ((), ())), preferred_element_type=f32
        )
    downg_ref[...] = lax.dot_general(
        active[...], grad[...], (((0,), (0,)), ((), ())), preferred_element_type=f32
    ).astype(bf16)
    upg_ref[...] = lax.dot_general(
        rows_ref[:, :width], pre_grad[...], (((0,), (0,)), ((), ())), preferred_element_type=f32
    ).astype(bf16)

    @pl.when(final)
    def _():
        for at in tiles:
            out = out_acc[at, :].astype(bf16)
            out_ref[at, :] = out
            back_ref[at, :width] = back_acc[at, :].astype(bf16)
            dot = jnp.sum(out.astype(f32) * cot_ref[at, :].astype(f32), -1, keepdims=True)
            back_ref[at, width:] = in_parts(dot)


def in_parts(column):
    high = column.astype(bf16).astype(f32)
    mid = (column - high).astype(bf16).astype(f32)
    lane = lax.broadcasted_iota(jnp.int32, (column.shape[0], LANES), 1)
    low = column - high - mid
    return jnp.where(lane == 0, high, jnp.where(lane == 1, mid, jnp.where(lane == 2, low, 0.0))).astype(bf16)


def one_expert(rows, cot, up, down):
    slots, width = cot.shape
    hidden = up.shape[1]
    hidden_tile, tile = hidden // 6, slots // 2
    full = whole_block((slots, width))
    broad = whole_block((slots, width + LANES))
    cols = pl.BlockSpec((width, hidden_tile), lambda j: (0, j))
    deep = pl.BlockSpec((hidden_tile, width), lambda j: (j, 0))
    return pl.pallas_call(
        functools.partial(expert_kernel, tile=tile),
        grid=(hidden // hidden_tile,),
        in_specs=[broad, full, cols, deep],
        out_specs=[full, broad, cols, deep],
        out_shape=[
            shape_of((slots, width), bf16), shape_of((slots, width + LANES), bf16), shape_of((width, hidden), bf16),
            shape_of((hidden, width), bf16),
        ],
        scratch_shapes=[
            pltpu.VMEM((slots, width), bf16), pltpu.VMEM((slots, width), f32), pltpu.VMEM((slots, width), f32),
            pltpu.VMEM((slots, hidden_tile), bf16), pltpu.VMEM((slots, hidden_tile), bf16),
        ],
        compiler_params=params(),
        name="one_expert",
    )(rows, cot, up, down)


def exp_barrier(spot, devices):
    barrier = pltpu.get_barrier_semaphore()
    for hop in range(1, devices):
        pl.semaphore_signal(barrier, inc=1, device_id={"exp": lax.rem(spot + hop, devices)}, device_id_type=MESH)
    pl.semaphore_wait(barrier, devices - 1)


class Dispatch:
    def __init__(self, rows_ref, target_ref, got_ref, staged, send_sem, recv_sem, devices):
        self.rows_ref, self.target_ref, self.got_ref, self.staged = rows_ref, target_ref, got_ref, staged
        self.send_sem, self.recv_sem, self.devices = send_sem, recv_sem, devices
        self.spot = lax.axis_index("exp")
        self.hops = [h for h in range(devices // 2, devices)] + [h for h in range(1, devices // 2)]

    def packed(self, k):
        capacity = self.got_ref.shape[1]
        slot = lax.broadcasted_iota(jnp.int32, (capacity, self.rows_ref.shape[0]), 0) + k * capacity
        pick = jnp.where(slot == self.target_ref[...], 1.0, 0.0).astype(bf16)
        return jnp.dot(pick, self.rows_ref[...], preferred_element_type=f32).astype(bf16)

    def copy(self, hop):
        return pltpu.make_async_remote_copy(
            src_ref=self.staged.at[hop - 1], dst_ref=self.got_ref.at[self.spot], send_sem=self.send_sem.at[hop - 1],
            recv_sem=self.recv_sem.at[hop - 1], device_id={"exp": lax.rem(self.spot + hop, self.devices)},
            device_id_type=MESH,
        )

    def start(self):
        for hop in self.hops:
            self.staged[hop - 1] = self.packed(lax.rem(self.spot + hop, self.devices))
            self.copy(hop).start()
        self.got_ref[self.spot] = self.packed(self.spot)

    def wait(self):
        for hop in self.hops:
            self.copy(hop).wait()


def route_kernel(
    mixed_ref, wout_ref, token_ref, gain_ref, router_ref, route_ref, target_ref, hidden_ref, rows_ref, prob_ref, got_ref,
    staged, send_sem, recv_sem, *, devices, experts, tile,
):
    exp_barrier(lax.axis_index("exp"), devices)
    width = wout_ref.shape[1]

    @pl.loop(0, mixed_ref.shape[0] // tile)
    def _(i):
        at = pl.ds(pl.multiple_of(i * tile, tile), tile)
        hidden = token_ref[at, :].astype(f32) + jnp.dot(mixed_ref[at, :], wout_ref[...], preferred_element_type=f32)
        hidden_ref[at, :] = hidden
        scale = lax.rsqrt(jnp.mean(hidden * hidden, -1, keepdims=True) + epsilon)
        low = (hidden * scale * gain_ref[...]).astype(bf16)
        rows_ref[at, :width] = low
        logits = jnp.dot(low, router_ref[...], preferred_element_type=f32)
        lane = lax.broadcasted_iota(jnp.int32, logits.shape, 1)
        logits = jnp.where(lane < experts, logits, -1e30)
        raised = jnp.exp(logits - jnp.max(logits, -1, keepdims=True))
        prob = raised / jnp.sum(raised, -1, keepdims=True)
        prob_ref[at, :] = prob
        gate = jnp.sum(jnp.where(lane == route_ref[at, :], prob, 0.0), -1, keepdims=True)
        rows_ref[at, width:] = in_parts(gate)

    moved = Dispatch(rows_ref, target_ref, got_ref, staged, send_sem, recv_sem, devices)
    moved.start()
    moved.wait()


def routed(mixed_low, w_out, token_low, gain, router_wide, route_col, target, capacity, devices, experts):
    vm = pl.BlockSpec(memory_space=pltpu.VMEM)
    dma = pltpu.SemaphoreType.DMA
    rows, width = token_low.shape
    return pl.pallas_call(
        functools.partial(route_kernel, devices=devices, experts=experts, tile=256),
        in_specs=[vm] * 7,
        out_specs=[vm] * 4,
        out_shape=[
            shape_of((rows, width), f32), shape_of((rows, width + LANES), bf16), shape_of((rows, LANES), f32),
            shape_of((devices, capacity, width + LANES), bf16),
        ],
        scratch_shapes=[pltpu.VMEM((devices - 1, capacity, width + LANES), bf16), dma((devices - 1,)), dma((devices - 1,))],
        compiler_params=pltpu.CompilerParams(collective_id=3, has_side_effects=True, vmem_limit_bytes=vmem_cap),
        name="routed",
    )(mixed_low, w_out, token_low, gain, router_wide, route_col, target[None, :])


def collect_kernel(
    sent_ref, target_ref, route_ref, rows_ref, prob_ref, hidden_ref, cot_ref, gain_ref, router_ref,
    hidden_grad_ref, branch_ref, gain_grad_ref, router_grad_ref, got, total, send_sem, recv_sem, *, devices, hops, tile,
):
    spot = lax.axis_index("exp")
    capacity = got.shape[1]
    count, width = hidden_ref.shape
    exp_barrier(spot, devices)
    copies = []
    for hop in hops:
        peer = lax.rem(spot + hop, devices)
        c = pltpu.make_async_remote_copy(
            src_ref=sent_ref.at[peer], dst_ref=got.at[devices - hop - 1], send_sem=send_sem.at[hop - 1],
            recv_sem=recv_sem.at[hop - 1], device_id={"exp": peer}, device_id_type=MESH,
        )
        c.start()
        copies.append(c)

    def spread_back(k, rows):
        slot = lax.broadcasted_iota(jnp.int32, (count, capacity), 1) + k * capacity
        pick = jnp.where(slot == target_ref[...], 1.0, 0.0).astype(bf16)
        return jnp.dot(pick, rows, preferred_element_type=f32)

    total[...] = spread_back(spot, sent_ref[spot])
    for hop, c in zip(hops, copies):
        c.wait_recv()
        total[...] += spread_back(lax.rem(spot + devices - hop, devices), got[devices - hop - 1])
    gain_grad_ref[...] = jnp.zeros_like(gain_grad_ref)
    router_grad_ref[...] = jnp.zeros_like(router_grad_ref)

    @pl.loop(0, count // tile)
    def _(i):
        at = pl.ds(pl.multiple_of(i * tile, tile), tile)
        parts = total[at, width:]
        gate_grad = parts[:, 0:1] + parts[:, 1:2] + parts[:, 2:3]
        prob = prob_ref[at, :]
        chosen = jnp.where(lax.broadcasted_iota(jnp.int32, prob.shape, 1) == route_ref[at, :], 1.0, 0.0)
        gate = jnp.sum(prob * chosen, -1, keepdims=True)
        logit_grad = prob * (chosen - gate) * gate_grad
        router_grad_ref[...] += lax.dot_general(
            logit_grad, rows_ref[at, :width].astype(f32), (((0,), (0,)), ((), ())), precision=highest,
            preferred_element_type=f32,
        )
        grad = total[at, :width] + jnp.dot(
            logit_grad, router_ref[...], precision=highest, preferred_element_type=f32
        )
        hidden = hidden_ref[at, :]
        scale = lax.rsqrt(jnp.mean(hidden * hidden, -1, keepdims=True) + epsilon)
        unit = hidden * scale
        gain_grad_ref[...] += jnp.sum(grad * unit, 0, keepdims=True)
        scaled = grad * gain_ref[...]
        hidden_grad = cot_ref[at, :].astype(f32) + scale * (
            scaled - unit * jnp.mean(scaled * unit, -1, keepdims=True)
        )
        hidden_grad_ref[at, :] = hidden_grad
        branch_ref[at, :] = hidden_grad.astype(bf16)

    for c in copies:
        c.wait_send()


def collect(blocks, target, route_col, rows, prob, hidden, cot, gain, router_t, devices):
    vm = pl.BlockSpec(memory_space=pltpu.VMEM)
    dma = pltpu.SemaphoreType.DMA
    capacity, wide = blocks.shape[1:]
    count, width = hidden.shape
    return pl.pallas_call(
        functools.partial(collect_kernel, devices=devices, hops=(2, 3, 1), tile=256),
        in_specs=[vm] * 9,
        out_specs=[vm] * 4,
        out_shape=[
            shape_of((count, width), f32), shape_of((count, width), bf16), shape_of((1, width), f32),
            shape_of((LANES, width), f32),
        ],
        scratch_shapes=[
            pltpu.VMEM((devices - 1, capacity, wide), bf16), pltpu.VMEM((count, wide), f32), dma((devices - 1,)),
            dma((devices - 1,)),
        ],
        compiler_params=pltpu.CompilerParams(collective_id=4, has_side_effects=True, vmem_limit_bytes=vmem_cap),
        name="collect",
    )(blocks, target[:, None], route_col, rows, prob, hidden, cot, gain, router_t)

SEGMENTS = 4
STARTS = (-4, 0, 1, 2)


def ring_order(place, peers):
    odd = lax.rem(place, 2)
    half = lax.div(place, 2)
    return half + odd * (peers - 1 - 2 * half)


def ring_member(position, peers):
    back = lax.div(2 * position, peers)
    return 2 * position + back * (2 * (peers - 1) + 1 - 4 * position)


class Rings:
    def __init__(self, own, total, sent, landed, send, recv, bases, sizes, peers):
        place = lax.axis_index("seq")
        self.own, self.total, self.sent, self.landed, self.send, self.recv = own, total, sent, landed, send, recv
        self.bases, self.sizes, self.peers = bases, sizes, peers
        self.position = ring_order(place, peers)
        self.after = ring_member(lax.rem(self.position + 1, peers), peers)
        self.before = ring_member(lax.rem(self.position + peers - 1, peers), peers)

    def rows(self, ring, steps):
        sign = 1 if ring % 2 == 0 else -1
        chunk = self.sizes[ring] // self.peers
        c = lax.rem(self.position + sign * steps + 2 * self.peers, self.peers)
        return pl.ds(pl.multiple_of(self.bases[ring] + c * chunk, 16), chunk)

    def target(self, ring):
        return {"seq": self.after if ring % 2 == 0 else self.before}

    def first(self, ring, s):
        chunk = self.sizes[ring] // self.peers
        return pltpu.make_async_remote_copy(
            src_ref=self.sent.at[ring, s, pl.ds(0, chunk)], dst_ref=self.landed.at[ring, s, pl.ds(0, chunk)],
            send_sem=self.send.at[ring, s], recv_sem=self.recv.at[ring, s], device_id=self.target(ring),
            device_id_type=MESH,
        )

    def second(self, ring, s):
        part = self.total.at[self.rows(ring, 1 - s)]
        at = self.peers - 1 + s
        return pltpu.make_async_remote_copy(
            src_ref=part, dst_ref=part, send_sem=self.send.at[ring, at], recv_sem=self.recv.at[ring, at],
            device_id=self.target(ring), device_id_type=MESH,
        )

    def begin(self, ring):
        chunk = self.sizes[ring] // self.peers
        self.sent[ring, 0, pl.ds(0, chunk)] = self.own[self.rows(ring, 0), :].astype(bf16)
        self.first(ring, 0).start()

    def advance(self, ring, s):
        peers, chunk = self.peers, self.sizes[ring] // self.peers

        @pl.when(jnp.logical_and(s >= 1, s <= peers - 2))
        def _():
            self.first(ring, s - 1).wait_recv()
            summed = self.landed[ring, s - 1, pl.ds(0, chunk)].astype(f32) + self.own[self.rows(ring, -s), :]
            self.sent[ring, s, pl.ds(0, chunk)] = summed.astype(bf16)
            self.first(ring, s).start()

        @pl.when(s == peers - 1)
        def _():
            self.first(ring, peers - 2).wait_recv()
            summed = self.landed[ring, peers - 2, pl.ds(0, chunk)].astype(f32) + self.own[self.rows(ring, 1), :]
            self.total[self.rows(ring, 1), :] = summed.astype(bf16)
            self.second(ring, 0).start()

        @pl.when(jnp.logical_and(s >= peers, s <= 2 * peers - 3))
        def _():
            self.second(ring, s - peers).wait_recv()
            self.second(ring, s - peers + 1).start()

        @pl.when(s == 2 * peers - 2)
        def _():
            self.second(ring, peers - 2).wait_recv()

    def drain(self):
        @pl.loop(0, self.peers - 1)
        def _(s):
            for ring in range(len(self.sizes)):
                self.first(ring, s).wait_send()
                self.second(ring, s).wait_send()


def finish_kernel(
    proj_ref, normed_ref, win_ref, outo_ref, small_ref, gain_ref, token_ref, hiddeng_ref, hidden_ref, rows_ref, target_ref,
    tok_ref,
    in_sum_ref, out_sum_ref, small_sum_ref, tokens_grad_ref, block_ref,
    own, total, near_stage, small_all, gain_part, near_in, near_small, far_in, far_small, pass_in, pass_small, sent, landed, near_send, near_recv, far_send, far_recv, ring_send, ring_recv,
    *, peers, bases, sizes, halo, tile, gain_row,
):
    spot = lax.axis_index("exp")
    width, wide = near_in.shape[1:]
    rows_out = outo_ref.shape[0]
    rows_small, share = near_small.shape[1:]
    folds = wide // share
    count = proj_ref.shape[0]
    third = width // 3
    near = spot + 1 - 2 * lax.rem(spot, 2)
    far = lax.rem(spot + 2, 4)
    across = lax.rem(near + 2, 4)
    rings = Rings(own, total, sent, landed, ring_send, ring_recv, bases, sizes, peers)
    barrier = pltpu.get_barrier_semaphore()
    for device in ({"exp": near}, {"exp": far}, {"seq": rings.after}, {"seq": rings.before}):
        pl.semaphore_signal(barrier, inc=1, device_id=device, device_id_type=MESH)
    pl.semaphore_wait(barrier, 4)

    def columns(k, size):
        return pl.ds(pl.multiple_of(k * size, size), size)

    def copy(source, target, send, recv, device):
        return pltpu.make_async_remote_copy(
            src_ref=source, dst_ref=target, send_sem=send, recv_sem=recv, device_id=device, device_id_type=MESH
        )

    def in_rows(i):
        return slice(i * third, (i + 1) * third)

    def near_copy(slot, piece):
        k = across if slot else near
        if piece == 4:
            source, target = small_all.at[:, columns(k, share)], near_small.at[slot]
        else:
            at = pl.ds((piece - 1) * third, third)
            source, target = near_stage.at[slot, at], near_in.at[slot, at]
        return copy(source, target, near_send.at[slot, piece], near_recv.at[slot, piece], {"exp": near})

    def far_copy(piece):
        if piece == 4:
            source, target = pass_small, far_small
        else:
            at = pl.ds((piece - 1) * third, third)
            source, target = pass_in.at[at], far_in.at[at]
        return copy(source, target, far_send.at[piece], far_recv.at[piece], {"exp": far})

    def in_tile(i, k):
        part = lax.dot_general(
            normed_ref[pl.ds(halo, count), in_rows(i)], proj_ref[:, columns(k, wide)], (((0,), (0,)), ((), ())),
            preferred_element_type=f32,
        )
        scaled = part * win_ref[in_rows(i), columns(k, wide)].astype(f32)
        gain_part[in_rows(i), :] += tree_sum(scaled[:, h * LANES : (h + 1) * LANES] for h in range(wide // LANES))
        return part

    def into_own(base, values, add):
        size = values.shape[0]
        for h in range(values.shape[1] // share):
            at = slice(base + h * size, base + (h + 1) * size)
            part = values[:, h * share : (h + 1) * share]
            if add:
                own[at, :] += part
            else:
                own[at, :] = part

    def pad_own(n, used):
        if used < sizes[n]:
            own[bases[n] + used : bases[n] + sizes[n], :] = jnp.zeros((sizes[n] - used, share), f32)

    small_base = bases[3] + folds * third
    into_own(bases[0], outo_ref[...].astype(f32), False)
    pad_own(0, folds * rows_out)
    rings.begin(0)
    gain_part[...] = jnp.zeros_like(gain_part)
    small_all[...] = small_ref[...]
    for i in range(3):
        for slot, k in ((1, across), (0, near)):
            near_stage[slot, in_rows(i), :] = in_tile(i, k).astype(bf16)
            near_copy(slot, 1 + i).start()
        distant = in_tile(i, far)
        near_copy(1, 1 + i).wait_recv()
        pass_in[in_rows(i), :] = (distant + near_in[1, in_rows(i), :].astype(f32)).astype(bf16)
        far_copy(1 + i).start()
        mine = in_tile(i, spot)
        near_copy(0, 1 + i).wait_recv()
        into_own(bases[1 + i], mine + near_in[0, in_rows(i), :].astype(f32), False)
        pad_own(1 + i, folds * third)
        rings.advance(0, jnp.int32(1 + i))
    quarter = width // 4
    for k in range(4):
        part = jnp.sum(gain_part[k * quarter : (k + 1) * quarter, :], -1, keepdims=True)
        eye = lax.broadcasted_iota(jnp.int32, (quarter, quarter), 0) == lax.broadcasted_iota(
            jnp.int32, (quarter, quarter), 1
        )
        row = jnp.sum(jnp.where(eye, part, 0.0), 0, keepdims=True) / gain_ref[:, k * quarter : (k + 1) * quarter]
        group = slice(gain_row, gain_row + 16)
        old = small_all[group, k * share : k * share + quarter].astype(f32)
        top = lax.broadcasted_iota(jnp.int32, old.shape, 0) == 0
        small_all[group, k * share : k * share + quarter] = jnp.where(top, row, old).astype(bf16)
    for slot in (1, 0):
        near_copy(slot, 4).start()
    near_copy(1, 4).wait_recv()
    pass_small[...] = (small_all[:, columns(far, share)].astype(f32) + near_small[1].astype(f32)).astype(bf16)
    far_copy(4).start()
    near_copy(0, 4).wait_recv()
    own[small_base : small_base + rows_small, :] = (
        small_all[:, columns(spot, share)].astype(f32) + near_small[0].astype(f32)
    )
    def arrived(ring):
        far_copy(ring).wait_recv()
        into_own(bases[ring], far_in[in_rows(ring - 1), :].astype(f32), True)
        if ring == SEGMENTS - 1:
            far_copy(4).wait_recv()
            own[small_base : small_base + rows_small, :] += far_small[...].astype(f32)
        rings.begin(ring)

    def place_rows(out_ref, values, i):
        group = out_ref.shape[0]
        steps = tile // group
        values = jnp.swapaxes(values.reshape(steps, group, width), 0, 1)
        out_ref[:, pl.ds(pl.multiple_of(i * steps, steps), steps), :] = values.astype(out_ref.dtype)

    def token_tile(i):
        at = pl.ds(pl.multiple_of(i * tile, tile), tile)
        grad = lax.dot_general(proj_ref[at, :], win_ref[...], (((1,), (1,)), ((), ())), preferred_element_type=f32)
        values = token_ref[at, :].astype(f32)
        scale = lax.rsqrt(jnp.mean(values * values, -1, keepdims=True) + epsilon)
        unit = values * scale
        scaled = grad * gain_ref[...]
        total_grad = hiddeng_ref[at, :] + scale * (scaled - unit * jnp.mean(scaled * unit, -1, keepdims=True))
        place_rows(tokens_grad_ref, total_grad, i)

    def block_tile(i):
        at = pl.ds(pl.multiple_of(i * tile, tile), tile)
        capacity = tok_ref.shape[1]
        parts = rows_ref[at, width:].astype(f32)
        gate = parts[:, 0:1] + parts[:, 1:2] + parts[:, 2:3]
        tok = jnp.zeros((tile, width), f32)
        for k in range(tok_ref.shape[0]):
            slot = lax.broadcasted_iota(jnp.int32, (tile, capacity), 1) + k * capacity
            pick = jnp.where(slot == target_ref[at, :], 1.0, 0.0).astype(bf16)
            tok = tok + jnp.dot(pick, tok_ref[k], preferred_element_type=f32)
        place_rows(block_ref, hidden_ref[at, :] + gate * tok, i)

    tiles = count // tile

    @pl.loop(0, 2 * peers - 1 + STARTS[-1])
    def _(turn):
        for ring in range(SEGMENTS):
            step = turn - STARTS[ring]
            if ring:

                @pl.when(step == 0)
                def _():
                    arrived(ring)

            rings.advance(ring, step)

        @pl.when(turn < tiles)
        def _():
            token_tile(turn)

        @pl.when(jnp.logical_and(turn >= tiles, turn < 2 * tiles))
        def _():
            block_tile(turn - tiles)

    for i in range(3):
        for h in range(folds):
            at = slice(bases[1 + i] + h * third, bases[1 + i] + (h + 1) * third)
            in_sum_ref[in_rows(i), h * share : (h + 1) * share] = total[at, :].astype(f32)
    for h in range(folds):
        at = slice(bases[0] + h * rows_out, bases[0] + (h + 1) * rows_out)
        out_sum_ref[:, h * share : (h + 1) * share] = total[at, :].astype(f32)
    small_sum_ref[...] = total[small_base : small_base + rows_small, :].astype(f32)
    for piece in range(1, 5):
        for slot in (1, 0):
            near_copy(slot, piece).wait_send()
        far_copy(piece).wait_send()
    rings.drain()


def finish(proj, normed_ext, w_in, out_own, small, gain, token_low, hidden_grad, hidden_one, moe_rows, target, tok, gain_row, group):
    peers, devices = lax.axis_size("seq"), lax.axis_size("exp")
    count, width = token_low.shape
    wide, rows_out = proj.shape[1] // devices, out_own.shape[0]
    rows_small, share = small.shape[0], small.shape[1] // devices
    folds, third, unit = wide // share, width // 3, 16 * peers
    used = (folds * rows_out, folds * third, folds * third, folds * third + rows_small)
    sizes = tuple(-(-u // unit) * unit for u in used)
    bases = tuple(sum(sizes[:i]) for i in range(SEGMENTS))
    length, chunk = sum(sizes), max(sizes) // peers
    vm = pl.BlockSpec(memory_space=pltpu.VMEM)
    dma = pltpu.SemaphoreType.DMA
    shapes = ((width, wide), (rows_small, share))
    return pl.pallas_call(
        functools.partial(
            finish_kernel, peers=peers, bases=bases, sizes=sizes, halo=normed_ext.shape[0] - count, tile=256,
            gain_row=gain_row,
        ),
        in_specs=[vm] * 12,
        out_specs=[vm] * 5,
        out_shape=[
            shape_of((width, wide), f32), shape_of((rows_out, wide), f32), shape_of((rows_small, share), f32),
            shape_of((group, count // group, width), f32), shape_of((group, count // group, width), bf16),
        ],
        scratch_shapes=[
            pltpu.VMEM((length, share), f32), pltpu.VMEM((length, share), bf16), pltpu.VMEM((2, width, wide), bf16),
            pltpu.VMEM(small.shape, bf16), pltpu.VMEM((width, LANES), f32),
        ]
        + [pltpu.VMEM((2,) + s, bf16) for s in shapes]
        + [pltpu.VMEM(s, bf16) for s in shapes]
        + [pltpu.VMEM(s, bf16) for s in shapes]
        + [pltpu.VMEM((SEGMENTS, peers - 1, chunk, share), bf16)] * 2
        + [dma((2, 5)), dma((2, 5)), dma((5,)), dma((5,)), dma((SEGMENTS, 2 * peers - 2)), dma((SEGMENTS, 2 * peers - 2))],
        compiler_params=pltpu.CompilerParams(collective_id=2, has_side_effects=True, vmem_limit_bytes=64 << 20),
        name="finish",
    )(
        proj, normed_ext, w_in, out_own, small, gain, token_low, hidden_grad, hidden_one, moe_rows, target[:, None], tok
    )

PIECES = 2


def gather_kernel(
    in_ref, small_ref, token_ref, cot_ref, ids_ref, win_ref, wsmall_ref, before_ref, before_ids, rows_ref, cot_rows_ref, edge_ref,
    near_sems, far_sems, pair_sems, edge_sems, own_sem, *, kernel_len,
):
    place, peers = lax.axis_index("seq"), lax.axis_size("seq")
    spot = lax.axis_index("exp")
    near = spot + 1 - 2 * lax.rem(spot, 2)
    far = lax.rem(spot + 2, 4)
    bit = lax.rem(place, 2)
    pair = place + 1 - 2 * bit
    width, wide = in_ref.shape
    share = small_ref.shape[1]
    chunk = width // 2 // PIECES
    has_before, has_after = place > 0, place < peers - 1
    barrier = pltpu.get_barrier_semaphore()
    for target in ({"exp": near}, {"exp": far}, {"seq": pair}):
        pl.semaphore_signal(barrier, inc=1, device_id=target, device_id_type=MESH)

    @pl.when(has_before)
    def _():
        pl.semaphore_signal(barrier, inc=1, device_id={"seq": place - 1}, device_id_type=MESH)

    @pl.when(has_after)
    def _():
        pl.semaphore_signal(barrier, inc=1, device_id={"seq": place + 1}, device_id_type=MESH)

    pl.semaphore_wait(barrier, 3 + has_before.astype(jnp.int32) + has_after.astype(jnp.int32))

    def columns(ref, k, size):
        return ref.at[:, pl.ds(pl.multiple_of(k * size, size), size)]

    def rows(k, half, piece):
        at = pl.multiple_of((half * PIECES + piece) * chunk, chunk)
        return win_ref.at[pl.ds(at, chunk), pl.ds(pl.multiple_of(k * wide, wide), wide)]

    def copy(source, target, sems, slot, device):
        return pltpu.make_async_remote_copy(
            src_ref=source, dst_ref=target, send_sem=sems.at[0, slot], recv_sem=sems.at[1, slot], device_id=device,
            device_id_type=MESH,
        )

    def edge_copies():
        return (
            copy(edge_ref, before_ref, edge_sems, 0, {"seq": place + 1}),
            copy(ids_ref, before_ids, edge_sems, 1, {"seq": place + 1}),
        )

    outward = []
    for piece in range(PIECES):
        at = pl.multiple_of((bit * PIECES + piece) * chunk, chunk)
        outward.append(copy(in_ref.at[pl.ds(at, chunk), :], rows(spot, bit, piece), far_sems, piece, {"exp": far}))
    outward.insert(0, copy(small_ref, columns(wsmall_ref, spot, share), far_sems, PIECES, {"exp": far}))
    for c in outward:
        c.start()
    beside = [
        copy(small_ref, columns(wsmall_ref, spot, share), near_sems, 0, {"exp": near}),
        copy(in_ref, columns(win_ref, spot, wide), near_sems, 1, {"exp": near}),
    ]
    for c in beside:
        c.start()
    group, part_len, features = token_ref.shape

    def by_place(source, start, steps):
        values = source[:, pl.ds(start, steps), :].astype(f32)
        return jnp.swapaxes(values, 0, 1).reshape(steps * group, features).astype(bf16)

    edge_ref[...] = by_place(token_ref, part_len - 8, 8)[(8 - kernel_len) * group :, :]

    @pl.when(has_after)
    def _():
        for c in edge_copies():
            c.start()

    @pl.when(jnp.logical_not(has_before))
    def _():
        before_ref[...] = jnp.zeros_like(before_ref)
        before_ids[...] = jnp.zeros_like(before_ids)

    own = [
        pltpu.make_async_copy(in_ref, columns(win_ref, spot, wide), own_sem.at[0]),
        pltpu.make_async_copy(small_ref, columns(wsmall_ref, spot, share), own_sem.at[1]),
    ]
    for c in own:
        c.start()
    tile = 16

    @pl.loop(0, part_len // tile)
    def _(i):
        start = pl.multiple_of(i * tile, tile)
        at = pl.ds(pl.multiple_of(i * tile * group, tile * group), tile * group)
        rows_ref[at, :] = by_place(token_ref, start, tile)
        cot_rows_ref[at, :] = by_place(cot_ref, start, tile)

    outward[0].wait_recv()
    beside.append(copy(columns(wsmall_ref, far, share), columns(wsmall_ref, far, share), near_sems, 2, {"exp": near}))
    beside[-1].start()
    crossing = []
    for piece in range(PIECES):
        outward[1 + piece].wait_recv()
        part = rows(far, bit, piece)
        crossing.append(copy(part, part, pair_sems, piece, {"seq": pair}))
        crossing[-1].start()
        beside.append(copy(part, part, near_sems, 3 + piece, {"exp": near}))
        beside[-1].start()
    for piece in range(PIECES):
        crossing[piece].wait_recv()
        part = rows(far, 1 - bit, piece)
        beside.append(copy(part, part, near_sems, 3 + PIECES + piece, {"exp": near}))
        beside[-1].start()
    for c in beside:
        c.wait_recv()
    for c in outward + beside + crossing:
        c.wait_send()
    for c in own:
        c.wait()

    @pl.when(has_before)
    def _():
        for c in edge_copies():
            c.wait_recv()

    @pl.when(has_after)
    def _():
        for c in edge_copies():
            c.wait_send()


def gather_weights(in_shard, small, tokens, cot, ids, kernel_len, devices):
    group, part_len, width = tokens.shape
    edge = shape_of((kernel_len * group, width), bf16)
    rows = shape_of((part_len * group, width), bf16)
    vm = pl.BlockSpec(memory_space=pltpu.VMEM)
    dma = pltpu.SemaphoreType.DMA
    return pl.pallas_call(
        functools.partial(gather_kernel, kernel_len=kernel_len),
        in_specs=[pl.BlockSpec(memory_space=pl.ANY), vm, vm, vm, vm],
        out_specs=[pl.BlockSpec(memory_space=pl.ANY), vm, vm, vm, vm, vm],
        out_shape=[
            shape_of((in_shard.shape[0], in_shard.shape[1] * devices), bf16),
            shape_of((small.shape[0], small.shape[1] * devices), bf16), shape_of(edge.shape, edge.dtype),
            shape_of(ids.shape, ids.dtype), rows, rows,
        ],
        scratch_shapes=[pltpu.VMEM(edge.shape, bf16), dma((2, 3 + 2 * PIECES)), dma((2, PIECES + 1)), dma((2, PIECES)), dma((2, 2)), dma((2,))],
        compiler_params=pltpu.CompilerParams(collective_id=5, has_side_effects=True, vmem_limit_bytes=32 << 20),
        name="gather_weights",
    )(in_shard, small, tokens, cot, ids)

def rms_norm(values, gain):
    return values * lax.rsqrt(jnp.mean(values * values, -1, keepdims=True) + epsilon) * gain


def passed_along(value, axis, steps):
    count = lax.axis_size(axis)
    initial, last = (max(0, -steps), min(count, count - steps))
    return lax.ppermute(value, axis, [(source, source + steps) for source in range(initial, last)])


def by_time(values):
    values = jnp.swapaxes(values, 0, 1)
    return values.reshape((values.shape[0] * values.shape[1],) + values.shape[2:])


def packed_small(norm_gain, conv_weight, conv_bias, x_proj, dt_proj, dt_bias, a_log, d_skip, moe_gain, router):
    share = conv_bias.shape[0]
    packed = [conv_weight, conv_bias[None], x_proj.T, dt_proj, dt_bias[None], a_log.T, d_skip[None]]
    narrow = jnp.concatenate([norm_gain[None], moe_gain[None], router.T], 0)
    total = jnp.concatenate(packed + [narrow.reshape(-1, share)], 0)
    return jnp.pad(total, ((0, -total.shape[0] % 16), (0, 0))), [p.shape[0] for p in packed], narrow.shape


def unpacked_small(whole, counts, narrow_shape, devices):
    out, at = [], 0
    for c in counts:
        out.append(whole[at : at + c])
        at += c
    share = whole.shape[1] // devices
    fold = narrow_shape[0] * narrow_shape[1] // share
    rest = whole[at : at + fold].reshape(fold, devices, share).transpose(1, 0, 2).reshape((devices,) + narrow_shape)
    rest = rest.transpose(1, 0, 2).reshape(narrow_shape[0], -1)
    return out, rest[0], rest[1], rest[2:].T


def local(
    tokens, segment_ids, routes, slot_index, norm_gain, in_proj, conv_weight, conv_bias, x_proj, dt_proj, dt_bias,
    a_log, d_skip, out_proj, moe_gain, router, expert_up, expert_down, cotangent,
):
    seq_count, part_len, width = tokens.shape
    row_count = seq_count * part_len
    group = seq_count
    kernel_len = conv_weight.shape[0]
    state_width = a_log.shape[1]
    rank_width = dt_proj.shape[0]
    halo = kernel_len * group
    devices = lax.axis_size("exp")
    doc_ids = segment_ids + 1
    edge_start = part_len - kernel_len
    edge_ids = jnp.pad(doc_ids[:, edge_start:], ((0, 0), (0, LANES - kernel_len)))
    small_shard, counts, narrow_shape = packed_small(
        norm_gain, conv_weight, conv_bias, x_proj, dt_proj, dt_bias, a_log, d_skip, moe_gain, router
    )
    w_in, small_whole, before_rows, before_ids, token_low, cot_rows = gather_weights(
        in_proj, small_shard, tokens, cotangent, edge_ids, kernel_len, devices
    )
    out_proj, small_whole = lax.optimization_barrier((out_proj, small_whole))
    w_out = lax.all_gather(out_proj, "exp", axis=0, tiled=True)
    (w_conv, b_conv, w_x_t, w_dt, b_dt, log_decay, skip_gain), gain_one, gain_two, w_router = unpacked_small(
        small_whole, counts, narrow_shape, devices
    )
    inner_width = w_out.shape[0]
    expert_total = w_router.shape[1]
    capacity = 5 * row_count // (4 * expert_total)
    blocks = inner_width // LANES

    ext_ids = jnp.concatenate([before_ids[:, :kernel_len], doc_ids], 1)
    match = jnp.stack([ext_ids[:, 1 + k : 1 + k + part_len] == doc_ids for k in range(kernel_len - 1)])
    match = jnp.transpose(match, (2, 1, 0)).reshape(row_count, kernel_len - 1).astype(f32)
    lanes = 2 * LANES
    gain_one = gain_one.astype(f32)[None]
    gain_two = gain_two.astype(f32)[None]
    route_rows = by_time(routes)
    slot_rows = by_time(slot_index)
    target = jnp.where(
        slot_rows < capacity, route_rows * capacity + slot_rows, expert_total * capacity
    )
    w_conv, b_conv = w_conv.astype(f32), b_conv.astype(f32)
    w_x = w_x_t.T
    ci, conv_low, gate, rate_low, bc, normed_ext = front(
        token_low, before_rows, gain_one, w_in, w_conv, b_conv, match, w_x, rank_width, halo, group, lanes
    )
    bias = b_dt.astype(f32)
    skip = skip_gain.astype(f32)
    a_mat = -jnp.exp(log_decay.astype(f32))
    a2 = a_mat * log2e
    a_blocks = a2.reshape(state_width, blocks, LANES).transpose(1, 0, 2)
    step, z, mixed_low, start, total, cot_recv = forward_scan(
        rate_low, w_dt, bias, conv_low, bc, match, a_blocks, gate, skip, cot_rows, target, capacity, group, devices
    )
    route_col = route_rows[:, None]
    router_wide = jnp.pad(w_router, ((0, 0), (0, LANES - expert_total)))
    hidden_one, moe_rows, prob, received = routed(
        mixed_low, w_out, token_low, gain_two, router_wide, route_col, target, capacity, devices, expert_total
    )
    expert_out, rows_back, up_grad, down_grad = one_expert(
        received.reshape(devices * capacity, width + LANES), cot_recv.reshape(devices * capacity, width),
        expert_up[0], expert_down[0],
    )
    hidden_grad, branch_grad, gain_two_grad, router_grad_t = collect(
        rows_back.reshape(devices, capacity, width + LANES), target, route_col, moe_rows, prob, hidden_one, cot_rows,
        gain_two, router_wide.astype(f32).T, devices,
    )
    peers = lax.axis_size("seq")
    order = [list(range(0, peers, 2)) + list(range(peers - 1, 0, -2))]

    def scattered(values):
        return lax.psum_scatter(values, "seq", scatter_dimension=0, axis_index_groups=order, tiled=True)

    def regathered(part):
        return lax.all_gather(part, "seq", axis=0, axis_index_groups=order, tiled=True)

    down_part = scattered(down_grad)
    up_part = scattered(up_grad)
    out_proj_grad = jnp.dot(mixed_low.T, branch_grad, preferred_element_type=f32)
    mixed_grad = jnp.dot(branch_grad, w_out.T, preferred_element_type=f32)
    out_proj_grad = out_proj_grad.astype(bf16)
    down_part, mixed_grad, out_proj_grad = lax.optimization_barrier((down_part, mixed_grad, out_proj_grad))
    down_sum = regathered(down_part)
    proj, rate_pre_low, cg, small_one, mixed_proj_grad, tok, out_own = backward_scan(
        mixed_grad, gate, z, step, conv_low, bc, match, a_blocks, total, start, rate_low, w_dt, bias, skip,
        expert_out.reshape(devices, capacity, width), out_proj_grad, group, devices,
    )
    up_part, cg = lax.optimization_barrier((up_part, cg))
    up_sum = regathered(up_part)
    proj, ends, small_two = conv_back(
        cg, conv_low, mixed_proj_grad, w_x, ci, w_conv, b_conv, match, proj, halo, group, lanes
    )
    edge_back = passed_along(ends[:halo].astype(bf16), "seq", -1).astype(f32)
    proj = lax.dynamic_update_slice(proj, (ends[halo:] + edge_back).astype(bf16), (row_count - halo, 0))

    narrow = jnp.concatenate([jnp.zeros_like(gain_two_grad), gain_two_grad, router_grad_t[:expert_total]], 0)
    share, own_width = inner_width // devices, width // devices
    narrow = narrow.reshape(narrow.shape[0], devices, own_width)
    narrow = jnp.pad(narrow, ((0, -narrow.shape[0] % 16), (0, 0), (0, share - own_width))).astype(bf16)
    packed = jnp.concatenate([small_one, small_two, narrow.reshape(-1, inner_width)], 0)
    gain_row = small_one.shape[0] + small_two.shape[0]
    in_sum, out_sum, sums, tokens_grad, block_out = finish(
        proj, normed_ext, w_in, out_own, packed, gain_one, token_low, hidden_grad, hidden_one, moe_rows,
        target, tok, gain_row, group,
    )
    at, own = 0, []
    for first, rows in (
        (0, rank_width), (rank_width, state_width), (rank_width + state_width, 1), (rank_width + state_width + 1, 1)
    ):
        own.append(sums[first : first + rows])
    at = small_one.shape[0]
    mixed_width = mixed_proj_grad.shape[1]
    for first, rows in ((0, mixed_width), (mixed_width, kernel_len), (mixed_width + kernel_len, 1)):
        own.append(sums[at + first : at + first + rows])
    at += small_two.shape[0]
    own_narrow = sums[at : at + 2 + expert_total, :own_width]
    return (
        block_out,
        tokens_grad,
        own_narrow[0],
        in_sum,
        own[5],
        own[6][0],
        own[4].T,
        own[0],
        own[2][0],
        own[1].T,
        own[3][0],
        out_sum,
        own_narrow[1],
        own_narrow[2:].T,
        up_sum.astype(f32)[None],
        down_sum.astype(f32)[None],
    )


def solution(mesh):
    in_specs = (
        P("exp", "seq", None),
        P("exp", "seq"),
        P("exp", "seq"),
        P("exp", "seq"),
        P("exp"),
        P(None, "exp"),
        P(None, "exp"),
        P("exp"),
        P("exp", None),
        P(None, "exp"),
        P("exp"),
        P("exp", None),
        P("exp"),
        P("exp", None),
        P("exp"),
        P("exp", None),
        P("exp", None, None),
        P("exp", None, None),
        P("exp", "seq", None),
    )
    out_specs = (
        P("exp", "seq", None),
        P("exp", "seq", None),
        P("exp"),
        P(None, "exp"),
        P(None, "exp"),
        P("exp"),
        P("exp", None),
        P(None, "exp"),
        P("exp"),
        P("exp", None),
        P("exp"),
        P("exp", None),
        P("exp"),
        P("exp", None),
        P("exp", None, None),
        P("exp", None, None),
    )
    return jax.shard_map(local, mesh=mesh, in_specs=in_specs, out_specs=out_specs, check_vma=False)
```

```python
import functools

import jax
import jax.numpy as jnp
from jax import lax
from jax.experimental import pallas as pl
from jax.experimental.pallas import tpu as pltpu
from jax.sharding import PartitionSpec as P

f32, bf16 = jnp.float32, jnp.bfloat16
highest = lax.Precision.HIGHEST
LANES = 128
MESH = pl.DeviceIdType.MESH
epsilon = 1e-05
log2e = 1.4426950408889634
cut = 1e8
ln2 = 0.6931471805599453
vmem_cap = 58 << 20


def tree_sum(parts):
    parts = list(parts)
    while len(parts) > 1:
        paired = [parts[i] + parts[i + 1] for i in range(0, len(parts) - 1, 2)]
        parts = paired + parts[len(parts) - len(parts) % 2 :]
    return parts[0]


UN = dict(state=8, scan=8, adj=8, fwd=4, bwd=4)


def spread(rows_ref, pick_ref, outs, states, group):
    shape = pick_ref.shape
    row = lax.broadcasted_iota(jnp.int32, shape, 0)
    lane = lax.broadcasted_iota(jnp.int32, shape, 1)
    pick_ref[...] = jnp.where(lax.rem(row, 2 * states) == lax.div(lane, LANES), 1.0, 0.0).astype(bf16)
    steps = rows_ref.shape[0] // group
    chunk = 16
    wide = 2 * LANES

    @pl.loop(0, steps // chunk)
    def _(i):
        rows = rows_ref[pl.ds(pl.multiple_of(i * chunk * group, chunk * group), chunk * group), :]
        for which, out_ref in outs:
            for n in range(0, states, 2):
                at = (which * states + n) * LANES
                part = jnp.dot(rows, pick_ref[:, at : at + wide], preferred_element_type=f32)
                for k in range(2):
                    out_ref[pl.ds(i * chunk, chunk), n + k] = part[:, k * LANES : (k + 1) * LANES].reshape(
                        chunk, group, LANES
                    )


def softplus(v):
    return jnp.maximum(v, 0.0) + jnp.log1p(jnp.exp(-jnp.abs(v)))


class Carry:
    def __init__(self, step, ends, total, a_all, held, got, sent, send_sem, recv_sem):
        self.step, self.ends, self.total, self.a_all = step, ends, total, a_all
        self.held, self.got, self.sent, self.send_sem, self.recv_sem = held, got, sent, send_sem, recv_sem
        self.place, self.peers = lax.axis_index("seq"), lax.axis_size("seq")
        self.rank = self.place if step > 0 else self.peers - 1 - self.place
        self.count, self.states = ends.shape[0], ends.shape[1]
        self.has_before, self.has_after = self.rank > 0, self.rank < self.peers - 1
        self.lag = jnp.minimum(self.rank, self.count)

    def enter(self, devices=1):
        spot = lax.axis_index("exp")
        barrier = pltpu.get_barrier_semaphore()

        @pl.when(self.has_before)
        def _():
            pl.semaphore_signal(barrier, inc=1, device_id={"seq": self.place - self.step}, device_id_type=MESH)

        @pl.when(self.has_after)
        def _():
            pl.semaphore_signal(barrier, inc=1, device_id={"seq": self.place + self.step}, device_id_type=MESH)

        for hop in range(1, devices):
            pl.semaphore_signal(barrier, inc=1, device_id={"exp": lax.rem(spot + hop, devices)}, device_id_type=MESH)
        neighbours = self.has_before.astype(jnp.int32) + self.has_after.astype(jnp.int32)
        pl.semaphore_wait(barrier, neighbours + (devices - 1))

    def hop(self, u):
        return pltpu.make_async_remote_copy(
            src_ref=self.sent.at[u], dst_ref=self.got.at[u], send_sem=self.send_sem.at[u], recv_sem=self.recv_sem.at[u],
            device_id={"seq": self.place + self.step}, device_id_type=MESH,
        )

    def handle(self, at):
        u = at - self.lag

        @pl.when(jnp.logical_and(u >= 0, u < self.count))
        def _():
            @pl.when(self.has_before)
            def _():
                self.hop(u).wait_recv()
                self.held[u] = self.got[u].astype(f32)

            @pl.when(jnp.logical_not(self.has_before))
            def _():
                self.held[u] = jnp.zeros(self.held.shape[1:], f32)

            @pl.when(self.has_after)
            def _():
                for n in range(self.states):
                    decay = jnp.exp2(self.a_all[u, n : n + 1, :] * self.total[u])
                    self.sent[u, n] = (self.ends[u, n] + decay * self.held[u, n]).astype(bf16)
                self.hop(u).start()

    def leave(self):
        @pl.loop(0, self.count)
        def _(u):
            @pl.when(self.has_after)
            def _():
                self.hop(u).wait_send()


def forward_kernel(
    rate_ref, wdt_ref, bias_ref, conv_ref, bc_ref, match_ref, a_all, gate_ref, skip_ref, cot_ref, target_ref,
    step_ref, z_ref, mixed_ref, start_ref, total_ref, cot_out,
    cot_got, pick_ref, kb_ref, b_all, c_all, step_all, ends, staged, cot_send, cot_recv, got, sent, send_sem, recv_sem, *, states, group, devices,
):
    at = pl.program_id(0)
    count = a_all.shape[0]
    j = lax.rem(at, count)
    carry_of = Carry(1, ends, total_ref, a_all, start_ref, got, sent, send_sem, recv_sem)
    rows = conv_ref.shape[0]
    moved = Dispatch(cot_ref, target_ref, cot_got, staged, cot_send, cot_recv, devices)

    @pl.when(at == 0)
    def _():
        carry_of.enter(devices)
        moved.start()
        kb_ref[...] = broad_cut(match_ref)
        spread(bc_ref, pick_ref, ((0, b_all), (1, c_all)), states, group)

    @pl.when(at < count)
    def _():
        pre = jnp.dot(rate_ref[...], wdt_ref[...], preferred_element_type=f32) + bias_ref[...]
        step = softplus(pre)
        step_ref[...] = step
        step_all[j] = step
        a_rows = [jnp.broadcast_to(a_all[j, n : n + 1, :], (group, LANES)) for n in range(states)]
        un = UN["state"]

        def body(i, carry):
            total, state = carry
            base = pl.multiple_of(i * un * group, un * group)
            x_two = conv_ref[pl.ds(base, un * group), :].astype(f32)
            for k in range(un):
                here = pl.ds(pl.multiple_of(base + k * group, group), group)
                dt = step_ref[here, :]
                masked = dt + kb_ref[here, :]
                u = dt * x_two[k * group : (k + 1) * group]
                total = total + masked
                state = [
                    jnp.exp2(masked * a_rows[n]) * state[n] + u * b_all[un * i + k, n] for n in range(states)
                ]
            return total, state

        zero = jnp.zeros((group, LANES), f32)
        total, state = lax.fori_loop(0, rows // (un * group), body, (zero, [zero] * states))
        total_ref[j] = total
        for n in range(states):
            ends[j, n] = state[n]

    carry_of.handle(at)

    @pl.when(at >= count)
    def _():
        a_rows = [jnp.broadcast_to(a_all[j, n : n + 1, :], (group, LANES)) for n in range(states)]
        un = UN["scan"]

        def body(i, state):
            base = pl.multiple_of(i * un * group, un * group)
            x_two = conv_ref[pl.ds(base, un * group), :].astype(f32)
            outs = []
            for k in range(un):
                here = pl.ds(pl.multiple_of(base + k * group, group), group)
                dt = step_all[j, here, :]
                masked = dt + kb_ref[here, :]
                u = dt * x_two[k * group : (k + 1) * group]
                state = [
                    jnp.exp2(masked * a_rows[n]) * state[n] + u * b_all[un * i + k, n] for n in range(states)
                ]
                outs.append(tree_sum(state[n] * c_all[un * i + k, n] for n in range(states)))
            whole = pl.ds(base, un * group)
            gate = gate_ref[whole, :]
            z = jnp.concatenate(outs, 0) + skip_ref[...] * x_two
            z_ref[whole, :] = z
            mixed_ref[whole, :] = (z * (gate * jax.nn.sigmoid(gate))).astype(bf16)
            return state

        lax.fori_loop(0, rows // (un * group), body, [start_ref[j, n] for n in range(states)])

    @pl.when(at == 2 * count - 1)
    def _():
        carry_of.leave()
        moved.wait()
        cot_out[...] = cot_got[...]


def broad_cut(match_ref):
    keep = match_ref[:, match_ref.shape[1] - 1 :]
    return jnp.broadcast_to((1.0 - keep) * cut, (match_ref.shape[0], LANES))


def backward_kernel(
    mg_ref, gate_ref, z_ref, step_ref, conv_ref, bc_ref, match_ref, a_all, total_ref, start_ref, rate_ref, wdt_ref,
    bias_ref, skip_ref, back_ref, outg_ref,
    gg_ref, low_ref, cg_ref, small_ref, mpg_ref, tok_ref, outo_ref,
    near_got, passed, far_got, mine, out_send, out_recv, out_load, back_send, back_recv, back_own, pick_ref, kb_ref, b_all, c_all, b_acc, c_acc, kept, dt_grad, g_all, rate_acc, ends, last, got, sent, send_sem, recv_sem, *, states, group, devices,
):
    at = pl.program_id(0)
    count = a_all.shape[0]
    j = lax.rem(at, count)
    carry_of = Carry(-1, ends, total_ref, a_all, last, got, sent, send_sem, recv_sem)
    steps = conv_ref.shape[0] // group
    rank = rate_ref.shape[1]
    zero = jnp.zeros((group, LANES), f32)
    spot = lax.axis_index("exp")

    def back_copy(hop):
        peer = lax.rem(spot + hop, devices)
        return pltpu.make_async_remote_copy(
            src_ref=back_ref.at[peer], dst_ref=tok_ref.at[spot], send_sem=back_send.at[hop - 1],
            recv_sem=back_recv.at[hop - 1], device_id={"exp": peer}, device_id_type=MESH,
        )

    near = spot + 1 - 2 * lax.rem(spot, 2)
    far = lax.rem(spot + 2, 4)
    across = lax.rem(near + 2, 4)
    rows_out = mine.shape[0]

    def out_rows(k):
        return outg_ref.at[pl.ds(pl.multiple_of(k * rows_out, rows_out), rows_out), :]

    def out_move(slot):
        if slot == 2:
            source, target, device = passed, far_got, far
        else:
            source, target, device = out_rows(across if slot else near), near_got.at[slot], near
        return pltpu.make_async_remote_copy(
            src_ref=source, dst_ref=target, send_sem=out_send.at[slot], recv_sem=out_recv.at[slot],
            device_id={"exp": device}, device_id_type=MESH,
        )

    def out_loads():
        return (
            pltpu.make_async_copy(out_rows(far), passed, out_load.at[0]),
            pltpu.make_async_copy(out_rows(spot), mine, out_load.at[1]),
        )

    def out_store():
        return pltpu.make_async_copy(mine, outo_ref, out_load.at[2])

    def own_copy():
        return pltpu.make_async_copy(back_ref.at[spot], tok_ref.at[spot], back_own.at[0])

    @pl.when(at == 0)
    def _():
        carry_of.enter(devices)
        out_move(1).start()
        out_move(0).start()
        for c in out_loads():
            c.start()
        own_copy().start()
        for hop in range(1, devices):
            back_copy(hop).start()
        kb_ref[...] = broad_cut(match_ref)
        spread(bc_ref, pick_ref, ((0, b_all), (1, c_all)), states, group)
        rate_acc[...] = jnp.zeros_like(rate_acc)

        @pl.loop(0, steps)
        def _(t):
            none = jnp.zeros((states, group, LANES), f32)
            b_acc[t] = none
            c_acc[t] = none

    @pl.when(at == 1)
    def _():
        for c in out_loads():
            c.wait()
        out_move(1).wait_recv()
        passed[...] = (passed[...].astype(f32) + near_got[1].astype(f32)).astype(bf16)
        out_move(2).start()

    @pl.when(at == 2 * count - 1)
    def _():
        out_move(0).wait_recv()
        out_move(2).wait_recv()
        mine[...] = (mine[...].astype(f32) + near_got[0].astype(f32) + far_got[...].astype(f32)).astype(bf16)
        out_store().start()

    @pl.when(at < count)
    def _():
        a_rows = [jnp.broadcast_to(a_all[j, n : n + 1, :], (group, LANES)) for n in range(states)]
        un = UN["adj"]

        def body(i, q):
            base = pl.multiple_of((steps // un - 1 - i) * un * group, un * group)
            whole = pl.ds(base, un * group)
            mixed_grad, gate = mg_ref[whole, :], gate_ref[whole, :]
            sig = jax.nn.sigmoid(gate)
            g_rows = mixed_grad * (gate * sig)
            g_all[j, whole, :] = g_rows.astype(bf16)
            gg_ref[whole, :] = (mixed_grad * z_ref[whole, :] * (sig * (1.0 + gate * (1.0 - sig)))).astype(bf16)
            for k in reversed(range(un)):
                t = un * (steps // un - 1 - i) + k
                here = pl.ds(pl.multiple_of(base + k * group, group), group)
                masked = step_ref[here, :] + kb_ref[here, :]
                g = g_rows[k * group : (k + 1) * group]
                q = [jnp.exp2(masked * a_rows[n]) * (c_all[t, n] * g + q[n]) for n in range(states)]
            return q

        q = lax.fori_loop(0, steps // un, body, [zero] * states)
        for n in range(states):
            ends[j, n] = q[n]

    carry_of.handle(at)

    @pl.when(at >= count)
    def _():
        a_rows = [jnp.broadcast_to(a_all[j, n : n + 1, :], (group, LANES)) for n in range(states)]
        fu, bu = UN["fwd"], UN["bwd"]

        def forward(i, state):
            base = pl.multiple_of(i * fu * group, fu * group)
            x_two = conv_ref[pl.ds(base, fu * group), :].astype(f32)
            g_two = g_all[j, pl.ds(base, fu * group), :].astype(f32)
            for k in range(fu):
                t = fu * i + k
                here = pl.ds(pl.multiple_of(base + k * group, group), group)
                dt = step_ref[here, :]
                masked = dt + kb_ref[here, :]
                g = g_two[k * group : (k + 1) * group]
                u = dt * x_two[k * group : (k + 1) * group]
                for n in range(states):
                    kept[t, n] = state[n]
                state = [jnp.exp2(masked * a_rows[n]) * state[n] + u * b_all[t, n] for n in range(states)]
                for n in range(states):
                    c_acc[t, n] += state[n] * g
            return state

        lax.fori_loop(0, steps // fu, forward, [start_ref[0, n] for n in range(states)])
        skip = skip_ref[...]

        def backward(i, carry):
            q, a_sum, skip_sum = carry
            base = pl.multiple_of((steps // bu - 1 - i) * bu * group, bu * group)
            x_two = conv_ref[pl.ds(base, bu * group), :].astype(f32)
            g_two = g_all[j, pl.ds(base, bu * group), :].astype(f32)
            for k in reversed(range(bu)):
                t = bu * (steps // bu - 1 - i) + k
                here = pl.ds(pl.multiple_of(base + k * group, group), group)
                dt = step_ref[here, :]
                masked = dt + kb_ref[here, :]
                g = g_two[k * group : (k + 1) * group]
                x = x_two[k * group : (k + 1) * group]
                u = dt * x
                skip_sum = skip_sum + g * x
                lam = [c_all[t, n] * g + q[n] for n in range(states)]
                for n in range(states):
                    b_acc[t, n] += lam[n] * u
                s_one = tree_sum(lam[n] * b_all[t, n] for n in range(states))
                q = [jnp.exp2(masked * a_rows[n]) * lam[n] for n in range(states)]
                w = [q[n] * kept[t, n] for n in range(states)]
                s_two = tree_sum(w[n] * a_rows[n] for n in range(states))
                a_sum = [a_sum[n] + dt * w[n] for n in range(states)]
                cg_ref[here, :] = skip * g + dt * s_one
                dt_grad[here, :] = x * s_one + ln2 * s_two
            return q, a_sum, skip_sum

        q, a_sum, skip_sum = lax.fori_loop(
            0, steps // bu, backward, ([last[j, n] for n in range(states)], [zero] * states, zero)
        )
        pre = jnp.dot(rate_ref[...], wdt_ref[...], preferred_element_type=f32) + bias_ref[...]
        pre_grad = dt_grad[...] * jax.nn.sigmoid(pre)
        low = pre_grad.astype(bf16)
        low_ref[...] = low
        rate_acc[...] += lax.dot_general(low, wdt_ref[...], (((1,), (1,)), ((), ())), preferred_element_type=f32)
        rows_of = [lax.dot_general(rate_ref[...], low, (((0,), (0,)), ((), ())), preferred_element_type=f32)]
        rows_of += [jnp.sum(a_sum[n], 0, keepdims=True) * a_all[j, n : n + 1, :] * ln2 for n in range(states)]
        rows_of += [jnp.sum(pre_grad, 0, keepdims=True), jnp.sum(skip_sum, 0, keepdims=True)]
        spare = small_ref.shape[0] - rank - states - 2
        small_ref[...] = jnp.concatenate(rows_of + [jnp.zeros((spare, LANES), f32)], 0).astype(bf16)

    @pl.when(at == 2 * count - 1)
    def _():
        carry_of.leave()
        out_store().wait()
        for slot in range(3):
            out_move(slot).wait_send()
        own_copy().wait()
        for hop in range(1, devices):
            back_copy(hop).wait()
        mpg_ref[:, :rank] = rate_acc[...].astype(bf16)
        lane = lax.broadcasted_iota(jnp.int32, (2 * LANES, 2 * states), 1)
        own = lax.broadcasted_iota(jnp.int32, (2 * LANES, 2 * states), 0) // LANES * states
        total = jnp.zeros((steps * group, 2 * states), f32)
        for n in range(states):
            both = [acc[:, n].reshape(steps * group, LANES) for acc in (b_acc, c_acc)]
            rows = jnp.concatenate(both, 1)
            pick = jnp.where(lane == own + n, 1.0, 0.0).astype(bf16)
            high = rows.astype(bf16)
            rest = (rows - high.astype(f32)).astype(bf16)
            total = total + jnp.dot(high, pick, preferred_element_type=f32)
            total = total + jnp.dot(rest, pick, preferred_element_type=f32)
        mpg_ref[:, rank:] = total.astype(bf16)


def rows_block(rows):
    return pl.BlockSpec((rows, LANES), lambda j: (0, j))


def whole_block(shape):
    return pl.BlockSpec(shape, lambda j: (0,) * len(shape))


def state_block(states, group):
    return pl.BlockSpec((1, states, group, LANES), lambda j: (j, 0, 0, 0))


def shape_of(shape, dtype):
    return jax.ShapeDtypeStruct(shape, dtype)


def params():
    return pltpu.CompilerParams(vmem_limit_bytes=vmem_cap)


def carry_scratch(shape):
    return [
        pltpu.VMEM(shape, bf16), pltpu.VMEM(shape, bf16), pltpu.SemaphoreType.DMA((shape[0],)),
        pltpu.SemaphoreType.DMA((shape[0],)),
    ]


def forward_scan(rate_low, w_dt, bias, conv_low, bc, match, a_blocks, gate, skip, cot, target, capacity, group, devices):
    rows, inner = conv_low.shape
    count, states, _ = a_blocks.shape
    rank = rate_low.shape[1]
    first = lambda at: (0, jnp.minimum(at, count - 1))
    both = lambda at: (0, lax.rem(at, count))
    second = lambda at: (0, jnp.maximum(at - count, 0))
    shape = (count, states, group, LANES)
    big = pltpu.VMEM((rows // group, states, group, LANES), f32)
    return pl.pallas_call(
        functools.partial(forward_kernel, states=states, group=group, devices=devices),
        grid=(2 * count,),
        in_specs=[
            whole_block((rows, rank)), pl.BlockSpec((rank, LANES), first), pl.BlockSpec((1, LANES), first),
            pl.BlockSpec((rows, LANES), both), whole_block(bc.shape),
            whole_block(match.shape), whole_block(a_blocks.shape), pl.BlockSpec((rows, LANES), second),
            pl.BlockSpec((1, LANES), second), whole_block(cot.shape), whole_block((1, rows)),
        ],
        out_specs=[
            pl.BlockSpec((rows, LANES), first), pl.BlockSpec((rows, LANES), second), pl.BlockSpec((rows, LANES), second),
            whole_block(shape), whole_block((count, group, LANES)), whole_block((devices, capacity, cot.shape[1])),
        ],
        out_shape=[
            shape_of((rows, inner), f32), shape_of((rows, inner), f32), shape_of((rows, inner), bf16),
            shape_of(shape, f32), shape_of((count, group, LANES), f32), shape_of((devices, capacity, cot.shape[1]), bf16),
        ],
        scratch_shapes=[pltpu.VMEM((devices, capacity, cot.shape[1]), bf16), pltpu.VMEM((bc.shape[1], 2 * states * LANES), bf16)]
        + [pltpu.VMEM((rows, LANES), f32), big, big]
        + [pltpu.VMEM((count, rows, LANES), f32), pltpu.VMEM(shape, f32)]
        + [pltpu.VMEM((devices - 1, capacity, cot.shape[1]), bf16)]
        + [pltpu.SemaphoreType.DMA((devices - 1,)), pltpu.SemaphoreType.DMA((devices - 1,))] + carry_scratch(shape),
        compiler_params=pltpu.CompilerParams(collective_id=0, has_side_effects=True, vmem_limit_bytes=vmem_cap),
        name="forward_scan",
    )(rate_low, w_dt, bias, conv_low, bc, match, a_blocks, gate, skip, cot, target[None, :])


def backward_scan(mixed_grad, gate, z, step, conv_low, bc, match, a_blocks, total, start, rate_low, w_dt, bias, skip, back, out_grad, group, devices):
    rows, inner = conv_low.shape
    count, states, _ = a_blocks.shape
    rank = rate_low.shape[1]
    small_rows = -(-(rank + states + 2) // 16) * 16
    out_piece = (out_grad.shape[0] // devices, out_grad.shape[1])
    dma = pltpu.SemaphoreType.DMA
    first = lambda at: (0, jnp.minimum(at, count - 1))
    both = lambda at: (0, lax.rem(at, count))
    second = lambda at: (0, jnp.maximum(at - count, 0))
    shape = (count, states, group, LANES)
    big = pltpu.VMEM((rows // group, states, group, LANES), f32)
    return pl.pallas_call(
        functools.partial(backward_kernel, states=states, group=group, devices=devices),
        grid=(2 * count,),
        in_specs=[
            pl.BlockSpec((rows, LANES), first), pl.BlockSpec((rows, LANES), first), pl.BlockSpec((rows, LANES), first),
            pl.BlockSpec((rows, LANES), both), pl.BlockSpec((rows, LANES), second), whole_block(bc.shape),
            whole_block(match.shape), whole_block(a_blocks.shape), whole_block(total.shape),
            pl.BlockSpec((1, states, group, LANES), lambda at: (jnp.maximum(at - count, 0), 0, 0, 0)),
            whole_block((rows, rank)), pl.BlockSpec((rank, LANES), second), pl.BlockSpec((1, LANES), second),
            pl.BlockSpec((1, LANES), second), pl.BlockSpec(memory_space=pl.ANY), pl.BlockSpec(memory_space=pl.ANY),
        ],
        out_specs=[
            pl.BlockSpec((rows, LANES), lambda at: (0, jnp.minimum(at, count - 1) + count)),
            pl.BlockSpec((rows, LANES), second), pl.BlockSpec((rows, LANES), second),
            pl.BlockSpec((small_rows, LANES), second), whole_block((rows, rank + 2 * states)),
            pl.BlockSpec(memory_space=pl.ANY), pl.BlockSpec(memory_space=pl.ANY),
        ],
        out_shape=[
            shape_of((rows, 2 * inner), bf16), shape_of((rows, inner), bf16), shape_of((rows, inner), f32),
            shape_of((small_rows, inner), bf16), shape_of((rows, rank + 2 * states), bf16), shape_of(back.shape, bf16),
            shape_of(out_piece, bf16),
        ],
        scratch_shapes=[pltpu.VMEM((2,) + out_piece, bf16), pltpu.VMEM(out_piece, bf16), pltpu.VMEM(out_piece, bf16)]
        + [pltpu.VMEM(out_piece, bf16), dma((3,)), dma((3,)), dma((3,)), dma((devices - 1,)), dma((devices - 1,))]
        + [dma((1,)), pltpu.VMEM((bc.shape[1], 2 * states * LANES), bf16), pltpu.VMEM((rows, LANES), f32), big, big, big, big, big]
        + [pltpu.VMEM((rows, LANES), f32), pltpu.VMEM((count, rows, LANES), bf16)]
        + [pltpu.VMEM((rows, rank), f32), pltpu.VMEM(shape, f32), pltpu.VMEM(shape, f32)] + carry_scratch(shape),
        compiler_params=pltpu.CompilerParams(collective_id=1, has_side_effects=True, vmem_limit_bytes=64 << 20),
        name="backward_scan",
    )(mixed_grad, gate, z, step, conv_low, bc, match, a_blocks, total, start, rate_low, w_dt, bias, skip, back, out_grad)

def broad_match(match_ref, wide):
    @pl.when(pl.program_id(0) == 0)
    def _():
        for k in range(match_ref.shape[1]):
            wide[k] = jnp.broadcast_to(match_ref[:, k : k + 1], wide.shape[1:])


def front_kernel(
    token_ref, before_ref, gain_ref, wc_ref, wg_ref, cw_ref, cb_ref, compact_ref, wx_ref, ci_ref, low_ref, gate_ref, rate_ref, bc_ref,
    normed_ref, mixed_ref, rows_f, match_ref, *, halo, group,
):
    rows = low_ref.shape[0]
    broad_match(compact_ref, match_ref)

    @pl.when(pl.program_id(0) == 0)
    def _():
        def put(at, source):
            values = source.astype(f32)
            scale = lax.rsqrt(jnp.mean(values * values, -1, keepdims=True) + epsilon)
            normed_ref[at, :] = (values * scale * gain_ref[...]).astype(bf16)

        put(slice(0, halo), before_ref[...])
        tile = 256

        @pl.loop(0, rows // tile)
        def _(i):
            put(pl.ds(pl.multiple_of(halo + i * tile, halo), tile), token_ref[pl.ds(pl.multiple_of(i * tile, tile), tile), :])

    taps = cw_ref.shape[0]
    ci = jnp.dot(normed_ref[...], wc_ref[...], preferred_element_type=f32).astype(bf16)
    ci_ref[...] = ci
    rows_f[...] = ci.astype(f32)
    total = conv_total(rows_f, cw_ref, cb_ref, match_ref, halo, group, rows, taps)
    low = (total * jax.nn.sigmoid(total)).astype(bf16)
    low_ref[...] = low
    gate_ref[...] = jnp.dot(normed_ref[halo:, :], wg_ref[...], preferred_element_type=f32)
    part = jnp.dot(low, wx_ref[...], preferred_element_type=f32)

    @pl.when(pl.program_id(0) == 0)
    def _():
        mixed_ref[...] = part

    @pl.when(pl.program_id(0) > 0)
    def _():
        mixed_ref[...] += part

    @pl.when(pl.program_id(0) == pl.num_programs(0) - 1)
    def _():
        rank, wide = rate_ref.shape[1], bc_ref.shape[1] // 3
        rate_ref[...] = mixed_ref[:, :rank].astype(bf16)
        rest = mixed_ref[:, rank:]
        for k in range(3):
            part_low = rest.astype(bf16)
            bc_ref[:, k * wide : (k + 1) * wide] = part_low
            rest = rest - part_low.astype(f32)


def conv_total(rows_f, cw_ref, cb_ref, match_ref, halo, group, rows, taps):
    total = cb_ref[...] + cw_ref[taps - 1 : taps, :] * rows_f[halo : halo + rows, :]
    for k in range(taps - 1):
        at = halo - (taps - 1 - k) * group
        total = total + cw_ref[k : k + 1, :] * rows_f[at : at + rows, :] * match_ref[k]
    return total


def front(token_low, before_rows, gain, w_in, conv_w, conv_b, match, w_x, rank, halo, group, lanes):
    width, inner = w_in.shape[0], w_in.shape[1] // 2
    total_rows = token_low.shape[0] + halo
    rows, taps, mixed_width = total_rows - halo, conv_w.shape[0], w_x.shape[1]
    count = inner // lanes
    cols = lambda r: pl.BlockSpec((r, lanes), lambda j: (0, j))
    return pl.pallas_call(
        functools.partial(front_kernel, halo=halo, group=group),
        grid=(count,),
        in_specs=[
            whole_block(token_low.shape), whole_block(before_rows.shape), whole_block(gain.shape), cols(width),
            pl.BlockSpec((width, lanes), lambda j: (0, j + count)),
            cols(taps), cols(1), whole_block(match.shape), pl.BlockSpec((lanes, mixed_width), lambda j: (j, 0)),
        ],
        out_specs=[
            cols(total_rows), cols(rows), cols(rows), whole_block((rows, rank)), whole_block((rows, 3 * (mixed_width - rank))),
            whole_block((total_rows, width)),
        ],
        out_shape=[
            shape_of((total_rows, inner), bf16), shape_of((rows, inner), bf16), shape_of((rows, inner), f32),
            shape_of((rows, rank), bf16), shape_of((rows, 3 * (mixed_width - rank)), bf16), shape_of((total_rows, width), bf16),
        ],
        scratch_shapes=[pltpu.VMEM((rows, mixed_width), f32), pltpu.VMEM((total_rows, lanes), f32), pltpu.VMEM((match.shape[1], rows, lanes), f32)],
        compiler_params=params(),
        name="front",
    )(token_low, before_rows, gain, w_in, w_in, conv_w, conv_b, match, w_x)


def conv_back_kernel(
    cg_ref, low_ref, mpg_ref, wx_ref, ci_ref, cw_ref, cb_ref, compact_ref, proj_ref, pg_ref, ext_ref, small_ref, rows_f, ext, match_ref,
    *, halo, group,
):
    broad_match(compact_ref, match_ref)
    rows = pg_ref.shape[0]
    taps = cw_ref.shape[0]
    grad = cg_ref[...] + lax.dot_general(
        mpg_ref[...], wx_ref[...], (((1,), (1,)), ((), ())), preferred_element_type=f32
    )
    rows_f[...] = ci_ref[...].astype(f32)
    total = conv_total(rows_f, cw_ref, cb_ref, match_ref, halo, group, rows, taps)
    sig = jax.nn.sigmoid(total)
    grad = grad * (sig * (1.0 + total * (1.0 - sig)))
    x_part = lax.dot_general(mpg_ref[...], low_ref[...], (((0,), (0,)), ((), ())), preferred_element_type=f32)
    taps_grad = [None] * taps
    ext[:halo, :] = jnp.zeros((halo, ext.shape[1]), f32)
    ext[halo:, :] = grad * cw_ref[taps - 1 : taps, :]
    taps_grad[taps - 1] = jnp.sum(grad * rows_f[halo:, :], 0, keepdims=True)
    for k in range(taps - 1):
        at = halo - (taps - 1 - k) * group
        own = grad * match_ref[k]
        taps_grad[k] = jnp.sum(own * rows_f[at : at + rows, :], 0, keepdims=True)
        ext[at : at + rows, :] += own * cw_ref[k : k + 1, :]
    pg_ref[...] = ext[halo:, :].astype(bf16)
    ext_ref[:halo, :] = ext[:halo, :]
    ext_ref[halo:, :] = ext[rows:, :]
    spare = small_ref.shape[0] - x_part.shape[0] - taps - 1
    parts = [x_part] + taps_grad + [jnp.sum(grad, 0, keepdims=True), jnp.zeros((spare, ext.shape[1]), f32)]
    small_ref[...] = jnp.concatenate(parts, 0).astype(bf16)


def conv_back(cg, conv_low, mpg, w_x, ci, conv_w, conv_b, match, proj, halo, group, lanes):
    rows, inner = cg.shape
    taps, mixed_width = conv_w.shape[0], w_x.shape[1]
    small_rows = -(-(mixed_width + taps + 1) // 16) * 16
    cols = lambda r: pl.BlockSpec((r, lanes), lambda j: (0, j))
    return pl.pallas_call(
        functools.partial(conv_back_kernel, halo=halo, group=group),
        grid=(inner // lanes,),
        in_specs=[
            cols(rows), cols(rows), whole_block((rows, mixed_width)), pl.BlockSpec((lanes, mixed_width), lambda j: (j, 0)),
            cols(rows + halo), cols(taps), cols(1), whole_block(match.shape),
            pl.BlockSpec(memory_space=pl.ANY),
        ],
        out_specs=[cols(rows), cols(2 * halo), cols(small_rows)],
        out_shape=[shape_of(proj.shape, bf16), shape_of((2 * halo, inner), f32), shape_of((small_rows, inner), bf16)],
        scratch_shapes=[pltpu.VMEM((rows + halo, lanes), f32), pltpu.VMEM((rows + halo, lanes), f32)]
        + [pltpu.VMEM((match.shape[1], rows, lanes), f32)],
        input_output_aliases={8: 0},
        compiler_params=params(),
        name="conv_back",
    )(cg, conv_low, mpg, w_x, ci, conv_w, conv_b, match, proj)

def routing(low, router, experts):
    logits = jnp.dot(low, router, preferred_element_type=f32)
    lane = lax.broadcasted_iota(jnp.int32, logits.shape, 1)
    logits = jnp.where(lane < experts, logits, -1e30)
    raised = jnp.exp(logits - jnp.max(logits, -1, keepdims=True))
    return raised / jnp.sum(raised, -1, keepdims=True)


def expert_kernel(
    rows_ref, cot_ref, up_ref, down_ref, router_ref, turned_ref, chosen_ref, out_ref, back_ref, upg_ref, downg_ref, routerg_ref,
    grad, out_acc, back_acc, active, pre_grad, prob, *, tile, experts,
):
    first = pl.program_id(0) == 0
    final = pl.program_id(0) == pl.num_programs(0) - 1
    slots, width = cot_ref.shape
    tiles = [slice(i * tile, (i + 1) * tile) for i in range(slots // tile)]

    @pl.when(first)
    def _():
        for at in tiles:
            own = routing(rows_ref[at, :], router_ref[...], experts)
            prob[at, :] = own
            gate = jnp.sum(own * chosen_ref[...], -1, keepdims=True)
            grad[at, :] = (gate * cot_ref[at, :].astype(f32)).astype(bf16)
            out_acc[at, :] = jnp.zeros((tile, width), f32)
            back_acc[at, :] = jnp.zeros((tile, width), f32)

    for at in tiles:
        pre = jnp.dot(rows_ref[at, :], up_ref[...], preferred_element_type=f32)
        act_grad = lax.dot_general(grad[at, :], down_ref[...], (((1,), (1,)), ((), ())), preferred_element_type=f32)
        half = 0.5 * lax.erf(pre * 0.7071067811865476) + 0.5
        active[at, :] = (pre * half).astype(bf16)
        slope = half + pre * (jnp.exp(pre * pre * -0.5) * 0.3989422804014327)
        pre_grad[at, :] = (act_grad * slope).astype(bf16)
    for at in tiles:
        out_acc[at, :] += jnp.dot(active[at, :], down_ref[...], preferred_element_type=f32)
        back_acc[at, :] += lax.dot_general(
            pre_grad[at, :], up_ref[...], (((1,), (1,)), ((), ())), preferred_element_type=f32
        )
    downg_ref[...] = lax.dot_general(
        active[...], grad[...], (((0,), (0,)), ((), ())), preferred_element_type=f32
    ).astype(bf16)
    upg_ref[...] = lax.dot_general(
        rows_ref[...], pre_grad[...], (((0,), (0,)), ((), ())), preferred_element_type=f32
    ).astype(bf16)

    @pl.when(final)
    def _():
        routerg_ref[...] = jnp.zeros_like(routerg_ref)
        for at in tiles:
            out = out_acc[at, :].astype(bf16)
            out_ref[at, :] = out
            gate_grad = jnp.sum(out.astype(f32) * cot_ref[at, :].astype(f32), -1, keepdims=True)
            own = prob[at, :]
            gate = jnp.sum(own * chosen_ref[...], -1, keepdims=True)
            logit_grad = own * (chosen_ref[...] - gate) * gate_grad
            routerg_ref[...] += lax.dot_general(
                logit_grad, rows_ref[at, :].astype(f32), (((0,), (0,)), ((), ())), precision=highest,
                preferred_element_type=f32,
            )
            through = jnp.dot(logit_grad, turned_ref[...], precision=highest, preferred_element_type=f32)
            back_ref[at, :] = (back_acc[at, :] + through).astype(bf16)


def one_expert(rows, cot, up, down, router_wide, chosen, experts):
    slots, width = cot.shape
    hidden = up.shape[1]
    hidden_tile, tile = hidden // 6, slots // 2
    full = whole_block((slots, width))
    cols = pl.BlockSpec((width, hidden_tile), lambda j: (0, j))
    deep = pl.BlockSpec((hidden_tile, width), lambda j: (j, 0))
    return pl.pallas_call(
        functools.partial(expert_kernel, tile=tile, experts=experts),
        grid=(hidden // hidden_tile,),
        in_specs=[
            full, full, cols, deep, whole_block(router_wide.shape), whole_block((LANES, width)), whole_block((1, LANES)),
        ],
        out_specs=[full, full, cols, deep, whole_block((LANES, width))],
        out_shape=[
            shape_of((slots, width), bf16), shape_of((slots, width), bf16), shape_of((width, hidden), bf16),
            shape_of((hidden, width), bf16), shape_of((LANES, width), f32),
        ],
        scratch_shapes=[
            pltpu.VMEM((slots, width), bf16), pltpu.VMEM((slots, width), f32), pltpu.VMEM((slots, width), f32),
            pltpu.VMEM((slots, hidden_tile), bf16), pltpu.VMEM((slots, hidden_tile), bf16), pltpu.VMEM((slots, LANES), f32),
        ],
        compiler_params=params(),
        name="one_expert",
    )(rows, cot, up, down, router_wide, router_wide.astype(f32).T, chosen)


def exp_barrier(spot, devices):
    barrier = pltpu.get_barrier_semaphore()
    for hop in range(1, devices):
        pl.semaphore_signal(barrier, inc=1, device_id={"exp": lax.rem(spot + hop, devices)}, device_id_type=MESH)
    pl.semaphore_wait(barrier, devices - 1)


class Dispatch:
    def __init__(self, rows_ref, target_ref, got_ref, staged, send_sem, recv_sem, devices):
        self.rows_ref, self.target_ref, self.got_ref, self.staged = rows_ref, target_ref, got_ref, staged
        self.send_sem, self.recv_sem, self.devices = send_sem, recv_sem, devices
        self.spot = lax.axis_index("exp")
        self.hops = [h for h in range(devices // 2, devices)] + [h for h in range(1, devices // 2)]

    def packed(self, k):
        capacity = self.got_ref.shape[1]
        slot = lax.broadcasted_iota(jnp.int32, (capacity, self.rows_ref.shape[0]), 0) + k * capacity
        pick = jnp.where(slot == self.target_ref[...], 1.0, 0.0).astype(bf16)
        return jnp.dot(pick, self.rows_ref[...], preferred_element_type=f32).astype(bf16)

    def copy(self, hop):
        return pltpu.make_async_remote_copy(
            src_ref=self.staged.at[hop - 1], dst_ref=self.got_ref.at[self.spot], send_sem=self.send_sem.at[hop - 1],
            recv_sem=self.recv_sem.at[hop - 1], device_id={"exp": lax.rem(self.spot + hop, self.devices)},
            device_id_type=MESH,
        )

    def start(self):
        for hop in self.hops:
            self.staged[hop - 1] = self.packed(lax.rem(self.spot + hop, self.devices))
            self.copy(hop).start()
        self.got_ref[self.spot] = self.packed(self.spot)

    def wait(self):
        for hop in self.hops:
            self.copy(hop).wait()


def route_kernel(
    mixed_ref, wout_ref, token_ref, gain_ref, router_ref, route_ref, target_ref, hidden_ref, gate_ref, got_ref, rows_ref,
    staged, send_sem, recv_sem, *, devices, experts, tile,
):
    exp_barrier(lax.axis_index("exp"), devices)
    width = wout_ref.shape[1]

    @pl.loop(0, mixed_ref.shape[0] // tile)
    def _(i):
        at = pl.ds(pl.multiple_of(i * tile, tile), tile)
        hidden = token_ref[at, :].astype(f32) + jnp.dot(mixed_ref[at, :], wout_ref[...], preferred_element_type=f32)
        hidden_ref[at, :] = hidden
        scale = lax.rsqrt(jnp.mean(hidden * hidden, -1, keepdims=True) + epsilon)
        low = (hidden * scale * gain_ref[...]).astype(bf16)
        rows_ref[at, :] = low
        prob = routing(low, router_ref[...], experts)
        lane = lax.broadcasted_iota(jnp.int32, prob.shape, 1)
        gate = jnp.sum(jnp.where(lane == route_ref[at, :], prob, 0.0), -1, keepdims=True)
        gate_ref[at, :] = jnp.broadcast_to(gate, (tile, LANES))

    moved = Dispatch(rows_ref, target_ref, got_ref, staged, send_sem, recv_sem, devices)
    moved.start()
    moved.wait()


def routed(mixed_low, w_out, token_low, gain, router_wide, route_col, target, capacity, devices, experts):
    vm = pl.BlockSpec(memory_space=pltpu.VMEM)
    dma = pltpu.SemaphoreType.DMA
    rows, width = token_low.shape
    return pl.pallas_call(
        functools.partial(route_kernel, devices=devices, experts=experts, tile=256),
        in_specs=[vm] * 7,
        out_specs=[vm] * 3,
        out_shape=[
            shape_of((rows, width), f32), shape_of((rows, LANES), f32), shape_of((devices, capacity, width), bf16),
        ],
        scratch_shapes=[
            pltpu.VMEM((rows, width), bf16), pltpu.VMEM((devices - 1, capacity, width), bf16), dma((devices - 1,)),
            dma((devices - 1,)),
        ],
        compiler_params=pltpu.CompilerParams(collective_id=3, has_side_effects=True, vmem_limit_bytes=vmem_cap),
        name="routed",
    )(mixed_low, w_out, token_low, gain, router_wide, route_col, target[None, :])


def collect_kernel(
    sent_ref, target_ref, hidden_ref, cot_ref, gain_ref, hidden_grad_ref, branch_ref, gain_grad_ref, got, total, send_sem,
    recv_sem, *, devices, hops, tile,
):
    spot = lax.axis_index("exp")
    capacity = got.shape[1]
    count, width = hidden_ref.shape
    exp_barrier(spot, devices)
    copies = []
    for hop in hops:
        peer = lax.rem(spot + hop, devices)
        c = pltpu.make_async_remote_copy(
            src_ref=sent_ref.at[peer], dst_ref=got.at[devices - hop - 1], send_sem=send_sem.at[hop - 1],
            recv_sem=recv_sem.at[hop - 1], device_id={"exp": peer}, device_id_type=MESH,
        )
        c.start()
        copies.append(c)

    def spread_back(k, rows):
        slot = lax.broadcasted_iota(jnp.int32, (count, capacity), 1) + k * capacity
        pick = jnp.where(slot == target_ref[...], 1.0, 0.0).astype(bf16)
        return jnp.dot(pick, rows, preferred_element_type=f32)

    total[...] = spread_back(spot, sent_ref[spot])
    for hop, c in zip(hops, copies):
        c.wait_recv()
        total[...] += spread_back(lax.rem(spot + devices - hop, devices), got[devices - hop - 1])
    gain_grad_ref[...] = jnp.zeros_like(gain_grad_ref)

    @pl.loop(0, count // tile)
    def _(i):
        at = pl.ds(pl.multiple_of(i * tile, tile), tile)
        grad = total[at, :]
        hidden = hidden_ref[at, :]
        scale = lax.rsqrt(jnp.mean(hidden * hidden, -1, keepdims=True) + epsilon)
        unit = hidden * scale
        gain_grad_ref[...] += jnp.sum(grad * unit, 0, keepdims=True)
        scaled = grad * gain_ref[...]
        hidden_grad = cot_ref[at, :].astype(f32) + scale * (
            scaled - unit * jnp.mean(scaled * unit, -1, keepdims=True)
        )
        hidden_grad_ref[at, :] = hidden_grad
        branch_ref[at, :] = hidden_grad.astype(bf16)

    for c in copies:
        c.wait_send()


def collect(blocks, target, hidden, cot, gain, devices):
    vm = pl.BlockSpec(memory_space=pltpu.VMEM)
    dma = pltpu.SemaphoreType.DMA
    capacity = blocks.shape[1]
    count, width = hidden.shape
    return pl.pallas_call(
        functools.partial(collect_kernel, devices=devices, hops=(2, 3, 1), tile=256),
        in_specs=[vm] * 5,
        out_specs=[vm] * 3,
        out_shape=[shape_of((count, width), f32), shape_of((count, width), bf16), shape_of((1, width), f32)],
        scratch_shapes=[
            pltpu.VMEM((devices - 1, capacity, width), bf16), pltpu.VMEM((count, width), f32), dma((devices - 1,)),
            dma((devices - 1,)),
        ],
        compiler_params=pltpu.CompilerParams(collective_id=4, has_side_effects=True, vmem_limit_bytes=vmem_cap),
        name="collect",
    )(blocks, target[:, None], hidden, cot, gain)

SEGMENTS = 4
STARTS = (-4, 0, 1, 2)


def ring_order(place, peers):
    odd = lax.rem(place, 2)
    half = lax.div(place, 2)
    return half + odd * (peers - 1 - 2 * half)


def ring_member(position, peers):
    back = lax.div(2 * position, peers)
    return 2 * position + back * (2 * (peers - 1) + 1 - 4 * position)


class Rings:
    def __init__(self, own, total, sent, landed, send, recv, bases, sizes, peers):
        place = lax.axis_index("seq")
        self.own, self.total, self.sent, self.landed, self.send, self.recv = own, total, sent, landed, send, recv
        self.bases, self.sizes, self.peers = bases, sizes, peers
        self.position = ring_order(place, peers)
        self.after = ring_member(lax.rem(self.position + 1, peers), peers)
        self.before = ring_member(lax.rem(self.position + peers - 1, peers), peers)

    def rows(self, ring, steps):
        sign = 1 if ring % 2 == 0 else -1
        chunk = self.sizes[ring] // self.peers
        c = lax.rem(self.position + sign * steps + 2 * self.peers, self.peers)
        return pl.ds(pl.multiple_of(self.bases[ring] + c * chunk, 16), chunk)

    def target(self, ring):
        return {"seq": self.after if ring % 2 == 0 else self.before}

    def first(self, ring, s):
        chunk = self.sizes[ring] // self.peers
        return pltpu.make_async_remote_copy(
            src_ref=self.sent.at[ring, s, pl.ds(0, chunk)], dst_ref=self.landed.at[ring, s, pl.ds(0, chunk)],
            send_sem=self.send.at[ring, s], recv_sem=self.recv.at[ring, s], device_id=self.target(ring),
            device_id_type=MESH,
        )

    def second(self, ring, s):
        part = self.total.at[self.rows(ring, 1 - s)]
        at = self.peers - 1 + s
        return pltpu.make_async_remote_copy(
            src_ref=part, dst_ref=part, send_sem=self.send.at[ring, at], recv_sem=self.recv.at[ring, at],
            device_id=self.target(ring), device_id_type=MESH,
        )

    def begin(self, ring):
        chunk = self.sizes[ring] // self.peers
        self.sent[ring, 0, pl.ds(0, chunk)] = self.own[self.rows(ring, 0), :].astype(bf16)
        self.first(ring, 0).start()

    def advance(self, ring, s):
        peers, chunk = self.peers, self.sizes[ring] // self.peers

        @pl.when(jnp.logical_and(s >= 1, s <= peers - 2))
        def _():
            self.first(ring, s - 1).wait_recv()
            summed = self.landed[ring, s - 1, pl.ds(0, chunk)].astype(f32) + self.own[self.rows(ring, -s), :]
            self.sent[ring, s, pl.ds(0, chunk)] = summed.astype(bf16)
            self.first(ring, s).start()

        @pl.when(s == peers - 1)
        def _():
            self.first(ring, peers - 2).wait_recv()
            summed = self.landed[ring, peers - 2, pl.ds(0, chunk)].astype(f32) + self.own[self.rows(ring, 1), :]
            self.total[self.rows(ring, 1), :] = summed.astype(bf16)
            self.second(ring, 0).start()

        @pl.when(jnp.logical_and(s >= peers, s <= 2 * peers - 3))
        def _():
            self.second(ring, s - peers).wait_recv()
            self.second(ring, s - peers + 1).start()

        @pl.when(s == 2 * peers - 2)
        def _():
            self.second(ring, peers - 2).wait_recv()

    def drain(self):
        @pl.loop(0, self.peers - 1)
        def _(s):
            for ring in range(len(self.sizes)):
                self.first(ring, s).wait_send()
                self.second(ring, s).wait_send()


def finish_kernel(
    proj_ref, normed_ref, win_ref, outo_ref, small_ref, gain_ref, token_ref, hiddeng_ref, hidden_ref, chance_ref, target_ref,
    tok_ref,
    in_sum_ref, out_sum_ref, small_sum_ref, tokens_grad_ref, block_ref,
    own, total, near_stage, small_all, gain_part, near_in, near_small, far_in, far_small, pass_in, pass_small, sent, landed, near_send, near_recv, far_send, far_recv, ring_send, ring_recv,
    *, peers, bases, sizes, halo, tile, gain_row,
):
    spot = lax.axis_index("exp")
    width, wide = near_in.shape[1:]
    rows_out = outo_ref.shape[0]
    rows_small, share = near_small.shape[1:]
    folds = wide // share
    count = proj_ref.shape[0]
    third = width // 3
    near = spot + 1 - 2 * lax.rem(spot, 2)
    far = lax.rem(spot + 2, 4)
    across = lax.rem(near + 2, 4)
    rings = Rings(own, total, sent, landed, ring_send, ring_recv, bases, sizes, peers)
    barrier = pltpu.get_barrier_semaphore()
    for device in ({"exp": near}, {"exp": far}, {"seq": rings.after}, {"seq": rings.before}):
        pl.semaphore_signal(barrier, inc=1, device_id=device, device_id_type=MESH)
    pl.semaphore_wait(barrier, 4)

    def columns(k, size):
        return pl.ds(pl.multiple_of(k * size, size), size)

    def copy(source, target, send, recv, device):
        return pltpu.make_async_remote_copy(
            src_ref=source, dst_ref=target, send_sem=send, recv_sem=recv, device_id=device, device_id_type=MESH
        )

    def in_rows(i):
        return slice(i * third, (i + 1) * third)

    def near_copy(slot, piece):
        k = across if slot else near
        if piece == 4:
            source, target = small_all.at[:, columns(k, share)], near_small.at[slot]
        else:
            at = pl.ds((piece - 1) * third, third)
            source, target = near_stage.at[slot, at], near_in.at[slot, at]
        return copy(source, target, near_send.at[slot, piece], near_recv.at[slot, piece], {"exp": near})

    def far_copy(piece):
        if piece == 4:
            source, target = pass_small, far_small
        else:
            at = pl.ds((piece - 1) * third, third)
            source, target = pass_in.at[at], far_in.at[at]
        return copy(source, target, far_send.at[piece], far_recv.at[piece], {"exp": far})

    def in_tile(i, k):
        part = lax.dot_general(
            normed_ref[pl.ds(halo, count), in_rows(i)], proj_ref[:, columns(k, wide)], (((0,), (0,)), ((), ())),
            preferred_element_type=f32,
        )
        scaled = part * win_ref[in_rows(i), columns(k, wide)].astype(f32)
        gain_part[in_rows(i), :] += tree_sum(scaled[:, h * LANES : (h + 1) * LANES] for h in range(wide // LANES))
        return part

    def into_own(base, values, add):
        size = values.shape[0]
        for h in range(values.shape[1] // share):
            at = slice(base + h * size, base + (h + 1) * size)
            part = values[:, h * share : (h + 1) * share]
            if add:
                own[at, :] += part
            else:
                own[at, :] = part

    def pad_own(n, used):
        if used < sizes[n]:
            own[bases[n] + used : bases[n] + sizes[n], :] = jnp.zeros((sizes[n] - used, share), f32)

    small_base = bases[3] + folds * third
    into_own(bases[0], outo_ref[...].astype(f32), False)
    pad_own(0, folds * rows_out)
    rings.begin(0)
    gain_part[...] = jnp.zeros_like(gain_part)
    small_all[...] = small_ref[...]
    for i in range(3):
        for slot, k in ((1, across), (0, near)):
            near_stage[slot, in_rows(i), :] = in_tile(i, k).astype(bf16)
            near_copy(slot, 1 + i).start()
        distant = in_tile(i, far)
        near_copy(1, 1 + i).wait_recv()
        pass_in[in_rows(i), :] = (distant + near_in[1, in_rows(i), :].astype(f32)).astype(bf16)
        far_copy(1 + i).start()
        mine = in_tile(i, spot)
        near_copy(0, 1 + i).wait_recv()
        into_own(bases[1 + i], mine + near_in[0, in_rows(i), :].astype(f32), False)
        pad_own(1 + i, folds * third)
        rings.advance(0, jnp.int32(1 + i))
    quarter = width // 4
    for k in range(4):
        part = jnp.sum(gain_part[k * quarter : (k + 1) * quarter, :], -1, keepdims=True)
        eye = lax.broadcasted_iota(jnp.int32, (quarter, quarter), 0) == lax.broadcasted_iota(
            jnp.int32, (quarter, quarter), 1
        )
        row = jnp.sum(jnp.where(eye, part, 0.0), 0, keepdims=True) / gain_ref[:, k * quarter : (k + 1) * quarter]
        group = slice(gain_row, gain_row + 16)
        old = small_all[group, k * share : k * share + quarter].astype(f32)
        top = lax.broadcasted_iota(jnp.int32, old.shape, 0) == 0
        small_all[group, k * share : k * share + quarter] = jnp.where(top, row, old).astype(bf16)
    for slot in (1, 0):
        near_copy(slot, 4).start()
    near_copy(1, 4).wait_recv()
    pass_small[...] = (small_all[:, columns(far, share)].astype(f32) + near_small[1].astype(f32)).astype(bf16)
    far_copy(4).start()
    near_copy(0, 4).wait_recv()
    own[small_base : small_base + rows_small, :] = (
        small_all[:, columns(spot, share)].astype(f32) + near_small[0].astype(f32)
    )
    def arrived(ring):
        far_copy(ring).wait_recv()
        into_own(bases[ring], far_in[in_rows(ring - 1), :].astype(f32), True)
        if ring == SEGMENTS - 1:
            far_copy(4).wait_recv()
            own[small_base : small_base + rows_small, :] += far_small[...].astype(f32)
        rings.begin(ring)

    def place_rows(out_ref, values, i):
        group = out_ref.shape[0]
        steps = tile // group
        values = jnp.swapaxes(values.reshape(steps, group, width), 0, 1)
        out_ref[:, pl.ds(pl.multiple_of(i * steps, steps), steps), :] = values.astype(out_ref.dtype)

    def token_tile(i):
        at = pl.ds(pl.multiple_of(i * tile, tile), tile)
        grad = lax.dot_general(proj_ref[at, :], win_ref[...], (((1,), (1,)), ((), ())), preferred_element_type=f32)
        values = token_ref[at, :].astype(f32)
        scale = lax.rsqrt(jnp.mean(values * values, -1, keepdims=True) + epsilon)
        unit = values * scale
        scaled = grad * gain_ref[...]
        total_grad = hiddeng_ref[at, :] + scale * (scaled - unit * jnp.mean(scaled * unit, -1, keepdims=True))
        place_rows(tokens_grad_ref, total_grad, i)

    def block_tile(i):
        at = pl.ds(pl.multiple_of(i * tile, tile), tile)
        capacity = tok_ref.shape[1]
        gate = chance_ref[at, 0:1]
        tok = jnp.zeros((tile, width), f32)
        for k in range(tok_ref.shape[0]):
            slot = lax.broadcasted_iota(jnp.int32, (tile, capacity), 1) + k * capacity
            pick = jnp.where(slot == target_ref[at, :], 1.0, 0.0).astype(bf16)
            tok = tok + jnp.dot(pick, tok_ref[k], preferred_element_type=f32)
        place_rows(block_ref, hidden_ref[at, :] + gate * tok, i)

    tiles = count // tile

    @pl.loop(0, 2 * peers - 1 + STARTS[-1])
    def _(turn):
        for ring in range(SEGMENTS):
            step = turn - STARTS[ring]
            if ring:

                @pl.when(step == 0)
                def _():
                    arrived(ring)

            rings.advance(ring, step)

        @pl.when(turn < tiles)
        def _():
            token_tile(turn)

        @pl.when(jnp.logical_and(turn >= tiles, turn < 2 * tiles))
        def _():
            block_tile(turn - tiles)

    for i in range(3):
        for h in range(folds):
            at = slice(bases[1 + i] + h * third, bases[1 + i] + (h + 1) * third)
            in_sum_ref[in_rows(i), h * share : (h + 1) * share] = total[at, :].astype(f32)
    for h in range(folds):
        at = slice(bases[0] + h * rows_out, bases[0] + (h + 1) * rows_out)
        out_sum_ref[:, h * share : (h + 1) * share] = total[at, :].astype(f32)
    small_sum_ref[...] = total[small_base : small_base + rows_small, :].astype(f32)
    for piece in range(1, 5):
        for slot in (1, 0):
            near_copy(slot, piece).wait_send()
        far_copy(piece).wait_send()
    rings.drain()


def finish(proj, normed_ext, w_in, out_own, small, gain, token_low, hidden_grad, hidden_one, chance, target, tok, gain_row, group):
    peers, devices = lax.axis_size("seq"), lax.axis_size("exp")
    count, width = token_low.shape
    wide, rows_out = proj.shape[1] // devices, out_own.shape[0]
    rows_small, share = small.shape[0], small.shape[1] // devices
    folds, third, unit = wide // share, width // 3, 16 * peers
    used = (folds * rows_out, folds * third, folds * third, folds * third + rows_small)
    sizes = tuple(-(-u // unit) * unit for u in used)
    bases = tuple(sum(sizes[:i]) for i in range(SEGMENTS))
    length, chunk = sum(sizes), max(sizes) // peers
    vm = pl.BlockSpec(memory_space=pltpu.VMEM)
    dma = pltpu.SemaphoreType.DMA
    shapes = ((width, wide), (rows_small, share))
    return pl.pallas_call(
        functools.partial(
            finish_kernel, peers=peers, bases=bases, sizes=sizes, halo=normed_ext.shape[0] - count, tile=256,
            gain_row=gain_row,
        ),
        in_specs=[vm] * 12,
        out_specs=[vm] * 5,
        out_shape=[
            shape_of((width, wide), f32), shape_of((rows_out, wide), f32), shape_of((rows_small, share), f32),
            shape_of((group, count // group, width), f32), shape_of((group, count // group, width), bf16),
        ],
        scratch_shapes=[
            pltpu.VMEM((length, share), f32), pltpu.VMEM((length, share), bf16), pltpu.VMEM((2, width, wide), bf16),
            pltpu.VMEM(small.shape, bf16), pltpu.VMEM((width, LANES), f32),
        ]
        + [pltpu.VMEM((2,) + s, bf16) for s in shapes]
        + [pltpu.VMEM(s, bf16) for s in shapes]
        + [pltpu.VMEM(s, bf16) for s in shapes]
        + [pltpu.VMEM((SEGMENTS, peers - 1, chunk, share), bf16)] * 2
        + [dma((2, 5)), dma((2, 5)), dma((5,)), dma((5,)), dma((SEGMENTS, 2 * peers - 2)), dma((SEGMENTS, 2 * peers - 2))],
        compiler_params=pltpu.CompilerParams(collective_id=2, has_side_effects=True, vmem_limit_bytes=64 << 20),
        name="finish",
    )(
        proj, normed_ext, w_in, out_own, small, gain, token_low, hidden_grad, hidden_one, chance, target[:, None], tok
    )

PIECES = 2


def gather_kernel(
    in_ref, small_ref, token_ref, cot_ref, ids_ref, win_ref, wsmall_ref, before_ref, before_ids, rows_ref, cot_rows_ref, edge_ref,
    near_sems, far_sems, pair_sems, edge_sems, own_sem, *, kernel_len,
):
    place, peers = lax.axis_index("seq"), lax.axis_size("seq")
    spot = lax.axis_index("exp")
    near = spot + 1 - 2 * lax.rem(spot, 2)
    far = lax.rem(spot + 2, 4)
    bit = lax.rem(place, 2)
    pair = place + 1 - 2 * bit
    width, wide = in_ref.shape
    share = small_ref.shape[1]
    chunk = width // 2 // PIECES
    has_before, has_after = place > 0, place < peers - 1
    barrier = pltpu.get_barrier_semaphore()
    for target in ({"exp": near}, {"exp": far}, {"seq": pair}):
        pl.semaphore_signal(barrier, inc=1, device_id=target, device_id_type=MESH)

    @pl.when(has_before)
    def _():
        pl.semaphore_signal(barrier, inc=1, device_id={"seq": place - 1}, device_id_type=MESH)

    @pl.when(has_after)
    def _():
        pl.semaphore_signal(barrier, inc=1, device_id={"seq": place + 1}, device_id_type=MESH)

    pl.semaphore_wait(barrier, 3 + has_before.astype(jnp.int32) + has_after.astype(jnp.int32))

    def columns(ref, k, size):
        return ref.at[:, pl.ds(pl.multiple_of(k * size, size), size)]

    def rows(k, half, piece):
        at = pl.multiple_of((half * PIECES + piece) * chunk, chunk)
        return win_ref.at[pl.ds(at, chunk), pl.ds(pl.multiple_of(k * wide, wide), wide)]

    def copy(source, target, sems, slot, device):
        return pltpu.make_async_remote_copy(
            src_ref=source, dst_ref=target, send_sem=sems.at[0, slot], recv_sem=sems.at[1, slot], device_id=device,
            device_id_type=MESH,
        )

    def edge_copies():
        return (
            copy(edge_ref, before_ref, edge_sems, 0, {"seq": place + 1}),
            copy(ids_ref, before_ids, edge_sems, 1, {"seq": place + 1}),
        )

    outward = []
    for piece in range(PIECES):
        at = pl.multiple_of((bit * PIECES + piece) * chunk, chunk)
        outward.append(copy(in_ref.at[pl.ds(at, chunk), :], rows(spot, bit, piece), far_sems, piece, {"exp": far}))
    outward.insert(0, copy(small_ref, columns(wsmall_ref, spot, share), far_sems, PIECES, {"exp": far}))
    for c in outward:
        c.start()
    beside = [
        copy(small_ref, columns(wsmall_ref, spot, share), near_sems, 0, {"exp": near}),
        copy(in_ref, columns(win_ref, spot, wide), near_sems, 1, {"exp": near}),
    ]
    for c in beside:
        c.start()
    group, part_len, features = token_ref.shape

    def by_place(source, start, steps):
        values = source[:, pl.ds(start, steps), :].astype(f32)
        return jnp.swapaxes(values, 0, 1).reshape(steps * group, features).astype(bf16)

    edge_ref[...] = by_place(token_ref, part_len - 8, 8)[(8 - kernel_len) * group :, :]

    @pl.when(has_after)
    def _():
        for c in edge_copies():
            c.start()

    @pl.when(jnp.logical_not(has_before))
    def _():
        before_ref[...] = jnp.zeros_like(before_ref)
        before_ids[...] = jnp.zeros_like(before_ids)

    own = [
        pltpu.make_async_copy(in_ref, columns(win_ref, spot, wide), own_sem.at[0]),
        pltpu.make_async_copy(small_ref, columns(wsmall_ref, spot, share), own_sem.at[1]),
    ]
    for c in own:
        c.start()
    tile = 16

    @pl.loop(0, part_len // tile)
    def _(i):
        start = pl.multiple_of(i * tile, tile)
        at = pl.ds(pl.multiple_of(i * tile * group, tile * group), tile * group)
        rows_ref[at, :] = by_place(token_ref, start, tile)
        cot_rows_ref[at, :] = by_place(cot_ref, start, tile)

    outward[0].wait_recv()
    beside.append(copy(columns(wsmall_ref, far, share), columns(wsmall_ref, far, share), near_sems, 2, {"exp": near}))
    beside[-1].start()
    crossing = []
    for piece in range(PIECES):
        outward[1 + piece].wait_recv()
        part = rows(far, bit, piece)
        crossing.append(copy(part, part, pair_sems, piece, {"seq": pair}))
        crossing[-1].start()
        beside.append(copy(part, part, near_sems, 3 + piece, {"exp": near}))
        beside[-1].start()
    for piece in range(PIECES):
        crossing[piece].wait_recv()
        part = rows(far, 1 - bit, piece)
        beside.append(copy(part, part, near_sems, 3 + PIECES + piece, {"exp": near}))
        beside[-1].start()
    for c in beside:
        c.wait_recv()
    for c in outward + beside + crossing:
        c.wait_send()
    for c in own:
        c.wait()

    @pl.when(has_before)
    def _():
        for c in edge_copies():
            c.wait_recv()

    @pl.when(has_after)
    def _():
        for c in edge_copies():
            c.wait_send()


def gather_weights(in_shard, small, tokens, cot, ids, kernel_len, devices):
    group, part_len, width = tokens.shape
    edge = shape_of((kernel_len * group, width), bf16)
    rows = shape_of((part_len * group, width), bf16)
    vm = pl.BlockSpec(memory_space=pltpu.VMEM)
    dma = pltpu.SemaphoreType.DMA
    return pl.pallas_call(
        functools.partial(gather_kernel, kernel_len=kernel_len),
        in_specs=[pl.BlockSpec(memory_space=pl.ANY), vm, vm, vm, vm],
        out_specs=[pl.BlockSpec(memory_space=pl.ANY), vm, vm, vm, vm, vm],
        out_shape=[
            shape_of((in_shard.shape[0], in_shard.shape[1] * devices), bf16),
            shape_of((small.shape[0], small.shape[1] * devices), bf16), shape_of(edge.shape, edge.dtype),
            shape_of(ids.shape, ids.dtype), rows, rows,
        ],
        scratch_shapes=[pltpu.VMEM(edge.shape, bf16), dma((2, 3 + 2 * PIECES)), dma((2, PIECES + 1)), dma((2, PIECES)), dma((2, 2)), dma((2,))],
        compiler_params=pltpu.CompilerParams(collective_id=5, has_side_effects=True, vmem_limit_bytes=32 << 20),
        name="gather_weights",
    )(in_shard, small, tokens, cot, ids)

def rms_norm(values, gain):
    return values * lax.rsqrt(jnp.mean(values * values, -1, keepdims=True) + epsilon) * gain


def passed_along(value, axis, steps):
    count = lax.axis_size(axis)
    initial, last = (max(0, -steps), min(count, count - steps))
    return lax.ppermute(value, axis, [(source, source + steps) for source in range(initial, last)])


def by_time(values):
    values = jnp.swapaxes(values, 0, 1)
    return values.reshape((values.shape[0] * values.shape[1],) + values.shape[2:])


def packed_small(norm_gain, conv_weight, conv_bias, x_proj, dt_proj, dt_bias, a_log, d_skip, moe_gain, router):
    share = conv_bias.shape[0]
    packed = [conv_weight, conv_bias[None], x_proj.T, dt_proj, dt_bias[None], a_log.T, d_skip[None]]
    narrow = jnp.concatenate([norm_gain[None], moe_gain[None], router.T], 0)
    total = jnp.concatenate(packed + [narrow.reshape(-1, share)], 0)
    return jnp.pad(total, ((0, -total.shape[0] % 16), (0, 0))), [p.shape[0] for p in packed], narrow.shape


def unpacked_small(whole, counts, narrow_shape, devices):
    out, at = [], 0
    for c in counts:
        out.append(whole[at : at + c])
        at += c
    share = whole.shape[1] // devices
    fold = narrow_shape[0] * narrow_shape[1] // share
    rest = whole[at : at + fold].reshape(fold, devices, share).transpose(1, 0, 2).reshape((devices,) + narrow_shape)
    rest = rest.transpose(1, 0, 2).reshape(narrow_shape[0], -1)
    return out, rest[0], rest[1], rest[2:].T


def local(
    tokens, segment_ids, routes, slot_index, norm_gain, in_proj, conv_weight, conv_bias, x_proj, dt_proj, dt_bias,
    a_log, d_skip, out_proj, moe_gain, router, expert_up, expert_down, cotangent,
):
    seq_count, part_len, width = tokens.shape
    row_count = seq_count * part_len
    group = seq_count
    kernel_len = conv_weight.shape[0]
    state_width = a_log.shape[1]
    rank_width = dt_proj.shape[0]
    halo = kernel_len * group
    devices = lax.axis_size("exp")
    doc_ids = segment_ids + 1
    edge_start = part_len - kernel_len
    edge_ids = jnp.pad(doc_ids[:, edge_start:], ((0, 0), (0, LANES - kernel_len)))
    small_shard, counts, narrow_shape = packed_small(
        norm_gain, conv_weight, conv_bias, x_proj, dt_proj, dt_bias, a_log, d_skip, moe_gain, router
    )
    w_in, small_whole, before_rows, before_ids, token_low, cot_rows = gather_weights(
        in_proj, small_shard, tokens, cotangent, edge_ids, kernel_len, devices
    )
    out_proj, small_whole = lax.optimization_barrier((out_proj, small_whole))
    w_out = lax.all_gather(out_proj, "exp", axis=0, tiled=True)
    (w_conv, b_conv, w_x_t, w_dt, b_dt, log_decay, skip_gain), gain_one, gain_two, w_router = unpacked_small(
        small_whole, counts, narrow_shape, devices
    )
    inner_width = w_out.shape[0]
    expert_total = w_router.shape[1]
    capacity = 5 * row_count // (4 * expert_total)
    blocks = inner_width // LANES

    ext_ids = jnp.concatenate([before_ids[:, :kernel_len], doc_ids], 1)
    match = jnp.stack([ext_ids[:, 1 + k : 1 + k + part_len] == doc_ids for k in range(kernel_len - 1)])
    match = jnp.transpose(match, (2, 1, 0)).reshape(row_count, kernel_len - 1).astype(f32)
    lanes = 2 * LANES
    gain_one = gain_one.astype(f32)[None]
    gain_two = gain_two.astype(f32)[None]
    route_rows = by_time(routes)
    slot_rows = by_time(slot_index)
    target = jnp.where(
        slot_rows < capacity, route_rows * capacity + slot_rows, expert_total * capacity
    )
    w_conv, b_conv = w_conv.astype(f32), b_conv.astype(f32)
    w_x = w_x_t.T
    ci, conv_low, gate, rate_low, bc, normed_ext = front(
        token_low, before_rows, gain_one, w_in, w_conv, b_conv, match, w_x, rank_width, halo, group, lanes
    )
    bias = b_dt.astype(f32)
    skip = skip_gain.astype(f32)
    a_mat = -jnp.exp(log_decay.astype(f32))
    a2 = a_mat * log2e
    a_blocks = a2.reshape(state_width, blocks, LANES).transpose(1, 0, 2)
    step, z, mixed_low, start, total, cot_recv = forward_scan(
        rate_low, w_dt, bias, conv_low, bc, match, a_blocks, gate, skip, cot_rows, target, capacity, group, devices
    )
    route_col = route_rows[:, None]
    router_wide = jnp.pad(w_router, ((0, 0), (0, LANES - expert_total)))
    hidden_one, chance, received = routed(
        mixed_low, w_out, token_low, gain_two, router_wide, route_col, target, capacity, devices, expert_total
    )
    chosen = (jnp.arange(LANES) == lax.axis_index("exp")).astype(f32)[None]
    expert_out, rows_back, up_grad, down_grad, router_grad_t = one_expert(
        received.reshape(devices * capacity, width), cot_recv.reshape(devices * capacity, width), expert_up[0],
        expert_down[0], router_wide, chosen, expert_total,
    )
    hidden_grad, branch_grad, gain_two_grad = collect(
        rows_back.reshape(devices, capacity, width), target, hidden_one, cot_rows, gain_two, devices
    )
    peers = lax.axis_size("seq")
    order = [list(range(0, peers, 2)) + list(range(peers - 1, 0, -2))]

    def scattered(values):
        return lax.psum_scatter(values, "seq", scatter_dimension=0, axis_index_groups=order, tiled=True)

    def regathered(part):
        return lax.all_gather(part, "seq", axis=0, axis_index_groups=order, tiled=True)

    down_part = scattered(down_grad)
    up_part = scattered(up_grad)
    out_proj_grad = jnp.dot(mixed_low.T, branch_grad, preferred_element_type=f32)
    mixed_grad = jnp.dot(branch_grad, w_out.T, preferred_element_type=f32)
    out_proj_grad = out_proj_grad.astype(bf16)
    down_part, mixed_grad, out_proj_grad = lax.optimization_barrier((down_part, mixed_grad, out_proj_grad))
    down_sum = regathered(down_part)
    proj, rate_pre_low, cg, small_one, mixed_proj_grad, tok, out_own = backward_scan(
        mixed_grad, gate, z, step, conv_low, bc, match, a_blocks, total, start, rate_low, w_dt, bias, skip,
        expert_out.reshape(devices, capacity, width), out_proj_grad, group, devices,
    )
    up_part, cg = lax.optimization_barrier((up_part, cg))
    up_sum = regathered(up_part)
    proj, ends, small_two = conv_back(
        cg, conv_low, mixed_proj_grad, w_x, ci, w_conv, b_conv, match, proj, halo, group, lanes
    )
    edge_back = passed_along(ends[:halo].astype(bf16), "seq", -1).astype(f32)
    proj = lax.dynamic_update_slice(proj, (ends[halo:] + edge_back).astype(bf16), (row_count - halo, 0))

    narrow = jnp.concatenate([jnp.zeros_like(gain_two_grad), gain_two_grad, router_grad_t[:expert_total]], 0)
    share, own_width = inner_width // devices, width // devices
    narrow = narrow.reshape(narrow.shape[0], devices, own_width)
    narrow = jnp.pad(narrow, ((0, -narrow.shape[0] % 16), (0, 0), (0, share - own_width))).astype(bf16)
    packed = jnp.concatenate([small_one, small_two, narrow.reshape(-1, inner_width)], 0)
    gain_row = small_one.shape[0] + small_two.shape[0]
    in_sum, out_sum, sums, tokens_grad, block_out = finish(
        proj, normed_ext, w_in, out_own, packed, gain_one, token_low, hidden_grad, hidden_one, chance,
        target, tok, gain_row, group,
    )
    at, own = 0, []
    for first, rows in (
        (0, rank_width), (rank_width, state_width), (rank_width + state_width, 1), (rank_width + state_width + 1, 1)
    ):
        own.append(sums[first : first + rows])
    at = small_one.shape[0]
    mixed_width = mixed_proj_grad.shape[1]
    for first, rows in ((0, mixed_width), (mixed_width, kernel_len), (mixed_width + kernel_len, 1)):
        own.append(sums[at + first : at + first + rows])
    at += small_two.shape[0]
    own_narrow = sums[at : at + 2 + expert_total, :own_width]
    return (
        block_out,
        tokens_grad,
        own_narrow[0],
        in_sum,
        own[5],
        own[6][0],
        own[4].T,
        own[0],
        own[2][0],
        own[1].T,
        own[3][0],
        out_sum,
        own_narrow[1],
        own_narrow[2:].T,
        up_sum.astype(f32)[None],
        down_sum.astype(f32)[None],
    )


def solution(mesh):
    in_specs = (
        P("exp", "seq", None),
        P("exp", "seq"),
        P("exp", "seq"),
        P("exp", "seq"),
        P("exp"),
        P(None, "exp"),
        P(None, "exp"),
        P("exp"),
        P("exp", None),
        P(None, "exp"),
        P("exp"),
        P("exp", None),
        P("exp"),
        P("exp", None),
        P("exp"),
        P("exp", None),
        P("exp", None, None),
        P("exp", None, None),
        P("exp", "seq", None),
    )
    out_specs = (
        P("exp", "seq", None),
        P("exp", "seq", None),
        P("exp"),
        P(None, "exp"),
        P(None, "exp"),
        P("exp"),
        P("exp", None),
        P(None, "exp"),
        P("exp"),
        P("exp", None),
        P("exp"),
        P("exp", None),
        P("exp"),
        P("exp", None),
        P("exp", None, None),
        P("exp", None, None),
    )
    return jax.shard_map(local, mesh=mesh, in_specs=in_specs, out_specs=out_specs, check_vma=False)
```

```python
import functools

import jax
import jax.numpy as jnp
from jax import lax
from jax.experimental import pallas as pl
from jax.experimental.pallas import tpu as pltpu
from jax.sharding import PartitionSpec as P

f32, bf16 = jnp.float32, jnp.bfloat16
highest = lax.Precision.HIGHEST
LANES = 128
MESH = pl.DeviceIdType.MESH
epsilon = 1e-05
log2e = 1.4426950408889634
cut = 1e8
ln2 = 0.6931471805599453
vmem_cap = 58 << 20


def tree_sum(parts):
    parts = list(parts)
    while len(parts) > 1:
        paired = [parts[i] + parts[i + 1] for i in range(0, len(parts) - 1, 2)]
        parts = paired + parts[len(parts) - len(parts) % 2 :]
    return parts[0]


UN = dict(state=8, scan=8, adj=8, fwd=4, bwd=4)


def spread(rows_ref, pick_ref, outs, states, group):
    shape = pick_ref.shape
    row = lax.broadcasted_iota(jnp.int32, shape, 0)
    lane = lax.broadcasted_iota(jnp.int32, shape, 1)
    pick_ref[...] = jnp.where(lax.rem(row, 2 * states) == lax.div(lane, LANES), 1.0, 0.0).astype(bf16)
    steps = rows_ref.shape[0] // group
    chunk = 16
    wide = 2 * LANES

    @pl.loop(0, steps // chunk)
    def _(i):
        rows = rows_ref[pl.ds(pl.multiple_of(i * chunk * group, chunk * group), chunk * group), :]
        for which, out_ref in outs:
            for n in range(0, states, 2):
                at = (which * states + n) * LANES
                part = jnp.dot(rows, pick_ref[:, at : at + wide], preferred_element_type=f32)
                for k in range(2):
                    out_ref[pl.ds(i * chunk, chunk), n + k] = part[:, k * LANES : (k + 1) * LANES].reshape(
                        chunk, group, LANES
                    )


def softplus(v):
    return jnp.maximum(v, 0.0) + jnp.log1p(jnp.exp(-jnp.abs(v)))


class Carry:
    def __init__(self, step, ends, total, a_all, held, got, sent, send_sem, recv_sem):
        self.step, self.ends, self.total, self.a_all = step, ends, total, a_all
        self.held, self.got, self.sent, self.send_sem, self.recv_sem = held, got, sent, send_sem, recv_sem
        self.place, self.peers = lax.axis_index("seq"), lax.axis_size("seq")
        self.rank = self.place if step > 0 else self.peers - 1 - self.place
        self.count, self.states = ends.shape[0], ends.shape[1]
        self.has_before, self.has_after = self.rank > 0, self.rank < self.peers - 1
        self.lag = jnp.minimum(self.rank, self.count)

    def enter(self, devices=1):
        spot = lax.axis_index("exp")
        barrier = pltpu.get_barrier_semaphore()

        @pl.when(self.has_before)
        def _():
            pl.semaphore_signal(barrier, inc=1, device_id={"seq": self.place - self.step}, device_id_type=MESH)

        @pl.when(self.has_after)
        def _():
            pl.semaphore_signal(barrier, inc=1, device_id={"seq": self.place + self.step}, device_id_type=MESH)

        for hop in range(1, devices):
            pl.semaphore_signal(barrier, inc=1, device_id={"exp": lax.rem(spot + hop, devices)}, device_id_type=MESH)
        neighbours = self.has_before.astype(jnp.int32) + self.has_after.astype(jnp.int32)
        pl.semaphore_wait(barrier, neighbours + (devices - 1))

    def hop(self, u):
        return pltpu.make_async_remote_copy(
            src_ref=self.sent.at[u], dst_ref=self.got.at[u], send_sem=self.send_sem.at[u], recv_sem=self.recv_sem.at[u],
            device_id={"seq": self.place + self.step}, device_id_type=MESH,
        )

    def handle(self, at):
        u = at - self.lag

        @pl.when(jnp.logical_and(u >= 0, u < self.count))
        def _():
            @pl.when(self.has_before)
            def _():
                self.hop(u).wait_recv()
                self.held[u] = self.got[u].astype(f32)

            @pl.when(jnp.logical_not(self.has_before))
            def _():
                self.held[u] = jnp.zeros(self.held.shape[1:], f32)

            @pl.when(self.has_after)
            def _():
                for n in range(self.states):
                    decay = jnp.exp2(self.a_all[u, n : n + 1, :] * self.total[u])
                    self.sent[u, n] = (self.ends[u, n] + decay * self.held[u, n]).astype(bf16)
                self.hop(u).start()

    def leave(self):
        @pl.loop(0, self.count)
        def _(u):
            @pl.when(self.has_after)
            def _():
                self.hop(u).wait_send()


def forward_kernel(
    rate_ref, wdt_ref, bias_ref, conv_ref, bc_ref, match_ref, a_all, gate_ref, skip_ref, cot_ref, target_ref,
    step_ref, z_ref, mixed_ref, start_ref, total_ref, cot_out,
    cot_got, pick_ref, kb_ref, b_all, c_all, step_all, ends, staged, cot_send, cot_recv, got, sent, send_sem, recv_sem, *, states, group, devices,
):
    at = pl.program_id(0)
    count = a_all.shape[0]
    j = lax.rem(at, count)
    carry_of = Carry(1, ends, total_ref, a_all, start_ref, got, sent, send_sem, recv_sem)
    rows = conv_ref.shape[0]
    moved = Dispatch(cot_ref, target_ref, cot_got, staged, cot_send, cot_recv, devices)

    @pl.when(at == 0)
    def _():
        carry_of.enter(devices)
        moved.start()
        kb_ref[...] = broad_cut(match_ref)
        spread(bc_ref, pick_ref, ((0, b_all), (1, c_all)), states, group)

    @pl.when(at < count)
    def _():
        pre = jnp.dot(rate_ref[...], wdt_ref[...], preferred_element_type=f32) + bias_ref[...]
        step = softplus(pre)
        step_ref[...] = step
        step_all[j] = step
        a_rows = [jnp.broadcast_to(a_all[j, n : n + 1, :], (group, LANES)) for n in range(states)]
        un = UN["state"]

        def body(i, carry):
            total, state = carry
            base = pl.multiple_of(i * un * group, un * group)
            x_two = conv_ref[pl.ds(base, un * group), :].astype(f32)
            for k in range(un):
                here = pl.ds(pl.multiple_of(base + k * group, group), group)
                dt = step_ref[here, :]
                masked = dt + kb_ref[here, :]
                u = dt * x_two[k * group : (k + 1) * group]
                total = total + masked
                state = [
                    jnp.exp2(masked * a_rows[n]) * state[n] + u * b_all[un * i + k, n] for n in range(states)
                ]
            return total, state

        zero = jnp.zeros((group, LANES), f32)
        total, state = lax.fori_loop(0, rows // (un * group), body, (zero, [zero] * states))
        total_ref[j] = total
        for n in range(states):
            ends[j, n] = state[n]

    carry_of.handle(at)

    @pl.when(at >= count)
    def _():
        a_rows = [jnp.broadcast_to(a_all[j, n : n + 1, :], (group, LANES)) for n in range(states)]
        un = UN["scan"]

        def body(i, state):
            base = pl.multiple_of(i * un * group, un * group)
            x_two = conv_ref[pl.ds(base, un * group), :].astype(f32)
            outs = []
            for k in range(un):
                here = pl.ds(pl.multiple_of(base + k * group, group), group)
                dt = step_all[j, here, :]
                masked = dt + kb_ref[here, :]
                u = dt * x_two[k * group : (k + 1) * group]
                state = [
                    jnp.exp2(masked * a_rows[n]) * state[n] + u * b_all[un * i + k, n] for n in range(states)
                ]
                outs.append(tree_sum(state[n] * c_all[un * i + k, n] for n in range(states)))
            whole = pl.ds(base, un * group)
            gate = gate_ref[whole, :]
            z = jnp.concatenate(outs, 0) + skip_ref[...] * x_two
            z_ref[whole, :] = z
            mixed_ref[whole, :] = (z * (gate * jax.nn.sigmoid(gate))).astype(bf16)
            return state

        lax.fori_loop(0, rows // (un * group), body, [start_ref[j, n] for n in range(states)])

    @pl.when(at == 2 * count - 1)
    def _():
        carry_of.leave()
        moved.wait()
        cot_out[...] = cot_got[...]


def broad_cut(match_ref):
    keep = match_ref[:, match_ref.shape[1] - 1 :]
    return jnp.broadcast_to((1.0 - keep) * cut, (match_ref.shape[0], LANES))


def backward_kernel(
    mg_ref, gate_ref, z_ref, step_ref, conv_ref, bc_ref, match_ref, a_all, total_ref, start_ref, rate_ref, wdt_ref,
    bias_ref, skip_ref, back_ref, outg_ref,
    gg_ref, low_ref, cg_ref, small_ref, mpg_ref, tok_ref, outo_ref,
    near_got, passed, far_got, mine, out_send, out_recv, out_load, back_send, back_recv, back_own, pick_ref, kb_ref, b_all, c_all, b_acc, c_acc, kept, dt_grad, g_all, rate_acc, ends, last, got, sent, send_sem, recv_sem, *, states, group, devices,
):
    at = pl.program_id(0)
    count = a_all.shape[0]
    j = lax.rem(at, count)
    carry_of = Carry(-1, ends, total_ref, a_all, last, got, sent, send_sem, recv_sem)
    steps = conv_ref.shape[0] // group
    rank = rate_ref.shape[1]
    zero = jnp.zeros((group, LANES), f32)
    spot = lax.axis_index("exp")

    def back_copy(hop):
        peer = lax.rem(spot + hop, devices)
        return pltpu.make_async_remote_copy(
            src_ref=back_ref.at[peer], dst_ref=tok_ref.at[spot], send_sem=back_send.at[hop - 1],
            recv_sem=back_recv.at[hop - 1], device_id={"exp": peer}, device_id_type=MESH,
        )

    near = spot + 1 - 2 * lax.rem(spot, 2)
    far = lax.rem(spot + 2, 4)
    across = lax.rem(near + 2, 4)
    rows_out = mine.shape[0]

    def out_rows(k):
        return outg_ref.at[pl.ds(pl.multiple_of(k * rows_out, rows_out), rows_out), :]

    def out_move(slot):
        if slot == 2:
            source, target, device = passed, far_got, far
        else:
            source, target, device = out_rows(across if slot else near), near_got.at[slot], near
        return pltpu.make_async_remote_copy(
            src_ref=source, dst_ref=target, send_sem=out_send.at[slot], recv_sem=out_recv.at[slot],
            device_id={"exp": device}, device_id_type=MESH,
        )

    def out_loads():
        return (
            pltpu.make_async_copy(out_rows(far), passed, out_load.at[0]),
            pltpu.make_async_copy(out_rows(spot), mine, out_load.at[1]),
        )

    def out_store():
        return pltpu.make_async_copy(mine, outo_ref, out_load.at[2])

    def own_copy():
        return pltpu.make_async_copy(back_ref.at[spot], tok_ref.at[spot], back_own.at[0])

    @pl.when(at == 0)
    def _():
        carry_of.enter(devices)
        out_move(1).start()
        out_move(0).start()
        for c in out_loads():
            c.start()
        own_copy().start()
        for hop in range(1, devices):
            back_copy(hop).start()
        kb_ref[...] = broad_cut(match_ref)
        spread(bc_ref, pick_ref, ((0, b_all), (1, c_all)), states, group)
        rate_acc[...] = jnp.zeros_like(rate_acc)

        @pl.loop(0, steps)
        def _(t):
            none = jnp.zeros((states, group, LANES), f32)
            b_acc[t] = none
            c_acc[t] = none

    @pl.when(at == 1)
    def _():
        for c in out_loads():
            c.wait()
        out_move(1).wait_recv()
        passed[...] = (passed[...].astype(f32) + near_got[1].astype(f32)).astype(bf16)
        out_move(2).start()

    @pl.when(at == 2 * count - 1)
    def _():
        out_move(0).wait_recv()
        out_move(2).wait_recv()
        mine[...] = (mine[...].astype(f32) + near_got[0].astype(f32) + far_got[...].astype(f32)).astype(bf16)
        out_store().start()

    @pl.when(at < count)
    def _():
        a_rows = [jnp.broadcast_to(a_all[j, n : n + 1, :], (group, LANES)) for n in range(states)]
        un = UN["adj"]

        def body(i, q):
            base = pl.multiple_of((steps // un - 1 - i) * un * group, un * group)
            whole = pl.ds(base, un * group)
            mixed_grad, gate = mg_ref[whole, :], gate_ref[whole, :]
            sig = jax.nn.sigmoid(gate)
            g_rows = mixed_grad * (gate * sig)
            g_all[j, whole, :] = g_rows.astype(bf16)
            gg_ref[whole, :] = (mixed_grad * z_ref[whole, :] * (sig * (1.0 + gate * (1.0 - sig)))).astype(bf16)
            for k in reversed(range(un)):
                t = un * (steps // un - 1 - i) + k
                here = pl.ds(pl.multiple_of(base + k * group, group), group)
                masked = step_ref[here, :] + kb_ref[here, :]
                g = g_rows[k * group : (k + 1) * group]
                q = [jnp.exp2(masked * a_rows[n]) * (c_all[t, n] * g + q[n]) for n in range(states)]
            return q

        q = lax.fori_loop(0, steps // un, body, [zero] * states)
        for n in range(states):
            ends[j, n] = q[n]

    carry_of.handle(at)

    @pl.when(at >= count)
    def _():
        a_rows = [jnp.broadcast_to(a_all[j, n : n + 1, :], (group, LANES)) for n in range(states)]
        fu, bu = UN["fwd"], UN["bwd"]

        def forward(i, state):
            base = pl.multiple_of(i * fu * group, fu * group)
            x_two = conv_ref[pl.ds(base, fu * group), :].astype(f32)
            g_two = g_all[j, pl.ds(base, fu * group), :].astype(f32)
            for k in range(fu):
                t = fu * i + k
                here = pl.ds(pl.multiple_of(base + k * group, group), group)
                dt = step_ref[here, :]
                masked = dt + kb_ref[here, :]
                g = g_two[k * group : (k + 1) * group]
                u = dt * x_two[k * group : (k + 1) * group]
                for n in range(states):
                    kept[t, n] = state[n]
                state = [jnp.exp2(masked * a_rows[n]) * state[n] + u * b_all[t, n] for n in range(states)]
                for n in range(states):
                    c_acc[t, n] += state[n] * g
            return state

        lax.fori_loop(0, steps // fu, forward, [start_ref[0, n] for n in range(states)])
        skip = skip_ref[...]

        def backward(i, carry):
            q, a_sum, skip_sum = carry
            base = pl.multiple_of((steps // bu - 1 - i) * bu * group, bu * group)
            x_two = conv_ref[pl.ds(base, bu * group), :].astype(f32)
            g_two = g_all[j, pl.ds(base, bu * group), :].astype(f32)
            for k in reversed(range(bu)):
                t = bu * (steps // bu - 1 - i) + k
                here = pl.ds(pl.multiple_of(base + k * group, group), group)
                dt = step_ref[here, :]
                masked = dt + kb_ref[here, :]
                g = g_two[k * group : (k + 1) * group]
                x = x_two[k * group : (k + 1) * group]
                u = dt * x
                skip_sum = skip_sum + g * x
                lam = [c_all[t, n] * g + q[n] for n in range(states)]
                for n in range(states):
                    b_acc[t, n] += lam[n] * u
                s_one = tree_sum(lam[n] * b_all[t, n] for n in range(states))
                q = [jnp.exp2(masked * a_rows[n]) * lam[n] for n in range(states)]
                w = [q[n] * kept[t, n] for n in range(states)]
                s_two = tree_sum(w[n] * a_rows[n] for n in range(states))
                a_sum = [a_sum[n] + dt * w[n] for n in range(states)]
                cg_ref[here, :] = skip * g + dt * s_one
                dt_grad[here, :] = x * s_one + ln2 * s_two
            return q, a_sum, skip_sum

        q, a_sum, skip_sum = lax.fori_loop(
            0, steps // bu, backward, ([last[j, n] for n in range(states)], [zero] * states, zero)
        )
        pre = jnp.dot(rate_ref[...], wdt_ref[...], preferred_element_type=f32) + bias_ref[...]
        pre_grad = dt_grad[...] * jax.nn.sigmoid(pre)
        low = pre_grad.astype(bf16)
        low_ref[...] = low
        rate_acc[...] += lax.dot_general(low, wdt_ref[...], (((1,), (1,)), ((), ())), preferred_element_type=f32)
        rows_of = [lax.dot_general(rate_ref[...], low, (((0,), (0,)), ((), ())), preferred_element_type=f32)]
        rows_of += [jnp.sum(a_sum[n], 0, keepdims=True) * a_all[j, n : n + 1, :] * ln2 for n in range(states)]
        rows_of += [jnp.sum(pre_grad, 0, keepdims=True), jnp.sum(skip_sum, 0, keepdims=True)]
        spare = small_ref.shape[0] - rank - states - 2
        small_ref[...] = jnp.concatenate(rows_of + [jnp.zeros((spare, LANES), f32)], 0).astype(bf16)

    @pl.when(at == 2 * count - 1)
    def _():
        carry_of.leave()
        out_store().wait()
        for slot in range(3):
            out_move(slot).wait_send()
        own_copy().wait()
        for hop in range(1, devices):
            back_copy(hop).wait()
        mpg_ref[:, :rank] = rate_acc[...].astype(bf16)
        lane = lax.broadcasted_iota(jnp.int32, (2 * LANES, 2 * states), 1)
        own = lax.broadcasted_iota(jnp.int32, (2 * LANES, 2 * states), 0) // LANES * states
        total = jnp.zeros((steps * group, 2 * states), f32)
        for n in range(states):
            both = [acc[:, n].reshape(steps * group, LANES) for acc in (b_acc, c_acc)]
            rows = jnp.concatenate(both, 1)
            pick = jnp.where(lane == own + n, 1.0, 0.0).astype(bf16)
            high = rows.astype(bf16)
            rest = (rows - high.astype(f32)).astype(bf16)
            total = total + jnp.dot(high, pick, preferred_element_type=f32)
            total = total + jnp.dot(rest, pick, preferred_element_type=f32)
        mpg_ref[:, rank:] = total.astype(bf16)


def rows_block(rows):
    return pl.BlockSpec((rows, LANES), lambda j: (0, j))


def whole_block(shape):
    return pl.BlockSpec(shape, lambda j: (0,) * len(shape))


def state_block(states, group):
    return pl.BlockSpec((1, states, group, LANES), lambda j: (j, 0, 0, 0))


def shape_of(shape, dtype):
    return jax.ShapeDtypeStruct(shape, dtype)


def params():
    return pltpu.CompilerParams(vmem_limit_bytes=vmem_cap)


def carry_scratch(shape):
    return [
        pltpu.VMEM(shape, bf16), pltpu.VMEM(shape, bf16), pltpu.SemaphoreType.DMA((shape[0],)),
        pltpu.SemaphoreType.DMA((shape[0],)),
    ]


def forward_scan(rate_low, w_dt, bias, conv_low, bc, match, a_blocks, gate, skip, cot, target, capacity, group, devices):
    rows, inner = conv_low.shape
    count, states, _ = a_blocks.shape
    rank = rate_low.shape[1]
    first = lambda at: (0, jnp.minimum(at, count - 1))
    both = lambda at: (0, lax.rem(at, count))
    second = lambda at: (0, jnp.maximum(at - count, 0))
    shape = (count, states, group, LANES)
    big = pltpu.VMEM((rows // group, states, group, LANES), f32)
    return pl.pallas_call(
        functools.partial(forward_kernel, states=states, group=group, devices=devices),
        grid=(2 * count,),
        in_specs=[
            whole_block((rows, rank)), pl.BlockSpec((rank, LANES), first), pl.BlockSpec((1, LANES), first),
            pl.BlockSpec((rows, LANES), both), whole_block(bc.shape),
            whole_block(match.shape), whole_block(a_blocks.shape), pl.BlockSpec((rows, LANES), second),
            pl.BlockSpec((1, LANES), second), whole_block(cot.shape), whole_block((1, rows)),
        ],
        out_specs=[
            pl.BlockSpec((rows, LANES), first), pl.BlockSpec((rows, LANES), second), pl.BlockSpec((rows, LANES), second),
            whole_block(shape), whole_block((count, group, LANES)), whole_block((devices, capacity, cot.shape[1])),
        ],
        out_shape=[
            shape_of((rows, inner), f32), shape_of((rows, inner), f32), shape_of((rows, inner), bf16),
            shape_of(shape, f32), shape_of((count, group, LANES), f32), shape_of((devices, capacity, cot.shape[1]), bf16),
        ],
        scratch_shapes=[pltpu.VMEM((devices, capacity, cot.shape[1]), bf16), pltpu.VMEM((bc.shape[1], 2 * states * LANES), bf16)]
        + [pltpu.VMEM((rows, LANES), f32), big, big]
        + [pltpu.VMEM((count, rows, LANES), f32), pltpu.VMEM(shape, f32)]
        + [pltpu.VMEM((devices - 1, capacity, cot.shape[1]), bf16)]
        + [pltpu.SemaphoreType.DMA((devices - 1,)), pltpu.SemaphoreType.DMA((devices - 1,))] + carry_scratch(shape),
        compiler_params=pltpu.CompilerParams(collective_id=0, has_side_effects=True, vmem_limit_bytes=vmem_cap),
        name="forward_scan",
    )(rate_low, w_dt, bias, conv_low, bc, match, a_blocks, gate, skip, cot, target[None, :])


def backward_scan(mixed_grad, gate, z, step, conv_low, bc, match, a_blocks, total, start, rate_low, w_dt, bias, skip, back, out_grad, group, devices):
    rows, inner = conv_low.shape
    count, states, _ = a_blocks.shape
    rank = rate_low.shape[1]
    small_rows = -(-(rank + states + 2) // 16) * 16
    out_piece = (out_grad.shape[0] // devices, out_grad.shape[1])
    dma = pltpu.SemaphoreType.DMA
    first = lambda at: (0, jnp.minimum(at, count - 1))
    both = lambda at: (0, lax.rem(at, count))
    second = lambda at: (0, jnp.maximum(at - count, 0))
    shape = (count, states, group, LANES)
    big = pltpu.VMEM((rows // group, states, group, LANES), f32)
    return pl.pallas_call(
        functools.partial(backward_kernel, states=states, group=group, devices=devices),
        grid=(2 * count,),
        in_specs=[
            pl.BlockSpec((rows, LANES), first), pl.BlockSpec((rows, LANES), first), pl.BlockSpec((rows, LANES), first),
            pl.BlockSpec((rows, LANES), both), pl.BlockSpec((rows, LANES), second), whole_block(bc.shape),
            whole_block(match.shape), whole_block(a_blocks.shape), whole_block(total.shape),
            pl.BlockSpec((1, states, group, LANES), lambda at: (jnp.maximum(at - count, 0), 0, 0, 0)),
            whole_block((rows, rank)), pl.BlockSpec((rank, LANES), second), pl.BlockSpec((1, LANES), second),
            pl.BlockSpec((1, LANES), second), pl.BlockSpec(memory_space=pl.ANY), pl.BlockSpec(memory_space=pl.ANY),
        ],
        out_specs=[
            pl.BlockSpec((rows, LANES), lambda at: (0, jnp.minimum(at, count - 1) + count)),
            pl.BlockSpec((rows, LANES), second), pl.BlockSpec((rows, LANES), second),
            pl.BlockSpec((small_rows, LANES), second), whole_block((rows, rank + 2 * states)),
            pl.BlockSpec(memory_space=pl.ANY), pl.BlockSpec(memory_space=pl.ANY),
        ],
        out_shape=[
            shape_of((rows, 2 * inner), bf16), shape_of((rows, inner), bf16), shape_of((rows, inner), f32),
            shape_of((small_rows, inner), bf16), shape_of((rows, rank + 2 * states), bf16), shape_of(back.shape, bf16),
            shape_of(out_piece, bf16),
        ],
        scratch_shapes=[pltpu.VMEM((2,) + out_piece, bf16), pltpu.VMEM(out_piece, bf16), pltpu.VMEM(out_piece, bf16)]
        + [pltpu.VMEM(out_piece, bf16), dma((3,)), dma((3,)), dma((3,)), dma((devices - 1,)), dma((devices - 1,))]
        + [dma((1,)), pltpu.VMEM((bc.shape[1], 2 * states * LANES), bf16), pltpu.VMEM((rows, LANES), f32), big, big, big, big, big]
        + [pltpu.VMEM((rows, LANES), f32), pltpu.VMEM((count, rows, LANES), bf16)]
        + [pltpu.VMEM((rows, rank), f32), pltpu.VMEM(shape, f32), pltpu.VMEM(shape, f32)] + carry_scratch(shape),
        compiler_params=pltpu.CompilerParams(collective_id=1, has_side_effects=True, vmem_limit_bytes=64 << 20),
        name="backward_scan",
    )(mixed_grad, gate, z, step, conv_low, bc, match, a_blocks, total, start, rate_low, w_dt, bias, skip, back, out_grad)

def broad_match(match_ref, wide):
    @pl.when(pl.program_id(0) == 0)
    def _():
        for k in range(match_ref.shape[1]):
            wide[k] = jnp.broadcast_to(match_ref[:, k : k + 1], wide.shape[1:])


def front_kernel(
    token_ref, before_ref, gain_ref, wc_ref, wg_ref, cw_ref, cb_ref, compact_ref, wx_ref, ci_ref, low_ref, gate_ref, rate_ref, bc_ref,
    normed_ref, mixed_ref, rows_f, match_ref, *, halo, group,
):
    rows = low_ref.shape[0]
    broad_match(compact_ref, match_ref)

    @pl.when(pl.program_id(0) == 0)
    def _():
        def put(at, source):
            values = source.astype(f32)
            scale = lax.rsqrt(jnp.mean(values * values, -1, keepdims=True) + epsilon)
            normed_ref[at, :] = (values * scale * gain_ref[...]).astype(bf16)

        put(slice(0, halo), before_ref[...])
        tile = 256

        @pl.loop(0, rows // tile)
        def _(i):
            put(pl.ds(pl.multiple_of(halo + i * tile, halo), tile), token_ref[pl.ds(pl.multiple_of(i * tile, tile), tile), :])

    taps = cw_ref.shape[0]
    ci = jnp.dot(normed_ref[...], wc_ref[...], preferred_element_type=f32).astype(bf16)
    ci_ref[...] = ci
    rows_f[...] = ci.astype(f32)
    total = conv_total(rows_f, cw_ref, cb_ref, match_ref, halo, group, rows, taps)
    low = (total * jax.nn.sigmoid(total)).astype(bf16)
    low_ref[...] = low
    gate_ref[...] = jnp.dot(normed_ref[halo:, :], wg_ref[...], preferred_element_type=f32)
    part = jnp.dot(low, wx_ref[...], preferred_element_type=f32)

    @pl.when(pl.program_id(0) == 0)
    def _():
        mixed_ref[...] = part

    @pl.when(pl.program_id(0) > 0)
    def _():
        mixed_ref[...] += part

    @pl.when(pl.program_id(0) == pl.num_programs(0) - 1)
    def _():
        rank, wide = rate_ref.shape[1], bc_ref.shape[1] // 3
        rate_ref[...] = mixed_ref[:, :rank].astype(bf16)
        rest = mixed_ref[:, rank:]
        for k in range(3):
            part_low = rest.astype(bf16)
            bc_ref[:, k * wide : (k + 1) * wide] = part_low
            rest = rest - part_low.astype(f32)


def conv_total(rows_f, cw_ref, cb_ref, match_ref, halo, group, rows, taps):
    total = cb_ref[...] + cw_ref[taps - 1 : taps, :] * rows_f[halo : halo + rows, :]
    for k in range(taps - 1):
        at = halo - (taps - 1 - k) * group
        total = total + cw_ref[k : k + 1, :] * rows_f[at : at + rows, :] * match_ref[k]
    return total


def front(token_low, before_rows, gain, w_in, conv_w, conv_b, match, w_x, rank, halo, group, lanes):
    width, inner = w_in.shape[0], w_in.shape[1] // 2
    total_rows = token_low.shape[0] + halo
    rows, taps, mixed_width = total_rows - halo, conv_w.shape[0], w_x.shape[1]
    count = inner // lanes
    cols = lambda r: pl.BlockSpec((r, lanes), lambda j: (0, j))
    return pl.pallas_call(
        functools.partial(front_kernel, halo=halo, group=group),
        grid=(count,),
        in_specs=[
            whole_block(token_low.shape), whole_block(before_rows.shape), whole_block(gain.shape), cols(width),
            pl.BlockSpec((width, lanes), lambda j: (0, j + count)),
            cols(taps), cols(1), whole_block(match.shape), pl.BlockSpec((lanes, mixed_width), lambda j: (j, 0)),
        ],
        out_specs=[
            cols(total_rows), cols(rows), cols(rows), whole_block((rows, rank)), whole_block((rows, 3 * (mixed_width - rank))),
            whole_block((total_rows, width)),
        ],
        out_shape=[
            shape_of((total_rows, inner), bf16), shape_of((rows, inner), bf16), shape_of((rows, inner), f32),
            shape_of((rows, rank), bf16), shape_of((rows, 3 * (mixed_width - rank)), bf16), shape_of((total_rows, width), bf16),
        ],
        scratch_shapes=[pltpu.VMEM((rows, mixed_width), f32), pltpu.VMEM((total_rows, lanes), f32), pltpu.VMEM((match.shape[1], rows, lanes), f32)],
        compiler_params=params(),
        name="front",
    )(token_low, before_rows, gain, w_in, w_in, conv_w, conv_b, match, w_x)


def conv_back_kernel(
    cg_ref, low_ref, mpg_ref, wx_ref, ci_ref, cw_ref, cb_ref, compact_ref, proj_ref, pg_ref, ext_ref, small_ref, rows_f, ext, match_ref,
    *, halo, group,
):
    broad_match(compact_ref, match_ref)
    rows = pg_ref.shape[0]
    taps = cw_ref.shape[0]
    grad = cg_ref[...] + lax.dot_general(
        mpg_ref[...], wx_ref[...], (((1,), (1,)), ((), ())), preferred_element_type=f32
    )
    rows_f[...] = ci_ref[...].astype(f32)
    total = conv_total(rows_f, cw_ref, cb_ref, match_ref, halo, group, rows, taps)
    sig = jax.nn.sigmoid(total)
    grad = grad * (sig * (1.0 + total * (1.0 - sig)))
    x_part = lax.dot_general(mpg_ref[...], low_ref[...], (((0,), (0,)), ((), ())), preferred_element_type=f32)
    taps_grad = [None] * taps
    ext[:halo, :] = jnp.zeros((halo, ext.shape[1]), f32)
    ext[halo:, :] = grad * cw_ref[taps - 1 : taps, :]
    taps_grad[taps - 1] = jnp.sum(grad * rows_f[halo:, :], 0, keepdims=True)
    for k in range(taps - 1):
        at = halo - (taps - 1 - k) * group
        own = grad * match_ref[k]
        taps_grad[k] = jnp.sum(own * rows_f[at : at + rows, :], 0, keepdims=True)
        ext[at : at + rows, :] += own * cw_ref[k : k + 1, :]
    pg_ref[...] = ext[halo:, :].astype(bf16)
    ext_ref[:halo, :] = ext[:halo, :]
    ext_ref[halo:, :] = ext[rows:, :]
    spare = small_ref.shape[0] - x_part.shape[0] - taps - 1
    parts = [x_part] + taps_grad + [jnp.sum(grad, 0, keepdims=True), jnp.zeros((spare, ext.shape[1]), f32)]
    small_ref[...] = jnp.concatenate(parts, 0).astype(bf16)


def conv_back(cg, conv_low, mpg, w_x, ci, conv_w, conv_b, match, proj, halo, group, lanes):
    rows, inner = cg.shape
    taps, mixed_width = conv_w.shape[0], w_x.shape[1]
    small_rows = -(-(mixed_width + taps + 1) // 16) * 16
    cols = lambda r: pl.BlockSpec((r, lanes), lambda j: (0, j))
    return pl.pallas_call(
        functools.partial(conv_back_kernel, halo=halo, group=group),
        grid=(inner // lanes,),
        in_specs=[
            cols(rows), cols(rows), whole_block((rows, mixed_width)), pl.BlockSpec((lanes, mixed_width), lambda j: (j, 0)),
            cols(rows + halo), cols(taps), cols(1), whole_block(match.shape),
            pl.BlockSpec(memory_space=pl.ANY),
        ],
        out_specs=[cols(rows), cols(2 * halo), cols(small_rows)],
        out_shape=[shape_of(proj.shape, bf16), shape_of((2 * halo, inner), f32), shape_of((small_rows, inner), bf16)],
        scratch_shapes=[pltpu.VMEM((rows + halo, lanes), f32), pltpu.VMEM((rows + halo, lanes), f32)]
        + [pltpu.VMEM((match.shape[1], rows, lanes), f32)],
        input_output_aliases={8: 0},
        compiler_params=params(),
        name="conv_back",
    )(cg, conv_low, mpg, w_x, ci, conv_w, conv_b, match, proj)

def routing(low, router, experts):
    logits = jnp.dot(low, router, preferred_element_type=f32)
    lane = lax.broadcasted_iota(jnp.int32, logits.shape, 1)
    logits = jnp.where(lane < experts, logits, -1e30)
    raised = jnp.exp(logits - jnp.max(logits, -1, keepdims=True))
    return raised / jnp.sum(raised, -1, keepdims=True)


def expert_kernel(
    rows_ref, cot_ref, up_ref, down_ref, router_ref, turned_ref, chosen_ref, out_ref, back_ref, upg_ref, downg_ref, routerg_ref,
    grad, out_acc, back_acc, active, pre_grad, prob, *, tile, experts,
):
    first = pl.program_id(0) == 0
    final = pl.program_id(0) == pl.num_programs(0) - 1
    slots, width = cot_ref.shape
    tiles = [slice(i * tile, (i + 1) * tile) for i in range(slots // tile)]

    @pl.when(first)
    def _():
        for at in tiles:
            own = routing(rows_ref[at, :], router_ref[...], experts)
            prob[at, :] = own
            gate = jnp.sum(own * chosen_ref[...], -1, keepdims=True)
            grad[at, :] = (gate * cot_ref[at, :].astype(f32)).astype(bf16)
            out_acc[at, :] = jnp.zeros((tile, width), f32)
            back_acc[at, :] = jnp.zeros((tile, width), f32)

    for at in tiles:
        pre = jnp.dot(rows_ref[at, :], up_ref[...], preferred_element_type=f32)
        act_grad = lax.dot_general(grad[at, :], down_ref[...], (((1,), (1,)), ((), ())), preferred_element_type=f32)
        half = 0.5 * lax.erf(pre * 0.7071067811865476) + 0.5
        active[at, :] = (pre * half).astype(bf16)
        slope = half + pre * (jnp.exp(pre * pre * -0.5) * 0.3989422804014327)
        pre_grad[at, :] = (act_grad * slope).astype(bf16)
    for at in tiles:
        out_acc[at, :] += jnp.dot(active[at, :], down_ref[...], preferred_element_type=f32)
        back_acc[at, :] += lax.dot_general(
            pre_grad[at, :], up_ref[...], (((1,), (1,)), ((), ())), preferred_element_type=f32
        )
    downg_ref[...] = lax.dot_general(
        active[...], grad[...], (((0,), (0,)), ((), ())), preferred_element_type=f32
    ).astype(bf16)
    upg_ref[...] = lax.dot_general(
        rows_ref[...], pre_grad[...], (((0,), (0,)), ((), ())), preferred_element_type=f32
    ).astype(bf16)

    @pl.when(final)
    def _():
        routerg_ref[...] = jnp.zeros_like(routerg_ref)
        for at in tiles:
            out = out_acc[at, :].astype(bf16)
            out_ref[at, :] = out
            gate_grad = jnp.sum(out.astype(f32) * cot_ref[at, :].astype(f32), -1, keepdims=True)
            own = prob[at, :]
            gate = jnp.sum(own * chosen_ref[...], -1, keepdims=True)
            logit_grad = own * (chosen_ref[...] - gate) * gate_grad
            routerg_ref[...] += lax.dot_general(
                logit_grad, rows_ref[at, :].astype(f32), (((0,), (0,)), ((), ())), precision=highest,
                preferred_element_type=f32,
            )
            through = jnp.dot(logit_grad, turned_ref[...], precision=highest, preferred_element_type=f32)
            back_ref[at, :] = (back_acc[at, :] + through).astype(bf16)


def one_expert(rows, cot, up, down, router_wide, chosen, experts):
    slots, width = cot.shape
    hidden = up.shape[1]
    hidden_tile, tile = hidden // 6, slots // 2
    full = whole_block((slots, width))
    cols = pl.BlockSpec((width, hidden_tile), lambda j: (0, j))
    deep = pl.BlockSpec((hidden_tile, width), lambda j: (j, 0))
    return pl.pallas_call(
        functools.partial(expert_kernel, tile=tile, experts=experts),
        grid=(hidden // hidden_tile,),
        in_specs=[
            full, full, cols, deep, whole_block(router_wide.shape), whole_block((LANES, width)), whole_block((1, LANES)),
        ],
        out_specs=[full, full, cols, deep, whole_block((LANES, width))],
        out_shape=[
            shape_of((slots, width), bf16), shape_of((slots, width), bf16), shape_of((width, hidden), bf16),
            shape_of((hidden, width), bf16), shape_of((LANES, width), f32),
        ],
        scratch_shapes=[
            pltpu.VMEM((slots, width), bf16), pltpu.VMEM((slots, width), f32), pltpu.VMEM((slots, width), f32),
            pltpu.VMEM((slots, hidden_tile), bf16), pltpu.VMEM((slots, hidden_tile), bf16), pltpu.VMEM((slots, LANES), f32),
        ],
        compiler_params=params(),
        name="one_expert",
    )(rows, cot, up, down, router_wide, router_wide.astype(f32).T, chosen)


def exp_barrier(spot, devices):
    barrier = pltpu.get_barrier_semaphore()
    for hop in range(1, devices):
        pl.semaphore_signal(barrier, inc=1, device_id={"exp": lax.rem(spot + hop, devices)}, device_id_type=MESH)
    pl.semaphore_wait(barrier, devices - 1)


class Dispatch:
    def __init__(self, rows_ref, target_ref, got_ref, staged, send_sem, recv_sem, devices):
        self.rows_ref, self.target_ref, self.got_ref, self.staged = rows_ref, target_ref, got_ref, staged
        self.send_sem, self.recv_sem, self.devices = send_sem, recv_sem, devices
        self.spot = lax.axis_index("exp")
        self.hops = [h for h in range(devices // 2, devices)] + [h for h in range(1, devices // 2)]

    def packed(self, k):
        capacity = self.got_ref.shape[1]
        slot = lax.broadcasted_iota(jnp.int32, (capacity, self.rows_ref.shape[0]), 0) + k * capacity
        pick = jnp.where(slot == self.target_ref[...], 1.0, 0.0).astype(bf16)
        return jnp.dot(pick, self.rows_ref[...], preferred_element_type=f32).astype(bf16)

    def copy(self, hop):
        return pltpu.make_async_remote_copy(
            src_ref=self.staged.at[hop - 1], dst_ref=self.got_ref.at[self.spot], send_sem=self.send_sem.at[hop - 1],
            recv_sem=self.recv_sem.at[hop - 1], device_id={"exp": lax.rem(self.spot + hop, self.devices)},
            device_id_type=MESH,
        )

    def start(self):
        for hop in self.hops:
            self.staged[hop - 1] = self.packed(lax.rem(self.spot + hop, self.devices))
            self.copy(hop).start()
        self.got_ref[self.spot] = self.packed(self.spot)

    def wait(self):
        for hop in self.hops:
            self.copy(hop).wait()


def route_kernel(
    mixed_ref, wout_ref, token_ref, gain_ref, router_ref, route_ref, target_ref, hidden_ref, gate_ref, got_ref, rows_ref,
    staged, send_sem, recv_sem, *, devices, experts, tile,
):
    exp_barrier(lax.axis_index("exp"), devices)
    width = wout_ref.shape[1]

    @pl.loop(0, mixed_ref.shape[0] // tile)
    def _(i):
        at = pl.ds(pl.multiple_of(i * tile, tile), tile)
        hidden = token_ref[at, :].astype(f32) + jnp.dot(mixed_ref[at, :], wout_ref[...], preferred_element_type=f32)
        hidden_ref[at, :] = hidden
        scale = lax.rsqrt(jnp.mean(hidden * hidden, -1, keepdims=True) + epsilon)
        low = (hidden * scale * gain_ref[...]).astype(bf16)
        rows_ref[at, :] = low
        prob = routing(low, router_ref[...], experts)
        lane = lax.broadcasted_iota(jnp.int32, prob.shape, 1)
        gate = jnp.sum(jnp.where(lane == route_ref[at, :], prob, 0.0), -1, keepdims=True)
        gate_ref[at, :] = jnp.broadcast_to(gate, (tile, LANES))

    moved = Dispatch(rows_ref, target_ref, got_ref, staged, send_sem, recv_sem, devices)
    moved.start()
    moved.wait()


def routed(mixed_low, w_out, token_low, gain, router_wide, route_col, target, capacity, devices, experts):
    vm = pl.BlockSpec(memory_space=pltpu.VMEM)
    dma = pltpu.SemaphoreType.DMA
    rows, width = token_low.shape
    return pl.pallas_call(
        functools.partial(route_kernel, devices=devices, experts=experts, tile=256),
        in_specs=[vm] * 7,
        out_specs=[vm] * 3,
        out_shape=[
            shape_of((rows, width), f32), shape_of((rows, LANES), f32), shape_of((devices, capacity, width), bf16),
        ],
        scratch_shapes=[
            pltpu.VMEM((rows, width), bf16), pltpu.VMEM((devices - 1, capacity, width), bf16), dma((devices - 1,)),
            dma((devices - 1,)),
        ],
        compiler_params=pltpu.CompilerParams(collective_id=3, has_side_effects=True, vmem_limit_bytes=vmem_cap),
        name="routed",
    )(mixed_low, w_out, token_low, gain, router_wide, route_col, target[None, :])


def collect_kernel(
    sent_ref, target_ref, hidden_ref, cot_ref, gain_ref, hidden_grad_ref, branch_ref, gain_grad_ref, got, total, send_sem,
    recv_sem, *, devices, hops, tile,
):
    spot = lax.axis_index("exp")
    capacity = got.shape[1]
    count, width = hidden_ref.shape
    exp_barrier(spot, devices)
    copies = []
    for hop in hops:
        peer = lax.rem(spot + hop, devices)
        c = pltpu.make_async_remote_copy(
            src_ref=sent_ref.at[peer], dst_ref=got.at[devices - hop - 1], send_sem=send_sem.at[hop - 1],
            recv_sem=recv_sem.at[hop - 1], device_id={"exp": peer}, device_id_type=MESH,
        )
        c.start()
        copies.append(c)

    def spread_back(k, rows):
        slot = lax.broadcasted_iota(jnp.int32, (count, capacity), 1) + k * capacity
        pick = jnp.where(slot == target_ref[...], 1.0, 0.0).astype(bf16)
        return jnp.dot(pick, rows, preferred_element_type=f32)

    total[...] = spread_back(spot, sent_ref[spot])
    for hop, c in zip(hops, copies):
        c.wait_recv()
        total[...] += spread_back(lax.rem(spot + devices - hop, devices), got[devices - hop - 1])
    gain_grad_ref[...] = jnp.zeros_like(gain_grad_ref)

    @pl.loop(0, count // tile)
    def _(i):
        at = pl.ds(pl.multiple_of(i * tile, tile), tile)
        grad = total[at, :]
        hidden = hidden_ref[at, :]
        scale = lax.rsqrt(jnp.mean(hidden * hidden, -1, keepdims=True) + epsilon)
        unit = hidden * scale
        gain_grad_ref[...] += jnp.sum(grad * unit, 0, keepdims=True)
        scaled = grad * gain_ref[...]
        hidden_grad = cot_ref[at, :].astype(f32) + scale * (
            scaled - unit * jnp.mean(scaled * unit, -1, keepdims=True)
        )
        hidden_grad_ref[at, :] = hidden_grad
        branch_ref[at, :] = hidden_grad.astype(bf16)

    for c in copies:
        c.wait_send()


def collect(blocks, target, hidden, cot, gain, devices):
    vm = pl.BlockSpec(memory_space=pltpu.VMEM)
    dma = pltpu.SemaphoreType.DMA
    capacity = blocks.shape[1]
    count, width = hidden.shape
    return pl.pallas_call(
        functools.partial(collect_kernel, devices=devices, hops=(2, 3, 1), tile=256),
        in_specs=[vm] * 5,
        out_specs=[vm] * 3,
        out_shape=[shape_of((count, width), f32), shape_of((count, width), bf16), shape_of((1, width), f32)],
        scratch_shapes=[
            pltpu.VMEM((devices - 1, capacity, width), bf16), pltpu.VMEM((count, width), f32), dma((devices - 1,)),
            dma((devices - 1,)),
        ],
        compiler_params=pltpu.CompilerParams(collective_id=4, has_side_effects=True, vmem_limit_bytes=vmem_cap),
        name="collect",
    )(blocks, target[:, None], hidden, cot, gain)

SEGMENTS = 4
WIDEN = 5
STARTS = (-4, 0, 1, 2)


def ring_order(place, peers):
    odd = lax.rem(place, 2)
    half = lax.div(place, 2)
    return half + odd * (peers - 1 - 2 * half)


def ring_member(position, peers):
    back = lax.div(2 * position, peers)
    return 2 * position + back * (2 * (peers - 1) + 1 - 4 * position)


class Rings:
    def __init__(self, own, total, sent, landed, send, recv, bases, sizes, peers):
        place = lax.axis_index("seq")
        self.own, self.total, self.sent, self.landed, self.send, self.recv = own, total, sent, landed, send, recv
        self.bases, self.sizes, self.peers = bases, sizes, peers
        self.position = ring_order(place, peers)
        self.after = ring_member(lax.rem(self.position + 1, peers), peers)
        self.before = ring_member(lax.rem(self.position + peers - 1, peers), peers)

    def rows(self, ring, steps):
        sign = 1 if ring % 2 == 0 else -1
        chunk = self.sizes[ring] // self.peers
        c = lax.rem(self.position + sign * steps + 2 * self.peers, self.peers)
        return pl.ds(pl.multiple_of(self.bases[ring] + c * chunk, 16), chunk)

    def target(self, ring):
        return {"seq": self.after if ring % 2 == 0 else self.before}

    def first(self, ring, s):
        chunk = self.sizes[ring] // self.peers
        return pltpu.make_async_remote_copy(
            src_ref=self.sent.at[ring, s, pl.ds(0, chunk)], dst_ref=self.landed.at[ring, s, pl.ds(0, chunk)],
            send_sem=self.send.at[ring, s], recv_sem=self.recv.at[ring, s], device_id=self.target(ring),
            device_id_type=MESH,
        )

    def second(self, ring, s):
        part = self.total.at[self.rows(ring, 1 - s)]
        at = self.peers - 1 + s
        return pltpu.make_async_remote_copy(
            src_ref=part, dst_ref=part, send_sem=self.send.at[ring, at], recv_sem=self.recv.at[ring, at],
            device_id=self.target(ring), device_id_type=MESH,
        )

    def begin(self, ring):
        chunk = self.sizes[ring] // self.peers
        self.sent[ring, 0, pl.ds(0, chunk)] = self.own[self.rows(ring, 0), :].astype(bf16)
        self.first(ring, 0).start()

    def advance(self, ring, s):
        peers, chunk = self.peers, self.sizes[ring] // self.peers

        @pl.when(jnp.logical_and(s >= 1, s <= peers - 2))
        def _():
            self.first(ring, s - 1).wait_recv()
            summed = self.landed[ring, s - 1, pl.ds(0, chunk)].astype(f32) + self.own[self.rows(ring, -s), :]
            self.sent[ring, s, pl.ds(0, chunk)] = summed.astype(bf16)
            self.first(ring, s).start()

        @pl.when(s == peers - 1)
        def _():
            self.first(ring, peers - 2).wait_recv()
            summed = self.landed[ring, peers - 2, pl.ds(0, chunk)].astype(f32) + self.own[self.rows(ring, 1), :]
            self.total[self.rows(ring, 1), :] = summed.astype(bf16)
            self.second(ring, 0).start()

        @pl.when(jnp.logical_and(s >= peers, s <= 2 * peers - 3))
        def _():
            self.second(ring, s - peers).wait_recv()
            self.second(ring, s - peers + 1).start()

        @pl.when(s == 2 * peers - 2)
        def _():
            self.second(ring, peers - 2).wait_recv()

    def drain(self):
        @pl.loop(0, self.peers - 1)
        def _(s):
            for ring in range(len(self.sizes)):
                self.first(ring, s).wait_send()
                self.second(ring, s).wait_send()


def finish_kernel(
    proj_ref, normed_ref, win_ref, outo_ref, small_ref, gain_ref, token_ref, hiddeng_ref, hidden_ref, chance_ref, target_ref,
    tok_ref, narrow_ref,
    in_sum_ref, out_sum_ref, small_sum_ref, tokens_grad_ref, block_ref, wide_ref,
    narrow_buf, wide_buf, narrow_sem, wide_sem,
    own, total, near_stage, small_all, gain_part, near_in, near_small, far_in, far_small, pass_in, pass_small, sent, landed, near_send, near_recv, far_send, far_recv, ring_send, ring_recv,
    *, peers, bases, sizes, halo, tile, gain_row,
):
    spot = lax.axis_index("exp")
    width, wide = near_in.shape[1:]
    rows_out = outo_ref.shape[0]
    rows_small, share = near_small.shape[1:]
    folds = wide // share
    count = proj_ref.shape[0]
    third = width // 3
    near = spot + 1 - 2 * lax.rem(spot, 2)
    far = lax.rem(spot + 2, 4)
    across = lax.rem(near + 2, 4)
    rings = Rings(own, total, sent, landed, ring_send, ring_recv, bases, sizes, peers)
    barrier = pltpu.get_barrier_semaphore()
    for device in ({"exp": near}, {"exp": far}, {"seq": rings.after}, {"seq": rings.before}):
        pl.semaphore_signal(barrier, inc=1, device_id=device, device_id_type=MESH)
    pl.semaphore_wait(barrier, 4)

    def columns(k, size):
        return pl.ds(pl.multiple_of(k * size, size), size)

    def copy(source, target, send, recv, device):
        return pltpu.make_async_remote_copy(
            src_ref=source, dst_ref=target, send_sem=send, recv_sem=recv, device_id=device, device_id_type=MESH
        )

    def in_rows(i):
        return slice(i * third, (i + 1) * third)

    def near_copy(slot, piece):
        k = across if slot else near
        if piece == 4:
            source, target = small_all.at[:, columns(k, share)], near_small.at[slot]
        else:
            at = pl.ds((piece - 1) * third, third)
            source, target = near_stage.at[slot, at], near_in.at[slot, at]
        return copy(source, target, near_send.at[slot, piece], near_recv.at[slot, piece], {"exp": near})

    def far_copy(piece):
        if piece == 4:
            source, target = pass_small, far_small
        else:
            at = pl.ds((piece - 1) * third, third)
            source, target = pass_in.at[at], far_in.at[at]
        return copy(source, target, far_send.at[piece], far_recv.at[piece], {"exp": far})

    def in_tile(i, k):
        part = lax.dot_general(
            normed_ref[pl.ds(halo, count), in_rows(i)], proj_ref[:, columns(k, wide)], (((0,), (0,)), ((), ())),
            preferred_element_type=f32,
        )
        scaled = part * win_ref[in_rows(i), columns(k, wide)].astype(f32)
        gain_part[in_rows(i), :] += tree_sum(scaled[:, h * LANES : (h + 1) * LANES] for h in range(wide // LANES))
        return part

    def into_own(base, values, add):
        size = values.shape[0]
        for h in range(values.shape[1] // share):
            at = slice(base + h * size, base + (h + 1) * size)
            part = values[:, h * share : (h + 1) * share]
            if add:
                own[at, :] += part
            else:
                own[at, :] = part

    def pad_own(n, used):
        if used < sizes[n]:
            own[bases[n] + used : bases[n] + sizes[n], :] = jnp.zeros((sizes[n] - used, share), f32)

    small_base = bases[3] + folds * third
    into_own(bases[0], outo_ref[...].astype(f32), False)
    pad_own(0, folds * rows_out)
    rings.begin(0)
    gain_part[...] = jnp.zeros_like(gain_part)
    small_all[...] = small_ref[...]
    for i in range(3):
        for slot, k in ((1, across), (0, near)):
            near_stage[slot, in_rows(i), :] = in_tile(i, k).astype(bf16)
            near_copy(slot, 1 + i).start()
        distant = in_tile(i, far)
        near_copy(1, 1 + i).wait_recv()
        pass_in[in_rows(i), :] = (distant + near_in[1, in_rows(i), :].astype(f32)).astype(bf16)
        far_copy(1 + i).start()
        mine = in_tile(i, spot)
        near_copy(0, 1 + i).wait_recv()
        into_own(bases[1 + i], mine + near_in[0, in_rows(i), :].astype(f32), False)
        pad_own(1 + i, folds * third)
        rings.advance(0, jnp.int32(1 + i))
    quarter = width // 4
    for k in range(4):
        part = jnp.sum(gain_part[k * quarter : (k + 1) * quarter, :], -1, keepdims=True)
        eye = lax.broadcasted_iota(jnp.int32, (quarter, quarter), 0) == lax.broadcasted_iota(
            jnp.int32, (quarter, quarter), 1
        )
        row = jnp.sum(jnp.where(eye, part, 0.0), 0, keepdims=True) / gain_ref[:, k * quarter : (k + 1) * quarter]
        group = slice(gain_row, gain_row + 16)
        old = small_all[group, k * share : k * share + quarter].astype(f32)
        top = lax.broadcasted_iota(jnp.int32, old.shape, 0) == 0
        small_all[group, k * share : k * share + quarter] = jnp.where(top, row, old).astype(bf16)
    for slot in (1, 0):
        near_copy(slot, 4).start()
    near_copy(1, 4).wait_recv()
    pass_small[...] = (small_all[:, columns(far, share)].astype(f32) + near_small[1].astype(f32)).astype(bf16)
    far_copy(4).start()
    near_copy(0, 4).wait_recv()
    own[small_base : small_base + rows_small, :] = (
        small_all[:, columns(spot, share)].astype(f32) + near_small[0].astype(f32)
    )
    def arrived(ring):
        far_copy(ring).wait_recv()
        into_own(bases[ring], far_in[in_rows(ring - 1), :].astype(f32), True)
        if ring == SEGMENTS - 1:
            far_copy(4).wait_recv()
            own[small_base : small_base + rows_small, :] += far_small[...].astype(f32)
        rings.begin(ring)

    def place_rows(out_ref, values, i):
        group = out_ref.shape[0]
        steps = tile // group
        values = jnp.swapaxes(values.reshape(steps, group, width), 0, 1)
        out_ref[:, pl.ds(pl.multiple_of(i * steps, steps), steps), :] = values.astype(out_ref.dtype)

    def token_tile(i):
        at = pl.ds(pl.multiple_of(i * tile, tile), tile)
        grad = lax.dot_general(proj_ref[at, :], win_ref[...], (((1,), (1,)), ((), ())), preferred_element_type=f32)
        values = token_ref[at, :].astype(f32)
        scale = lax.rsqrt(jnp.mean(values * values, -1, keepdims=True) + epsilon)
        unit = values * scale
        scaled = grad * gain_ref[...]
        total_grad = hiddeng_ref[at, :] + scale * (scaled - unit * jnp.mean(scaled * unit, -1, keepdims=True))
        place_rows(tokens_grad_ref, total_grad, i)

    def block_tile(i):
        at = pl.ds(pl.multiple_of(i * tile, tile), tile)
        capacity = tok_ref.shape[1]
        gate = chance_ref[at, 0:1]
        tok = jnp.zeros((tile, width), f32)
        for k in range(tok_ref.shape[0]):
            slot = lax.broadcasted_iota(jnp.int32, (tile, capacity), 1) + k * capacity
            pick = jnp.where(slot == target_ref[at, :], 1.0, 0.0).astype(bf16)
            tok = tok + jnp.dot(pick, tok_ref[k], preferred_element_type=f32)
        place_rows(block_ref, hidden_ref[at, :] + gate * tok, i)

    tiles = count // tile
    pieces, piece = narrow_ref.shape[0] // tile, tile

    def load(i):
        at = pl.ds(pl.multiple_of(i * piece, piece), piece)
        return pltpu.make_async_copy(narrow_ref.at[at], narrow_buf.at[lax.rem(i, 2)], narrow_sem.at[lax.rem(i, 2)])

    def store(i):
        at = pl.ds(pl.multiple_of(i * piece, piece), piece)
        return pltpu.make_async_copy(wide_buf.at[lax.rem(i, 2)], wide_ref.at[at], wide_sem.at[lax.rem(i, 2)])

    load(0).start()

    def widen(i):
        @pl.when(i + 1 < pieces)
        def _():
            load(i + 1).start()

        load(i).wait()

        @pl.when(i >= 2)
        def _():
            store(i - 2).wait()

        wide_buf[lax.rem(i, 2)] = narrow_buf[lax.rem(i, 2)].astype(f32)
        store(i).start()

    @pl.loop(0, 2 * peers - 1 + STARTS[-1])
    def _(turn):
        for ring in range(SEGMENTS):
            step = turn - STARTS[ring]
            if ring:

                @pl.when(step == 0)
                def _():
                    arrived(ring)

            rings.advance(ring, step)

        late = turn - WIDEN

        @pl.when(jnp.logical_and(late >= 0, late < pieces))
        def _():
            widen(late)

        @pl.when(turn < tiles)
        def _():
            token_tile(turn)

        @pl.when(jnp.logical_and(turn >= tiles, turn < 2 * tiles))
        def _():
            block_tile(turn - tiles)

    for i in (pieces - 2, pieces - 1):
        store(i).wait()
    for i in range(3):
        for h in range(folds):
            at = slice(bases[1 + i] + h * third, bases[1 + i] + (h + 1) * third)
            in_sum_ref[in_rows(i), h * share : (h + 1) * share] = total[at, :].astype(f32)
    for h in range(folds):
        at = slice(bases[0] + h * rows_out, bases[0] + (h + 1) * rows_out)
        out_sum_ref[:, h * share : (h + 1) * share] = total[at, :].astype(f32)
    small_sum_ref[...] = total[small_base : small_base + rows_small, :].astype(f32)
    for piece in range(1, 5):
        for slot in (1, 0):
            near_copy(slot, piece).wait_send()
        far_copy(piece).wait_send()
    rings.drain()


def finish(proj, normed_ext, w_in, out_own, small, gain, token_low, hidden_grad, hidden_one, chance, target, tok, narrow, gain_row, group):
    peers, devices = lax.axis_size("seq"), lax.axis_size("exp")
    count, width = token_low.shape
    wide, rows_out = proj.shape[1] // devices, out_own.shape[0]
    rows_small, share = small.shape[0], small.shape[1] // devices
    folds, third, unit = wide // share, width // 3, 16 * peers
    used = (folds * rows_out, folds * third, folds * third, folds * third + rows_small)
    sizes = tuple(-(-u // unit) * unit for u in used)
    bases = tuple(sum(sizes[:i]) for i in range(SEGMENTS))
    length, chunk = sum(sizes), max(sizes) // peers
    vm = pl.BlockSpec(memory_space=pltpu.VMEM)
    dma = pltpu.SemaphoreType.DMA
    shapes = ((width, wide), (rows_small, share))
    return pl.pallas_call(
        functools.partial(
            finish_kernel, peers=peers, bases=bases, sizes=sizes, halo=normed_ext.shape[0] - count, tile=256,
            gain_row=gain_row,
        ),
        in_specs=[vm] * 12 + [pl.BlockSpec(memory_space=pl.ANY)],
        out_specs=[vm] * 5 + [pl.BlockSpec(memory_space=pl.ANY)],
        out_shape=[
            shape_of((width, wide), f32), shape_of((rows_out, wide), f32), shape_of((rows_small, share), f32),
            shape_of((group, count // group, width), f32), shape_of((group, count // group, width), bf16), shape_of(narrow.shape, f32),
        ],
        scratch_shapes=[
            pltpu.VMEM((2, 256, narrow.shape[1]), bf16), pltpu.VMEM((2, 256, narrow.shape[1]), f32), dma((2,)), dma((2,)),
            pltpu.VMEM((length, share), f32), pltpu.VMEM((length, share), bf16), pltpu.VMEM((2, width, wide), bf16),
            pltpu.VMEM(small.shape, bf16), pltpu.VMEM((width, LANES), f32),
        ]
        + [pltpu.VMEM((2,) + s, bf16) for s in shapes]
        + [pltpu.VMEM(s, bf16) for s in shapes]
        + [pltpu.VMEM(s, bf16) for s in shapes]
        + [pltpu.VMEM((SEGMENTS, peers - 1, chunk, share), bf16)] * 2
        + [dma((2, 5)), dma((2, 5)), dma((5,)), dma((5,)), dma((SEGMENTS, 2 * peers - 2)), dma((SEGMENTS, 2 * peers - 2))],
        compiler_params=pltpu.CompilerParams(collective_id=2, has_side_effects=True, vmem_limit_bytes=64 << 20),
        name="finish",
    )(
        proj, normed_ext, w_in, out_own, small, gain, token_low, hidden_grad, hidden_one, chance, target[:, None], tok,
        narrow,
    )

PIECES = 2


def gather_kernel(
    in_ref, small_ref, token_ref, cot_ref, ids_ref, win_ref, wsmall_ref, before_ref, before_ids, rows_ref, cot_rows_ref, edge_ref,
    near_sems, far_sems, pair_sems, edge_sems, own_sem, *, kernel_len,
):
    place, peers = lax.axis_index("seq"), lax.axis_size("seq")
    spot = lax.axis_index("exp")
    near = spot + 1 - 2 * lax.rem(spot, 2)
    far = lax.rem(spot + 2, 4)
    bit = lax.rem(place, 2)
    pair = place + 1 - 2 * bit
    width, wide = in_ref.shape
    share = small_ref.shape[1]
    chunk = width // 2 // PIECES
    has_before, has_after = place > 0, place < peers - 1
    barrier = pltpu.get_barrier_semaphore()
    for target in ({"exp": near}, {"exp": far}, {"seq": pair}):
        pl.semaphore_signal(barrier, inc=1, device_id=target, device_id_type=MESH)

    @pl.when(has_before)
    def _():
        pl.semaphore_signal(barrier, inc=1, device_id={"seq": place - 1}, device_id_type=MESH)

    @pl.when(has_after)
    def _():
        pl.semaphore_signal(barrier, inc=1, device_id={"seq": place + 1}, device_id_type=MESH)

    pl.semaphore_wait(barrier, 3 + has_before.astype(jnp.int32) + has_after.astype(jnp.int32))

    def columns(ref, k, size):
        return ref.at[:, pl.ds(pl.multiple_of(k * size, size), size)]

    def rows(k, half, piece):
        at = pl.multiple_of((half * PIECES + piece) * chunk, chunk)
        return win_ref.at[pl.ds(at, chunk), pl.ds(pl.multiple_of(k * wide, wide), wide)]

    def copy(source, target, sems, slot, device):
        return pltpu.make_async_remote_copy(
            src_ref=source, dst_ref=target, send_sem=sems.at[0, slot], recv_sem=sems.at[1, slot], device_id=device,
            device_id_type=MESH,
        )

    def edge_copies():
        return (
            copy(edge_ref, before_ref, edge_sems, 0, {"seq": place + 1}),
            copy(ids_ref, before_ids, edge_sems, 1, {"seq": place + 1}),
        )

    outward = []
    for piece in range(PIECES):
        at = pl.multiple_of((bit * PIECES + piece) * chunk, chunk)
        outward.append(copy(in_ref.at[pl.ds(at, chunk), :], rows(spot, bit, piece), far_sems, piece, {"exp": far}))
    outward.insert(0, copy(small_ref, columns(wsmall_ref, spot, share), far_sems, PIECES, {"exp": far}))
    for c in outward:
        c.start()
    beside = [
        copy(small_ref, columns(wsmall_ref, spot, share), near_sems, 0, {"exp": near}),
        copy(in_ref, columns(win_ref, spot, wide), near_sems, 1, {"exp": near}),
    ]
    for c in beside:
        c.start()
    group, part_len, features = token_ref.shape

    def by_place(source, start, steps):
        values = source[:, pl.ds(start, steps), :].astype(f32)
        return jnp.swapaxes(values, 0, 1).reshape(steps * group, features).astype(bf16)

    edge_ref[...] = by_place(token_ref, part_len - 8, 8)[(8 - kernel_len) * group :, :]

    @pl.when(has_after)
    def _():
        for c in edge_copies():
            c.start()

    @pl.when(jnp.logical_not(has_before))
    def _():
        before_ref[...] = jnp.zeros_like(before_ref)
        before_ids[...] = jnp.zeros_like(before_ids)

    own = [
        pltpu.make_async_copy(in_ref, columns(win_ref, spot, wide), own_sem.at[0]),
        pltpu.make_async_copy(small_ref, columns(wsmall_ref, spot, share), own_sem.at[1]),
    ]
    for c in own:
        c.start()
    tile = 16

    @pl.loop(0, part_len // tile)
    def _(i):
        start = pl.multiple_of(i * tile, tile)
        at = pl.ds(pl.multiple_of(i * tile * group, tile * group), tile * group)
        rows_ref[at, :] = by_place(token_ref, start, tile)
        cot_rows_ref[at, :] = by_place(cot_ref, start, tile)

    outward[0].wait_recv()
    beside.append(copy(columns(wsmall_ref, far, share), columns(wsmall_ref, far, share), near_sems, 2, {"exp": near}))
    beside[-1].start()
    crossing = []
    for piece in range(PIECES):
        outward[1 + piece].wait_recv()
        part = rows(far, bit, piece)
        crossing.append(copy(part, part, pair_sems, piece, {"seq": pair}))
        crossing[-1].start()
        beside.append(copy(part, part, near_sems, 3 + piece, {"exp": near}))
        beside[-1].start()
    for piece in range(PIECES):
        crossing[piece].wait_recv()
        part = rows(far, 1 - bit, piece)
        beside.append(copy(part, part, near_sems, 3 + PIECES + piece, {"exp": near}))
        beside[-1].start()
    for c in beside:
        c.wait_recv()
    for c in outward + beside + crossing:
        c.wait_send()
    for c in own:
        c.wait()

    @pl.when(has_before)
    def _():
        for c in edge_copies():
            c.wait_recv()

    @pl.when(has_after)
    def _():
        for c in edge_copies():
            c.wait_send()


def gather_weights(in_shard, small, tokens, cot, ids, kernel_len, devices):
    group, part_len, width = tokens.shape
    edge = shape_of((kernel_len * group, width), bf16)
    rows = shape_of((part_len * group, width), bf16)
    vm = pl.BlockSpec(memory_space=pltpu.VMEM)
    dma = pltpu.SemaphoreType.DMA
    return pl.pallas_call(
        functools.partial(gather_kernel, kernel_len=kernel_len),
        in_specs=[pl.BlockSpec(memory_space=pl.ANY), vm, vm, vm, vm],
        out_specs=[pl.BlockSpec(memory_space=pl.ANY), vm, vm, vm, vm, vm],
        out_shape=[
            shape_of((in_shard.shape[0], in_shard.shape[1] * devices), bf16),
            shape_of((small.shape[0], small.shape[1] * devices), bf16), shape_of(edge.shape, edge.dtype),
            shape_of(ids.shape, ids.dtype), rows, rows,
        ],
        scratch_shapes=[pltpu.VMEM(edge.shape, bf16), dma((2, 3 + 2 * PIECES)), dma((2, PIECES + 1)), dma((2, PIECES)), dma((2, 2)), dma((2,))],
        compiler_params=pltpu.CompilerParams(collective_id=5, has_side_effects=True, vmem_limit_bytes=32 << 20),
        name="gather_weights",
    )(in_shard, small, tokens, cot, ids)

def rms_norm(values, gain):
    return values * lax.rsqrt(jnp.mean(values * values, -1, keepdims=True) + epsilon) * gain


def passed_along(value, axis, steps):
    count = lax.axis_size(axis)
    initial, last = (max(0, -steps), min(count, count - steps))
    return lax.ppermute(value, axis, [(source, source + steps) for source in range(initial, last)])


def by_time(values):
    values = jnp.swapaxes(values, 0, 1)
    return values.reshape((values.shape[0] * values.shape[1],) + values.shape[2:])


def packed_small(norm_gain, conv_weight, conv_bias, x_proj, dt_proj, dt_bias, a_log, d_skip, moe_gain, router):
    share = conv_bias.shape[0]
    packed = [conv_weight, conv_bias[None], x_proj.T, dt_proj, dt_bias[None], a_log.T, d_skip[None]]
    narrow = jnp.concatenate([norm_gain[None], moe_gain[None], router.T], 0)
    total = jnp.concatenate(packed + [narrow.reshape(-1, share)], 0)
    return jnp.pad(total, ((0, -total.shape[0] % 16), (0, 0))), [p.shape[0] for p in packed], narrow.shape


def unpacked_small(whole, counts, narrow_shape, devices):
    out, at = [], 0
    for c in counts:
        out.append(whole[at : at + c])
        at += c
    share = whole.shape[1] // devices
    fold = narrow_shape[0] * narrow_shape[1] // share
    rest = whole[at : at + fold].reshape(fold, devices, share).transpose(1, 0, 2).reshape((devices,) + narrow_shape)
    rest = rest.transpose(1, 0, 2).reshape(narrow_shape[0], -1)
    return out, rest[0], rest[1], rest[2:].T


def local(
    tokens, segment_ids, routes, slot_index, norm_gain, in_proj, conv_weight, conv_bias, x_proj, dt_proj, dt_bias,
    a_log, d_skip, out_proj, moe_gain, router, expert_up, expert_down, cotangent,
):
    seq_count, part_len, width = tokens.shape
    row_count = seq_count * part_len
    group = seq_count
    kernel_len = conv_weight.shape[0]
    state_width = a_log.shape[1]
    rank_width = dt_proj.shape[0]
    halo = kernel_len * group
    devices = lax.axis_size("exp")
    doc_ids = segment_ids + 1
    edge_start = part_len - kernel_len
    edge_ids = jnp.pad(doc_ids[:, edge_start:], ((0, 0), (0, LANES - kernel_len)))
    small_shard, counts, narrow_shape = packed_small(
        norm_gain, conv_weight, conv_bias, x_proj, dt_proj, dt_bias, a_log, d_skip, moe_gain, router
    )
    w_in, small_whole, before_rows, before_ids, token_low, cot_rows = gather_weights(
        in_proj, small_shard, tokens, cotangent, edge_ids, kernel_len, devices
    )
    out_proj, small_whole = lax.optimization_barrier((out_proj, small_whole))
    w_out = lax.all_gather(out_proj, "exp", axis=0, tiled=True)
    (w_conv, b_conv, w_x_t, w_dt, b_dt, log_decay, skip_gain), gain_one, gain_two, w_router = unpacked_small(
        small_whole, counts, narrow_shape, devices
    )
    inner_width = w_out.shape[0]
    expert_total = w_router.shape[1]
    capacity = 5 * row_count // (4 * expert_total)
    blocks = inner_width // LANES

    ext_ids = jnp.concatenate([before_ids[:, :kernel_len], doc_ids], 1)
    match = jnp.stack([ext_ids[:, 1 + k : 1 + k + part_len] == doc_ids for k in range(kernel_len - 1)])
    match = jnp.transpose(match, (2, 1, 0)).reshape(row_count, kernel_len - 1).astype(f32)
    lanes = 2 * LANES
    gain_one = gain_one.astype(f32)[None]
    gain_two = gain_two.astype(f32)[None]
    route_rows = by_time(routes)
    slot_rows = by_time(slot_index)
    target = jnp.where(
        slot_rows < capacity, route_rows * capacity + slot_rows, expert_total * capacity
    )
    w_conv, b_conv = w_conv.astype(f32), b_conv.astype(f32)
    w_x = w_x_t.T
    ci, conv_low, gate, rate_low, bc, normed_ext = front(
        token_low, before_rows, gain_one, w_in, w_conv, b_conv, match, w_x, rank_width, halo, group, lanes
    )
    bias = b_dt.astype(f32)
    skip = skip_gain.astype(f32)
    a_mat = -jnp.exp(log_decay.astype(f32))
    a2 = a_mat * log2e
    a_blocks = a2.reshape(state_width, blocks, LANES).transpose(1, 0, 2)
    step, z, mixed_low, start, total, cot_recv = forward_scan(
        rate_low, w_dt, bias, conv_low, bc, match, a_blocks, gate, skip, cot_rows, target, capacity, group, devices
    )
    route_col = route_rows[:, None]
    router_wide = jnp.pad(w_router, ((0, 0), (0, LANES - expert_total)))
    hidden_one, chance, received = routed(
        mixed_low, w_out, token_low, gain_two, router_wide, route_col, target, capacity, devices, expert_total
    )
    chosen = (jnp.arange(LANES) == lax.axis_index("exp")).astype(f32)[None]
    expert_out, rows_back, up_grad, down_grad, router_grad_t = one_expert(
        received.reshape(devices * capacity, width), cot_recv.reshape(devices * capacity, width), expert_up[0],
        expert_down[0], router_wide, chosen, expert_total,
    )
    hidden_grad, branch_grad, gain_two_grad = collect(
        rows_back.reshape(devices, capacity, width), target, hidden_one, cot_rows, gain_two, devices
    )
    peers = lax.axis_size("seq")
    order = [list(range(0, peers, 2)) + list(range(peers - 1, 0, -2))]

    def scattered(values):
        return lax.psum_scatter(values, "seq", scatter_dimension=0, axis_index_groups=order, tiled=True)

    def regathered(part):
        return lax.all_gather(part, "seq", axis=0, axis_index_groups=order, tiled=True)

    down_part = scattered(down_grad)
    up_part = scattered(up_grad)
    out_proj_grad = jnp.dot(mixed_low.T, branch_grad, preferred_element_type=f32)
    mixed_grad = jnp.dot(branch_grad, w_out.T, preferred_element_type=f32)
    out_proj_grad = out_proj_grad.astype(bf16)
    down_part, mixed_grad, out_proj_grad = lax.optimization_barrier((down_part, mixed_grad, out_proj_grad))
    down_sum = regathered(down_part)
    proj, rate_pre_low, cg, small_one, mixed_proj_grad, tok, out_own = backward_scan(
        mixed_grad, gate, z, step, conv_low, bc, match, a_blocks, total, start, rate_low, w_dt, bias, skip,
        expert_out.reshape(devices, capacity, width), out_proj_grad, group, devices,
    )
    up_part, cg = lax.optimization_barrier((up_part, cg))
    up_sum = regathered(up_part)
    proj, ends, small_two = conv_back(
        cg, conv_low, mixed_proj_grad, w_x, ci, w_conv, b_conv, match, proj, halo, group, lanes
    )
    edge_back = passed_along(ends[:halo].astype(bf16), "seq", -1).astype(f32)
    proj = lax.dynamic_update_slice(proj, (ends[halo:] + edge_back).astype(bf16), (row_count - halo, 0))

    narrow = jnp.concatenate([jnp.zeros_like(gain_two_grad), gain_two_grad, router_grad_t[:expert_total]], 0)
    share, own_width = inner_width // devices, width // devices
    narrow = narrow.reshape(narrow.shape[0], devices, own_width)
    narrow = jnp.pad(narrow, ((0, -narrow.shape[0] % 16), (0, 0), (0, share - own_width))).astype(bf16)
    packed = jnp.concatenate([small_one, small_two, narrow.reshape(-1, inner_width)], 0)
    gain_row = small_one.shape[0] + small_two.shape[0]
    in_sum, out_sum, sums, tokens_grad, block_out, down_wide = finish(
        proj, normed_ext, w_in, out_own, packed, gain_one, token_low, hidden_grad, hidden_one, chance,
        target, tok, down_sum, gain_row, group,
    )
    at, own = 0, []
    for first, rows in (
        (0, rank_width), (rank_width, state_width), (rank_width + state_width, 1), (rank_width + state_width + 1, 1)
    ):
        own.append(sums[first : first + rows])
    at = small_one.shape[0]
    mixed_width = mixed_proj_grad.shape[1]
    for first, rows in ((0, mixed_width), (mixed_width, kernel_len), (mixed_width + kernel_len, 1)):
        own.append(sums[at + first : at + first + rows])
    at += small_two.shape[0]
    own_narrow = sums[at : at + 2 + expert_total, :own_width]
    return (
        block_out,
        tokens_grad,
        own_narrow[0],
        in_sum,
        own[5],
        own[6][0],
        own[4].T,
        own[0],
        own[2][0],
        own[1].T,
        own[3][0],
        out_sum,
        own_narrow[1],
        own_narrow[2:].T,
        up_sum.astype(f32)[None],
        down_wide[None],
    )


def solution(mesh):
    in_specs = (
        P("exp", "seq", None),
        P("exp", "seq"),
        P("exp", "seq"),
        P("exp", "seq"),
        P("exp"),
        P(None, "exp"),
        P(None, "exp"),
        P("exp"),
        P("exp", None),
        P(None, "exp"),
        P("exp"),
        P("exp", None),
        P("exp"),
        P("exp", None),
        P("exp"),
        P("exp", None),
        P("exp", None, None),
        P("exp", None, None),
        P("exp", "seq", None),
    )
    out_specs = (
        P("exp", "seq", None),
        P("exp", "seq", None),
        P("exp"),
        P(None, "exp"),
        P(None, "exp"),
        P("exp"),
        P("exp", None),
        P(None, "exp"),
        P("exp"),
        P("exp", None),
        P("exp"),
        P("exp", None),
        P("exp"),
        P("exp", None),
        P("exp", None, None),
        P("exp", None, None),
    )
    return jax.shard_map(local, mesh=mesh, in_specs=in_specs, out_specs=out_specs, check_vma=False)
```
